256 devices in a mesh: slab: 64 (over x, z, core), img: 4 (over y).
Axes of the slice: x: 4, y: 4, z: 8, core: 2. Of those that a mesh axis runs over, the one named last changes fastest.
Arguments:
- volume: bfloat16 [32768, 256], P('slab'), may hold values from -6 to 6
- interp: bfloat16 [4, 64, 16, 32768], P('img', None, None, 'slab'), may hold values from -0.09375 to 0.09375
- block_index: int32 [4, 64, 64], P('img'), may hold values from 0 to 7
- images: bfloat16 [4, 1024, 128, 256], P('img', 'slab'), may hold values from -6 to 6
- defocus: float32 [4, 1024], P('img', 'slab'), may hold values from 5000 to 25000
- orient: int32 [4, 1024, 4], P('img', 'slab'), may hold values from 0 to 63, all different within a row
Outputs:
- update: float32 [32768, 256], P('slab')
- weights: float32 [4, 1024, 64], P('img', 'slab')
The draws below stay inside these ranges and needn't reach their ends.
Inputs may be any that keep to these rules, and one draw needn't show every extreme that they name: `orient`: each image lists 4 different orientations of its group.
All inputs are finite; a program needn't handle non-finite values.
Results may differ from the reference program's by a relative error of at most 0.0077.
Values may be sent and summed in bfloat16 or wider, within the bound.
A program may use at most 64 MiB of HBM per device.

```python
import math
import jax
import jax.numpy as jnp
from jax import lax

CUR = 128
BOX = 256
PB = 16
ROWS_SLAB = 512
TOPK = 4
NS = 16
NSLAB = 64
NGRP = 4
OGRP = 64
IMAGES_G = 1024
VROWS = 32768
NBLK = 8
N_SLAB = 64


def touch_ends(values, rng, low, largest):
    longest = values.shape.index(max(values.shape))
    spots = []
    for shift in (0, 1):
        where = [jax.random.randint(jax.random.fold_in(rng, axis), (), 0, length) for axis, length in enumerate(values.shape)]
        where[longest] = (where[longest] + shift) % values.shape[longest]
        spots.append(tuple(where))
    return values.at[spots[0]].set(low).at[spots[1]].set(largest)


def shard_levels(rng, dims, shards, least, top_value):
    def one(axis_at, shards_of):
        steps = jax.random.uniform(jax.random.fold_in(jax.random.fold_in(rng, 6), axis_at), (shards_of,), jnp.float32, least / len(shards), top_value / len(shards))
        return jnp.repeat(jnp.exp(steps), dims[axis_at] // shards_of).reshape((-1,) + (1,) * (len(dims) - axis_at - 1))

    gain = one(*shards[0])
    for cut in shards[1:]:
        gain = gain * one(*cut)
    return gain


def distinct(own_key, rows, number_of, top, lift):
    order = jax.random.permutation(jax.random.fold_in(own_key, 1), number_of)
    boost = order
    for power in range(3):
        boost = boost * boost // number_of
    boost = boost * lift // number_of
    chance = jax.random.randint(jax.random.fold_in(own_key, 2), (rows, number_of), 0, 4096) + boost
    sure = jax.random.permutation(jax.random.fold_in(own_key, 3), rows)[jnp.arange(number_of) % rows]
    chance = jnp.where(jnp.arange(rows)[:, None] == sure[None, :], 1 << 14, chance)
    score = chance * number_of + jnp.arange(number_of)
    return lax.top_k(score.astype(jnp.int32), top)[1].astype(jnp.int32)


def normal_values(key, dims, width, reach, shards=(), held_as=jnp.bfloat16):
    entries = width * jax.random.normal(key, dims, jnp.float32)
    if shards:
        entries = entries * shard_levels(key, dims, shards, -0.22, 0.18)
    return jnp.clip(entries, -reach, reach).astype(held_as)


def setup_inputs(seed: int = 0) -> dict:
    splits = jax.random.split(jax.random.key(seed), 7)
    volume = normal_values(splits[0], (VROWS, 2 * CUR), 1.0, 6.0, ((0, 64),))
    interp = normal_values(splits[1], (NGRP, OGRP, PB, VROWS), (ROWS_SLAB * N_SLAB * PB // CUR) ** -0.5, 0.09375, ((0, 4), (3, 64)))
    block_index = touch_ends(jax.random.randint(splits[2], (NGRP, OGRP, NSLAB), 0, NBLK), jax.random.fold_in(splits[2], 1), 0, NBLK - 1).astype(jnp.int32)
    images = normal_values(splits[3], (NGRP, IMAGES_G, CUR, 2 * CUR), 1.0, 6.0, ((0, 4), (1, 64)))
    defocus = jnp.clip(5000.0 + 20000.0 * jax.random.uniform(splits[4], (NGRP, IMAGES_G), jnp.float32) ** shard_levels(splits[4], (NGRP, IMAGES_G), ((0, 4), (1, 64)), -0.2, 0.2), 5000.0, 25000.0)
    orient = distinct(splits[5], NGRP * IMAGES_G, OGRP, TOPK, 1024).reshape((NGRP, IMAGES_G, TOPK))
    return {"volume": volume, "interp": interp, "block_index": block_index, "images": images, "defocus": defocus, "orient": orient}


wave_length = 0.0197
aberration = 27000000.0
amplitude = 0.1
grid_side = 4

def phase_tables(fourier, shifts, box):
    freq = (jnp.arange(fourier, dtype=jnp.int32) - fourier // 2).astype(jnp.float32)
    shift_steps = jnp.arange(shifts, dtype=jnp.int32)
    shift_x = (2 * (shift_steps // grid_side) - (grid_side - 1)).astype(jnp.float32)
    shift_y = (2 * (shift_steps % grid_side) - (grid_side - 1)).astype(jnp.float32)
    angle = 2.0 * math.pi / box * (freq[:, None, None] * shift_x + freq[None, :, None] * shift_y)
    forward = jnp.stack([jnp.cos(angle), jnp.sin(angle)], axis=1).reshape(2 * fourier * fourier, shifts)
    backward = jnp.stack([jnp.cos(angle), -jnp.sin(angle)], axis=1).reshape(2 * fourier * fourier, shifts)
    return (forward.astype(jnp.bfloat16), backward.T.astype(jnp.bfloat16))

def contrast(defocus_blk, fourier, box):
    freq = (jnp.arange(fourier, dtype=jnp.int32) - fourier // 2).astype(jnp.float32)
    wave_sq = (freq[:, None] * freq[:, None] + freq[None, :] * freq[None, :]) / (box * box)
    phase = math.pi * wave_length * defocus_blk[:, None, None] * wave_sq
    phase = phase - 0.5 * math.pi * aberration * wave_length ** 3 * wave_sq * wave_sq
    return -(math.sqrt(1.0 - amplitude * amplitude) * jnp.sin(phase) + amplitude * jnp.cos(phase))

def correlate(panels, image_blk, list_blk, defocus_blk, phase_fwd, phase_back, box):
    count = image_blk.shape[0]
    fourier = image_blk.shape[1]
    picks = list_blk.shape[1]
    shifts = phase_fwd.shape[1]
    ctf = contrast(defocus_blk, fourier, box)
    weighted = ctf[:, :, None, :] * image_blk.astype(jnp.float32).reshape(count, fourier, 2, fourier)
    real_u = weighted[:, None, :, 0]
    imag_u = weighted[:, None, :, 1]
    chosen = panels[list_blk].astype(jnp.float32).reshape(count, picks, fourier, 2, fourier)
    real_p = chosen[:, :, :, 0]
    imag_p = chosen[:, :, :, 1]
    product = jnp.stack([real_p * real_u + imag_p * imag_u, real_p * imag_u - imag_p * real_u], axis=3)
    product = product.astype(jnp.bfloat16).reshape(count * picks, 2 * fourier * fourier)
    scores = jnp.dot(product, phase_fwd, preferred_element_type=jnp.float32) / fourier
    scores = scores.reshape(count, picks * shifts)
    squared = scores * scores
    weights = squared / (lax.optimization_barrier(jnp.mean(squared, axis=1, keepdims=True)) + 1e-05)
    rounded = weights.astype(jnp.bfloat16).reshape(count * picks, shifts)
    spread = jnp.dot(rounded, phase_back, preferred_element_type=jnp.float32)
    spread = spread.reshape(count, picks, fourier, 2, fourier)
    real_e = spread[:, :, :, 0]
    imag_e = spread[:, :, :, 1]
    backed = jnp.stack([real_u * real_e - imag_u * imag_e, real_u * imag_e + imag_u * real_e], axis=3)
    backed = backed.astype(jnp.bfloat16).reshape(count * picks, 2 * fourier * fourier)
    return (weights, backed)

def reference(volume, interp, block_index, images, defocus, orient):
    phase_fwd, phase_back = phase_tables(CUR, NS, BOX)
    levels = jnp.arange(NBLK, dtype=jnp.int32)
    stacked_vol = volume.astype(jnp.float32).reshape(NSLAB, ROWS_SLAB, 2 * CUR)
    block = math.gcd(IMAGES_G, 128)
    block_total = IMAGES_G // block
    columns = jnp.zeros((NSLAB, ROWS_SLAB, 2 * CUR), jnp.float32)
    weight_list = []
    for group in range(NGRP):
        inter_g = interp[group].astype(jnp.float32).reshape(OGRP, PB, NSLAB, ROWS_SLAB)
        partial_value = jnp.einsum('jpsr,srx->jspx', inter_g, stacked_vol, precision=lax.Precision.HIGHEST)
        onehot = (block_index[group][:, :, None] == levels).astype(jnp.float32)
        panels = jnp.einsum('jsb,jspx->jbpx', onehot, partial_value, precision=lax.Precision.HIGHEST)
        panels = panels.reshape(OGRP, CUR, 2 * CUR).astype(jnp.bfloat16)

        def step_fn(accum, pieces):
            image_blk, list_blk, defocus_blk = pieces
            weights, backed = correlate(panels, image_blk, list_blk, defocus_blk, phase_fwd, phase_back, BOX)
            accum = accum + jax.ops.segment_sum(backed.astype(jnp.float32), list_blk.reshape(-1), num_segments=OGRP)
            return (accum, weights)
        start = jnp.zeros((OGRP, 2 * CUR * CUR), jnp.float32)
        accum, weights = lax.scan(step_fn, start, (images[group].reshape(block_total, block, CUR, 2 * CUR), orient[group].reshape(block_total, block, TOPK), defocus[group].reshape(block_total, block)))
        weight_list.append(weights.reshape(IMAGES_G, TOPK * NS))
        back_slices = accum.astype(jnp.bfloat16).reshape(OGRP, NBLK, PB, 2 * CUR)
        taken = jnp.take_along_axis(back_slices, block_index[group][:, :, None, None], axis=1)
        columns = columns + jnp.einsum('jpsr,jspx->srx', inter_g, taken.astype(jnp.float32), precision=lax.Precision.HIGHEST)
    update = (columns / math.sqrt(IMAGES_G)).reshape(VROWS, 2 * CUR)
    return (update, jnp.stack(weight_list))
```

```python
import math

import jax
import jax.numpy as jnp
from jax import lax
from jax.sharding import PartitionSpec as P

BOX = 256
NS = 16


wave_length = 0.0197
aberration = 27000000.0
amplitude = 0.1
grid_side = 4


def phase_tables(fourier, shifts, box):
    freq = (jnp.arange(fourier, dtype=jnp.int32) - fourier // 2).astype(jnp.float32)
    shift_steps = jnp.arange(shifts, dtype=jnp.int32)
    shift_x = (2 * (shift_steps // grid_side) - (grid_side - 1)).astype(jnp.float32)
    shift_y = (2 * (shift_steps % grid_side) - (grid_side - 1)).astype(jnp.float32)
    angle = 2.0 * math.pi / box * (freq[:, None, None] * shift_x + freq[None, :, None] * shift_y)
    forward = jnp.stack([jnp.cos(angle), jnp.sin(angle)], axis=1).reshape(
        2 * fourier * fourier, shifts
    )
    backward = jnp.stack([jnp.cos(angle), -jnp.sin(angle)], axis=1).reshape(
        2 * fourier * fourier, shifts
    )
    return (forward.astype(jnp.bfloat16), backward.T.astype(jnp.bfloat16))


def contrast(defocus_blk, fourier, box):
    freq = (jnp.arange(fourier, dtype=jnp.int32) - fourier // 2).astype(jnp.float32)
    wave_sq = (freq[:, None] * freq[:, None] + freq[None, :] * freq[None, :]) / (box * box)
    phase = math.pi * wave_length * defocus_blk[:, None, None] * wave_sq
    phase = phase - 0.5 * math.pi * aberration * wave_length**3 * wave_sq * wave_sq
    return -(math.sqrt(1.0 - amplitude * amplitude) * jnp.sin(phase) + amplitude * jnp.cos(phase))


def correlate(panels, image_blk, list_blk, defocus_blk, phase_fwd, phase_back, box):
    count = image_blk.shape[0]
    fourier = image_blk.shape[1]
    picks = list_blk.shape[1]
    shifts = phase_fwd.shape[1]
    ctf = contrast(defocus_blk, fourier, box)
    weighted = ctf[:, :, None, :] * image_blk.astype(jnp.float32).reshape(
        count, fourier, 2, fourier
    )
    real_u = weighted[:, None, :, 0]
    imag_u = weighted[:, None, :, 1]
    chosen = panels[list_blk].astype(jnp.float32).reshape(count, picks, fourier, 2, fourier)
    real_p = chosen[:, :, :, 0]
    imag_p = chosen[:, :, :, 1]
    product = jnp.stack(
        [real_p * real_u + imag_p * imag_u, real_p * imag_u - imag_p * real_u], axis=3
    )
    product = product.astype(jnp.bfloat16).reshape(count * picks, 2 * fourier * fourier)
    scores = jnp.dot(product, phase_fwd, preferred_element_type=jnp.float32) / fourier
    scores = scores.reshape(count, picks * shifts)
    squared = scores * scores
    weights = squared / (jnp.mean(squared, axis=1, keepdims=True) + 1e-05)
    rounded = weights.astype(jnp.bfloat16).reshape(count * picks, shifts)
    spread = jnp.dot(rounded, phase_back, preferred_element_type=jnp.float32)
    spread = spread.reshape(count, picks, fourier, 2, fourier)
    real_e = spread[:, :, :, 0]
    imag_e = spread[:, :, :, 1]
    backed = jnp.stack(
        [real_u * real_e - imag_u * imag_e, real_u * imag_e + imag_u * real_e], axis=3
    )
    backed = backed.astype(jnp.bfloat16).reshape(count * picks, 2 * fourier * fourier)
    return (weights, backed)


def on_device(volume, interp, block_index, images, defocus, orient):
    slab_count = lax.axis_size("slab")
    slab_index = lax.axis_index("slab")
    orient_count = interp.shape[1]
    ori_dev = orient_count // slab_count
    block_rows = interp.shape[2]
    fourier = images.shape[2]
    block_count = fourier // block_rows
    img_dev = images.shape[1]
    picks = orient.shape[2]
    levels = jnp.arange(block_count, dtype=jnp.int32)
    partial_value = jnp.einsum("jpr,rx->jpx", interp[0], volume, preferred_element_type=jnp.float32)
    owned_idx = lax.dynamic_slice_in_dim(block_index[0], slab_index * ori_dev, ori_dev, 0)
    received = lax.all_to_all(
        partial_value.reshape(slab_count, ori_dev * block_rows, 2 * fourier),
        "slab",
        split_axis=0,
        concat_axis=0,
        tiled=True,
    ).reshape(slab_count, ori_dev, block_rows, 2 * fourier)
    place = (owned_idx[:, :, None] == levels).astype(jnp.float32)
    summed = jnp.einsum(
        "osb,sopx->obpx", place, received, precision=lax.Precision.HIGHEST,
        preferred_element_type=jnp.float32,
    ).reshape(ori_dev, fourier, 2 * fourier)
    panels = lax.all_gather(summed.astype(jnp.bfloat16), "slab", axis=0, tiled=True)
    phase_fwd, phase_back = phase_tables(fourier, NS, BOX)
    blk = math.gcd(img_dev, 32)
    blk_total = img_dev // blk

    def per_block(pieces):
        image_blk, list_blk, defocus_blk = pieces
        return correlate(panels, image_blk, list_blk, defocus_blk, phase_fwd, phase_back, BOX)

    weights, backs = lax.map(
        per_block,
        (
            images[0].reshape(blk_total, blk, fourier, 2 * fourier),
            orient[0].reshape(blk_total, blk, picks),
            defocus[0].reshape(blk_total, blk),
        ),
    )
    all_slices = backs.reshape(img_dev * picks, 2 * fourier * fourier)
    member = (
        orient[0].reshape(-1)[:, None] == jnp.arange(orient_count, dtype=jnp.int32)[None, :]
    ).astype(jnp.bfloat16)
    contrib = lax.dot_general(
        member, all_slices, (((0,), (0,)), ((), ())), preferred_element_type=jnp.float32
    ).reshape(orient_count, fourier, 2 * fourier)
    back_own = lax.psum_scatter(contrib, "slab", scatter_dimension=0, tiled=True).astype(jnp.bfloat16)
    back_own = back_own.reshape(ori_dev, block_count, block_rows, 2 * fourier)
    chosen_back = (owned_idx[:, :, None] == levels).astype(jnp.bfloat16)
    outgoing = jnp.einsum(
        "osb,obpx->sopx", chosen_back, back_own, preferred_element_type=jnp.float32
    )
    outgoing = outgoing.astype(jnp.bfloat16).reshape(slab_count * ori_dev, block_rows, 2 * fourier)
    incoming = lax.all_to_all(outgoing, "slab", split_axis=0, concat_axis=0, tiled=True)
    column = jnp.einsum("jpr,jpx->rx", interp[0], incoming, preferred_element_type=jnp.float32)
    summed_cols = lax.psum(column, "img")
    update = summed_cols / math.sqrt(img_dev * slab_count)
    return (update, weights)


def solution(mesh):
    return jax.shard_map(
        on_device,
        mesh=mesh,
        in_specs=(
            P("slab", None),
            P("img", None, None, "slab"),
            P("img", None, None),
            P("img", "slab", None, None),
            P("img", "slab"),
            P("img", "slab", None),
        ),
        out_specs=(P("slab", None), P("img", "slab", None)),
        check_vma=False,
    )
```

```python
import math

import jax
import jax.numpy as jnp
from jax import lax
from jax.sharding import PartitionSpec as P

BOX = 256
NS = 16


wave_length = 0.0197
aberration = 27000000.0
amplitude = 0.1
grid_side = 4


def phase_tables(fourier, shifts, box):
    freq = (jnp.arange(fourier, dtype=jnp.int32) - fourier // 2).astype(jnp.float32)
    shift_steps = jnp.arange(shifts, dtype=jnp.int32)
    shift_x = (2 * (shift_steps // grid_side) - (grid_side - 1)).astype(jnp.float32)
    shift_y = (2 * (shift_steps % grid_side) - (grid_side - 1)).astype(jnp.float32)
    angle = 2.0 * math.pi / box * (freq[:, None, None] * shift_x + freq[None, :, None] * shift_y)
    forward = jnp.stack([jnp.cos(angle), jnp.sin(angle)], axis=1).reshape(
        2 * fourier * fourier, shifts
    )
    backward = jnp.stack([jnp.cos(angle), -jnp.sin(angle)], axis=1).reshape(
        2 * fourier * fourier, shifts
    )
    return (forward.astype(jnp.bfloat16), backward.T.astype(jnp.bfloat16))


def contrast(defocus_blk, fourier, box):
    freq = (jnp.arange(fourier, dtype=jnp.int32) - fourier // 2).astype(jnp.float32)
    wave_sq = (freq[:, None] * freq[:, None] + freq[None, :] * freq[None, :]) / (box * box)
    phase = math.pi * wave_length * defocus_blk[:, None, None] * wave_sq
    phase = phase - 0.5 * math.pi * aberration * wave_length**3 * wave_sq * wave_sq
    return -(math.sqrt(1.0 - amplitude * amplitude) * jnp.sin(phase) + amplitude * jnp.cos(phase))


def correlate(panels, image_blk, list_blk, defocus_blk, phase_fwd, phase_back, box):
    count = image_blk.shape[0]
    fourier = image_blk.shape[1]
    picks = list_blk.shape[1]
    shifts = phase_fwd.shape[1]
    ctf = contrast(defocus_blk, fourier, box)
    weighted = ctf[:, :, None, :] * image_blk.astype(jnp.float32).reshape(
        count, fourier, 2, fourier
    )
    real_u = weighted[:, None, :, 0]
    imag_u = weighted[:, None, :, 1]
    chosen = panels[list_blk].astype(jnp.float32).reshape(count, picks, fourier, 2, fourier)
    real_p = chosen[:, :, :, 0]
    imag_p = chosen[:, :, :, 1]
    product = jnp.stack(
        [real_p * real_u + imag_p * imag_u, real_p * imag_u - imag_p * real_u], axis=3
    )
    product = product.astype(jnp.bfloat16).reshape(count * picks, 2 * fourier * fourier)
    scores = jnp.dot(product, phase_fwd, preferred_element_type=jnp.float32) / fourier
    scores = scores.reshape(count, picks * shifts)
    squared = scores * scores
    weights = squared / (jnp.mean(squared, axis=1, keepdims=True) + 1e-05)
    rounded = weights.astype(jnp.bfloat16).reshape(count * picks, shifts)
    spread = jnp.dot(rounded, phase_back, preferred_element_type=jnp.float32)
    spread = spread.reshape(count, picks, fourier, 2, fourier)
    real_e = spread[:, :, :, 0]
    imag_e = spread[:, :, :, 1]
    backed = jnp.stack(
        [real_u * real_e - imag_u * imag_e, real_u * imag_e + imag_u * real_e], axis=3
    )
    backed = backed.astype(jnp.bfloat16).reshape(count * picks, 2 * fourier * fourier)
    return (weights, backed)


def on_device(volume, interp, block_index, images, defocus, orient):
    slab_count = lax.axis_size("slab")
    slab_index = lax.axis_index("slab")
    orient_count = interp.shape[1]
    ori_dev = orient_count // slab_count
    block_rows = interp.shape[2]
    fourier = images.shape[2]
    block_count = fourier // block_rows
    img_dev = images.shape[1]
    picks = orient.shape[2]
    levels = jnp.arange(block_count, dtype=jnp.int32)
    partial_value = jnp.einsum("jpr,rx->jpx", interp[0], volume, preferred_element_type=jnp.float32)
    owned_idx = lax.dynamic_slice_in_dim(block_index[0], slab_index * ori_dev, ori_dev, 0)
    received = lax.all_to_all(
        partial_value.reshape(slab_count, ori_dev * block_rows, 2 * fourier),
        "slab",
        split_axis=0,
        concat_axis=0,
        tiled=True,
    ).reshape(slab_count, ori_dev, block_rows, 2 * fourier)
    place = (owned_idx[:, :, None] == levels).astype(jnp.float32)
    summed = jnp.einsum(
        "osb,sopx->obpx", place, received, precision=lax.Precision.HIGHEST,
        preferred_element_type=jnp.float32,
    ).reshape(ori_dev, fourier, 2 * fourier)
    panels = lax.all_gather(summed.astype(jnp.bfloat16), "slab", axis=0, tiled=True)
    phase_fwd, phase_back = phase_tables(fourier, NS, BOX)
    blk = math.gcd(img_dev, 32)
    blk_total = img_dev // blk

    def per_block(pieces):
        image_blk, list_blk, defocus_blk = pieces
        return correlate(panels, image_blk, list_blk, defocus_blk, phase_fwd, phase_back, BOX)

    weights, backs = lax.map(
        per_block,
        (
            images[0].reshape(blk_total, blk, fourier, 2 * fourier),
            orient[0].reshape(blk_total, blk, picks),
            defocus[0].reshape(blk_total, blk),
        ),
    )
    all_slices = backs.reshape(img_dev * picks, 2 * fourier * fourier)
    member = (
        orient[0].reshape(-1)[:, None] == jnp.arange(orient_count, dtype=jnp.int32)[None, :]
    ).astype(jnp.bfloat16)
    contrib = lax.dot_general(
        member, all_slices, (((0,), (0,)), ((), ())), preferred_element_type=jnp.float32
    ).reshape(orient_count, fourier, 2 * fourier)
    back_own = lax.psum_scatter(
        contrib.astype(jnp.bfloat16), "slab", scatter_dimension=0, tiled=True
    )
    back_own = back_own.reshape(ori_dev, block_count, block_rows, 2 * fourier)
    chosen_back = (owned_idx[:, :, None] == levels).astype(jnp.bfloat16)
    outgoing = jnp.einsum(
        "osb,obpx->sopx", chosen_back, back_own, preferred_element_type=jnp.float32
    )
    outgoing = outgoing.astype(jnp.bfloat16).reshape(slab_count * ori_dev, block_rows, 2 * fourier)
    incoming = lax.all_to_all(outgoing, "slab", split_axis=0, concat_axis=0, tiled=True)
    column = jnp.einsum("jpr,jpx->rx", interp[0], incoming, preferred_element_type=jnp.float32)
    summed_cols = lax.psum(column, "img")
    update = summed_cols / math.sqrt(img_dev * slab_count)
    return (update, weights)


def solution(mesh):
    return jax.shard_map(
        on_device,
        mesh=mesh,
        in_specs=(
            P("slab", None),
            P("img", None, None, "slab"),
            P("img", None, None),
            P("img", "slab", None, None),
            P("img", "slab"),
            P("img", "slab", None),
        ),
        out_specs=(P("slab", None), P("img", "slab", None)),
        check_vma=False,
    )
```

```python
import math

import jax
import jax.numpy as jnp
from jax import lax
from jax.sharding import PartitionSpec as P

BOX = 256
NS = 16


wave_length = 0.0197
aberration = 27000000.0
amplitude = 0.1
grid_side = 4


def phase_tables(fourier, shifts, box):
    freq = (jnp.arange(fourier, dtype=jnp.int32) - fourier // 2).astype(jnp.float32)
    shift_steps = jnp.arange(shifts, dtype=jnp.int32)
    shift_x = (2 * (shift_steps // grid_side) - (grid_side - 1)).astype(jnp.float32)
    shift_y = (2 * (shift_steps % grid_side) - (grid_side - 1)).astype(jnp.float32)
    angle = 2.0 * math.pi / box * (freq[:, None, None] * shift_x + freq[None, :, None] * shift_y)
    forward = jnp.stack([jnp.cos(angle), jnp.sin(angle)], axis=1).reshape(
        2 * fourier * fourier, shifts
    )
    backward = jnp.stack([jnp.cos(angle), -jnp.sin(angle)], axis=1).reshape(
        2 * fourier * fourier, shifts
    )
    return (forward.astype(jnp.bfloat16), backward.T.astype(jnp.bfloat16))


def contrast(defocus_blk, fourier, box):
    freq = (jnp.arange(fourier, dtype=jnp.int32) - fourier // 2).astype(jnp.float32)
    wave_sq = (freq[:, None] * freq[:, None] + freq[None, :] * freq[None, :]) / (box * box)
    phase = math.pi * wave_length * defocus_blk[:, None, None] * wave_sq
    phase = phase - 0.5 * math.pi * aberration * wave_length**3 * wave_sq * wave_sq
    return -(math.sqrt(1.0 - amplitude * amplitude) * jnp.sin(phase) + amplitude * jnp.cos(phase))


def correlate(panels, image_blk, list_blk, defocus_blk, phase_fwd, phase_back, box):
    count = image_blk.shape[0]
    fourier = image_blk.shape[1]
    picks = list_blk.shape[1]
    shifts = phase_fwd.shape[1]
    ctf = contrast(defocus_blk, fourier, box)
    weighted = ctf[:, :, None, :] * image_blk.astype(jnp.float32).reshape(
        count, fourier, 2, fourier
    )
    real_u = weighted[:, None, :, 0]
    imag_u = weighted[:, None, :, 1]
    chosen = panels[list_blk].astype(jnp.float32).reshape(count, picks, fourier, 2, fourier)
    real_p = chosen[:, :, :, 0]
    imag_p = chosen[:, :, :, 1]
    product = jnp.stack(
        [real_p * real_u + imag_p * imag_u, real_p * imag_u - imag_p * real_u], axis=3
    )
    product = product.astype(jnp.bfloat16).reshape(count * picks, 2 * fourier * fourier)
    scores = jnp.dot(product, phase_fwd, preferred_element_type=jnp.float32) / fourier
    scores = scores.reshape(count, picks * shifts)
    squared = scores * scores
    weights = squared / (jnp.mean(squared, axis=1, keepdims=True) + 1e-05)
    rounded = weights.astype(jnp.bfloat16).reshape(count * picks, shifts)
    spread = jnp.dot(rounded, phase_back, preferred_element_type=jnp.float32)
    spread = spread.reshape(count, picks, fourier, 2, fourier)
    real_e = spread[:, :, :, 0]
    imag_e = spread[:, :, :, 1]
    backed = jnp.stack(
        [real_u * real_e - imag_u * imag_e, real_u * imag_e + imag_u * real_e], axis=3
    )
    backed = backed.astype(jnp.bfloat16).reshape(count * picks, 2 * fourier * fourier)
    return (weights, backed)


def on_device(volume, interp, block_index, images, defocus, orient):
    slab_count = lax.axis_size("slab")
    slab_index = lax.axis_index("slab")
    orient_count = interp.shape[1]
    ori_dev = orient_count // slab_count
    block_rows = interp.shape[2]
    fourier = images.shape[2]
    block_count = fourier // block_rows
    img_dev = images.shape[1]
    picks = orient.shape[2]
    levels = jnp.arange(block_count, dtype=jnp.int32)
    partial_value = jnp.einsum("jpr,rx->jpx", interp[0], volume, preferred_element_type=jnp.float32)
    owned_idx = lax.dynamic_slice_in_dim(block_index[0], slab_index * ori_dev, ori_dev, 0)
    received = lax.all_to_all(
        partial_value.reshape(slab_count, ori_dev * block_rows, 2 * fourier),
        "slab",
        split_axis=0,
        concat_axis=0,
        tiled=True,
    ).reshape(slab_count, ori_dev, block_rows, 2 * fourier)
    place = (owned_idx[:, :, None] == levels).astype(jnp.float32)
    summed = jnp.einsum(
        "osb,sopx->obpx", place, received, precision=lax.Precision.HIGHEST,
        preferred_element_type=jnp.float32,
    ).reshape(ori_dev, fourier, 2 * fourier)
    panels = lax.all_gather(summed.astype(jnp.bfloat16), "slab", axis=0, tiled=True)
    phase_fwd, phase_back = phase_tables(fourier, NS, BOX)
    blk = math.gcd(img_dev, 32)
    blk_total = img_dev // blk

    def per_block(pieces):
        image_blk, list_blk, defocus_blk = pieces
        return correlate(panels, image_blk, list_blk, defocus_blk, phase_fwd, phase_back, BOX)

    weights, backs = lax.map(
        per_block,
        (
            images[0].reshape(blk_total, blk, fourier, 2 * fourier),
            orient[0].reshape(blk_total, blk, picks),
            defocus[0].reshape(blk_total, blk),
        ),
    )
    all_slices = backs.reshape(img_dev * picks, 2 * fourier * fourier)
    member = (
        orient[0].reshape(-1)[:, None] == jnp.arange(orient_count, dtype=jnp.int32)[None, :]
    ).astype(jnp.bfloat16)
    contrib = lax.dot_general(
        member, all_slices, (((0,), (0,)), ((), ())), preferred_element_type=jnp.float32
    ).reshape(orient_count, fourier, 2 * fourier)
    gathered = lax.all_to_all(
        contrib.astype(jnp.bfloat16), "slab", split_axis=0, concat_axis=0, tiled=True
    ).reshape(slab_count, ori_dev, fourier, 2 * fourier)
    back_own = jnp.sum(gathered.astype(jnp.float32), axis=0).astype(jnp.bfloat16)
    back_own = back_own.reshape(ori_dev, block_count, block_rows, 2 * fourier)
    chosen_back = (owned_idx[:, :, None] == levels).astype(jnp.bfloat16)
    outgoing = jnp.einsum(
        "osb,obpx->sopx", chosen_back, back_own, preferred_element_type=jnp.float32
    )
    outgoing = outgoing.astype(jnp.bfloat16).reshape(slab_count * ori_dev, block_rows, 2 * fourier)
    incoming = lax.all_to_all(outgoing, "slab", split_axis=0, concat_axis=0, tiled=True)
    column = jnp.einsum("jpr,jpx->rx", interp[0], incoming, preferred_element_type=jnp.float32)
    summed_cols = lax.psum(column, "img")
    update = summed_cols / math.sqrt(img_dev * slab_count)
    return (update, weights)


def solution(mesh):
    return jax.shard_map(
        on_device,
        mesh=mesh,
        in_specs=(
            P("slab", None),
            P("img", None, None, "slab"),
            P("img", None, None),
            P("img", "slab", None, None),
            P("img", "slab"),
            P("img", "slab", None),
        ),
        out_specs=(P("slab", None), P("img", "slab", None)),
        check_vma=False,
    )
```

```python
import math

import jax
import jax.numpy as jnp
from jax import lax
from jax.experimental import pallas as pl
from jax.experimental.pallas import tpu as pltpu
from jax.sharding import PartitionSpec as P

BOX = 256
NS = 16


wave_length = 0.0197
aberration = 27000000.0
amplitude = 0.1
grid_side = 4


def phase_tables(fourier, shifts, box):
    freq = (jnp.arange(fourier, dtype=jnp.int32) - fourier // 2).astype(jnp.float32)
    shift_steps = jnp.arange(shifts, dtype=jnp.int32)
    shift_x = (2 * (shift_steps // grid_side) - (grid_side - 1)).astype(jnp.float32)
    shift_y = (2 * (shift_steps % grid_side) - (grid_side - 1)).astype(jnp.float32)
    angle = 2.0 * math.pi / box * (freq[:, None, None] * shift_x + freq[None, :, None] * shift_y)
    forward = jnp.stack([jnp.cos(angle), jnp.sin(angle)], axis=1).reshape(
        2 * fourier * fourier, shifts
    )
    backward = jnp.stack([jnp.cos(angle), -jnp.sin(angle)], axis=1).reshape(
        2 * fourier * fourier, shifts
    )
    return (forward.astype(jnp.bfloat16), backward.T.astype(jnp.bfloat16))


def contrast(defocus_blk, fourier, box):
    freq = (jnp.arange(fourier, dtype=jnp.int32) - fourier // 2).astype(jnp.float32)
    wave_sq = (freq[:, None] * freq[:, None] + freq[None, :] * freq[None, :]) / (box * box)
    phase = math.pi * wave_length * defocus_blk[:, None, None] * wave_sq
    phase = phase - 0.5 * math.pi * aberration * wave_length**3 * wave_sq * wave_sq
    return -(math.sqrt(1.0 - amplitude * amplitude) * jnp.sin(phase) + amplitude * jnp.cos(phase))


def correlate(panels, image_blk, list_blk, defocus_blk, phase_fwd, phase_back, box):
    count = image_blk.shape[0]
    fourier = image_blk.shape[1]
    picks = list_blk.shape[1]
    shifts = phase_fwd.shape[1]
    ctf = contrast(defocus_blk, fourier, box)
    weighted = ctf[:, :, None, :] * image_blk.astype(jnp.float32).reshape(
        count, fourier, 2, fourier
    )
    real_u = weighted[:, None, :, 0]
    imag_u = weighted[:, None, :, 1]
    chosen = panels[list_blk].astype(jnp.float32).reshape(count, picks, fourier, 2, fourier)
    real_p = chosen[:, :, :, 0]
    imag_p = chosen[:, :, :, 1]
    product = jnp.stack(
        [real_p * real_u + imag_p * imag_u, real_p * imag_u - imag_p * real_u], axis=3
    )
    product = product.astype(jnp.bfloat16).reshape(count * picks, 2 * fourier * fourier)
    scores = jnp.dot(product, phase_fwd, preferred_element_type=jnp.float32) / fourier
    scores = scores.reshape(count, picks * shifts)
    squared = scores * scores
    weights = squared / (jnp.mean(squared, axis=1, keepdims=True) + 1e-05)
    rounded = weights.astype(jnp.bfloat16).reshape(count * picks, shifts)
    spread = jnp.dot(rounded, phase_back, preferred_element_type=jnp.float32)
    spread = spread.reshape(count, picks, fourier, 2, fourier)
    real_e = spread[:, :, :, 0]
    imag_e = spread[:, :, :, 1]
    backed = jnp.stack(
        [real_u * real_e - imag_u * imag_e, real_u * imag_e + imag_u * real_e], axis=3
    )
    backed = backed.astype(jnp.bfloat16).reshape(count * picks, 2 * fourier * fourier)
    return (weights, backed)


def _a2a_kernel(x_ref, o_ref, send_sems, recv_sems, local_sem):
    count = x_ref.shape[0]
    me = lax.axis_index("slab")
    grp = lax.axis_index("img")
    mesh_ids = pl.DeviceIdType.MESH
    barrier = pltpu.get_barrier_semaphore()

    def greet(i, carry):
        peer = lax.rem(me + 1 + i, count)
        pl.semaphore_signal(barrier, inc=1, device_id=(peer, grp), device_id_type=mesh_ids)
        return carry

    lax.fori_loop(0, count - 1, greet, 0)
    pl.semaphore_wait(barrier, count - 1)
    local = pltpu.make_async_copy(x_ref.at[me], o_ref.at[me], local_sem)
    local.start()

    def outgoing(peer):
        return pltpu.make_async_remote_copy(
            src_ref=x_ref.at[peer],
            dst_ref=o_ref.at[me],
            send_sem=send_sems.at[peer],
            recv_sem=recv_sems.at[me],
            device_id=(peer, grp),
            device_id_type=mesh_ids,
        )

    def incoming(src):
        return pltpu.make_async_remote_copy(
            src_ref=x_ref.at[src],
            dst_ref=o_ref.at[src],
            send_sem=send_sems.at[src],
            recv_sem=recv_sems.at[src],
            device_id=(src, grp),
            device_id_type=mesh_ids,
        )

    def send(i, carry):
        outgoing(lax.rem(me + 1 + i, count)).start()
        return carry

    lax.fori_loop(0, count - 1, send, 0)

    def finish(i, carry):
        outgoing(lax.rem(me + 1 + i, count)).wait_send()
        incoming(lax.rem(me + count - 1 - i, count)).wait_recv()
        return carry

    lax.fori_loop(0, count - 1, finish, 0)
    local.wait()


def slab_all_to_all(x, cid):
    count = x.shape[0]
    return pl.pallas_call(
        _a2a_kernel,
        out_shape=jax.ShapeDtypeStruct(x.shape, x.dtype),
        in_specs=[pl.BlockSpec(memory_space=pl.ANY)],
        out_specs=pl.BlockSpec(memory_space=pl.ANY),
        scratch_shapes=[
            pltpu.SemaphoreType.DMA((count,)),
            pltpu.SemaphoreType.DMA((count,)),
            pltpu.SemaphoreType.DMA,
        ],
        compiler_params=pltpu.CompilerParams(collective_id=cid, has_side_effects=True),
    )(x)


def on_device(volume, interp, block_index, images, defocus, orient):
    slab_count = lax.axis_size("slab")
    slab_index = lax.axis_index("slab")
    orient_count = interp.shape[1]
    ori_dev = orient_count // slab_count
    block_rows = interp.shape[2]
    fourier = images.shape[2]
    block_count = fourier // block_rows
    img_dev = images.shape[1]
    picks = orient.shape[2]
    levels = jnp.arange(block_count, dtype=jnp.int32)
    partial_value = jnp.einsum("jpr,rx->jpx", interp[0], volume, preferred_element_type=jnp.float32)
    owned_idx = lax.dynamic_slice_in_dim(block_index[0], slab_index * ori_dev, ori_dev, 0)
    received = lax.all_to_all(
        partial_value.reshape(slab_count, ori_dev * block_rows, 2 * fourier),
        "slab",
        split_axis=0,
        concat_axis=0,
        tiled=True,
    ).reshape(slab_count, ori_dev, block_rows, 2 * fourier)
    place = (owned_idx[:, :, None] == levels).astype(jnp.float32)
    summed = jnp.einsum(
        "osb,sopx->obpx", place, received, precision=lax.Precision.HIGHEST,
        preferred_element_type=jnp.float32,
    ).reshape(ori_dev, fourier, 2 * fourier)
    panels = lax.all_gather(summed.astype(jnp.bfloat16), "slab", axis=0, tiled=True)
    phase_fwd, phase_back = phase_tables(fourier, NS, BOX)
    blk = math.gcd(img_dev, 32)
    blk_total = img_dev // blk

    def per_block(pieces):
        image_blk, list_blk, defocus_blk = pieces
        return correlate(panels, image_blk, list_blk, defocus_blk, phase_fwd, phase_back, BOX)

    weights, backs = lax.map(
        per_block,
        (
            images[0].reshape(blk_total, blk, fourier, 2 * fourier),
            orient[0].reshape(blk_total, blk, picks),
            defocus[0].reshape(blk_total, blk),
        ),
    )
    all_slices = backs.reshape(img_dev * picks, 2 * fourier * fourier)
    member = (
        orient[0].reshape(-1)[:, None] == jnp.arange(orient_count, dtype=jnp.int32)[None, :]
    ).astype(jnp.bfloat16)
    contrib = lax.dot_general(
        member, all_slices, (((0,), (0,)), ((), ())), preferred_element_type=jnp.float32
    ).reshape(orient_count, fourier, 2 * fourier)
    gathered = slab_all_to_all(contrib.astype(jnp.bfloat16), 0).reshape(slab_count, ori_dev, fourier, 2 * fourier)
    back_own = jnp.sum(gathered.astype(jnp.float32), axis=0).astype(jnp.bfloat16)
    back_own = back_own.reshape(ori_dev, block_count, block_rows, 2 * fourier)
    chosen_back = (owned_idx[:, :, None] == levels).astype(jnp.bfloat16)
    outgoing = jnp.einsum(
        "osb,obpx->sopx", chosen_back, back_own, preferred_element_type=jnp.float32
    )
    outgoing = outgoing.astype(jnp.bfloat16).reshape(slab_count * ori_dev, block_rows, 2 * fourier)
    incoming = lax.all_to_all(outgoing, "slab", split_axis=0, concat_axis=0, tiled=True)
    column = jnp.einsum("jpr,jpx->rx", interp[0], incoming, preferred_element_type=jnp.float32)
    summed_cols = lax.psum(column, "img")
    update = summed_cols / math.sqrt(img_dev * slab_count)
    return (update, weights)


def solution(mesh):
    return jax.shard_map(
        on_device,
        mesh=mesh,
        in_specs=(
            P("slab", None),
            P("img", None, None, "slab"),
            P("img", None, None),
            P("img", "slab", None, None),
            P("img", "slab"),
            P("img", "slab", None),
        ),
        out_specs=(P("slab", None), P("img", "slab", None)),
        check_vma=False,
    )
```

```python
import math

import jax
import jax.numpy as jnp
from jax import lax
from jax.sharding import PartitionSpec as P

BOX = 256
NS = 16
SLAB = ("sx", "sz", "sc")


wave_length = 0.0197
aberration = 27000000.0
amplitude = 0.1
grid_side = 4


def phase_tables(fourier, shifts, box):
    freq = (jnp.arange(fourier, dtype=jnp.int32) - fourier // 2).astype(jnp.float32)
    shift_steps = jnp.arange(shifts, dtype=jnp.int32)
    shift_x = (2 * (shift_steps // grid_side) - (grid_side - 1)).astype(jnp.float32)
    shift_y = (2 * (shift_steps % grid_side) - (grid_side - 1)).astype(jnp.float32)
    angle = 2.0 * math.pi / box * (freq[:, None, None] * shift_x + freq[None, :, None] * shift_y)
    forward = jnp.stack([jnp.cos(angle), jnp.sin(angle)], axis=1).reshape(
        2 * fourier * fourier, shifts
    )
    backward = jnp.stack([jnp.cos(angle), -jnp.sin(angle)], axis=1).reshape(
        2 * fourier * fourier, shifts
    )
    return (forward.astype(jnp.bfloat16), backward.T.astype(jnp.bfloat16))


def contrast(defocus_blk, fourier, box):
    freq = (jnp.arange(fourier, dtype=jnp.int32) - fourier // 2).astype(jnp.float32)
    wave_sq = (freq[:, None] * freq[:, None] + freq[None, :] * freq[None, :]) / (box * box)
    phase = math.pi * wave_length * defocus_blk[:, None, None] * wave_sq
    phase = phase - 0.5 * math.pi * aberration * wave_length**3 * wave_sq * wave_sq
    return -(math.sqrt(1.0 - amplitude * amplitude) * jnp.sin(phase) + amplitude * jnp.cos(phase))


def correlate(panels, image_blk, list_blk, defocus_blk, phase_fwd, phase_back, box):
    count = image_blk.shape[0]
    fourier = image_blk.shape[1]
    picks = list_blk.shape[1]
    shifts = phase_fwd.shape[1]
    ctf = contrast(defocus_blk, fourier, box)
    weighted = ctf[:, :, None, :] * image_blk.astype(jnp.float32).reshape(
        count, fourier, 2, fourier
    )
    real_u = weighted[:, None, :, 0]
    imag_u = weighted[:, None, :, 1]
    chosen = panels[list_blk].astype(jnp.float32).reshape(count, picks, fourier, 2, fourier)
    real_p = chosen[:, :, :, 0]
    imag_p = chosen[:, :, :, 1]
    product = jnp.stack(
        [real_p * real_u + imag_p * imag_u, real_p * imag_u - imag_p * real_u], axis=3
    )
    product = product.astype(jnp.bfloat16).reshape(count * picks, 2 * fourier * fourier)
    scores = jnp.dot(product, phase_fwd, preferred_element_type=jnp.float32) / fourier
    scores = scores.reshape(count, picks * shifts)
    squared = scores * scores
    weights = squared / (jnp.mean(squared, axis=1, keepdims=True) + 1e-05)
    rounded = weights.astype(jnp.bfloat16).reshape(count * picks, shifts)
    spread = jnp.dot(rounded, phase_back, preferred_element_type=jnp.float32)
    spread = spread.reshape(count, picks, fourier, 2, fourier)
    real_e = spread[:, :, :, 0]
    imag_e = spread[:, :, :, 1]
    backed = jnp.stack(
        [real_u * real_e - imag_u * imag_e, real_u * imag_e + imag_u * real_e], axis=3
    )
    backed = backed.astype(jnp.bfloat16).reshape(count * picks, 2 * fourier * fourier)
    return (weights, backed)


def on_device(volume, interp, block_index, images, defocus, orient):
    slab_count = lax.axis_size(SLAB)
    slab_index = lax.axis_index(SLAB)
    orient_count = interp.shape[1]
    ori_dev = orient_count // slab_count
    block_rows = interp.shape[2]
    fourier = images.shape[2]
    block_count = fourier // block_rows
    img_dev = images.shape[1]
    picks = orient.shape[2]
    levels = jnp.arange(block_count, dtype=jnp.int32)
    partial_value = jnp.einsum("jpr,rx->jpx", interp[0], volume, preferred_element_type=jnp.float32)
    owned_idx = lax.dynamic_slice_in_dim(block_index[0], slab_index * ori_dev, ori_dev, 0)
    received = lax.all_to_all(
        partial_value.reshape(slab_count, ori_dev * block_rows, 2 * fourier),
        SLAB,
        split_axis=0,
        concat_axis=0,
        tiled=True,
    ).reshape(slab_count, ori_dev, block_rows, 2 * fourier)
    place = (owned_idx[:, :, None] == levels).astype(jnp.float32)
    summed = jnp.einsum(
        "osb,sopx->obpx", place, received, precision=lax.Precision.HIGHEST,
        preferred_element_type=jnp.float32,
    ).reshape(ori_dev, fourier, 2 * fourier)
    panels = lax.all_gather(summed.astype(jnp.bfloat16), SLAB, axis=0, tiled=True)
    phase_fwd, phase_back = phase_tables(fourier, NS, BOX)
    blk = math.gcd(img_dev, 32)
    blk_total = img_dev // blk

    def per_block(pieces):
        image_blk, list_blk, defocus_blk = pieces
        return correlate(panels, image_blk, list_blk, defocus_blk, phase_fwd, phase_back, BOX)

    weights, backs = lax.map(
        per_block,
        (
            images[0].reshape(blk_total, blk, fourier, 2 * fourier),
            orient[0].reshape(blk_total, blk, picks),
            defocus[0].reshape(blk_total, blk),
        ),
    )
    all_slices = backs.reshape(img_dev * picks, 2 * fourier * fourier)
    sizes = tuple(lax.axis_size(a) for a in SLAB)
    perm = jnp.arange(orient_count, dtype=jnp.int32).reshape(sizes + (ori_dev,))
    perm = perm.transpose(2, 0, 1, 3).reshape(-1)
    member = (orient[0].reshape(-1)[:, None] == perm[None, :]).astype(jnp.bfloat16)
    contrib = lax.dot_general(
        member, all_slices, (((0,), (0,)), ((), ())), preferred_element_type=jnp.float32
    ).reshape(orient_count, fourier, 2 * fourier)
    for axis in (SLAB[2], SLAB[0], SLAB[1]):
        contrib = lax.psum_scatter(contrib, axis, scatter_dimension=0, tiled=True)
    back_own = contrib.astype(jnp.bfloat16)
    back_own = back_own.reshape(ori_dev, block_count, block_rows, 2 * fourier)
    chosen_back = (owned_idx[:, :, None] == levels).astype(jnp.bfloat16)
    outgoing = jnp.einsum(
        "osb,obpx->sopx", chosen_back, back_own, preferred_element_type=jnp.float32
    )
    outgoing = outgoing.astype(jnp.bfloat16).reshape(slab_count * ori_dev, block_rows, 2 * fourier)
    incoming = lax.all_to_all(outgoing, SLAB, split_axis=0, concat_axis=0, tiled=True)
    column = jnp.einsum("jpr,jpx->rx", interp[0], incoming, preferred_element_type=jnp.float32)
    summed_cols = lax.psum(column, "img")
    update = summed_cols / math.sqrt(img_dev * slab_count)
    return (update, weights)


def solution(mesh):
    devices = mesh.devices
    cores = 2
    xs = len({d.coords[0] for d in devices.reshape(-1)}) if hasattr(devices.reshape(-1)[0], "coords") else 4
    split = devices.reshape((xs, devices.shape[0] // (xs * cores), cores) + devices.shape[1:])
    fine = jax.sharding.Mesh(split, SLAB + ("img",))
    return jax.shard_map(
        on_device,
        mesh=fine,
        in_specs=(
            P(SLAB, None),
            P("img", None, None, SLAB),
            P("img", None, None),
            P("img", SLAB, None, None),
            P("img", SLAB),
            P("img", SLAB, None),
        ),
        out_specs=(P(SLAB, None), P("img", SLAB, None)),
        check_vma=False,
    )
```

```python
import math

import jax
import jax.numpy as jnp
from jax import lax
from jax.experimental import pallas as pl
from jax.experimental.pallas import tpu as pltpu
from jax.sharding import PartitionSpec as P

BOX = 256
NS = 16


wave_length = 0.0197
aberration = 27000000.0
amplitude = 0.1
grid_side = 4


def phase_tables(fourier, shifts, box):
    freq = (jnp.arange(fourier, dtype=jnp.int32) - fourier // 2).astype(jnp.float32)
    shift_steps = jnp.arange(shifts, dtype=jnp.int32)
    shift_x = (2 * (shift_steps // grid_side) - (grid_side - 1)).astype(jnp.float32)
    shift_y = (2 * (shift_steps % grid_side) - (grid_side - 1)).astype(jnp.float32)
    angle = 2.0 * math.pi / box * (freq[:, None, None] * shift_x + freq[None, :, None] * shift_y)
    forward = jnp.stack([jnp.cos(angle), jnp.sin(angle)], axis=1).reshape(
        2 * fourier * fourier, shifts
    )
    backward = jnp.stack([jnp.cos(angle), -jnp.sin(angle)], axis=1).reshape(
        2 * fourier * fourier, shifts
    )
    return (forward.astype(jnp.bfloat16), backward.T.astype(jnp.bfloat16))


def contrast(defocus_blk, fourier, box):
    freq = (jnp.arange(fourier, dtype=jnp.int32) - fourier // 2).astype(jnp.float32)
    wave_sq = (freq[:, None] * freq[:, None] + freq[None, :] * freq[None, :]) / (box * box)
    phase = math.pi * wave_length * defocus_blk[:, None, None] * wave_sq
    phase = phase - 0.5 * math.pi * aberration * wave_length**3 * wave_sq * wave_sq
    return -(math.sqrt(1.0 - amplitude * amplitude) * jnp.sin(phase) + amplitude * jnp.cos(phase))


def correlate(panels, image_blk, list_blk, defocus_blk, phase_fwd, phase_back, box):
    count = image_blk.shape[0]
    fourier = image_blk.shape[1]
    picks = list_blk.shape[1]
    shifts = phase_fwd.shape[1]
    ctf = contrast(defocus_blk, fourier, box)
    weighted = ctf[:, :, None, :] * image_blk.astype(jnp.float32).reshape(
        count, fourier, 2, fourier
    )
    real_u = weighted[:, None, :, 0]
    imag_u = weighted[:, None, :, 1]
    chosen = panels[list_blk].astype(jnp.float32).reshape(count, picks, fourier, 2, fourier)
    real_p = chosen[:, :, :, 0]
    imag_p = chosen[:, :, :, 1]
    product = jnp.stack(
        [real_p * real_u + imag_p * imag_u, real_p * imag_u - imag_p * real_u], axis=3
    )
    product = product.astype(jnp.bfloat16).reshape(count * picks, 2 * fourier * fourier)
    scores = jnp.dot(product, phase_fwd, preferred_element_type=jnp.float32) / fourier
    scores = scores.reshape(count, picks * shifts)
    squared = scores * scores
    weights = squared / (jnp.mean(squared, axis=1, keepdims=True) + 1e-05)
    rounded = weights.astype(jnp.bfloat16).reshape(count * picks, shifts)
    spread = jnp.dot(rounded, phase_back, preferred_element_type=jnp.float32)
    spread = spread.reshape(count, picks, fourier, 2, fourier)
    real_e = spread[:, :, :, 0]
    imag_e = spread[:, :, :, 1]
    backed = jnp.stack(
        [real_u * real_e - imag_u * imag_e, real_u * imag_e + imag_u * real_e], axis=3
    )
    backed = backed.astype(jnp.bfloat16).reshape(count * picks, 2 * fourier * fourier)
    return (weights, backed)


def _correlate_kernel(orient_ref, panels_ref, image_ref, ctf_ref, cos_ref, sin_ref, w_ref, acc_ref):
    i = pl.program_id(0)
    picks = w_ref.shape[1] // cos_ref.shape[0]
    shifts = cos_ref.shape[0]
    half = ctf_ref.shape[2]

    @pl.when(i == 0)
    def _():
        acc_ref[...] = jnp.zeros_like(acc_ref)

    ctf = ctf_ref[0]
    image = image_ref[0].astype(jnp.float32)
    ur = ctf * image[:, :half]
    ui = ctf * image[:, half:]
    rows = []
    for k in range(picks):
        panel = panels_ref[orient_ref[i * picks + k]].astype(jnp.float32)
        pr = panel[:, :half]
        pi = panel[:, half:]
        prod_re = (pr * ur + pi * ui).astype(jnp.bfloat16).astype(jnp.float32)
        prod_im = (pr * ui - pi * ur).astype(jnp.bfloat16).astype(jnp.float32)
        for t in range(shifts):
            v = prod_re * cos_ref[t] + prod_im * sin_ref[t]
            rows.append(jnp.sum(v, axis=0, keepdims=True))
    scores = jnp.sum(jnp.concatenate(rows, axis=0), axis=1, keepdims=True) / half
    squared = scores * scores
    mean = jnp.sum(squared, axis=0, keepdims=True) / squared.shape[0]
    weights = squared / (mean + 1e-05)
    w_ref[0] = weights
    wround = weights.astype(jnp.bfloat16).astype(jnp.float32)
    for k in range(picks):
        er = jnp.zeros_like(ur)
        ei = jnp.zeros_like(ur)
        for t in range(shifts):
            wt = wround[k * shifts + t : k * shifts + t + 1, :]
            er = er + wt * cos_ref[t]
            ei = ei - wt * sin_ref[t]
        slice_re = (ur * er - ui * ei).astype(jnp.bfloat16).astype(jnp.float32)
        slice_im = (ur * ei + ui * er).astype(jnp.bfloat16).astype(jnp.float32)
        j = orient_ref[i * picks + k]
        acc_ref[j, :, :half] += slice_re
        acc_ref[j, :, half:] += slice_im


def correlate_all(panels, images, orient, defocus):
    count, fourier, width = images.shape
    picks = orient.shape[1]
    orient_count = panels.shape[0]
    ctf = contrast(defocus, fourier, BOX)
    freq = (jnp.arange(fourier, dtype=jnp.int32) - fourier // 2).astype(jnp.float32)
    shift_steps = jnp.arange(NS, dtype=jnp.int32)
    shift_x = (2 * (shift_steps // grid_side) - (grid_side - 1)).astype(jnp.float32)
    shift_y = (2 * (shift_steps % grid_side) - (grid_side - 1)).astype(jnp.float32)
    angle = 2.0 * math.pi / BOX * (
        freq[None, :, None] * shift_x[:, None, None] + freq[None, None, :] * shift_y[:, None, None]
    )
    cos_t = jnp.cos(angle).astype(jnp.bfloat16).astype(jnp.float32)
    sin_t = jnp.sin(angle).astype(jnp.bfloat16).astype(jnp.float32)
    grid_spec = pltpu.PrefetchScalarGridSpec(
        num_scalar_prefetch=1,
        grid=(count,),
        in_specs=[
            pl.BlockSpec((orient_count, fourier, width), lambda i, o: (0, 0, 0)),
            pl.BlockSpec((1, fourier, width), lambda i, o: (i, 0, 0)),
            pl.BlockSpec((1, fourier, fourier), lambda i, o: (i, 0, 0)),
            pl.BlockSpec((NS, fourier, fourier), lambda i, o: (0, 0, 0)),
            pl.BlockSpec((NS, fourier, fourier), lambda i, o: (0, 0, 0)),
        ],
        out_specs=[
            pl.BlockSpec((1, picks * NS, 1), lambda i, o: (i, 0, 0)),
            pl.BlockSpec((orient_count, fourier, width), lambda i, o: (0, 0, 0)),
        ],
    )
    weights, contrib = pl.pallas_call(
        _correlate_kernel,
        grid_spec=grid_spec,
        out_shape=[
            jax.ShapeDtypeStruct((count, picks * NS, 1), jnp.float32),
            jax.ShapeDtypeStruct((orient_count, fourier, width), jnp.float32),
        ],
        compiler_params=pltpu.CompilerParams(
            dimension_semantics=("arbitrary",), vmem_limit_bytes=56 * 1024 * 1024
        ),
    )(orient.reshape(-1), panels, images, ctf, cos_t, sin_t)
    return weights.reshape(count, picks * NS), contrib


def on_device(volume, interp, block_index, images, defocus, orient):
    slab_count = lax.axis_size("slab")
    slab_index = lax.axis_index("slab")
    orient_count = interp.shape[1]
    ori_dev = orient_count // slab_count
    block_rows = interp.shape[2]
    fourier = images.shape[2]
    block_count = fourier // block_rows
    img_dev = images.shape[1]
    picks = orient.shape[2]
    levels = jnp.arange(block_count, dtype=jnp.int32)
    partial_value = jnp.einsum("jpr,rx->jpx", interp[0], volume, preferred_element_type=jnp.float32)
    owned_idx = lax.dynamic_slice_in_dim(block_index[0], slab_index * ori_dev, ori_dev, 0)
    received = lax.all_to_all(
        partial_value.reshape(slab_count, ori_dev * block_rows, 2 * fourier),
        "slab",
        split_axis=0,
        concat_axis=0,
        tiled=True,
    ).reshape(slab_count, ori_dev, block_rows, 2 * fourier)
    place = (owned_idx[:, :, None] == levels).astype(jnp.float32)
    summed = jnp.einsum(
        "osb,sopx->obpx", place, received, precision=lax.Precision.HIGHEST,
        preferred_element_type=jnp.float32,
    ).reshape(ori_dev, fourier, 2 * fourier)
    panels = lax.all_gather(summed.astype(jnp.bfloat16), "slab", axis=0, tiled=True)
    weights, contrib = correlate_all(panels, images[0], orient[0], defocus[0])
    gathered = lax.all_to_all(
        contrib.astype(jnp.bfloat16), "slab", split_axis=0, concat_axis=0, tiled=True
    ).reshape(slab_count, ori_dev, fourier, 2 * fourier)
    back_own = jnp.sum(gathered.astype(jnp.float32), axis=0).astype(jnp.bfloat16)
    back_own = back_own.reshape(ori_dev, block_count, block_rows, 2 * fourier)
    chosen_back = (owned_idx[:, :, None] == levels).astype(jnp.bfloat16)
    outgoing = jnp.einsum(
        "osb,obpx->sopx", chosen_back, back_own, preferred_element_type=jnp.float32
    )
    outgoing = outgoing.astype(jnp.bfloat16).reshape(slab_count * ori_dev, block_rows, 2 * fourier)
    incoming = lax.all_to_all(outgoing, "slab", split_axis=0, concat_axis=0, tiled=True)
    column = jnp.einsum("jpr,jpx->rx", interp[0], incoming, preferred_element_type=jnp.float32)
    summed_cols = lax.psum(column, "img")
    update = summed_cols / math.sqrt(img_dev * slab_count)
    return (update, weights[None])


def solution(mesh):
    return jax.shard_map(
        on_device,
        mesh=mesh,
        in_specs=(
            P("slab", None),
            P("img", None, None, "slab"),
            P("img", None, None),
            P("img", "slab", None, None),
            P("img", "slab"),
            P("img", "slab", None),
        ),
        out_specs=(P("slab", None), P("img", "slab", None)),
        check_vma=False,
    )
```

```python
import math

import jax
import jax.numpy as jnp
from jax import lax
from jax.experimental import pallas as pl
from jax.experimental.pallas import tpu as pltpu
from jax.sharding import PartitionSpec as P

BOX = 256
NS = 16
SLAB = ("sx", "sz", "sc")


wave_length = 0.0197
aberration = 27000000.0
amplitude = 0.1
grid_side = 4


def phase_tables(fourier, shifts, box):
    freq = (jnp.arange(fourier, dtype=jnp.int32) - fourier // 2).astype(jnp.float32)
    shift_steps = jnp.arange(shifts, dtype=jnp.int32)
    shift_x = (2 * (shift_steps // grid_side) - (grid_side - 1)).astype(jnp.float32)
    shift_y = (2 * (shift_steps % grid_side) - (grid_side - 1)).astype(jnp.float32)
    angle = 2.0 * math.pi / box * (freq[:, None, None] * shift_x + freq[None, :, None] * shift_y)
    forward = jnp.stack([jnp.cos(angle), jnp.sin(angle)], axis=1).reshape(
        2 * fourier * fourier, shifts
    )
    backward = jnp.stack([jnp.cos(angle), -jnp.sin(angle)], axis=1).reshape(
        2 * fourier * fourier, shifts
    )
    return (forward.astype(jnp.bfloat16), backward.T.astype(jnp.bfloat16))


def contrast(defocus_blk, fourier, box):
    freq = (jnp.arange(fourier, dtype=jnp.int32) - fourier // 2).astype(jnp.float32)
    wave_sq = (freq[:, None] * freq[:, None] + freq[None, :] * freq[None, :]) / (box * box)
    phase = math.pi * wave_length * defocus_blk[:, None, None] * wave_sq
    phase = phase - 0.5 * math.pi * aberration * wave_length**3 * wave_sq * wave_sq
    return -(math.sqrt(1.0 - amplitude * amplitude) * jnp.sin(phase) + amplitude * jnp.cos(phase))


def correlate(panels, image_blk, list_blk, defocus_blk, phase_fwd, phase_back, box):
    count = image_blk.shape[0]
    fourier = image_blk.shape[1]
    picks = list_blk.shape[1]
    shifts = phase_fwd.shape[1]
    ctf = contrast(defocus_blk, fourier, box)
    weighted = ctf[:, :, None, :] * image_blk.astype(jnp.float32).reshape(
        count, fourier, 2, fourier
    )
    real_u = weighted[:, None, :, 0]
    imag_u = weighted[:, None, :, 1]
    chosen = panels[list_blk].astype(jnp.float32).reshape(count, picks, fourier, 2, fourier)
    real_p = chosen[:, :, :, 0]
    imag_p = chosen[:, :, :, 1]
    product = jnp.stack(
        [real_p * real_u + imag_p * imag_u, real_p * imag_u - imag_p * real_u], axis=3
    )
    product = product.astype(jnp.bfloat16).reshape(count * picks, 2 * fourier * fourier)
    scores = jnp.dot(product, phase_fwd, preferred_element_type=jnp.float32) / fourier
    scores = scores.reshape(count, picks * shifts)
    squared = scores * scores
    weights = squared / (jnp.mean(squared, axis=1, keepdims=True) + 1e-05)
    rounded = weights.astype(jnp.bfloat16).reshape(count * picks, shifts)
    spread = jnp.dot(rounded, phase_back, preferred_element_type=jnp.float32)
    spread = spread.reshape(count, picks, fourier, 2, fourier)
    real_e = spread[:, :, :, 0]
    imag_e = spread[:, :, :, 1]
    backed = jnp.stack(
        [real_u * real_e - imag_u * imag_e, real_u * imag_e + imag_u * real_e], axis=3
    )
    backed = backed.astype(jnp.bfloat16).reshape(count * picks, 2 * fourier * fourier)
    return (weights, backed)


def _correlate_kernel(orient_ref, row_ref, panels_ref, image_ref, ctf_ref, cos_ref, sin_ref, w_ref, acc_ref):
    i = pl.program_id(0)
    picks = w_ref.shape[1] // cos_ref.shape[0]
    shifts = cos_ref.shape[0]
    half = ctf_ref.shape[2]

    @pl.when(i == 0)
    def _():
        acc_ref[...] = jnp.zeros_like(acc_ref)

    ctf = ctf_ref[0]
    image = image_ref[0].astype(jnp.float32)
    ur = ctf * image[:, :half]
    ui = ctf * image[:, half:]
    rows = []
    for k in range(picks):
        panel = panels_ref[orient_ref[i * picks + k]].astype(jnp.float32)
        pr = panel[:, :half]
        pi = panel[:, half:]
        prod_re = (pr * ur + pi * ui).astype(jnp.bfloat16).astype(jnp.float32)
        prod_im = (pr * ui - pi * ur).astype(jnp.bfloat16).astype(jnp.float32)
        for t in range(shifts):
            v = prod_re * cos_ref[t] + prod_im * sin_ref[t]
            rows.append(jnp.sum(v, axis=0, keepdims=True))
    scores = jnp.sum(jnp.concatenate(rows, axis=0), axis=1, keepdims=True) / half
    squared = scores * scores
    mean = jnp.sum(squared, axis=0, keepdims=True) / squared.shape[0]
    weights = squared / (mean + 1e-05)
    w_ref[0] = weights
    wround = weights.astype(jnp.bfloat16).astype(jnp.float32)
    for k in range(picks):
        er = jnp.zeros_like(ur)
        ei = jnp.zeros_like(ur)
        for t in range(shifts):
            wt = wround[k * shifts + t : k * shifts + t + 1, :]
            er = er + wt * cos_ref[t]
            ei = ei - wt * sin_ref[t]
        slice_re = (ur * er - ui * ei).astype(jnp.bfloat16).astype(jnp.float32)
        slice_im = (ur * ei + ui * er).astype(jnp.bfloat16).astype(jnp.float32)
        j = row_ref[i * picks + k]
        acc_ref[j, :, :half] += slice_re
        acc_ref[j, :, half:] += slice_im


def correlate_all(panels, images, orient, rows, defocus):
    count, fourier, width = images.shape
    picks = orient.shape[1]
    orient_count = panels.shape[0]
    ctf = contrast(defocus, fourier, BOX)
    freq = (jnp.arange(fourier, dtype=jnp.int32) - fourier // 2).astype(jnp.float32)
    shift_steps = jnp.arange(NS, dtype=jnp.int32)
    shift_x = (2 * (shift_steps // grid_side) - (grid_side - 1)).astype(jnp.float32)
    shift_y = (2 * (shift_steps % grid_side) - (grid_side - 1)).astype(jnp.float32)
    angle = 2.0 * math.pi / BOX * (
        freq[None, :, None] * shift_x[:, None, None] + freq[None, None, :] * shift_y[:, None, None]
    )
    cos_t = jnp.cos(angle).astype(jnp.bfloat16).astype(jnp.float32)
    sin_t = jnp.sin(angle).astype(jnp.bfloat16).astype(jnp.float32)
    grid_spec = pltpu.PrefetchScalarGridSpec(
        num_scalar_prefetch=2,
        grid=(count,),
        in_specs=[
            pl.BlockSpec((orient_count, fourier, width), lambda i, o, w: (0, 0, 0)),
            pl.BlockSpec((1, fourier, width), lambda i, o, w: (i, 0, 0)),
            pl.BlockSpec((1, fourier, fourier), lambda i, o, w: (i, 0, 0)),
            pl.BlockSpec((NS, fourier, fourier), lambda i, o, w: (0, 0, 0)),
            pl.BlockSpec((NS, fourier, fourier), lambda i, o, w: (0, 0, 0)),
        ],
        out_specs=[
            pl.BlockSpec((1, picks * NS, 1), lambda i, o, w: (i, 0, 0)),
            pl.BlockSpec((orient_count, fourier, width), lambda i, o, w: (0, 0, 0)),
        ],
    )
    weights, contrib = pl.pallas_call(
        _correlate_kernel,
        grid_spec=grid_spec,
        out_shape=[
            jax.ShapeDtypeStruct((count, picks * NS, 1), jnp.float32),
            jax.ShapeDtypeStruct((orient_count, fourier, width), jnp.float32),
        ],
        compiler_params=pltpu.CompilerParams(
            dimension_semantics=("arbitrary",), vmem_limit_bytes=56 * 1024 * 1024
        ),
    )(orient.reshape(-1), rows.reshape(-1), panels, images, ctf, cos_t, sin_t)
    return weights.reshape(count, picks * NS), contrib


def on_device(volume, interp, block_index, images, defocus, orient):
    slab_count = lax.axis_size(SLAB)
    slab_index = lax.axis_index(SLAB)
    orient_count = interp.shape[1]
    ori_dev = orient_count // slab_count
    block_rows = interp.shape[2]
    fourier = images.shape[2]
    block_count = fourier // block_rows
    img_dev = images.shape[1]
    picks = orient.shape[2]
    levels = jnp.arange(block_count, dtype=jnp.int32)
    partial_value = jnp.einsum("jpr,rx->jpx", interp[0], volume, preferred_element_type=jnp.float32)
    owned_idx = lax.dynamic_slice_in_dim(block_index[0], slab_index * ori_dev, ori_dev, 0)
    received = lax.all_to_all(
        partial_value.reshape(slab_count, ori_dev * block_rows, 2 * fourier),
        SLAB,
        split_axis=0,
        concat_axis=0,
        tiled=True,
    ).reshape(slab_count, ori_dev, block_rows, 2 * fourier)
    place = (owned_idx[:, :, None] == levels).astype(jnp.float32)
    summed = jnp.einsum(
        "osb,sopx->obpx", place, received, precision=lax.Precision.HIGHEST,
        preferred_element_type=jnp.float32,
    ).reshape(ori_dev, fourier, 2 * fourier)
    panels = lax.all_gather(summed.astype(jnp.bfloat16), SLAB, axis=0, tiled=True)
    sizes = tuple(lax.axis_size(a) for a in SLAB)
    inv_perm = jnp.arange(orient_count, dtype=jnp.int32).reshape(
        (sizes[2], sizes[0], sizes[1], ori_dev)
    ).transpose(1, 2, 0, 3).reshape(-1)
    weights, contrib = correlate_all(panels, images[0], orient[0], inv_perm[orient[0]], defocus[0])
    for axis in (SLAB[2], SLAB[0], SLAB[1]):
        parts = lax.axis_size(axis)
        moved = lax.all_to_all(
            contrib.astype(jnp.bfloat16), axis, split_axis=0, concat_axis=0, tiled=True
        )
        contrib = jnp.sum(
            moved.astype(jnp.float32).reshape((parts, -1) + moved.shape[1:]), axis=0
        )
    back_own = contrib.astype(jnp.bfloat16)
    back_own = back_own.reshape(ori_dev, block_count, block_rows, 2 * fourier)
    chosen_back = (owned_idx[:, :, None] == levels).astype(jnp.bfloat16)
    outgoing = jnp.einsum(
        "osb,obpx->sopx", chosen_back, back_own, preferred_element_type=jnp.float32
    )
    outgoing = outgoing.astype(jnp.bfloat16).reshape(slab_count * ori_dev, block_rows, 2 * fourier)
    incoming = lax.all_to_all(outgoing, SLAB, split_axis=0, concat_axis=0, tiled=True)
    column = jnp.einsum("jpr,jpx->rx", interp[0], incoming, preferred_element_type=jnp.float32)
    summed_cols = lax.psum(column, "img")
    update = summed_cols / math.sqrt(img_dev * slab_count)
    return (update, weights[None])


def solution(mesh):
    devices = mesh.devices
    cores = 2
    xs = len({d.coords[0] for d in devices.reshape(-1)}) if hasattr(devices.reshape(-1)[0], "coords") else 4
    split = devices.reshape((xs, devices.shape[0] // (xs * cores), cores) + devices.shape[1:])
    fine = jax.sharding.Mesh(split, SLAB + ("img",))
    return jax.shard_map(
        on_device,
        mesh=fine,
        in_specs=(
            P(SLAB, None),
            P("img", None, None, SLAB),
            P("img", None, None),
            P("img", SLAB, None, None),
            P("img", SLAB),
            P("img", SLAB, None),
        ),
        out_specs=(P(SLAB, None), P("img", SLAB, None)),
        check_vma=False,
    )
```

```python
import math

import jax
import jax.numpy as jnp
from jax import lax
from jax.experimental import pallas as pl
from jax.experimental.pallas import tpu as pltpu
from jax.sharding import PartitionSpec as P

BOX = 256
NS = 16
SLAB = ("sx", "sz", "sc")


wave_length = 0.0197
aberration = 27000000.0
amplitude = 0.1
grid_side = 4


def phase_tables(fourier, shifts, box):
    freq = (jnp.arange(fourier, dtype=jnp.int32) - fourier // 2).astype(jnp.float32)
    shift_steps = jnp.arange(shifts, dtype=jnp.int32)
    shift_x = (2 * (shift_steps // grid_side) - (grid_side - 1)).astype(jnp.float32)
    shift_y = (2 * (shift_steps % grid_side) - (grid_side - 1)).astype(jnp.float32)
    angle = 2.0 * math.pi / box * (freq[:, None, None] * shift_x + freq[None, :, None] * shift_y)
    forward = jnp.stack([jnp.cos(angle), jnp.sin(angle)], axis=1).reshape(
        2 * fourier * fourier, shifts
    )
    backward = jnp.stack([jnp.cos(angle), -jnp.sin(angle)], axis=1).reshape(
        2 * fourier * fourier, shifts
    )
    return (forward.astype(jnp.bfloat16), backward.T.astype(jnp.bfloat16))


def contrast(defocus_blk, fourier, box):
    freq = (jnp.arange(fourier, dtype=jnp.int32) - fourier // 2).astype(jnp.float32)
    wave_sq = (freq[:, None] * freq[:, None] + freq[None, :] * freq[None, :]) / (box * box)
    phase = math.pi * wave_length * defocus_blk[:, None, None] * wave_sq
    phase = phase - 0.5 * math.pi * aberration * wave_length**3 * wave_sq * wave_sq
    return -(math.sqrt(1.0 - amplitude * amplitude) * jnp.sin(phase) + amplitude * jnp.cos(phase))


def correlate(panels, image_blk, list_blk, defocus_blk, phase_fwd, phase_back, box):
    count = image_blk.shape[0]
    fourier = image_blk.shape[1]
    picks = list_blk.shape[1]
    shifts = phase_fwd.shape[1]
    ctf = contrast(defocus_blk, fourier, box)
    weighted = ctf[:, :, None, :] * image_blk.astype(jnp.float32).reshape(
        count, fourier, 2, fourier
    )
    real_u = weighted[:, None, :, 0]
    imag_u = weighted[:, None, :, 1]
    chosen = panels[list_blk].astype(jnp.float32).reshape(count, picks, fourier, 2, fourier)
    real_p = chosen[:, :, :, 0]
    imag_p = chosen[:, :, :, 1]
    product = jnp.stack(
        [real_p * real_u + imag_p * imag_u, real_p * imag_u - imag_p * real_u], axis=3
    )
    product = product.astype(jnp.bfloat16).reshape(count * picks, 2 * fourier * fourier)
    scores = jnp.dot(product, phase_fwd, preferred_element_type=jnp.float32) / fourier
    scores = scores.reshape(count, picks * shifts)
    squared = scores * scores
    weights = squared / (jnp.mean(squared, axis=1, keepdims=True) + 1e-05)
    rounded = weights.astype(jnp.bfloat16).reshape(count * picks, shifts)
    spread = jnp.dot(rounded, phase_back, preferred_element_type=jnp.float32)
    spread = spread.reshape(count, picks, fourier, 2, fourier)
    real_e = spread[:, :, :, 0]
    imag_e = spread[:, :, :, 1]
    backed = jnp.stack(
        [real_u * real_e - imag_u * imag_e, real_u * imag_e + imag_u * real_e], axis=3
    )
    backed = backed.astype(jnp.bfloat16).reshape(count * picks, 2 * fourier * fourier)
    return (weights, backed)


def _correlate_kernel(orient_ref, row_ref, panels_ref, image_ref, ctf_ref, cos_ref, sin_ref, w_ref, acc_ref):
    i = pl.program_id(0)
    picks = w_ref.shape[1] // cos_ref.shape[0]
    shifts = cos_ref.shape[0]
    half = ctf_ref.shape[2]

    @pl.when(i == 0)
    def _():
        acc_ref[...] = jnp.zeros_like(acc_ref)

    ctf = ctf_ref[0]
    image = image_ref[0].astype(jnp.float32)
    ur = ctf * image[:, :half]
    ui = ctf * image[:, half:]
    rows = []
    for k in range(picks):
        panel = panels_ref[orient_ref[i * picks + k]].astype(jnp.float32)
        pr = panel[:, :half]
        pi = panel[:, half:]
        prod_re = (pr * ur + pi * ui).astype(jnp.bfloat16).astype(jnp.float32)
        prod_im = (pr * ui - pi * ur).astype(jnp.bfloat16).astype(jnp.float32)
        for t in range(shifts):
            v = prod_re * cos_ref[t] + prod_im * sin_ref[t]
            rows.append(jnp.sum(v, axis=0, keepdims=True))
    scores = jnp.sum(jnp.concatenate(rows, axis=0), axis=1, keepdims=True) / half
    squared = scores * scores
    mean = jnp.sum(squared, axis=0, keepdims=True) / squared.shape[0]
    weights = squared / (mean + 1e-05)
    w_ref[0] = weights
    wround = weights.astype(jnp.bfloat16).astype(jnp.float32)
    for k in range(picks):
        er = jnp.zeros_like(ur)
        ei = jnp.zeros_like(ur)
        for t in range(shifts):
            wt = wround[k * shifts + t : k * shifts + t + 1, :]
            er = er + wt * cos_ref[t]
            ei = ei - wt * sin_ref[t]
        slice_re = (ur * er - ui * ei).astype(jnp.bfloat16).astype(jnp.float32)
        slice_im = (ur * ei + ui * er).astype(jnp.bfloat16).astype(jnp.float32)
        j = row_ref[i * picks + k]
        acc_ref[j, :, :half] += slice_re
        acc_ref[j, :, half:] += slice_im


def correlate_all(panels, images, orient, rows, defocus):
    count, fourier, width = images.shape
    picks = orient.shape[1]
    orient_count = panels.shape[0]
    ctf = contrast(defocus, fourier, BOX)
    freq = (jnp.arange(fourier, dtype=jnp.int32) - fourier // 2).astype(jnp.float32)
    shift_steps = jnp.arange(NS, dtype=jnp.int32)
    shift_x = (2 * (shift_steps // grid_side) - (grid_side - 1)).astype(jnp.float32)
    shift_y = (2 * (shift_steps % grid_side) - (grid_side - 1)).astype(jnp.float32)
    angle = 2.0 * math.pi / BOX * (
        freq[None, :, None] * shift_x[:, None, None] + freq[None, None, :] * shift_y[:, None, None]
    )
    cos_t = jnp.cos(angle).astype(jnp.bfloat16).astype(jnp.float32)
    sin_t = jnp.sin(angle).astype(jnp.bfloat16).astype(jnp.float32)
    grid_spec = pltpu.PrefetchScalarGridSpec(
        num_scalar_prefetch=2,
        grid=(count,),
        in_specs=[
            pl.BlockSpec((orient_count, fourier, width), lambda i, o, w: (0, 0, 0)),
            pl.BlockSpec((1, fourier, width), lambda i, o, w: (i, 0, 0)),
            pl.BlockSpec((1, fourier, fourier), lambda i, o, w: (i, 0, 0)),
            pl.BlockSpec((NS, fourier, fourier), lambda i, o, w: (0, 0, 0)),
            pl.BlockSpec((NS, fourier, fourier), lambda i, o, w: (0, 0, 0)),
        ],
        out_specs=[
            pl.BlockSpec((1, picks * NS, 1), lambda i, o, w: (i, 0, 0)),
            pl.BlockSpec((orient_count, fourier, width), lambda i, o, w: (0, 0, 0)),
        ],
    )
    weights, contrib = pl.pallas_call(
        _correlate_kernel,
        grid_spec=grid_spec,
        out_shape=[
            jax.ShapeDtypeStruct((count, picks * NS, 1), jnp.float32),
            jax.ShapeDtypeStruct((orient_count, fourier, width), jnp.float32),
        ],
        compiler_params=pltpu.CompilerParams(
            dimension_semantics=("arbitrary",), vmem_limit_bytes=56 * 1024 * 1024
        ),
    )(orient.reshape(-1), rows.reshape(-1), panels, images, ctf, cos_t, sin_t)
    return weights.reshape(count, picks * NS), contrib


def _img_gather_kernel(x_ref, o_ref, send_sems, recv_sems, local_sem):
    count = o_ref.shape[0]
    me = lax.axis_index("img")
    here = tuple(lax.axis_index(a) for a in SLAB)
    mesh_ids = pl.DeviceIdType.MESH
    barrier = pltpu.get_barrier_semaphore()
    for i in range(count - 1):
        peer = lax.rem(me + 1 + i, count)
        pl.semaphore_signal(barrier, inc=1, device_id=here + (peer,), device_id_type=mesh_ids)
    pl.semaphore_wait(barrier, count - 1)
    local = pltpu.make_async_copy(x_ref, o_ref.at[me], local_sem)
    local.start()
    sends = []
    for i in range(count - 1):
        peer = lax.rem(me + 1 + i, count)
        copy = pltpu.make_async_remote_copy(
            src_ref=x_ref,
            dst_ref=o_ref.at[me],
            send_sem=send_sems.at[i],
            recv_sem=recv_sems.at[me],
            device_id=here + (peer,),
            device_id_type=mesh_ids,
        )
        copy.start()
        sends.append(copy)
    for i in range(count - 1):
        src = lax.rem(me + 1 + i, count)
        sends[i].wait_send()
        pltpu.make_async_remote_copy(
            src_ref=x_ref,
            dst_ref=o_ref.at[src],
            send_sem=send_sems.at[i],
            recv_sem=recv_sems.at[src],
            device_id=here + (src,),
            device_id_type=mesh_ids,
        ).wait_recv()
    local.wait()


def img_gather(x, count, cid):
    return pl.pallas_call(
        _img_gather_kernel,
        out_shape=jax.ShapeDtypeStruct((count,) + x.shape, x.dtype),
        in_specs=[pl.BlockSpec(memory_space=pl.ANY)],
        out_specs=pl.BlockSpec(memory_space=pl.ANY),
        scratch_shapes=[
            pltpu.SemaphoreType.DMA((count,)),
            pltpu.SemaphoreType.DMA((count,)),
            pltpu.SemaphoreType.DMA,
        ],
        compiler_params=pltpu.CompilerParams(collective_id=cid, has_side_effects=True),
    )(x)


def on_device(volume, interp, block_index, images, defocus, orient):
    slab_count = lax.axis_size(SLAB)
    slab_index = lax.axis_index(SLAB)
    orient_count = interp.shape[1]
    ori_dev = orient_count // slab_count
    block_rows = interp.shape[2]
    fourier = images.shape[2]
    block_count = fourier // block_rows
    img_dev = images.shape[1]
    picks = orient.shape[2]
    levels = jnp.arange(block_count, dtype=jnp.int32)
    partial_value = jnp.einsum("jpr,rx->jpx", interp[0], volume, preferred_element_type=jnp.float32)
    owned_idx = lax.dynamic_slice_in_dim(block_index[0], slab_index * ori_dev, ori_dev, 0)
    received = lax.all_to_all(
        partial_value.reshape(slab_count, ori_dev * block_rows, 2 * fourier),
        SLAB,
        split_axis=0,
        concat_axis=0,
        tiled=True,
    ).reshape(slab_count, ori_dev, block_rows, 2 * fourier)
    place = (owned_idx[:, :, None] == levels).astype(jnp.float32)
    summed = jnp.einsum(
        "osb,sopx->obpx", place, received, precision=lax.Precision.HIGHEST,
        preferred_element_type=jnp.float32,
    ).reshape(ori_dev, fourier, 2 * fourier)
    panels = lax.all_gather(summed.astype(jnp.bfloat16), SLAB, axis=0, tiled=True)
    sizes = tuple(lax.axis_size(a) for a in SLAB)
    inv_perm = jnp.arange(orient_count, dtype=jnp.int32).reshape(
        (sizes[2], sizes[0], sizes[1], ori_dev)
    ).transpose(1, 2, 0, 3).reshape(-1)
    weights, contrib = correlate_all(panels, images[0], orient[0], inv_perm[orient[0]], defocus[0])
    for axis in (SLAB[2], SLAB[0], SLAB[1]):
        parts = lax.axis_size(axis)
        moved = lax.all_to_all(
            contrib.astype(jnp.bfloat16), axis, split_axis=0, concat_axis=0, tiled=True
        )
        contrib = jnp.sum(
            moved.astype(jnp.float32).reshape((parts, -1) + moved.shape[1:]), axis=0
        )
    back_own = contrib.astype(jnp.bfloat16)
    back_own = back_own.reshape(ori_dev, block_count, block_rows, 2 * fourier)
    chosen_back = (owned_idx[:, :, None] == levels).astype(jnp.bfloat16)
    outgoing = jnp.einsum(
        "osb,obpx->sopx", chosen_back, back_own, preferred_element_type=jnp.float32
    )
    outgoing = outgoing.astype(jnp.bfloat16).reshape(slab_count * ori_dev, block_rows, 2 * fourier)
    incoming = lax.all_to_all(outgoing, SLAB, split_axis=0, concat_axis=0, tiled=True)
    column = jnp.einsum("jpr,jpx->rx", interp[0], incoming, preferred_element_type=jnp.float32)
    summed_cols = jnp.sum(img_gather(column, lax.axis_size("img"), 0), axis=0)
    update = summed_cols / math.sqrt(img_dev * slab_count)
    return (update, weights[None])


def solution(mesh):
    devices = mesh.devices
    cores = 2
    xs = len({d.coords[0] for d in devices.reshape(-1)}) if hasattr(devices.reshape(-1)[0], "coords") else 4
    split = devices.reshape((xs, devices.shape[0] // (xs * cores), cores) + devices.shape[1:])
    fine = jax.sharding.Mesh(split, SLAB + ("img",))
    return jax.shard_map(
        on_device,
        mesh=fine,
        in_specs=(
            P(SLAB, None),
            P("img", None, None, SLAB),
            P("img", None, None),
            P("img", SLAB, None, None),
            P("img", SLAB),
            P("img", SLAB, None),
        ),
        out_specs=(P(SLAB, None), P("img", SLAB, None)),
        check_vma=False,
    )
```

```python
import math

import jax
import jax.numpy as jnp
from jax import lax
from jax.experimental import pallas as pl
from jax.experimental.pallas import tpu as pltpu
from jax.sharding import PartitionSpec as P

BOX = 256
NS = 16
SLAB = ("sx", "sz", "sc")


wave_length = 0.0197
aberration = 27000000.0
amplitude = 0.1
grid_side = 4


def phase_tables(fourier, shifts, box):
    freq = (jnp.arange(fourier, dtype=jnp.int32) - fourier // 2).astype(jnp.float32)
    shift_steps = jnp.arange(shifts, dtype=jnp.int32)
    shift_x = (2 * (shift_steps // grid_side) - (grid_side - 1)).astype(jnp.float32)
    shift_y = (2 * (shift_steps % grid_side) - (grid_side - 1)).astype(jnp.float32)
    angle = 2.0 * math.pi / box * (freq[:, None, None] * shift_x + freq[None, :, None] * shift_y)
    forward = jnp.stack([jnp.cos(angle), jnp.sin(angle)], axis=1).reshape(
        2 * fourier * fourier, shifts
    )
    backward = jnp.stack([jnp.cos(angle), -jnp.sin(angle)], axis=1).reshape(
        2 * fourier * fourier, shifts
    )
    return (forward.astype(jnp.bfloat16), backward.T.astype(jnp.bfloat16))


def contrast(defocus_blk, fourier, box):
    freq = (jnp.arange(fourier, dtype=jnp.int32) - fourier // 2).astype(jnp.float32)
    wave_sq = (freq[:, None] * freq[:, None] + freq[None, :] * freq[None, :]) / (box * box)
    phase = math.pi * wave_length * defocus_blk[:, None, None] * wave_sq
    phase = phase - 0.5 * math.pi * aberration * wave_length**3 * wave_sq * wave_sq
    return -(math.sqrt(1.0 - amplitude * amplitude) * jnp.sin(phase) + amplitude * jnp.cos(phase))


def correlate(panels, image_blk, list_blk, defocus_blk, phase_fwd, phase_back, box):
    count = image_blk.shape[0]
    fourier = image_blk.shape[1]
    picks = list_blk.shape[1]
    shifts = phase_fwd.shape[1]
    ctf = contrast(defocus_blk, fourier, box)
    weighted = ctf[:, :, None, :] * image_blk.astype(jnp.float32).reshape(
        count, fourier, 2, fourier
    )
    real_u = weighted[:, None, :, 0]
    imag_u = weighted[:, None, :, 1]
    chosen = panels[list_blk].astype(jnp.float32).reshape(count, picks, fourier, 2, fourier)
    real_p = chosen[:, :, :, 0]
    imag_p = chosen[:, :, :, 1]
    product = jnp.stack(
        [real_p * real_u + imag_p * imag_u, real_p * imag_u - imag_p * real_u], axis=3
    )
    product = product.astype(jnp.bfloat16).reshape(count * picks, 2 * fourier * fourier)
    scores = jnp.dot(product, phase_fwd, preferred_element_type=jnp.float32) / fourier
    scores = scores.reshape(count, picks * shifts)
    squared = scores * scores
    weights = squared / (jnp.mean(squared, axis=1, keepdims=True) + 1e-05)
    rounded = weights.astype(jnp.bfloat16).reshape(count * picks, shifts)
    spread = jnp.dot(rounded, phase_back, preferred_element_type=jnp.float32)
    spread = spread.reshape(count, picks, fourier, 2, fourier)
    real_e = spread[:, :, :, 0]
    imag_e = spread[:, :, :, 1]
    backed = jnp.stack(
        [real_u * real_e - imag_u * imag_e, real_u * imag_e + imag_u * real_e], axis=3
    )
    backed = backed.astype(jnp.bfloat16).reshape(count * picks, 2 * fourier * fourier)
    return (weights, backed)


def _correlate_kernel(orient_ref, row_ref, panels_ref, image_ref, ctf_ref, cos_ref, sin_ref, w_ref, acc_ref):
    i = pl.program_id(0)
    picks = w_ref.shape[1] // cos_ref.shape[0]
    shifts = cos_ref.shape[0]
    half = ctf_ref.shape[2]

    @pl.when(i == 0)
    def _():
        acc_ref[...] = jnp.zeros_like(acc_ref)

    ctf = ctf_ref[0]
    image = image_ref[0].astype(jnp.float32)
    ur = ctf * image[:, :half]
    ui = ctf * image[:, half:]
    rows = []
    for k in range(picks):
        panel = panels_ref[row_ref[i * picks + k]].astype(jnp.float32)
        pr = panel[:, :half]
        pi = panel[:, half:]
        prod_re = (pr * ur + pi * ui).astype(jnp.bfloat16).astype(jnp.float32)
        prod_im = (pr * ui - pi * ur).astype(jnp.bfloat16).astype(jnp.float32)
        for t in range(shifts):
            v = prod_re * cos_ref[t] + prod_im * sin_ref[t]
            rows.append(jnp.sum(v, axis=0, keepdims=True))
    scores = jnp.sum(jnp.concatenate(rows, axis=0), axis=1, keepdims=True) / half
    squared = scores * scores
    mean = jnp.sum(squared, axis=0, keepdims=True) / squared.shape[0]
    weights = squared / (mean + 1e-05)
    w_ref[0] = weights
    wround = weights.astype(jnp.bfloat16).astype(jnp.float32)
    for k in range(picks):
        er = jnp.zeros_like(ur)
        ei = jnp.zeros_like(ur)
        for t in range(shifts):
            wt = wround[k * shifts + t : k * shifts + t + 1, :]
            er = er + wt * cos_ref[t]
            ei = ei - wt * sin_ref[t]
        slice_re = (ur * er - ui * ei).astype(jnp.bfloat16).astype(jnp.float32)
        slice_im = (ur * ei + ui * er).astype(jnp.bfloat16).astype(jnp.float32)
        j = row_ref[i * picks + k]
        acc_ref[j, :, :half] += slice_re
        acc_ref[j, :, half:] += slice_im


def correlate_all(panels, images, orient, rows, defocus):
    count, fourier, width = images.shape
    picks = orient.shape[1]
    orient_count = panels.shape[0]
    ctf = contrast(defocus, fourier, BOX)
    freq = (jnp.arange(fourier, dtype=jnp.int32) - fourier // 2).astype(jnp.float32)
    shift_steps = jnp.arange(NS, dtype=jnp.int32)
    shift_x = (2 * (shift_steps // grid_side) - (grid_side - 1)).astype(jnp.float32)
    shift_y = (2 * (shift_steps % grid_side) - (grid_side - 1)).astype(jnp.float32)
    angle = 2.0 * math.pi / BOX * (
        freq[None, :, None] * shift_x[:, None, None] + freq[None, None, :] * shift_y[:, None, None]
    )
    cos_t = jnp.cos(angle).astype(jnp.bfloat16).astype(jnp.float32)
    sin_t = jnp.sin(angle).astype(jnp.bfloat16).astype(jnp.float32)
    grid_spec = pltpu.PrefetchScalarGridSpec(
        num_scalar_prefetch=2,
        grid=(count,),
        in_specs=[
            pl.BlockSpec((orient_count, fourier, width), lambda i, o, w: (0, 0, 0)),
            pl.BlockSpec((1, fourier, width), lambda i, o, w: (i, 0, 0)),
            pl.BlockSpec((1, fourier, fourier), lambda i, o, w: (i, 0, 0)),
            pl.BlockSpec((NS, fourier, fourier), lambda i, o, w: (0, 0, 0)),
            pl.BlockSpec((NS, fourier, fourier), lambda i, o, w: (0, 0, 0)),
        ],
        out_specs=[
            pl.BlockSpec((1, picks * NS, 1), lambda i, o, w: (i, 0, 0)),
            pl.BlockSpec((orient_count, fourier, width), lambda i, o, w: (0, 0, 0)),
        ],
    )
    weights, contrib = pl.pallas_call(
        _correlate_kernel,
        grid_spec=grid_spec,
        out_shape=[
            jax.ShapeDtypeStruct((count, picks * NS, 1), jnp.float32),
            jax.ShapeDtypeStruct((orient_count, fourier, width), jnp.float32),
        ],
        compiler_params=pltpu.CompilerParams(
            dimension_semantics=("arbitrary",), vmem_limit_bytes=56 * 1024 * 1024
        ),
    )(orient.reshape(-1), rows.reshape(-1), panels, images, ctf, cos_t, sin_t)
    return weights.reshape(count, picks * NS), contrib


def _img_gather_kernel(x_ref, o_ref, send_sems, recv_sems, local_sem):
    count = o_ref.shape[0]
    me = lax.axis_index("img")
    here = tuple(lax.axis_index(a) for a in SLAB)
    mesh_ids = pl.DeviceIdType.MESH
    barrier = pltpu.get_barrier_semaphore()
    for i in range(count - 1):
        peer = lax.rem(me + 1 + i, count)
        pl.semaphore_signal(barrier, inc=1, device_id=here + (peer,), device_id_type=mesh_ids)
    pl.semaphore_wait(barrier, count - 1)
    local = pltpu.make_async_copy(x_ref, o_ref.at[me], local_sem)
    local.start()
    sends = []
    for i in range(count - 1):
        peer = lax.rem(me + 1 + i, count)
        copy = pltpu.make_async_remote_copy(
            src_ref=x_ref,
            dst_ref=o_ref.at[me],
            send_sem=send_sems.at[i],
            recv_sem=recv_sems.at[me],
            device_id=here + (peer,),
            device_id_type=mesh_ids,
        )
        copy.start()
        sends.append(copy)
    for i in range(count - 1):
        src = lax.rem(me + 1 + i, count)
        sends[i].wait_send()
        pltpu.make_async_remote_copy(
            src_ref=x_ref,
            dst_ref=o_ref.at[src],
            send_sem=send_sems.at[i],
            recv_sem=recv_sems.at[src],
            device_id=here + (src,),
            device_id_type=mesh_ids,
        ).wait_recv()
    local.wait()


def img_gather(x, count, cid):
    return pl.pallas_call(
        _img_gather_kernel,
        out_shape=jax.ShapeDtypeStruct((count,) + x.shape, x.dtype),
        in_specs=[pl.BlockSpec(memory_space=pl.ANY)],
        out_specs=pl.BlockSpec(memory_space=pl.ANY),
        scratch_shapes=[
            pltpu.SemaphoreType.DMA((count,)),
            pltpu.SemaphoreType.DMA((count,)),
            pltpu.SemaphoreType.DMA,
        ],
        compiler_params=pltpu.CompilerParams(collective_id=cid, has_side_effects=True),
    )(x)


def on_device(volume, interp, block_index, images, defocus, orient):
    slab_count = lax.axis_size(SLAB)
    slab_index = lax.axis_index(SLAB)
    orient_count = interp.shape[1]
    ori_dev = orient_count // slab_count
    block_rows = interp.shape[2]
    fourier = images.shape[2]
    block_count = fourier // block_rows
    img_dev = images.shape[1]
    picks = orient.shape[2]
    levels = jnp.arange(block_count, dtype=jnp.int32)
    partial_value = jnp.einsum("jpr,rx->jpx", interp[0], volume, preferred_element_type=jnp.float32)
    owned_idx = lax.dynamic_slice_in_dim(block_index[0], slab_index * ori_dev, ori_dev, 0)
    received = lax.all_to_all(
        partial_value.reshape(slab_count, ori_dev * block_rows, 2 * fourier),
        SLAB,
        split_axis=0,
        concat_axis=0,
        tiled=True,
    ).reshape(slab_count, ori_dev, block_rows, 2 * fourier)
    place = (owned_idx[:, :, None] == levels).astype(jnp.float32)
    summed = jnp.einsum(
        "osb,sopx->obpx", place, received, precision=lax.Precision.HIGHEST,
        preferred_element_type=jnp.float32,
    ).reshape(ori_dev, fourier, 2 * fourier)
    panels = summed.astype(jnp.bfloat16)
    for axis in (SLAB[1], SLAB[0], SLAB[2]):
        parts = lax.axis_size(axis)
        panels = lax.all_to_all(
            jnp.broadcast_to(panels[None], (parts,) + panels.shape),
            axis, split_axis=0, concat_axis=0, tiled=True,
        ).reshape((-1,) + panels.shape[1:])
    sizes = tuple(lax.axis_size(a) for a in SLAB)
    inv_perm = jnp.arange(orient_count, dtype=jnp.int32).reshape(
        (sizes[2], sizes[0], sizes[1], ori_dev)
    ).transpose(1, 2, 0, 3).reshape(-1)
    weights, contrib = correlate_all(panels, images[0], orient[0], inv_perm[orient[0]], defocus[0])
    for axis in (SLAB[2], SLAB[0], SLAB[1]):
        parts = lax.axis_size(axis)
        moved = lax.all_to_all(
            contrib.astype(jnp.bfloat16), axis, split_axis=0, concat_axis=0, tiled=True
        )
        contrib = jnp.sum(
            moved.astype(jnp.float32).reshape((parts, -1) + moved.shape[1:]), axis=0
        )
    back_own = contrib.astype(jnp.bfloat16)
    back_own = back_own.reshape(ori_dev, block_count, block_rows, 2 * fourier)
    chosen_back = (owned_idx[:, :, None] == levels).astype(jnp.bfloat16)
    outgoing = jnp.einsum(
        "osb,obpx->sopx", chosen_back, back_own, preferred_element_type=jnp.float32
    )
    outgoing = outgoing.astype(jnp.bfloat16).reshape(slab_count * ori_dev, block_rows, 2 * fourier)
    incoming = lax.all_to_all(outgoing, SLAB, split_axis=0, concat_axis=0, tiled=True)
    column = jnp.einsum("jpr,jpx->rx", interp[0], incoming, preferred_element_type=jnp.float32)
    summed_cols = jnp.sum(img_gather(column, lax.axis_size("img"), 0), axis=0)
    update = summed_cols / math.sqrt(img_dev * slab_count)
    return (update, weights[None])


def solution(mesh):
    devices = mesh.devices
    cores = 2
    xs = len({d.coords[0] for d in devices.reshape(-1)}) if hasattr(devices.reshape(-1)[0], "coords") else 4
    split = devices.reshape((xs, devices.shape[0] // (xs * cores), cores) + devices.shape[1:])
    fine = jax.sharding.Mesh(split, SLAB + ("img",))
    return jax.shard_map(
        on_device,
        mesh=fine,
        in_specs=(
            P(SLAB, None),
            P("img", None, None, SLAB),
            P("img", None, None),
            P("img", SLAB, None, None),
            P("img", SLAB),
            P("img", SLAB, None),
        ),
        out_specs=(P(SLAB, None), P("img", SLAB, None)),
        check_vma=False,
    )
```

```python
import math

import jax
import jax.numpy as jnp
from jax import lax
from jax.experimental import pallas as pl
from jax.experimental.pallas import tpu as pltpu
from jax.sharding import PartitionSpec as P

BOX = 256
NS = 16
SLAB = ("sx", "sz", "sc")


wave_length = 0.0197
aberration = 27000000.0
amplitude = 0.1
grid_side = 4


def phase_tables(fourier, shifts, box):
    freq = (jnp.arange(fourier, dtype=jnp.int32) - fourier // 2).astype(jnp.float32)
    shift_steps = jnp.arange(shifts, dtype=jnp.int32)
    shift_x = (2 * (shift_steps // grid_side) - (grid_side - 1)).astype(jnp.float32)
    shift_y = (2 * (shift_steps % grid_side) - (grid_side - 1)).astype(jnp.float32)
    angle = 2.0 * math.pi / box * (freq[:, None, None] * shift_x + freq[None, :, None] * shift_y)
    forward = jnp.stack([jnp.cos(angle), jnp.sin(angle)], axis=1).reshape(
        2 * fourier * fourier, shifts
    )
    backward = jnp.stack([jnp.cos(angle), -jnp.sin(angle)], axis=1).reshape(
        2 * fourier * fourier, shifts
    )
    return (forward.astype(jnp.bfloat16), backward.T.astype(jnp.bfloat16))


def contrast(defocus_blk, fourier, box):
    freq = (jnp.arange(fourier, dtype=jnp.int32) - fourier // 2).astype(jnp.float32)
    wave_sq = (freq[:, None] * freq[:, None] + freq[None, :] * freq[None, :]) / (box * box)
    phase = math.pi * wave_length * defocus_blk[:, None, None] * wave_sq
    phase = phase - 0.5 * math.pi * aberration * wave_length**3 * wave_sq * wave_sq
    return -(math.sqrt(1.0 - amplitude * amplitude) * jnp.sin(phase) + amplitude * jnp.cos(phase))


def correlate(panels, image_blk, list_blk, defocus_blk, phase_fwd, phase_back, box):
    count = image_blk.shape[0]
    fourier = image_blk.shape[1]
    picks = list_blk.shape[1]
    shifts = phase_fwd.shape[1]
    ctf = contrast(defocus_blk, fourier, box)
    weighted = ctf[:, :, None, :] * image_blk.astype(jnp.float32).reshape(
        count, fourier, 2, fourier
    )
    real_u = weighted[:, None, :, 0]
    imag_u = weighted[:, None, :, 1]
    chosen = panels[list_blk].astype(jnp.float32).reshape(count, picks, fourier, 2, fourier)
    real_p = chosen[:, :, :, 0]
    imag_p = chosen[:, :, :, 1]
    product = jnp.stack(
        [real_p * real_u + imag_p * imag_u, real_p * imag_u - imag_p * real_u], axis=3
    )
    product = product.astype(jnp.bfloat16).reshape(count * picks, 2 * fourier * fourier)
    scores = jnp.dot(product, phase_fwd, preferred_element_type=jnp.float32) / fourier
    scores = scores.reshape(count, picks * shifts)
    squared = scores * scores
    weights = squared / (jnp.mean(squared, axis=1, keepdims=True) + 1e-05)
    rounded = weights.astype(jnp.bfloat16).reshape(count * picks, shifts)
    spread = jnp.dot(rounded, phase_back, preferred_element_type=jnp.float32)
    spread = spread.reshape(count, picks, fourier, 2, fourier)
    real_e = spread[:, :, :, 0]
    imag_e = spread[:, :, :, 1]
    backed = jnp.stack(
        [real_u * real_e - imag_u * imag_e, real_u * imag_e + imag_u * real_e], axis=3
    )
    backed = backed.astype(jnp.bfloat16).reshape(count * picks, 2 * fourier * fourier)
    return (weights, backed)


def _correlate_kernel(orient_ref, row_ref, panels_ref, image_ref, ctf_ref, cos_ref, sin_ref, w_ref, acc_ref):
    i = pl.program_id(0)
    picks = w_ref.shape[1] // cos_ref.shape[0]
    shifts = cos_ref.shape[0]
    half = ctf_ref.shape[2]

    @pl.when(i == 0)
    def _():
        acc_ref[...] = jnp.zeros_like(acc_ref)

    ctf = ctf_ref[0]
    image = image_ref[0].astype(jnp.float32)
    ur = ctf * image[:, :half]
    ui = ctf * image[:, half:]
    rows = []
    for k in range(picks):
        panel = panels_ref[row_ref[i * picks + k]].astype(jnp.float32)
        pr = panel[:, :half]
        pi = panel[:, half:]
        prod_re = (pr * ur + pi * ui).astype(jnp.bfloat16).astype(jnp.float32)
        prod_im = (pr * ui - pi * ur).astype(jnp.bfloat16).astype(jnp.float32)
        for t in range(shifts):
            v = prod_re * cos_ref[t] + prod_im * sin_ref[t]
            rows.append(jnp.sum(v, axis=0, keepdims=True))
    scores = jnp.sum(jnp.concatenate(rows, axis=0), axis=1, keepdims=True) / half
    squared = scores * scores
    mean = jnp.sum(squared, axis=0, keepdims=True) / squared.shape[0]
    weights = squared / (mean + 1e-05)
    w_ref[0] = weights
    wround = weights.astype(jnp.bfloat16).astype(jnp.float32)
    for k in range(picks):
        er = jnp.zeros_like(ur)
        ei = jnp.zeros_like(ur)
        for t in range(shifts):
            wt = wround[k * shifts + t : k * shifts + t + 1, :]
            er = er + wt * cos_ref[t]
            ei = ei - wt * sin_ref[t]
        slice_re = (ur * er - ui * ei).astype(jnp.bfloat16).astype(jnp.float32)
        slice_im = (ur * ei + ui * er).astype(jnp.bfloat16).astype(jnp.float32)
        j = row_ref[i * picks + k]
        acc_ref[j, :, :half] += slice_re
        acc_ref[j, :, half:] += slice_im


def correlate_all(panels, images, orient, rows, defocus):
    count, fourier, width = images.shape
    picks = orient.shape[1]
    orient_count = panels.shape[0]
    ctf = contrast(defocus, fourier, BOX)
    freq = (jnp.arange(fourier, dtype=jnp.int32) - fourier // 2).astype(jnp.float32)
    shift_steps = jnp.arange(NS, dtype=jnp.int32)
    shift_x = (2 * (shift_steps // grid_side) - (grid_side - 1)).astype(jnp.float32)
    shift_y = (2 * (shift_steps % grid_side) - (grid_side - 1)).astype(jnp.float32)
    angle = 2.0 * math.pi / BOX * (
        freq[None, :, None] * shift_x[:, None, None] + freq[None, None, :] * shift_y[:, None, None]
    )
    cos_t = jnp.cos(angle).astype(jnp.bfloat16).astype(jnp.float32)
    sin_t = jnp.sin(angle).astype(jnp.bfloat16).astype(jnp.float32)
    grid_spec = pltpu.PrefetchScalarGridSpec(
        num_scalar_prefetch=2,
        grid=(count,),
        in_specs=[
            pl.BlockSpec((orient_count, fourier, width), lambda i, o, w: (0, 0, 0)),
            pl.BlockSpec((1, fourier, width), lambda i, o, w: (i, 0, 0)),
            pl.BlockSpec((1, fourier, fourier), lambda i, o, w: (i, 0, 0)),
            pl.BlockSpec((NS, fourier, fourier), lambda i, o, w: (0, 0, 0)),
            pl.BlockSpec((NS, fourier, fourier), lambda i, o, w: (0, 0, 0)),
        ],
        out_specs=[
            pl.BlockSpec((1, picks * NS, 1), lambda i, o, w: (i, 0, 0)),
            pl.BlockSpec((orient_count, fourier, width), lambda i, o, w: (0, 0, 0)),
        ],
    )
    weights, contrib = pl.pallas_call(
        _correlate_kernel,
        grid_spec=grid_spec,
        out_shape=[
            jax.ShapeDtypeStruct((count, picks * NS, 1), jnp.float32),
            jax.ShapeDtypeStruct((orient_count, fourier, width), jnp.float32),
        ],
        compiler_params=pltpu.CompilerParams(
            dimension_semantics=("arbitrary",), vmem_limit_bytes=56 * 1024 * 1024
        ),
    )(orient.reshape(-1), rows.reshape(-1), panels, images, ctf, cos_t, sin_t)
    return weights.reshape(count, picks * NS), contrib


def _img_gather_kernel(x_ref, o_ref, send_sems, recv_sems, local_sem):
    count = o_ref.shape[0]
    me = lax.axis_index("img")
    here = tuple(lax.axis_index(a) for a in SLAB)
    mesh_ids = pl.DeviceIdType.MESH
    barrier = pltpu.get_barrier_semaphore()
    for i in range(count - 1):
        peer = lax.rem(me + 1 + i, count)
        pl.semaphore_signal(barrier, inc=1, device_id=here + (peer,), device_id_type=mesh_ids)
    pl.semaphore_wait(barrier, count - 1)
    local = pltpu.make_async_copy(x_ref, o_ref.at[me], local_sem)
    local.start()
    sends = []
    for i in range(count - 1):
        peer = lax.rem(me + 1 + i, count)
        copy = pltpu.make_async_remote_copy(
            src_ref=x_ref,
            dst_ref=o_ref.at[me],
            send_sem=send_sems.at[i],
            recv_sem=recv_sems.at[me],
            device_id=here + (peer,),
            device_id_type=mesh_ids,
        )
        copy.start()
        sends.append(copy)
    for i in range(count - 1):
        src = lax.rem(me + 1 + i, count)
        sends[i].wait_send()
        pltpu.make_async_remote_copy(
            src_ref=x_ref,
            dst_ref=o_ref.at[src],
            send_sem=send_sems.at[i],
            recv_sem=recv_sems.at[src],
            device_id=here + (src,),
            device_id_type=mesh_ids,
        ).wait_recv()
    local.wait()


def img_gather(x, count, cid):
    return pl.pallas_call(
        _img_gather_kernel,
        out_shape=jax.ShapeDtypeStruct((count,) + x.shape, x.dtype),
        in_specs=[pl.BlockSpec(memory_space=pl.ANY)],
        out_specs=pl.BlockSpec(memory_space=pl.ANY),
        scratch_shapes=[
            pltpu.SemaphoreType.DMA((count,)),
            pltpu.SemaphoreType.DMA((count,)),
            pltpu.SemaphoreType.DMA,
        ],
        compiler_params=pltpu.CompilerParams(collective_id=cid, has_side_effects=True),
    )(x)


def _a2a_kernel(x_ref, o_ref, send_sems, recv_sems, local_sem):
    count = x_ref.shape[0]
    sizes = tuple(lax.axis_size(a) for a in SLAB)
    me = lax.axis_index(SLAB)
    grp = lax.axis_index("img")
    mesh_ids = pl.DeviceIdType.MESH
    barrier = pltpu.get_barrier_semaphore()

    def where(peer):
        return (peer // (sizes[1] * sizes[2]), (peer // sizes[2]) % sizes[1], peer % sizes[2], grp)

    def greet(i, carry):
        pl.semaphore_signal(
            barrier, inc=1, device_id=where(lax.rem(me + 1 + i, count)), device_id_type=mesh_ids
        )
        return carry

    lax.fori_loop(0, count - 1, greet, 0)
    pl.semaphore_wait(barrier, count - 1)
    local = pltpu.make_async_copy(x_ref.at[me], o_ref.at[me], local_sem)
    local.start()

    def outgoing(peer):
        return pltpu.make_async_remote_copy(
            src_ref=x_ref.at[peer],
            dst_ref=o_ref.at[me],
            send_sem=send_sems.at[peer],
            recv_sem=recv_sems.at[me],
            device_id=where(peer),
            device_id_type=mesh_ids,
        )

    def incoming(src):
        return pltpu.make_async_remote_copy(
            src_ref=x_ref.at[src],
            dst_ref=o_ref.at[src],
            send_sem=send_sems.at[src],
            recv_sem=recv_sems.at[src],
            device_id=where(src),
            device_id_type=mesh_ids,
        )

    def send(i, carry):
        outgoing(lax.rem(me + 1 + i, count)).start()
        return carry

    lax.fori_loop(0, count - 1, send, 0)

    def finish(i, carry):
        outgoing(lax.rem(me + 1 + i, count)).wait_send()
        incoming(lax.rem(me + count - 1 - i, count)).wait_recv()
        return carry

    lax.fori_loop(0, count - 1, finish, 0)
    local.wait()


def slab_all_to_all(x, cid):
    count = x.shape[0]
    return pl.pallas_call(
        _a2a_kernel,
        out_shape=jax.ShapeDtypeStruct(x.shape, x.dtype),
        in_specs=[pl.BlockSpec(memory_space=pl.ANY)],
        out_specs=pl.BlockSpec(memory_space=pl.ANY),
        scratch_shapes=[
            pltpu.SemaphoreType.DMA((count,)),
            pltpu.SemaphoreType.DMA((count,)),
            pltpu.SemaphoreType.DMA,
        ],
        compiler_params=pltpu.CompilerParams(collective_id=cid, has_side_effects=True),
    )(x)


def on_device(volume, interp, block_index, images, defocus, orient):
    slab_count = lax.axis_size(SLAB)
    slab_index = lax.axis_index(SLAB)
    orient_count = interp.shape[1]
    ori_dev = orient_count // slab_count
    block_rows = interp.shape[2]
    fourier = images.shape[2]
    block_count = fourier // block_rows
    img_dev = images.shape[1]
    picks = orient.shape[2]
    levels = jnp.arange(block_count, dtype=jnp.int32)
    partial_value = jnp.einsum("jpr,rx->jpx", interp[0], volume, preferred_element_type=jnp.float32)
    owned_idx = lax.dynamic_slice_in_dim(block_index[0], slab_index * ori_dev, ori_dev, 0)
    received = slab_all_to_all(
        partial_value.reshape(slab_count, ori_dev * block_rows, 2 * fourier), 1
    ).reshape(slab_count, ori_dev, block_rows, 2 * fourier)
    place = (owned_idx[:, :, None] == levels).astype(jnp.float32)
    summed = jnp.einsum(
        "osb,sopx->obpx", place, received, precision=lax.Precision.HIGHEST,
        preferred_element_type=jnp.float32,
    ).reshape(ori_dev, fourier, 2 * fourier)
    panels = summed.astype(jnp.bfloat16)
    for axis in (SLAB[1], SLAB[0], SLAB[2]):
        parts = lax.axis_size(axis)
        panels = lax.all_to_all(
            jnp.broadcast_to(panels[None], (parts,) + panels.shape),
            axis, split_axis=0, concat_axis=0, tiled=True,
        ).reshape((-1,) + panels.shape[1:])
    sizes = tuple(lax.axis_size(a) for a in SLAB)
    inv_perm = jnp.arange(orient_count, dtype=jnp.int32).reshape(
        (sizes[2], sizes[0], sizes[1], ori_dev)
    ).transpose(1, 2, 0, 3).reshape(-1)
    weights, contrib = correlate_all(panels, images[0], orient[0], inv_perm[orient[0]], defocus[0])
    for axis in (SLAB[2], SLAB[0], SLAB[1]):
        parts = lax.axis_size(axis)
        moved = lax.all_to_all(
            contrib.astype(jnp.bfloat16), axis, split_axis=0, concat_axis=0, tiled=True
        )
        contrib = jnp.sum(
            moved.astype(jnp.float32).reshape((parts, -1) + moved.shape[1:]), axis=0
        )
    back_own = contrib.astype(jnp.bfloat16)
    back_own = back_own.reshape(ori_dev, block_count, block_rows, 2 * fourier)
    chosen_back = (owned_idx[:, :, None] == levels).astype(jnp.bfloat16)
    outgoing = jnp.einsum(
        "osb,obpx->sopx", chosen_back, back_own, preferred_element_type=jnp.float32
    )
    outgoing = outgoing.astype(jnp.bfloat16).reshape(slab_count * ori_dev, block_rows, 2 * fourier)
    incoming = lax.all_to_all(outgoing, SLAB, split_axis=0, concat_axis=0, tiled=True)
    column = jnp.einsum("jpr,jpx->rx", interp[0], incoming, preferred_element_type=jnp.float32)
    summed_cols = jnp.sum(img_gather(column, lax.axis_size("img"), 0), axis=0)
    update = summed_cols / math.sqrt(img_dev * slab_count)
    return (update, weights[None])


def solution(mesh):
    devices = mesh.devices
    cores = 2
    xs = len({d.coords[0] for d in devices.reshape(-1)}) if hasattr(devices.reshape(-1)[0], "coords") else 4
    split = devices.reshape((xs, devices.shape[0] // (xs * cores), cores) + devices.shape[1:])
    fine = jax.sharding.Mesh(split, SLAB + ("img",))
    return jax.shard_map(
        on_device,
        mesh=fine,
        in_specs=(
            P(SLAB, None),
            P("img", None, None, SLAB),
            P("img", None, None),
            P("img", SLAB, None, None),
            P("img", SLAB),
            P("img", SLAB, None),
        ),
        out_specs=(P(SLAB, None), P("img", SLAB, None)),
        check_vma=False,
    )
```

```python
import math

import jax
import jax.numpy as jnp
from jax import lax
from jax.experimental import pallas as pl
from jax.experimental.pallas import tpu as pltpu
from jax.sharding import PartitionSpec as P

BOX = 256
NS = 16
SLAB = ("sx", "sz", "sc")


wave_length = 0.0197
aberration = 27000000.0
amplitude = 0.1
grid_side = 4


def phase_tables(fourier, shifts, box):
    freq = (jnp.arange(fourier, dtype=jnp.int32) - fourier // 2).astype(jnp.float32)
    shift_steps = jnp.arange(shifts, dtype=jnp.int32)
    shift_x = (2 * (shift_steps // grid_side) - (grid_side - 1)).astype(jnp.float32)
    shift_y = (2 * (shift_steps % grid_side) - (grid_side - 1)).astype(jnp.float32)
    angle = 2.0 * math.pi / box * (freq[:, None, None] * shift_x + freq[None, :, None] * shift_y)
    forward = jnp.stack([jnp.cos(angle), jnp.sin(angle)], axis=1).reshape(
        2 * fourier * fourier, shifts
    )
    backward = jnp.stack([jnp.cos(angle), -jnp.sin(angle)], axis=1).reshape(
        2 * fourier * fourier, shifts
    )
    return (forward.astype(jnp.bfloat16), backward.T.astype(jnp.bfloat16))


def contrast(defocus_blk, fourier, box):
    freq = (jnp.arange(fourier, dtype=jnp.int32) - fourier // 2).astype(jnp.float32)
    wave_sq = (freq[:, None] * freq[:, None] + freq[None, :] * freq[None, :]) / (box * box)
    phase = math.pi * wave_length * defocus_blk[:, None, None] * wave_sq
    phase = phase - 0.5 * math.pi * aberration * wave_length**3 * wave_sq * wave_sq
    return -(math.sqrt(1.0 - amplitude * amplitude) * jnp.sin(phase) + amplitude * jnp.cos(phase))


def correlate(panels, image_blk, list_blk, defocus_blk, phase_fwd, phase_back, box):
    count = image_blk.shape[0]
    fourier = image_blk.shape[1]
    picks = list_blk.shape[1]
    shifts = phase_fwd.shape[1]
    ctf = contrast(defocus_blk, fourier, box)
    weighted = ctf[:, :, None, :] * image_blk.astype(jnp.float32).reshape(
        count, fourier, 2, fourier
    )
    real_u = weighted[:, None, :, 0]
    imag_u = weighted[:, None, :, 1]
    chosen = panels[list_blk].astype(jnp.float32).reshape(count, picks, fourier, 2, fourier)
    real_p = chosen[:, :, :, 0]
    imag_p = chosen[:, :, :, 1]
    product = jnp.stack(
        [real_p * real_u + imag_p * imag_u, real_p * imag_u - imag_p * real_u], axis=3
    )
    product = product.astype(jnp.bfloat16).reshape(count * picks, 2 * fourier * fourier)
    scores = jnp.dot(product, phase_fwd, preferred_element_type=jnp.float32) / fourier
    scores = scores.reshape(count, picks * shifts)
    squared = scores * scores
    weights = squared / (jnp.mean(squared, axis=1, keepdims=True) + 1e-05)
    rounded = weights.astype(jnp.bfloat16).reshape(count * picks, shifts)
    spread = jnp.dot(rounded, phase_back, preferred_element_type=jnp.float32)
    spread = spread.reshape(count, picks, fourier, 2, fourier)
    real_e = spread[:, :, :, 0]
    imag_e = spread[:, :, :, 1]
    backed = jnp.stack(
        [real_u * real_e - imag_u * imag_e, real_u * imag_e + imag_u * real_e], axis=3
    )
    backed = backed.astype(jnp.bfloat16).reshape(count * picks, 2 * fourier * fourier)
    return (weights, backed)


def _correlate_kernel(orient_ref, row_ref, panels_ref, image_ref, ctf_ref, cos_ref, sin_ref, w_ref, out_ref, acc_ref):
    i = pl.program_id(0)
    picks = w_ref.shape[1] // cos_ref.shape[0]
    shifts = cos_ref.shape[0]
    half = ctf_ref.shape[2]

    @pl.when(i == 0)
    def _():
        acc_ref[...] = jnp.zeros_like(acc_ref)

    ctf = ctf_ref[0]
    image = image_ref[0].astype(jnp.float32)
    ur = ctf * image[:, :half]
    ui = ctf * image[:, half:]
    rows = []
    for k in range(picks):
        panel = panels_ref[row_ref[i * picks + k]].astype(jnp.float32)
        pr = panel[:, :half]
        pi = panel[:, half:]
        prod_re = (pr * ur + pi * ui).astype(jnp.bfloat16).astype(jnp.float32)
        prod_im = (pr * ui - pi * ur).astype(jnp.bfloat16).astype(jnp.float32)
        for t in range(shifts):
            v = prod_re * cos_ref[t] + prod_im * sin_ref[t]
            rows.append(jnp.sum(v, axis=0, keepdims=True))
    scores = jnp.sum(jnp.concatenate(rows, axis=0), axis=1, keepdims=True) / half
    squared = scores * scores
    mean = jnp.sum(squared, axis=0, keepdims=True) / squared.shape[0]
    weights = squared / (mean + 1e-05)
    w_ref[0] = weights
    wround = weights.astype(jnp.bfloat16).astype(jnp.float32)
    for k in range(picks):
        er = jnp.zeros_like(ur)
        ei = jnp.zeros_like(ur)
        for t in range(shifts):
            wt = wround[k * shifts + t : k * shifts + t + 1, :]
            er = er + wt * cos_ref[t]
            ei = ei - wt * sin_ref[t]
        slice_re = (ur * er - ui * ei).astype(jnp.bfloat16).astype(jnp.float32)
        slice_im = (ur * ei + ui * er).astype(jnp.bfloat16).astype(jnp.float32)
        j = row_ref[i * picks + k]
        acc_ref[j, :, :half] += slice_re
        acc_ref[j, :, half:] += slice_im

    @pl.when(i == pl.num_programs(0) - 1)
    def _():
        out_ref[...] = acc_ref[...].astype(out_ref.dtype)


def correlate_all(panels, images, orient, rows, defocus):
    count, fourier, width = images.shape
    picks = orient.shape[1]
    orient_count = panels.shape[0]
    ctf = contrast(defocus, fourier, BOX)
    freq = (jnp.arange(fourier, dtype=jnp.int32) - fourier // 2).astype(jnp.float32)
    shift_steps = jnp.arange(NS, dtype=jnp.int32)
    shift_x = (2 * (shift_steps // grid_side) - (grid_side - 1)).astype(jnp.float32)
    shift_y = (2 * (shift_steps % grid_side) - (grid_side - 1)).astype(jnp.float32)
    angle = 2.0 * math.pi / BOX * (
        freq[None, :, None] * shift_x[:, None, None] + freq[None, None, :] * shift_y[:, None, None]
    )
    cos_t = jnp.cos(angle).astype(jnp.bfloat16).astype(jnp.float32)
    sin_t = jnp.sin(angle).astype(jnp.bfloat16).astype(jnp.float32)
    grid_spec = pltpu.PrefetchScalarGridSpec(
        num_scalar_prefetch=2,
        grid=(count,),
        in_specs=[
            pl.BlockSpec((orient_count, fourier, width), lambda i, o, w: (0, 0, 0)),
            pl.BlockSpec((1, fourier, width), lambda i, o, w: (i, 0, 0)),
            pl.BlockSpec((1, fourier, fourier), lambda i, o, w: (i, 0, 0)),
            pl.BlockSpec((NS, fourier, fourier), lambda i, o, w: (0, 0, 0)),
            pl.BlockSpec((NS, fourier, fourier), lambda i, o, w: (0, 0, 0)),
        ],
        out_specs=[
            pl.BlockSpec((1, picks * NS, 1), lambda i, o, w: (i, 0, 0)),
            pl.BlockSpec((orient_count, fourier, width), lambda i, o, w: (0, 0, 0)),
        ],
        scratch_shapes=[pltpu.VMEM((orient_count, fourier, width), jnp.float32)],
    )
    weights, contrib = pl.pallas_call(
        _correlate_kernel,
        grid_spec=grid_spec,
        out_shape=[
            jax.ShapeDtypeStruct((count, picks * NS, 1), jnp.float32),
            jax.ShapeDtypeStruct((orient_count, fourier, width), jnp.bfloat16),
        ],
        compiler_params=pltpu.CompilerParams(
            dimension_semantics=("arbitrary",), vmem_limit_bytes=56 * 1024 * 1024
        ),
    )(orient.reshape(-1), rows.reshape(-1), panels, images, ctf, cos_t, sin_t)
    return weights.reshape(count, picks * NS), contrib


def _img_sum_kernel(x_ref, o_ref, gat, qbuf, s1, r1, s2, r2, l1, l2):
    count, rows = gat.shape[0], gat.shape[1]
    me = lax.axis_index("img")
    here = tuple(lax.axis_index(a) for a in SLAB)
    mesh_ids = pl.DeviceIdType.MESH
    barrier = pltpu.get_barrier_semaphore()
    peers = [lax.rem(me + 1 + i, count) for i in range(count - 1)]
    for peer in peers:
        pl.semaphore_signal(barrier, inc=1, device_id=here + (peer,), device_id_type=mesh_ids)
    pl.semaphore_wait(barrier, count - 1)

    def part(p):
        return x_ref.at[pl.ds(pl.multiple_of(p * rows, rows), rows)]

    local = pltpu.make_async_copy(part(me), gat.at[me], l1)
    local.start()
    sends = []
    for i, peer in enumerate(peers):
        copy = pltpu.make_async_remote_copy(
            src_ref=part(peer), dst_ref=gat.at[me], send_sem=s1.at[i], recv_sem=r1.at[me],
            device_id=here + (peer,), device_id_type=mesh_ids,
        )
        copy.start()
        sends.append(copy)
    for i, peer in enumerate(peers):
        sends[i].wait_send()
        pltpu.make_async_remote_copy(
            src_ref=part(peer), dst_ref=gat.at[peer], send_sem=s1.at[i], recv_sem=r1.at[peer],
            device_id=here + (peer,), device_id_type=mesh_ids,
        ).wait_recv()
    local.wait()
    qbuf[...] = jnp.sum(gat[...], axis=0)
    local = pltpu.make_async_copy(qbuf, o_ref.at[me], l2)
    local.start()
    sends = []
    for i, peer in enumerate(peers):
        copy = pltpu.make_async_remote_copy(
            src_ref=qbuf, dst_ref=o_ref.at[me], send_sem=s2.at[i], recv_sem=r2.at[me],
            device_id=here + (peer,), device_id_type=mesh_ids,
        )
        copy.start()
        sends.append(copy)
    for i, peer in enumerate(peers):
        sends[i].wait_send()
        pltpu.make_async_remote_copy(
            src_ref=qbuf, dst_ref=o_ref.at[peer], send_sem=s2.at[i], recv_sem=r2.at[peer],
            device_id=here + (peer,), device_id_type=mesh_ids,
        ).wait_recv()
    local.wait()


def img_sum(x, count, cid):
    rows = x.shape[0] // count
    out = pl.pallas_call(
        _img_sum_kernel,
        out_shape=jax.ShapeDtypeStruct((count, rows) + x.shape[1:], x.dtype),
        in_specs=[pl.BlockSpec(memory_space=pltpu.VMEM)],
        out_specs=pl.BlockSpec(memory_space=pl.ANY),
        scratch_shapes=[
            pltpu.VMEM((count, rows) + x.shape[1:], x.dtype),
            pltpu.VMEM((rows,) + x.shape[1:], x.dtype),
            pltpu.SemaphoreType.DMA((count,)),
            pltpu.SemaphoreType.DMA((count,)),
            pltpu.SemaphoreType.DMA((count,)),
            pltpu.SemaphoreType.DMA((count,)),
            pltpu.SemaphoreType.DMA,
            pltpu.SemaphoreType.DMA,
        ],
        compiler_params=pltpu.CompilerParams(collective_id=cid, has_side_effects=True),
    )(x)
    return out.reshape(x.shape)


def _a2a_kernel(x_ref, o_ref, send_sems, recv_sems, local_sem):
    count = x_ref.shape[0]
    sizes = tuple(lax.axis_size(a) for a in SLAB)
    me = lax.axis_index(SLAB)
    grp = lax.axis_index("img")
    mesh_ids = pl.DeviceIdType.MESH
    barrier = pltpu.get_barrier_semaphore()

    def where(peer):
        return (peer // (sizes[1] * sizes[2]), (peer // sizes[2]) % sizes[1], peer % sizes[2], grp)

    def greet(i, carry):
        pl.semaphore_signal(
            barrier, inc=1, device_id=where(lax.rem(me + 1 + i, count)), device_id_type=mesh_ids
        )
        return carry

    lax.fori_loop(0, count - 1, greet, 0)
    pl.semaphore_wait(barrier, count - 1)
    local = pltpu.make_async_copy(x_ref.at[me], o_ref.at[me], local_sem)
    local.start()

    def outgoing(peer):
        return pltpu.make_async_remote_copy(
            src_ref=x_ref.at[peer],
            dst_ref=o_ref.at[me],
            send_sem=send_sems.at[peer],
            recv_sem=recv_sems.at[me],
            device_id=where(peer),
            device_id_type=mesh_ids,
        )

    def incoming(src):
        return pltpu.make_async_remote_copy(
            src_ref=x_ref.at[src],
            dst_ref=o_ref.at[src],
            send_sem=send_sems.at[src],
            recv_sem=recv_sems.at[src],
            device_id=where(src),
            device_id_type=mesh_ids,
        )

    def send(i, carry):
        outgoing(lax.rem(me + 1 + i, count)).start()
        return carry

    lax.fori_loop(0, count - 1, send, 0)

    def finish(i, carry):
        outgoing(lax.rem(me + 1 + i, count)).wait_send()
        incoming(lax.rem(me + count - 1 - i, count)).wait_recv()
        return carry

    lax.fori_loop(0, count - 1, finish, 0)
    local.wait()


def slab_all_to_all(x, cid):
    count = x.shape[0]
    return pl.pallas_call(
        _a2a_kernel,
        out_shape=jax.ShapeDtypeStruct(x.shape, x.dtype),
        in_specs=[pl.BlockSpec(memory_space=pl.ANY)],
        out_specs=pl.BlockSpec(memory_space=pl.ANY),
        scratch_shapes=[
            pltpu.SemaphoreType.DMA((count,)),
            pltpu.SemaphoreType.DMA((count,)),
            pltpu.SemaphoreType.DMA,
        ],
        compiler_params=pltpu.CompilerParams(collective_id=cid, has_side_effects=True),
    )(x)


def on_device(volume, interp, block_index, images, defocus, orient):
    slab_count = lax.axis_size(SLAB)
    slab_index = lax.axis_index(SLAB)
    orient_count = interp.shape[1]
    ori_dev = orient_count // slab_count
    block_rows = interp.shape[2]
    fourier = images.shape[2]
    block_count = fourier // block_rows
    img_dev = images.shape[1]
    picks = orient.shape[2]
    levels = jnp.arange(block_count, dtype=jnp.int32)
    partial_value = jnp.einsum("jpr,rx->jpx", interp[0], volume, preferred_element_type=jnp.float32)
    owned_idx = lax.dynamic_slice_in_dim(block_index[0], slab_index * ori_dev, ori_dev, 0)
    received = slab_all_to_all(
        partial_value.reshape(slab_count, ori_dev * block_rows, 2 * fourier), 1
    ).reshape(slab_count, ori_dev, block_rows, 2 * fourier)
    place = (owned_idx[:, :, None] == levels).astype(jnp.float32)
    summed = jnp.einsum(
        "osb,sopx->obpx", place, received, precision=lax.Precision.HIGHEST,
        preferred_element_type=jnp.float32,
    ).reshape(ori_dev, fourier, 2 * fourier)
    panels = summed.astype(jnp.bfloat16)
    for axis in (SLAB[1], SLAB[0], SLAB[2]):
        parts = lax.axis_size(axis)
        panels = lax.all_to_all(
            jnp.broadcast_to(panels[None], (parts,) + panels.shape),
            axis, split_axis=0, concat_axis=0, tiled=True,
        ).reshape((-1,) + panels.shape[1:])
    sizes = tuple(lax.axis_size(a) for a in SLAB)
    inv_perm = jnp.arange(orient_count, dtype=jnp.int32).reshape(
        (sizes[2], sizes[0], sizes[1], ori_dev)
    ).transpose(1, 2, 0, 3).reshape(-1)
    weights, contrib = correlate_all(panels, images[0], orient[0], inv_perm[orient[0]], defocus[0])
    for axis in (SLAB[2], SLAB[0], SLAB[1]):
        parts = lax.axis_size(axis)
        moved = lax.all_to_all(
            contrib.astype(jnp.bfloat16), axis, split_axis=0, concat_axis=0, tiled=True
        )
        contrib = jnp.sum(
            moved.astype(jnp.float32).reshape((parts, -1) + moved.shape[1:]), axis=0
        )
    back_own = contrib.astype(jnp.bfloat16)
    back_own = back_own.reshape(ori_dev, block_count, block_rows, 2 * fourier)
    chosen_back = (owned_idx[:, :, None] == levels).astype(jnp.bfloat16)
    outgoing = jnp.einsum(
        "osb,obpx->sopx", chosen_back, back_own, preferred_element_type=jnp.float32
    )
    outgoing = outgoing.astype(jnp.bfloat16).reshape(slab_count * ori_dev, block_rows, 2 * fourier)
    incoming = lax.all_to_all(outgoing, SLAB, split_axis=0, concat_axis=0, tiled=True)
    column = jnp.einsum("jpr,jpx->rx", interp[0], incoming, preferred_element_type=jnp.float32)
    summed_cols = img_sum(column, lax.axis_size("img"), 0)
    update = summed_cols / math.sqrt(img_dev * slab_count)
    return (update, weights[None])


def solution(mesh):
    devices = mesh.devices
    cores = 2
    xs = len({d.coords[0] for d in devices.reshape(-1)}) if hasattr(devices.reshape(-1)[0], "coords") else 4
    split = devices.reshape((xs, devices.shape[0] // (xs * cores), cores) + devices.shape[1:])
    fine = jax.sharding.Mesh(split, SLAB + ("img",))
    return jax.shard_map(
        on_device,
        mesh=fine,
        in_specs=(
            P(SLAB, None),
            P("img", None, None, SLAB),
            P("img", None, None),
            P("img", SLAB, None, None),
            P("img", SLAB),
            P("img", SLAB, None),
        ),
        out_specs=(P(SLAB, None), P("img", SLAB, None)),
        check_vma=False,
    )
```

```python
import math

import jax
import jax.numpy as jnp
from jax import lax
from jax.experimental import pallas as pl
from jax.experimental.pallas import tpu as pltpu
from jax.sharding import PartitionSpec as P

BOX = 256
NS = 16
SLAB = ("sx", "sz", "sc")


wave_length = 0.0197
aberration = 27000000.0
amplitude = 0.1
grid_side = 4


def phase_tables(fourier, shifts, box):
    freq = (jnp.arange(fourier, dtype=jnp.int32) - fourier // 2).astype(jnp.float32)
    shift_steps = jnp.arange(shifts, dtype=jnp.int32)
    shift_x = (2 * (shift_steps // grid_side) - (grid_side - 1)).astype(jnp.float32)
    shift_y = (2 * (shift_steps % grid_side) - (grid_side - 1)).astype(jnp.float32)
    angle = 2.0 * math.pi / box * (freq[:, None, None] * shift_x + freq[None, :, None] * shift_y)
    forward = jnp.stack([jnp.cos(angle), jnp.sin(angle)], axis=1).reshape(
        2 * fourier * fourier, shifts
    )
    backward = jnp.stack([jnp.cos(angle), -jnp.sin(angle)], axis=1).reshape(
        2 * fourier * fourier, shifts
    )
    return (forward.astype(jnp.bfloat16), backward.T.astype(jnp.bfloat16))


def contrast(defocus_blk, fourier, box):
    freq = (jnp.arange(fourier, dtype=jnp.int32) - fourier // 2).astype(jnp.float32)
    wave_sq = (freq[:, None] * freq[:, None] + freq[None, :] * freq[None, :]) / (box * box)
    phase = math.pi * wave_length * defocus_blk[:, None, None] * wave_sq
    phase = phase - 0.5 * math.pi * aberration * wave_length**3 * wave_sq * wave_sq
    return -(math.sqrt(1.0 - amplitude * amplitude) * jnp.sin(phase) + amplitude * jnp.cos(phase))


def correlate(panels, image_blk, list_blk, defocus_blk, phase_fwd, phase_back, box):
    count = image_blk.shape[0]
    fourier = image_blk.shape[1]
    picks = list_blk.shape[1]
    shifts = phase_fwd.shape[1]
    ctf = contrast(defocus_blk, fourier, box)
    weighted = ctf[:, :, None, :] * image_blk.astype(jnp.float32).reshape(
        count, fourier, 2, fourier
    )
    real_u = weighted[:, None, :, 0]
    imag_u = weighted[:, None, :, 1]
    chosen = panels[list_blk].astype(jnp.float32).reshape(count, picks, fourier, 2, fourier)
    real_p = chosen[:, :, :, 0]
    imag_p = chosen[:, :, :, 1]
    product = jnp.stack(
        [real_p * real_u + imag_p * imag_u, real_p * imag_u - imag_p * real_u], axis=3
    )
    product = product.astype(jnp.bfloat16).reshape(count * picks, 2 * fourier * fourier)
    scores = jnp.dot(product, phase_fwd, preferred_element_type=jnp.float32) / fourier
    scores = scores.reshape(count, picks * shifts)
    squared = scores * scores
    weights = squared / (jnp.mean(squared, axis=1, keepdims=True) + 1e-05)
    rounded = weights.astype(jnp.bfloat16).reshape(count * picks, shifts)
    spread = jnp.dot(rounded, phase_back, preferred_element_type=jnp.float32)
    spread = spread.reshape(count, picks, fourier, 2, fourier)
    real_e = spread[:, :, :, 0]
    imag_e = spread[:, :, :, 1]
    backed = jnp.stack(
        [real_u * real_e - imag_u * imag_e, real_u * imag_e + imag_u * real_e], axis=3
    )
    backed = backed.astype(jnp.bfloat16).reshape(count * picks, 2 * fourier * fourier)
    return (weights, backed)


def _correlate_kernel(orient_ref, row_ref, panels_ref, image_ref, ctf_ref, cos_ref, sin_ref, w_ref, out_ref, acc_ref):
    i = pl.program_id(0)
    mirror = cos_ref.shape[0]
    shifts = 2 * mirror
    picks = w_ref.shape[1] // shifts
    half = ctf_ref.shape[2]

    @pl.when(i == 0)
    def _():
        acc_ref[...] = jnp.zeros_like(acc_ref)

    ctf = ctf_ref[0]
    image = image_ref[0].astype(jnp.float32)
    ur = ctf * image[:, :half]
    ui = ctf * image[:, half:]
    rows = []
    for k in range(picks):
        panel = panels_ref[row_ref[i * picks + k]].astype(jnp.float32)
        pr = panel[:, :half]
        pi = panel[:, half:]
        prod_re = (pr * ur + pi * ui).astype(jnp.bfloat16).astype(jnp.float32)
        prod_im = (pr * ui - pi * ur).astype(jnp.bfloat16).astype(jnp.float32)
        even = []
        odd = []
        for t in range(mirror):
            even.append(jnp.sum(prod_re * cos_ref[t], axis=0, keepdims=True))
            odd.append(jnp.sum(prod_im * sin_ref[t], axis=0, keepdims=True))
        rows.extend(even[t] + odd[t] for t in range(mirror))
        rows.extend(even[shifts - 1 - t] - odd[shifts - 1 - t] for t in range(mirror, shifts))
    scores = jnp.sum(jnp.concatenate(rows, axis=0), axis=1, keepdims=True) / half
    squared = scores * scores
    mean = jnp.sum(squared, axis=0, keepdims=True) / squared.shape[0]
    weights = squared / (mean + 1e-05)
    w_ref[0] = weights
    wround = weights.astype(jnp.bfloat16).astype(jnp.float32)
    for k in range(picks):
        er = jnp.zeros_like(ur)
        ei = jnp.zeros_like(ur)
        for t in range(mirror):
            wt = wround[k * shifts + t : k * shifts + t + 1, :]
            wm = wround[k * shifts + shifts - 1 - t : k * shifts + shifts - t, :]
            er = er + (wt + wm) * cos_ref[t]
            ei = ei - (wt - wm) * sin_ref[t]
        slice_re = (ur * er - ui * ei).astype(jnp.bfloat16).astype(jnp.float32)
        slice_im = (ur * ei + ui * er).astype(jnp.bfloat16).astype(jnp.float32)
        j = row_ref[i * picks + k]
        acc_ref[j, :, :half] += slice_re
        acc_ref[j, :, half:] += slice_im

    @pl.when(i == pl.num_programs(0) - 1)
    def _():
        out_ref[...] = acc_ref[...].astype(out_ref.dtype)


def correlate_all(panels, images, orient, rows, defocus):
    count, fourier, width = images.shape
    picks = orient.shape[1]
    orient_count = panels.shape[0]
    ctf = contrast(defocus, fourier, BOX)
    freq = (jnp.arange(fourier, dtype=jnp.int32) - fourier // 2).astype(jnp.float32)
    shift_steps = jnp.arange(NS // 2, dtype=jnp.int32)
    shift_x = (2 * (shift_steps // grid_side) - (grid_side - 1)).astype(jnp.float32)
    shift_y = (2 * (shift_steps % grid_side) - (grid_side - 1)).astype(jnp.float32)
    angle = 2.0 * math.pi / BOX * (
        freq[None, :, None] * shift_x[:, None, None] + freq[None, None, :] * shift_y[:, None, None]
    )
    cos_t = jnp.cos(angle).astype(jnp.bfloat16).astype(jnp.float32)
    sin_t = jnp.sin(angle).astype(jnp.bfloat16).astype(jnp.float32)
    grid_spec = pltpu.PrefetchScalarGridSpec(
        num_scalar_prefetch=2,
        grid=(count,),
        in_specs=[
            pl.BlockSpec((orient_count, fourier, width), lambda i, o, w: (0, 0, 0)),
            pl.BlockSpec((1, fourier, width), lambda i, o, w: (i, 0, 0)),
            pl.BlockSpec((1, fourier, fourier), lambda i, o, w: (i, 0, 0)),
            pl.BlockSpec((NS // 2, fourier, fourier), lambda i, o, w: (0, 0, 0)),
            pl.BlockSpec((NS // 2, fourier, fourier), lambda i, o, w: (0, 0, 0)),
        ],
        out_specs=[
            pl.BlockSpec((1, picks * NS, 1), lambda i, o, w: (i, 0, 0)),
            pl.BlockSpec((orient_count, fourier, width), lambda i, o, w: (0, 0, 0)),
        ],
        scratch_shapes=[pltpu.VMEM((orient_count, fourier, width), jnp.float32)],
    )
    weights, contrib = pl.pallas_call(
        _correlate_kernel,
        grid_spec=grid_spec,
        out_shape=[
            jax.ShapeDtypeStruct((count, picks * NS, 1), jnp.float32),
            jax.ShapeDtypeStruct((orient_count, fourier, width), jnp.bfloat16),
        ],
        compiler_params=pltpu.CompilerParams(
            dimension_semantics=("arbitrary",), vmem_limit_bytes=56 * 1024 * 1024
        ),
    )(orient.reshape(-1), rows.reshape(-1), panels, images, ctf, cos_t, sin_t)
    return weights.reshape(count, picks * NS), contrib


def _img_sum_kernel(x_ref, o_ref, gat, qbuf, s1, r1, s2, r2, l1, l2):
    count, rows = gat.shape[0], gat.shape[1]
    me = lax.axis_index("img")
    here = tuple(lax.axis_index(a) for a in SLAB)
    mesh_ids = pl.DeviceIdType.MESH
    barrier = pltpu.get_barrier_semaphore()
    peers = [lax.rem(me + 1 + i, count) for i in range(count - 1)]
    for peer in peers:
        pl.semaphore_signal(barrier, inc=1, device_id=here + (peer,), device_id_type=mesh_ids)
    pl.semaphore_wait(barrier, count - 1)

    def part(p):
        return x_ref.at[pl.ds(pl.multiple_of(p * rows, rows), rows)]

    local = pltpu.make_async_copy(part(me), gat.at[me], l1)
    local.start()
    sends = []
    for i, peer in enumerate(peers):
        copy = pltpu.make_async_remote_copy(
            src_ref=part(peer), dst_ref=gat.at[me], send_sem=s1.at[i], recv_sem=r1.at[me],
            device_id=here + (peer,), device_id_type=mesh_ids,
        )
        copy.start()
        sends.append(copy)
    for i, peer in enumerate(peers):
        sends[i].wait_send()
        pltpu.make_async_remote_copy(
            src_ref=part(peer), dst_ref=gat.at[peer], send_sem=s1.at[i], recv_sem=r1.at[peer],
            device_id=here + (peer,), device_id_type=mesh_ids,
        ).wait_recv()
    local.wait()
    qbuf[...] = jnp.sum(gat[...], axis=0)
    local = pltpu.make_async_copy(qbuf, o_ref.at[me], l2)
    local.start()
    sends = []
    for i, peer in enumerate(peers):
        copy = pltpu.make_async_remote_copy(
            src_ref=qbuf, dst_ref=o_ref.at[me], send_sem=s2.at[i], recv_sem=r2.at[me],
            device_id=here + (peer,), device_id_type=mesh_ids,
        )
        copy.start()
        sends.append(copy)
    for i, peer in enumerate(peers):
        sends[i].wait_send()
        pltpu.make_async_remote_copy(
            src_ref=qbuf, dst_ref=o_ref.at[peer], send_sem=s2.at[i], recv_sem=r2.at[peer],
            device_id=here + (peer,), device_id_type=mesh_ids,
        ).wait_recv()
    local.wait()


def img_sum(x, count, cid):
    rows = x.shape[0] // count
    out = pl.pallas_call(
        _img_sum_kernel,
        out_shape=jax.ShapeDtypeStruct((count, rows) + x.shape[1:], x.dtype),
        in_specs=[pl.BlockSpec(memory_space=pltpu.VMEM)],
        out_specs=pl.BlockSpec(memory_space=pl.ANY),
        scratch_shapes=[
            pltpu.VMEM((count, rows) + x.shape[1:], x.dtype),
            pltpu.VMEM((rows,) + x.shape[1:], x.dtype),
            pltpu.SemaphoreType.DMA((count,)),
            pltpu.SemaphoreType.DMA((count,)),
            pltpu.SemaphoreType.DMA((count,)),
            pltpu.SemaphoreType.DMA((count,)),
            pltpu.SemaphoreType.DMA,
            pltpu.SemaphoreType.DMA,
        ],
        compiler_params=pltpu.CompilerParams(collective_id=cid, has_side_effects=True),
    )(x)
    return out.reshape(x.shape)


def _a2a_kernel(x_ref, o_ref, send_sems, recv_sems, local_sem):
    count = x_ref.shape[0]
    sizes = tuple(lax.axis_size(a) for a in SLAB)
    me = lax.axis_index(SLAB)
    grp = lax.axis_index("img")
    mesh_ids = pl.DeviceIdType.MESH
    barrier = pltpu.get_barrier_semaphore()

    def where(peer):
        return (peer // (sizes[1] * sizes[2]), (peer // sizes[2]) % sizes[1], peer % sizes[2], grp)

    def greet(i, carry):
        pl.semaphore_signal(
            barrier, inc=1, device_id=where(lax.rem(me + 1 + i, count)), device_id_type=mesh_ids
        )
        return carry

    lax.fori_loop(0, count - 1, greet, 0)
    pl.semaphore_wait(barrier, count - 1)
    local = pltpu.make_async_copy(x_ref.at[me], o_ref.at[me], local_sem)
    local.start()

    def outgoing(peer):
        return pltpu.make_async_remote_copy(
            src_ref=x_ref.at[peer],
            dst_ref=o_ref.at[me],
            send_sem=send_sems.at[peer],
            recv_sem=recv_sems.at[me],
            device_id=where(peer),
            device_id_type=mesh_ids,
        )

    def incoming(src):
        return pltpu.make_async_remote_copy(
            src_ref=x_ref.at[src],
            dst_ref=o_ref.at[src],
            send_sem=send_sems.at[src],
            recv_sem=recv_sems.at[src],
            device_id=where(src),
            device_id_type=mesh_ids,
        )

    def send(i, carry):
        outgoing(lax.rem(me + 1 + i, count)).start()
        return carry

    lax.fori_loop(0, count - 1, send, 0)

    def finish(i, carry):
        outgoing(lax.rem(me + 1 + i, count)).wait_send()
        incoming(lax.rem(me + count - 1 - i, count)).wait_recv()
        return carry

    lax.fori_loop(0, count - 1, finish, 0)
    local.wait()


def slab_all_to_all(x, cid):
    count = x.shape[0]
    return pl.pallas_call(
        _a2a_kernel,
        out_shape=jax.ShapeDtypeStruct(x.shape, x.dtype),
        in_specs=[pl.BlockSpec(memory_space=pl.ANY)],
        out_specs=pl.BlockSpec(memory_space=pl.ANY),
        scratch_shapes=[
            pltpu.SemaphoreType.DMA((count,)),
            pltpu.SemaphoreType.DMA((count,)),
            pltpu.SemaphoreType.DMA,
        ],
        compiler_params=pltpu.CompilerParams(collective_id=cid, has_side_effects=True),
    )(x)


def on_device(volume, interp, block_index, images, defocus, orient):
    slab_count = lax.axis_size(SLAB)
    slab_index = lax.axis_index(SLAB)
    orient_count = interp.shape[1]
    ori_dev = orient_count // slab_count
    block_rows = interp.shape[2]
    fourier = images.shape[2]
    block_count = fourier // block_rows
    img_dev = images.shape[1]
    picks = orient.shape[2]
    levels = jnp.arange(block_count, dtype=jnp.int32)
    partial_value = jnp.einsum("jpr,rx->jpx", interp[0], volume, preferred_element_type=jnp.float32)
    owned_idx = lax.dynamic_slice_in_dim(block_index[0], slab_index * ori_dev, ori_dev, 0)
    received = slab_all_to_all(
        partial_value.reshape(slab_count, ori_dev * block_rows, 2 * fourier), 1
    ).reshape(slab_count, ori_dev, block_rows, 2 * fourier)
    place = (owned_idx[:, :, None] == levels).astype(jnp.float32)
    summed = jnp.einsum(
        "osb,sopx->obpx", place, received, precision=lax.Precision.HIGHEST,
        preferred_element_type=jnp.float32,
    ).reshape(ori_dev, fourier, 2 * fourier)
    panels = summed.astype(jnp.bfloat16)
    for axis in (SLAB[1], SLAB[0], SLAB[2]):
        parts = lax.axis_size(axis)
        panels = lax.all_to_all(
            jnp.broadcast_to(panels[None], (parts,) + panels.shape),
            axis, split_axis=0, concat_axis=0, tiled=True,
        ).reshape((-1,) + panels.shape[1:])
    sizes = tuple(lax.axis_size(a) for a in SLAB)
    inv_perm = jnp.arange(orient_count, dtype=jnp.int32).reshape(
        (sizes[2], sizes[0], sizes[1], ori_dev)
    ).transpose(1, 2, 0, 3).reshape(-1)
    weights, contrib = correlate_all(panels, images[0], orient[0], inv_perm[orient[0]], defocus[0])
    for axis in (SLAB[2], SLAB[0], SLAB[1]):
        parts = lax.axis_size(axis)
        moved = lax.all_to_all(
            contrib.astype(jnp.bfloat16), axis, split_axis=0, concat_axis=0, tiled=True
        )
        contrib = jnp.sum(
            moved.astype(jnp.float32).reshape((parts, -1) + moved.shape[1:]), axis=0
        )
    back_own = contrib.astype(jnp.bfloat16)
    back_own = back_own.reshape(ori_dev, block_count, block_rows, 2 * fourier)
    chosen_back = (owned_idx[:, :, None] == levels).astype(jnp.bfloat16)
    outgoing = jnp.einsum(
        "osb,obpx->sopx", chosen_back, back_own, preferred_element_type=jnp.float32
    )
    outgoing = outgoing.astype(jnp.bfloat16).reshape(slab_count * ori_dev, block_rows, 2 * fourier)
    incoming = lax.all_to_all(outgoing, SLAB, split_axis=0, concat_axis=0, tiled=True)
    column = jnp.einsum("jpr,jpx->rx", interp[0], incoming, preferred_element_type=jnp.float32)
    summed_cols = img_sum(column, lax.axis_size("img"), 0)
    update = summed_cols / math.sqrt(img_dev * slab_count)
    return (update, weights[None])


def solution(mesh):
    devices = mesh.devices
    cores = 2
    xs = len({d.coords[0] for d in devices.reshape(-1)}) if hasattr(devices.reshape(-1)[0], "coords") else 4
    split = devices.reshape((xs, devices.shape[0] // (xs * cores), cores) + devices.shape[1:])
    fine = jax.sharding.Mesh(split, SLAB + ("img",))
    return jax.shard_map(
        on_device,
        mesh=fine,
        in_specs=(
            P(SLAB, None),
            P("img", None, None, SLAB),
            P("img", None, None),
            P("img", SLAB, None, None),
            P("img", SLAB),
            P("img", SLAB, None),
        ),
        out_specs=(P(SLAB, None), P("img", SLAB, None)),
        check_vma=False,
    )
```

```python
import math

import jax
import jax.numpy as jnp
from jax import lax
from jax.experimental import pallas as pl
from jax.experimental.pallas import tpu as pltpu
from jax.sharding import PartitionSpec as P

BOX = 256
NS = 16
SLAB = ("sx", "sz", "sc")


wave_length = 0.0197
aberration = 27000000.0
amplitude = 0.1
grid_side = 4


def phase_tables(fourier, shifts, box):
    freq = (jnp.arange(fourier, dtype=jnp.int32) - fourier // 2).astype(jnp.float32)
    shift_steps = jnp.arange(shifts, dtype=jnp.int32)
    shift_x = (2 * (shift_steps // grid_side) - (grid_side - 1)).astype(jnp.float32)
    shift_y = (2 * (shift_steps % grid_side) - (grid_side - 1)).astype(jnp.float32)
    angle = 2.0 * math.pi / box * (freq[:, None, None] * shift_x + freq[None, :, None] * shift_y)
    forward = jnp.stack([jnp.cos(angle), jnp.sin(angle)], axis=1).reshape(
        2 * fourier * fourier, shifts
    )
    backward = jnp.stack([jnp.cos(angle), -jnp.sin(angle)], axis=1).reshape(
        2 * fourier * fourier, shifts
    )
    return (forward.astype(jnp.bfloat16), backward.T.astype(jnp.bfloat16))


def contrast(defocus_blk, fourier, box):
    freq = (jnp.arange(fourier, dtype=jnp.int32) - fourier // 2).astype(jnp.float32)
    wave_sq = (freq[:, None] * freq[:, None] + freq[None, :] * freq[None, :]) / (box * box)
    phase = math.pi * wave_length * defocus_blk[:, None, None] * wave_sq
    phase = phase - 0.5 * math.pi * aberration * wave_length**3 * wave_sq * wave_sq
    return -(math.sqrt(1.0 - amplitude * amplitude) * jnp.sin(phase) + amplitude * jnp.cos(phase))


def correlate(panels, image_blk, list_blk, defocus_blk, phase_fwd, phase_back, box):
    count = image_blk.shape[0]
    fourier = image_blk.shape[1]
    picks = list_blk.shape[1]
    shifts = phase_fwd.shape[1]
    ctf = contrast(defocus_blk, fourier, box)
    weighted = ctf[:, :, None, :] * image_blk.astype(jnp.float32).reshape(
        count, fourier, 2, fourier
    )
    real_u = weighted[:, None, :, 0]
    imag_u = weighted[:, None, :, 1]
    chosen = panels[list_blk].astype(jnp.float32).reshape(count, picks, fourier, 2, fourier)
    real_p = chosen[:, :, :, 0]
    imag_p = chosen[:, :, :, 1]
    product = jnp.stack(
        [real_p * real_u + imag_p * imag_u, real_p * imag_u - imag_p * real_u], axis=3
    )
    product = product.astype(jnp.bfloat16).reshape(count * picks, 2 * fourier * fourier)
    scores = jnp.dot(product, phase_fwd, preferred_element_type=jnp.float32) / fourier
    scores = scores.reshape(count, picks * shifts)
    squared = scores * scores
    weights = squared / (jnp.mean(squared, axis=1, keepdims=True) + 1e-05)
    rounded = weights.astype(jnp.bfloat16).reshape(count * picks, shifts)
    spread = jnp.dot(rounded, phase_back, preferred_element_type=jnp.float32)
    spread = spread.reshape(count, picks, fourier, 2, fourier)
    real_e = spread[:, :, :, 0]
    imag_e = spread[:, :, :, 1]
    backed = jnp.stack(
        [real_u * real_e - imag_u * imag_e, real_u * imag_e + imag_u * real_e], axis=3
    )
    backed = backed.astype(jnp.bfloat16).reshape(count * picks, 2 * fourier * fourier)
    return (weights, backed)


def _correlate_kernel(orient_ref, row_ref, panels_ref, image_ref, ctf_ref, cos_ref, sin_ref, w_ref, out_ref, acc_ref):
    i = pl.program_id(0)
    mirror = cos_ref.shape[0]
    shifts = 2 * mirror
    picks = w_ref.shape[1] // shifts
    half = ctf_ref.shape[2]

    @pl.when(i == 0)
    def _():
        acc_ref[...] = jnp.zeros_like(acc_ref)

    ctf = ctf_ref[0]
    image = image_ref[0].astype(jnp.float32)
    ur = ctf * image[:, :half]
    ui = ctf * image[:, half:]
    rows = []
    for k in range(picks):
        panel = panels_ref[row_ref[i * picks + k]].astype(jnp.float32)
        pr = panel[:, :half]
        pi = panel[:, half:]
        prod_re = (pr * ur + pi * ui).astype(jnp.bfloat16).astype(jnp.float32)
        prod_im = (pr * ui - pi * ur).astype(jnp.bfloat16).astype(jnp.float32)
        even = []
        odd = []
        for t in range(mirror):
            even.append(jnp.sum(prod_re * cos_ref[t], axis=0, keepdims=True))
            odd.append(jnp.sum(prod_im * sin_ref[t], axis=0, keepdims=True))
        rows.extend(even[t] + odd[t] for t in range(mirror))
        rows.extend(even[shifts - 1 - t] - odd[shifts - 1 - t] for t in range(mirror, shifts))
    scores = jnp.sum(jnp.concatenate(rows, axis=0), axis=1, keepdims=True) / half
    squared = scores * scores
    mean = jnp.sum(squared, axis=0, keepdims=True) / squared.shape[0]
    weights = squared / (mean + 1e-05)
    w_ref[0] = weights
    wround = weights.astype(jnp.bfloat16).astype(jnp.float32)
    for k in range(picks):
        er = jnp.zeros_like(ur)
        ei = jnp.zeros_like(ur)
        for t in range(mirror):
            wt = wround[k * shifts + t : k * shifts + t + 1, :]
            wm = wround[k * shifts + shifts - 1 - t : k * shifts + shifts - t, :]
            er = er + (wt + wm) * cos_ref[t]
            ei = ei - (wt - wm) * sin_ref[t]
        slice_re = (ur * er - ui * ei).astype(jnp.bfloat16).astype(jnp.float32)
        slice_im = (ur * ei + ui * er).astype(jnp.bfloat16).astype(jnp.float32)
        j = row_ref[i * picks + k]
        acc_ref[j, :, :half] += slice_re
        acc_ref[j, :, half:] += slice_im

    @pl.when(i == pl.num_programs(0) - 1)
    def _():
        out_ref[...] = acc_ref[...].astype(out_ref.dtype)


def correlate_all(panels, images, orient, rows, defocus):
    count, fourier, width = images.shape
    picks = orient.shape[1]
    orient_count = panels.shape[0]
    ctf = contrast(defocus, fourier, BOX)
    freq = (jnp.arange(fourier, dtype=jnp.int32) - fourier // 2).astype(jnp.float32)
    shift_steps = jnp.arange(NS // 2, dtype=jnp.int32)
    shift_x = (2 * (shift_steps // grid_side) - (grid_side - 1)).astype(jnp.float32)
    shift_y = (2 * (shift_steps % grid_side) - (grid_side - 1)).astype(jnp.float32)
    angle = 2.0 * math.pi / BOX * (
        freq[None, :, None] * shift_x[:, None, None] + freq[None, None, :] * shift_y[:, None, None]
    )
    cos_t = jnp.cos(angle).astype(jnp.bfloat16).astype(jnp.float32)
    sin_t = jnp.sin(angle).astype(jnp.bfloat16).astype(jnp.float32)
    grid_spec = pltpu.PrefetchScalarGridSpec(
        num_scalar_prefetch=2,
        grid=(count,),
        in_specs=[
            pl.BlockSpec((orient_count, fourier, width), lambda i, o, w: (0, 0, 0)),
            pl.BlockSpec((1, fourier, width), lambda i, o, w: (i, 0, 0)),
            pl.BlockSpec((1, fourier, fourier), lambda i, o, w: (i, 0, 0)),
            pl.BlockSpec((NS // 2, fourier, fourier), lambda i, o, w: (0, 0, 0)),
            pl.BlockSpec((NS // 2, fourier, fourier), lambda i, o, w: (0, 0, 0)),
        ],
        out_specs=[
            pl.BlockSpec((1, picks * NS, 1), lambda i, o, w: (i, 0, 0)),
            pl.BlockSpec((orient_count, fourier, width), lambda i, o, w: (0, 0, 0)),
        ],
        scratch_shapes=[pltpu.VMEM((orient_count, fourier, width), jnp.float32)],
    )
    weights, contrib = pl.pallas_call(
        _correlate_kernel,
        grid_spec=grid_spec,
        out_shape=[
            jax.ShapeDtypeStruct((count, picks * NS, 1), jnp.float32),
            jax.ShapeDtypeStruct((orient_count, fourier, width), jnp.bfloat16),
        ],
        compiler_params=pltpu.CompilerParams(
            dimension_semantics=("arbitrary",), vmem_limit_bytes=56 * 1024 * 1024
        ),
    )(orient.reshape(-1), rows.reshape(-1), panels, images, ctf, cos_t, sin_t)
    return weights.reshape(count, picks * NS), contrib


def _pair_sum_kernel(x_ref, o_ref, own, recv, send_sem, recv_sem, local_sem):
    half = own.shape[0]
    me = lax.axis_index(SLAB[2])
    mate = 1 - me
    where = (lax.axis_index(SLAB[0]), lax.axis_index(SLAB[1]), mate, lax.axis_index("img"))
    mesh_ids = pl.DeviceIdType.MESH
    barrier = pltpu.get_barrier_semaphore()
    pl.semaphore_signal(barrier, inc=1, device_id=where, device_id_type=mesh_ids)
    pl.semaphore_wait(barrier, 1)
    local = pltpu.make_async_copy(x_ref.at[pl.ds(me * half, half)], own, local_sem)
    local.start()
    copy = pltpu.make_async_remote_copy(
        src_ref=x_ref.at[pl.ds(mate * half, half)], dst_ref=recv, send_sem=send_sem,
        recv_sem=recv_sem, device_id=where, device_id_type=mesh_ids,
    )
    copy.start()
    local.wait()
    copy.wait()

    def add(b, carry):
        o_ref[b] = (own[b].astype(jnp.float32) + recv[b].astype(jnp.float32)).astype(o_ref.dtype)
        return carry

    lax.fori_loop(0, half, add, 0)


def pair_sum(x, cid):
    half = x.shape[0] // 2
    return pl.pallas_call(
        _pair_sum_kernel,
        out_shape=jax.ShapeDtypeStruct((half,) + x.shape[1:], x.dtype),
        in_specs=[pl.BlockSpec(memory_space=pl.ANY)],
        out_specs=pl.BlockSpec(memory_space=pltpu.VMEM),
        scratch_shapes=[
            pltpu.VMEM((half,) + x.shape[1:], x.dtype),
            pltpu.VMEM((half,) + x.shape[1:], x.dtype),
            pltpu.SemaphoreType.DMA,
            pltpu.SemaphoreType.DMA,
            pltpu.SemaphoreType.DMA,
        ],
        compiler_params=pltpu.CompilerParams(
            collective_id=cid, has_side_effects=True, vmem_limit_bytes=48 * 1024 * 1024
        ),
    )(x)


def _img_sum_kernel(x_ref, o_ref, gat, qbuf, s1, r1, s2, r2, l1, l2):
    count, rows = gat.shape[0], gat.shape[1]
    me = lax.axis_index("img")
    here = tuple(lax.axis_index(a) for a in SLAB)
    mesh_ids = pl.DeviceIdType.MESH
    barrier = pltpu.get_barrier_semaphore()
    peers = [lax.rem(me + 1 + i, count) for i in range(count - 1)]
    for peer in peers:
        pl.semaphore_signal(barrier, inc=1, device_id=here + (peer,), device_id_type=mesh_ids)
    pl.semaphore_wait(barrier, count - 1)

    def part(p):
        return x_ref.at[pl.ds(pl.multiple_of(p * rows, rows), rows)]

    local = pltpu.make_async_copy(part(me), gat.at[me], l1)
    local.start()
    sends = []
    for i, peer in enumerate(peers):
        copy = pltpu.make_async_remote_copy(
            src_ref=part(peer), dst_ref=gat.at[me], send_sem=s1.at[i], recv_sem=r1.at[me],
            device_id=here + (peer,), device_id_type=mesh_ids,
        )
        copy.start()
        sends.append(copy)
    for i, peer in enumerate(peers):
        sends[i].wait_send()
        pltpu.make_async_remote_copy(
            src_ref=part(peer), dst_ref=gat.at[peer], send_sem=s1.at[i], recv_sem=r1.at[peer],
            device_id=here + (peer,), device_id_type=mesh_ids,
        ).wait_recv()
    local.wait()
    qbuf[...] = jnp.sum(gat[...], axis=0)
    local = pltpu.make_async_copy(qbuf, o_ref.at[me], l2)
    local.start()
    sends = []
    for i, peer in enumerate(peers):
        copy = pltpu.make_async_remote_copy(
            src_ref=qbuf, dst_ref=o_ref.at[me], send_sem=s2.at[i], recv_sem=r2.at[me],
            device_id=here + (peer,), device_id_type=mesh_ids,
        )
        copy.start()
        sends.append(copy)
    for i, peer in enumerate(peers):
        sends[i].wait_send()
        pltpu.make_async_remote_copy(
            src_ref=qbuf, dst_ref=o_ref.at[peer], send_sem=s2.at[i], recv_sem=r2.at[peer],
            device_id=here + (peer,), device_id_type=mesh_ids,
        ).wait_recv()
    local.wait()


def img_sum(x, count, cid):
    rows = x.shape[0] // count
    out = pl.pallas_call(
        _img_sum_kernel,
        out_shape=jax.ShapeDtypeStruct((count, rows) + x.shape[1:], x.dtype),
        in_specs=[pl.BlockSpec(memory_space=pltpu.VMEM)],
        out_specs=pl.BlockSpec(memory_space=pl.ANY),
        scratch_shapes=[
            pltpu.VMEM((count, rows) + x.shape[1:], x.dtype),
            pltpu.VMEM((rows,) + x.shape[1:], x.dtype),
            pltpu.SemaphoreType.DMA((count,)),
            pltpu.SemaphoreType.DMA((count,)),
            pltpu.SemaphoreType.DMA((count,)),
            pltpu.SemaphoreType.DMA((count,)),
            pltpu.SemaphoreType.DMA,
            pltpu.SemaphoreType.DMA,
        ],
        compiler_params=pltpu.CompilerParams(collective_id=cid, has_side_effects=True),
    )(x)
    return out.reshape(x.shape)


def _a2a_kernel(x_ref, o_ref, send_sems, recv_sems, local_sem):
    count = x_ref.shape[0]
    sizes = tuple(lax.axis_size(a) for a in SLAB)
    me = lax.axis_index(SLAB)
    grp = lax.axis_index("img")
    mesh_ids = pl.DeviceIdType.MESH
    barrier = pltpu.get_barrier_semaphore()

    def where(peer):
        return (peer // (sizes[1] * sizes[2]), (peer // sizes[2]) % sizes[1], peer % sizes[2], grp)

    def greet(i, carry):
        pl.semaphore_signal(
            barrier, inc=1, device_id=where(lax.rem(me + 1 + i, count)), device_id_type=mesh_ids
        )
        return carry

    lax.fori_loop(0, count - 1, greet, 0)
    pl.semaphore_wait(barrier, count - 1)
    local = pltpu.make_async_copy(x_ref.at[me], o_ref.at[me], local_sem)
    local.start()

    def outgoing(peer):
        return pltpu.make_async_remote_copy(
            src_ref=x_ref.at[peer],
            dst_ref=o_ref.at[me],
            send_sem=send_sems.at[peer],
            recv_sem=recv_sems.at[me],
            device_id=where(peer),
            device_id_type=mesh_ids,
        )

    def incoming(src):
        return pltpu.make_async_remote_copy(
            src_ref=x_ref.at[src],
            dst_ref=o_ref.at[src],
            send_sem=send_sems.at[src],
            recv_sem=recv_sems.at[src],
            device_id=where(src),
            device_id_type=mesh_ids,
        )

    def send(i, carry):
        outgoing(lax.rem(me + 1 + i, count)).start()
        return carry

    lax.fori_loop(0, count - 1, send, 0)

    def finish(i, carry):
        outgoing(lax.rem(me + 1 + i, count)).wait_send()
        incoming(lax.rem(me + count - 1 - i, count)).wait_recv()
        return carry

    lax.fori_loop(0, count - 1, finish, 0)
    local.wait()


def slab_all_to_all(x, cid):
    count = x.shape[0]
    return pl.pallas_call(
        _a2a_kernel,
        out_shape=jax.ShapeDtypeStruct(x.shape, x.dtype),
        in_specs=[pl.BlockSpec(memory_space=pl.ANY)],
        out_specs=pl.BlockSpec(memory_space=pl.ANY),
        scratch_shapes=[
            pltpu.SemaphoreType.DMA((count,)),
            pltpu.SemaphoreType.DMA((count,)),
            pltpu.SemaphoreType.DMA,
        ],
        compiler_params=pltpu.CompilerParams(collective_id=cid, has_side_effects=True),
    )(x)


def on_device(volume, interp, block_index, images, defocus, orient):
    slab_count = lax.axis_size(SLAB)
    slab_index = lax.axis_index(SLAB)
    orient_count = interp.shape[1]
    ori_dev = orient_count // slab_count
    block_rows = interp.shape[2]
    fourier = images.shape[2]
    block_count = fourier // block_rows
    img_dev = images.shape[1]
    picks = orient.shape[2]
    levels = jnp.arange(block_count, dtype=jnp.int32)
    partial_value = jnp.einsum("jpr,rx->jpx", interp[0], volume, preferred_element_type=jnp.float32)
    owned_idx = lax.dynamic_slice_in_dim(block_index[0], slab_index * ori_dev, ori_dev, 0)
    received = slab_all_to_all(
        partial_value.reshape(slab_count, ori_dev * block_rows, 2 * fourier), 1
    ).reshape(slab_count, ori_dev, block_rows, 2 * fourier)
    place = (owned_idx[:, :, None] == levels).astype(jnp.float32)
    summed = jnp.einsum(
        "osb,sopx->obpx", place, received, precision=lax.Precision.HIGHEST,
        preferred_element_type=jnp.float32,
    ).reshape(ori_dev, fourier, 2 * fourier)
    panels = summed.astype(jnp.bfloat16)
    for axis in (SLAB[1], SLAB[0], SLAB[2]):
        parts = lax.axis_size(axis)
        panels = lax.all_to_all(
            jnp.broadcast_to(panels[None], (parts,) + panels.shape),
            axis, split_axis=0, concat_axis=0, tiled=True,
        ).reshape((-1,) + panels.shape[1:])
    sizes = tuple(lax.axis_size(a) for a in SLAB)
    inv_perm = jnp.arange(orient_count, dtype=jnp.int32).reshape(
        (sizes[2], sizes[0], sizes[1], ori_dev)
    ).transpose(1, 2, 0, 3).reshape(-1)
    weights, contrib = correlate_all(panels, images[0], orient[0], inv_perm[orient[0]], defocus[0])
    contrib = pair_sum(contrib, 2)
    for axis in (SLAB[0], SLAB[1]):
        parts = lax.axis_size(axis)
        moved = lax.all_to_all(
            contrib.astype(jnp.bfloat16), axis, split_axis=0, concat_axis=0, tiled=True
        )
        contrib = jnp.sum(
            moved.astype(jnp.float32).reshape((parts, -1) + moved.shape[1:]), axis=0
        )
    back_own = contrib.astype(jnp.bfloat16)
    back_own = back_own.reshape(ori_dev, block_count, block_rows, 2 * fourier)
    chosen_back = (owned_idx[:, :, None] == levels).astype(jnp.bfloat16)
    outgoing = jnp.einsum(
        "osb,obpx->sopx", chosen_back, back_own, preferred_element_type=jnp.float32
    )
    outgoing = outgoing.astype(jnp.bfloat16).reshape(slab_count * ori_dev, block_rows, 2 * fourier)
    incoming = lax.all_to_all(outgoing, SLAB, split_axis=0, concat_axis=0, tiled=True)
    column = jnp.einsum("jpr,jpx->rx", interp[0], incoming, preferred_element_type=jnp.float32)
    summed_cols = img_sum(column, lax.axis_size("img"), 0)
    update = summed_cols / math.sqrt(img_dev * slab_count)
    return (update, weights[None])


def solution(mesh):
    devices = mesh.devices
    cores = 2
    xs = len({d.coords[0] for d in devices.reshape(-1)}) if hasattr(devices.reshape(-1)[0], "coords") else 4
    split = devices.reshape((xs, devices.shape[0] // (xs * cores), cores) + devices.shape[1:])
    fine = jax.sharding.Mesh(split, SLAB + ("img",))
    return jax.shard_map(
        on_device,
        mesh=fine,
        in_specs=(
            P(SLAB, None),
            P("img", None, None, SLAB),
            P("img", None, None),
            P("img", SLAB, None, None),
            P("img", SLAB),
            P("img", SLAB, None),
        ),
        out_specs=(P(SLAB, None), P("img", SLAB, None)),
        check_vma=False,
    )
```

```python
import functools
import math

import jax
import jax.numpy as jnp
from jax import lax
from jax.experimental import pallas as pl
from jax.experimental.pallas import tpu as pltpu
from jax.sharding import PartitionSpec as P

BOX = 256
NS = 16
SLAB = ("sx", "sz", "sc")


wave_length = 0.0197
aberration = 27000000.0
amplitude = 0.1
grid_side = 4


def phase_tables(fourier, shifts, box):
    freq = (jnp.arange(fourier, dtype=jnp.int32) - fourier // 2).astype(jnp.float32)
    shift_steps = jnp.arange(shifts, dtype=jnp.int32)
    shift_x = (2 * (shift_steps // grid_side) - (grid_side - 1)).astype(jnp.float32)
    shift_y = (2 * (shift_steps % grid_side) - (grid_side - 1)).astype(jnp.float32)
    angle = 2.0 * math.pi / box * (freq[:, None, None] * shift_x + freq[None, :, None] * shift_y)
    forward = jnp.stack([jnp.cos(angle), jnp.sin(angle)], axis=1).reshape(
        2 * fourier * fourier, shifts
    )
    backward = jnp.stack([jnp.cos(angle), -jnp.sin(angle)], axis=1).reshape(
        2 * fourier * fourier, shifts
    )
    return (forward.astype(jnp.bfloat16), backward.T.astype(jnp.bfloat16))


def contrast(defocus_blk, fourier, box):
    freq = (jnp.arange(fourier, dtype=jnp.int32) - fourier // 2).astype(jnp.float32)
    wave_sq = (freq[:, None] * freq[:, None] + freq[None, :] * freq[None, :]) / (box * box)
    phase = math.pi * wave_length * defocus_blk[:, None, None] * wave_sq
    phase = phase - 0.5 * math.pi * aberration * wave_length**3 * wave_sq * wave_sq
    return -(math.sqrt(1.0 - amplitude * amplitude) * jnp.sin(phase) + amplitude * jnp.cos(phase))


def correlate(panels, image_blk, list_blk, defocus_blk, phase_fwd, phase_back, box):
    count = image_blk.shape[0]
    fourier = image_blk.shape[1]
    picks = list_blk.shape[1]
    shifts = phase_fwd.shape[1]
    ctf = contrast(defocus_blk, fourier, box)
    weighted = ctf[:, :, None, :] * image_blk.astype(jnp.float32).reshape(
        count, fourier, 2, fourier
    )
    real_u = weighted[:, None, :, 0]
    imag_u = weighted[:, None, :, 1]
    chosen = panels[list_blk].astype(jnp.float32).reshape(count, picks, fourier, 2, fourier)
    real_p = chosen[:, :, :, 0]
    imag_p = chosen[:, :, :, 1]
    product = jnp.stack(
        [real_p * real_u + imag_p * imag_u, real_p * imag_u - imag_p * real_u], axis=3
    )
    product = product.astype(jnp.bfloat16).reshape(count * picks, 2 * fourier * fourier)
    scores = jnp.dot(product, phase_fwd, preferred_element_type=jnp.float32) / fourier
    scores = scores.reshape(count, picks * shifts)
    squared = scores * scores
    weights = squared / (jnp.mean(squared, axis=1, keepdims=True) + 1e-05)
    rounded = weights.astype(jnp.bfloat16).reshape(count * picks, shifts)
    spread = jnp.dot(rounded, phase_back, preferred_element_type=jnp.float32)
    spread = spread.reshape(count, picks, fourier, 2, fourier)
    real_e = spread[:, :, :, 0]
    imag_e = spread[:, :, :, 1]
    backed = jnp.stack(
        [real_u * real_e - imag_u * imag_e, real_u * imag_e + imag_u * real_e], axis=3
    )
    backed = backed.astype(jnp.bfloat16).reshape(count * picks, 2 * fourier * fourier)
    return (weights, backed)


def _correlate_kernel(orient_ref, row_ref, panels_ref, image_ref, ctf_ref, cos_ref, sin_ref, w_ref, out_ref, acc_ref):
    i = pl.program_id(0)
    mirror = cos_ref.shape[0]
    shifts = 2 * mirror
    picks = w_ref.shape[1] // shifts
    half = ctf_ref.shape[2]

    @pl.when(i == 0)
    def _():
        acc_ref[...] = jnp.zeros_like(acc_ref)

    ctf = ctf_ref[0]
    image = image_ref[0].astype(jnp.float32)
    ur = ctf * image[:, :half]
    ui = ctf * image[:, half:]
    rows = []
    for k in range(picks):
        panel = panels_ref[row_ref[i * picks + k]].astype(jnp.float32)
        pr = panel[:, :half]
        pi = panel[:, half:]
        prod_re = (pr * ur + pi * ui).astype(jnp.bfloat16).astype(jnp.float32)
        prod_im = (pr * ui - pi * ur).astype(jnp.bfloat16).astype(jnp.float32)
        even = []
        odd = []
        for t in range(mirror):
            even.append(jnp.sum(prod_re * cos_ref[t], axis=0, keepdims=True))
            odd.append(jnp.sum(prod_im * sin_ref[t], axis=0, keepdims=True))
        rows.extend(even[t] + odd[t] for t in range(mirror))
        rows.extend(even[shifts - 1 - t] - odd[shifts - 1 - t] for t in range(mirror, shifts))
    scores = jnp.sum(jnp.concatenate(rows, axis=0), axis=1, keepdims=True) / half
    squared = scores * scores
    mean = jnp.sum(squared, axis=0, keepdims=True) / squared.shape[0]
    weights = squared / (mean + 1e-05)
    w_ref[0] = weights
    wround = weights.astype(jnp.bfloat16).astype(jnp.float32)
    for k in range(picks):
        er = jnp.zeros_like(ur)
        ei = jnp.zeros_like(ur)
        for t in range(mirror):
            wt = wround[k * shifts + t : k * shifts + t + 1, :]
            wm = wround[k * shifts + shifts - 1 - t : k * shifts + shifts - t, :]
            er = er + (wt + wm) * cos_ref[t]
            ei = ei - (wt - wm) * sin_ref[t]
        slice_re = (ur * er - ui * ei).astype(jnp.bfloat16).astype(jnp.float32)
        slice_im = (ur * ei + ui * er).astype(jnp.bfloat16).astype(jnp.float32)
        j = row_ref[i * picks + k]
        acc_ref[j, :, :half] += slice_re
        acc_ref[j, :, half:] += slice_im

    @pl.when(i == pl.num_programs(0) - 1)
    def _():
        out_ref[...] = acc_ref[...].astype(out_ref.dtype)


def correlate_all(panels, images, orient, rows, defocus):
    count, fourier, width = images.shape
    picks = orient.shape[1]
    orient_count = panels.shape[0]
    ctf = contrast(defocus, fourier, BOX)
    freq = (jnp.arange(fourier, dtype=jnp.int32) - fourier // 2).astype(jnp.float32)
    shift_steps = jnp.arange(NS // 2, dtype=jnp.int32)
    shift_x = (2 * (shift_steps // grid_side) - (grid_side - 1)).astype(jnp.float32)
    shift_y = (2 * (shift_steps % grid_side) - (grid_side - 1)).astype(jnp.float32)
    angle = 2.0 * math.pi / BOX * (
        freq[None, :, None] * shift_x[:, None, None] + freq[None, None, :] * shift_y[:, None, None]
    )
    cos_t = jnp.cos(angle).astype(jnp.bfloat16).astype(jnp.float32)
    sin_t = jnp.sin(angle).astype(jnp.bfloat16).astype(jnp.float32)
    grid_spec = pltpu.PrefetchScalarGridSpec(
        num_scalar_prefetch=2,
        grid=(count,),
        in_specs=[
            pl.BlockSpec((orient_count, fourier, width), lambda i, o, w: (0, 0, 0)),
            pl.BlockSpec((1, fourier, width), lambda i, o, w: (i, 0, 0)),
            pl.BlockSpec((1, fourier, fourier), lambda i, o, w: (i, 0, 0)),
            pl.BlockSpec((NS // 2, fourier, fourier), lambda i, o, w: (0, 0, 0)),
            pl.BlockSpec((NS // 2, fourier, fourier), lambda i, o, w: (0, 0, 0)),
        ],
        out_specs=[
            pl.BlockSpec((1, picks * NS, 1), lambda i, o, w: (i, 0, 0)),
            pl.BlockSpec((orient_count, fourier, width), lambda i, o, w: (0, 0, 0)),
        ],
        scratch_shapes=[pltpu.VMEM((orient_count, fourier, width), jnp.float32)],
    )
    weights, contrib = pl.pallas_call(
        _correlate_kernel,
        grid_spec=grid_spec,
        out_shape=[
            jax.ShapeDtypeStruct((count, picks * NS, 1), jnp.float32),
            jax.ShapeDtypeStruct((orient_count, fourier, width), jnp.bfloat16),
        ],
        compiler_params=pltpu.CompilerParams(
            dimension_semantics=("arbitrary",), vmem_limit_bytes=56 * 1024 * 1024
        ),
    )(orient.reshape(-1), rows.reshape(-1), panels, images, ctf, cos_t, sin_t)
    return weights.reshape(count, picks * NS), contrib


def _pair_sum_kernel(x_ref, o_ref, own, recv, send_sem, recv_sem, local_sem):
    half = own.shape[0]
    me = lax.axis_index(SLAB[2])
    mate = 1 - me
    where = (lax.axis_index(SLAB[0]), lax.axis_index(SLAB[1]), mate, lax.axis_index("img"))
    mesh_ids = pl.DeviceIdType.MESH
    barrier = pltpu.get_barrier_semaphore()
    pl.semaphore_signal(barrier, inc=1, device_id=where, device_id_type=mesh_ids)
    pl.semaphore_wait(barrier, 1)
    local = pltpu.make_async_copy(x_ref.at[pl.ds(me * half, half)], own, local_sem)
    local.start()
    copy = pltpu.make_async_remote_copy(
        src_ref=x_ref.at[pl.ds(mate * half, half)], dst_ref=recv, send_sem=send_sem,
        recv_sem=recv_sem, device_id=where, device_id_type=mesh_ids,
    )
    copy.start()
    local.wait()
    copy.wait()

    def add(b, carry):
        o_ref[b] = (own[b].astype(jnp.float32) + recv[b].astype(jnp.float32)).astype(o_ref.dtype)
        return carry

    lax.fori_loop(0, half, add, 0)


def pair_sum(x, cid):
    half = x.shape[0] // 2
    return pl.pallas_call(
        _pair_sum_kernel,
        out_shape=jax.ShapeDtypeStruct((half,) + x.shape[1:], x.dtype),
        in_specs=[pl.BlockSpec(memory_space=pl.ANY)],
        out_specs=pl.BlockSpec(memory_space=pltpu.VMEM),
        scratch_shapes=[
            pltpu.VMEM((half,) + x.shape[1:], x.dtype),
            pltpu.VMEM((half,) + x.shape[1:], x.dtype),
            pltpu.SemaphoreType.DMA,
            pltpu.SemaphoreType.DMA,
            pltpu.SemaphoreType.DMA,
        ],
        compiler_params=pltpu.CompilerParams(
            collective_id=cid, has_side_effects=True, vmem_limit_bytes=48 * 1024 * 1024
        ),
    )(x)


def _axis_sum_kernel(axis, x_ref, o_ref, got, send_sems, recv_sems, local_sem):
    count, chunk = got.shape[0], got.shape[1]
    me = lax.axis_index(axis)
    names = SLAB + ("img",)
    coords = [lax.axis_index(a) for a in names]
    at = names.index(axis)
    mesh_ids = pl.DeviceIdType.MESH
    peers = [lax.rem(me + 1 + i, count) for i in range(count - 1)]

    def where(peer):
        return tuple(coords[:at]) + (peer,) + tuple(coords[at + 1:])

    barrier = pltpu.get_barrier_semaphore()
    for peer in peers:
        pl.semaphore_signal(barrier, inc=1, device_id=where(peer), device_id_type=mesh_ids)
    pl.semaphore_wait(barrier, count - 1)

    def part(p):
        return x_ref.at[pl.ds(p * chunk, chunk)]

    local = pltpu.make_async_copy(part(me), got.at[me], local_sem)
    local.start()
    sends = []
    for i, peer in enumerate(peers):
        copy = pltpu.make_async_remote_copy(
            src_ref=part(peer), dst_ref=got.at[me], send_sem=send_sems.at[i], recv_sem=recv_sems.at[me],
            device_id=where(peer), device_id_type=mesh_ids,
        )
        copy.start()
        sends.append(copy)
    for i, peer in enumerate(peers):
        sends[i].wait_send()
        pltpu.make_async_remote_copy(
            src_ref=part(peer), dst_ref=got.at[peer], send_sem=send_sems.at[i], recv_sem=recv_sems.at[peer],
            device_id=where(peer), device_id_type=mesh_ids,
        ).wait_recv()
    local.wait()

    def add(b, carry):
        total = got[0, b].astype(jnp.float32)
        for p in range(1, count):
            total = total + got[p, b].astype(jnp.float32)
        o_ref[b] = total.astype(o_ref.dtype)
        return carry

    lax.fori_loop(0, chunk, add, 0)


def axis_sum(x, axis, cid):
    count = lax.axis_size(axis)
    chunk = x.shape[0] // count
    return pl.pallas_call(
        functools.partial(_axis_sum_kernel, axis),
        out_shape=jax.ShapeDtypeStruct((chunk,) + x.shape[1:], x.dtype),
        in_specs=[pl.BlockSpec(memory_space=pl.ANY)],
        out_specs=pl.BlockSpec(memory_space=pltpu.VMEM),
        scratch_shapes=[
            pltpu.VMEM((count, chunk) + x.shape[1:], x.dtype),
            pltpu.SemaphoreType.DMA((count,)),
            pltpu.SemaphoreType.DMA((count,)),
            pltpu.SemaphoreType.DMA,
        ],
        compiler_params=pltpu.CompilerParams(
            collective_id=cid, has_side_effects=True, vmem_limit_bytes=48 * 1024 * 1024
        ),
    )(x)


def _img_sum_kernel(x_ref, o_ref, gat, qbuf, s1, r1, s2, r2, l1, l2):
    count, rows = gat.shape[0], gat.shape[1]
    me = lax.axis_index("img")
    here = tuple(lax.axis_index(a) for a in SLAB)
    mesh_ids = pl.DeviceIdType.MESH
    barrier = pltpu.get_barrier_semaphore()
    peers = [lax.rem(me + 1 + i, count) for i in range(count - 1)]
    for peer in peers:
        pl.semaphore_signal(barrier, inc=1, device_id=here + (peer,), device_id_type=mesh_ids)
    pl.semaphore_wait(barrier, count - 1)

    def part(p):
        return x_ref.at[pl.ds(pl.multiple_of(p * rows, rows), rows)]

    local = pltpu.make_async_copy(part(me), gat.at[me], l1)
    local.start()
    sends = []
    for i, peer in enumerate(peers):
        copy = pltpu.make_async_remote_copy(
            src_ref=part(peer), dst_ref=gat.at[me], send_sem=s1.at[i], recv_sem=r1.at[me],
            device_id=here + (peer,), device_id_type=mesh_ids,
        )
        copy.start()
        sends.append(copy)
    for i, peer in enumerate(peers):
        sends[i].wait_send()
        pltpu.make_async_remote_copy(
            src_ref=part(peer), dst_ref=gat.at[peer], send_sem=s1.at[i], recv_sem=r1.at[peer],
            device_id=here + (peer,), device_id_type=mesh_ids,
        ).wait_recv()
    local.wait()
    qbuf[...] = jnp.sum(gat[...], axis=0)
    local = pltpu.make_async_copy(qbuf, o_ref.at[me], l2)
    local.start()
    sends = []
    for i, peer in enumerate(peers):
        copy = pltpu.make_async_remote_copy(
            src_ref=qbuf, dst_ref=o_ref.at[me], send_sem=s2.at[i], recv_sem=r2.at[me],
            device_id=here + (peer,), device_id_type=mesh_ids,
        )
        copy.start()
        sends.append(copy)
    for i, peer in enumerate(peers):
        sends[i].wait_send()
        pltpu.make_async_remote_copy(
            src_ref=qbuf, dst_ref=o_ref.at[peer], send_sem=s2.at[i], recv_sem=r2.at[peer],
            device_id=here + (peer,), device_id_type=mesh_ids,
        ).wait_recv()
    local.wait()


def img_sum(x, count, cid):
    rows = x.shape[0] // count
    out = pl.pallas_call(
        _img_sum_kernel,
        out_shape=jax.ShapeDtypeStruct((count, rows) + x.shape[1:], x.dtype),
        in_specs=[pl.BlockSpec(memory_space=pltpu.VMEM)],
        out_specs=pl.BlockSpec(memory_space=pl.ANY),
        scratch_shapes=[
            pltpu.VMEM((count, rows) + x.shape[1:], x.dtype),
            pltpu.VMEM((rows,) + x.shape[1:], x.dtype),
            pltpu.SemaphoreType.DMA((count,)),
            pltpu.SemaphoreType.DMA((count,)),
            pltpu.SemaphoreType.DMA((count,)),
            pltpu.SemaphoreType.DMA((count,)),
            pltpu.SemaphoreType.DMA,
            pltpu.SemaphoreType.DMA,
        ],
        compiler_params=pltpu.CompilerParams(collective_id=cid, has_side_effects=True),
    )(x)
    return out.reshape(x.shape)


def _a2a_kernel(x_ref, o_ref, send_sems, recv_sems, local_sem):
    count = x_ref.shape[0]
    sizes = tuple(lax.axis_size(a) for a in SLAB)
    me = lax.axis_index(SLAB)
    grp = lax.axis_index("img")
    mesh_ids = pl.DeviceIdType.MESH
    barrier = pltpu.get_barrier_semaphore()

    def where(peer):
        return (peer // (sizes[1] * sizes[2]), (peer // sizes[2]) % sizes[1], peer % sizes[2], grp)

    def greet(i, carry):
        pl.semaphore_signal(
            barrier, inc=1, device_id=where(lax.rem(me + 1 + i, count)), device_id_type=mesh_ids
        )
        return carry

    lax.fori_loop(0, count - 1, greet, 0)
    pl.semaphore_wait(barrier, count - 1)
    local = pltpu.make_async_copy(x_ref.at[me], o_ref.at[me], local_sem)
    local.start()

    def outgoing(peer):
        return pltpu.make_async_remote_copy(
            src_ref=x_ref.at[peer],
            dst_ref=o_ref.at[me],
            send_sem=send_sems.at[peer],
            recv_sem=recv_sems.at[me],
            device_id=where(peer),
            device_id_type=mesh_ids,
        )

    def incoming(src):
        return pltpu.make_async_remote_copy(
            src_ref=x_ref.at[src],
            dst_ref=o_ref.at[src],
            send_sem=send_sems.at[src],
            recv_sem=recv_sems.at[src],
            device_id=where(src),
            device_id_type=mesh_ids,
        )

    def send(i, carry):
        outgoing(lax.rem(me + 1 + i, count)).start()
        return carry

    lax.fori_loop(0, count - 1, send, 0)

    def finish(i, carry):
        outgoing(lax.rem(me + 1 + i, count)).wait_send()
        incoming(lax.rem(me + count - 1 - i, count)).wait_recv()
        return carry

    lax.fori_loop(0, count - 1, finish, 0)
    local.wait()


def slab_all_to_all(x, cid):
    count = x.shape[0]
    return pl.pallas_call(
        _a2a_kernel,
        out_shape=jax.ShapeDtypeStruct(x.shape, x.dtype),
        in_specs=[pl.BlockSpec(memory_space=pl.ANY)],
        out_specs=pl.BlockSpec(memory_space=pl.ANY),
        scratch_shapes=[
            pltpu.SemaphoreType.DMA((count,)),
            pltpu.SemaphoreType.DMA((count,)),
            pltpu.SemaphoreType.DMA,
        ],
        compiler_params=pltpu.CompilerParams(collective_id=cid, has_side_effects=True),
    )(x)


def on_device(volume, interp, block_index, images, defocus, orient):
    slab_count = lax.axis_size(SLAB)
    slab_index = lax.axis_index(SLAB)
    orient_count = interp.shape[1]
    ori_dev = orient_count // slab_count
    block_rows = interp.shape[2]
    fourier = images.shape[2]
    block_count = fourier // block_rows
    img_dev = images.shape[1]
    picks = orient.shape[2]
    levels = jnp.arange(block_count, dtype=jnp.int32)
    partial_value = jnp.einsum("jpr,rx->jpx", interp[0], volume, preferred_element_type=jnp.float32)
    owned_idx = lax.dynamic_slice_in_dim(block_index[0], slab_index * ori_dev, ori_dev, 0)
    received = slab_all_to_all(
        partial_value.reshape(slab_count, ori_dev * block_rows, 2 * fourier), 1
    ).reshape(slab_count, ori_dev, block_rows, 2 * fourier)
    place = (owned_idx[:, :, None] == levels).astype(jnp.float32)
    summed = jnp.einsum(
        "osb,sopx->obpx", place, received, precision=lax.Precision.HIGHEST,
        preferred_element_type=jnp.float32,
    ).reshape(ori_dev, fourier, 2 * fourier)
    panels = summed.astype(jnp.bfloat16)
    for axis in (SLAB[1], SLAB[0], SLAB[2]):
        parts = lax.axis_size(axis)
        panels = lax.all_to_all(
            jnp.broadcast_to(panels[None], (parts,) + panels.shape),
            axis, split_axis=0, concat_axis=0, tiled=True,
        ).reshape((-1,) + panels.shape[1:])
    sizes = tuple(lax.axis_size(a) for a in SLAB)
    inv_perm = jnp.arange(orient_count, dtype=jnp.int32).reshape(
        (sizes[2], sizes[0], sizes[1], ori_dev)
    ).transpose(1, 2, 0, 3).reshape(-1)
    weights, contrib = correlate_all(panels, images[0], orient[0], inv_perm[orient[0]], defocus[0])
    contrib = pair_sum(contrib, 2)
    contrib = axis_sum(contrib, SLAB[0], 3)
    back_own = axis_sum(contrib, SLAB[1], 4)
    back_own = back_own.reshape(ori_dev, block_count, block_rows, 2 * fourier)
    chosen_back = (owned_idx[:, :, None] == levels).astype(jnp.bfloat16)
    outgoing = jnp.einsum(
        "osb,obpx->sopx", chosen_back, back_own, preferred_element_type=jnp.float32
    )
    outgoing = outgoing.astype(jnp.bfloat16).reshape(slab_count * ori_dev, block_rows, 2 * fourier)
    incoming = lax.all_to_all(outgoing, SLAB, split_axis=0, concat_axis=0, tiled=True)
    column = jnp.einsum("jpr,jpx->rx", interp[0], incoming, preferred_element_type=jnp.float32)
    summed_cols = img_sum(column, lax.axis_size("img"), 0)
    update = summed_cols / math.sqrt(img_dev * slab_count)
    return (update, weights[None])


def solution(mesh):
    devices = mesh.devices
    cores = 2
    xs = len({d.coords[0] for d in devices.reshape(-1)}) if hasattr(devices.reshape(-1)[0], "coords") else 4
    split = devices.reshape((xs, devices.shape[0] // (xs * cores), cores) + devices.shape[1:])
    fine = jax.sharding.Mesh(split, SLAB + ("img",))
    return jax.shard_map(
        on_device,
        mesh=fine,
        in_specs=(
            P(SLAB, None),
            P("img", None, None, SLAB),
            P("img", None, None),
            P("img", SLAB, None, None),
            P("img", SLAB),
            P("img", SLAB, None),
        ),
        out_specs=(P(SLAB, None), P("img", SLAB, None)),
        check_vma=False,
    )
```

```python
import functools
import math

import jax
import jax.numpy as jnp
from jax import lax
from jax.experimental import pallas as pl
from jax.experimental.pallas import tpu as pltpu
from jax.sharding import PartitionSpec as P

BOX = 256
NS = 16
SLAB = ("sx", "sz", "sc")


wave_length = 0.0197
aberration = 27000000.0
amplitude = 0.1
grid_side = 4


def phase_tables(fourier, shifts, box):
    freq = (jnp.arange(fourier, dtype=jnp.int32) - fourier // 2).astype(jnp.float32)
    shift_steps = jnp.arange(shifts, dtype=jnp.int32)
    shift_x = (2 * (shift_steps // grid_side) - (grid_side - 1)).astype(jnp.float32)
    shift_y = (2 * (shift_steps % grid_side) - (grid_side - 1)).astype(jnp.float32)
    angle = 2.0 * math.pi / box * (freq[:, None, None] * shift_x + freq[None, :, None] * shift_y)
    forward = jnp.stack([jnp.cos(angle), jnp.sin(angle)], axis=1).reshape(
        2 * fourier * fourier, shifts
    )
    backward = jnp.stack([jnp.cos(angle), -jnp.sin(angle)], axis=1).reshape(
        2 * fourier * fourier, shifts
    )
    return (forward.astype(jnp.bfloat16), backward.T.astype(jnp.bfloat16))


def contrast(defocus_blk, fourier, box):
    freq = (jnp.arange(fourier, dtype=jnp.int32) - fourier // 2).astype(jnp.float32)
    wave_sq = (freq[:, None] * freq[:, None] + freq[None, :] * freq[None, :]) / (box * box)
    phase = math.pi * wave_length * defocus_blk[:, None, None] * wave_sq
    phase = phase - 0.5 * math.pi * aberration * wave_length**3 * wave_sq * wave_sq
    return -(math.sqrt(1.0 - amplitude * amplitude) * jnp.sin(phase) + amplitude * jnp.cos(phase))


def correlate(panels, image_blk, list_blk, defocus_blk, phase_fwd, phase_back, box):
    count = image_blk.shape[0]
    fourier = image_blk.shape[1]
    picks = list_blk.shape[1]
    shifts = phase_fwd.shape[1]
    ctf = contrast(defocus_blk, fourier, box)
    weighted = ctf[:, :, None, :] * image_blk.astype(jnp.float32).reshape(
        count, fourier, 2, fourier
    )
    real_u = weighted[:, None, :, 0]
    imag_u = weighted[:, None, :, 1]
    chosen = panels[list_blk].astype(jnp.float32).reshape(count, picks, fourier, 2, fourier)
    real_p = chosen[:, :, :, 0]
    imag_p = chosen[:, :, :, 1]
    product = jnp.stack(
        [real_p * real_u + imag_p * imag_u, real_p * imag_u - imag_p * real_u], axis=3
    )
    product = product.astype(jnp.bfloat16).reshape(count * picks, 2 * fourier * fourier)
    scores = jnp.dot(product, phase_fwd, preferred_element_type=jnp.float32) / fourier
    scores = scores.reshape(count, picks * shifts)
    squared = scores * scores
    weights = squared / (jnp.mean(squared, axis=1, keepdims=True) + 1e-05)
    rounded = weights.astype(jnp.bfloat16).reshape(count * picks, shifts)
    spread = jnp.dot(rounded, phase_back, preferred_element_type=jnp.float32)
    spread = spread.reshape(count, picks, fourier, 2, fourier)
    real_e = spread[:, :, :, 0]
    imag_e = spread[:, :, :, 1]
    backed = jnp.stack(
        [real_u * real_e - imag_u * imag_e, real_u * imag_e + imag_u * real_e], axis=3
    )
    backed = backed.astype(jnp.bfloat16).reshape(count * picks, 2 * fourier * fourier)
    return (weights, backed)


def _correlate_kernel(orient_ref, row_ref, panels_ref, image_ref, ctf_ref, cos_ref, sin_ref, w_ref, out_ref, acc_ref):
    i = pl.program_id(0)
    mirror = cos_ref.shape[0]
    shifts = 2 * mirror
    picks = w_ref.shape[1] // shifts
    half = ctf_ref.shape[2]

    @pl.when(i == 0)
    def _():
        acc_ref[...] = jnp.zeros_like(acc_ref)

    ctf = ctf_ref[0]
    image = image_ref[0].astype(jnp.float32)
    ur = ctf * image[:, :half]
    ui = ctf * image[:, half:]
    rows = []
    for k in range(picks):
        panel = panels_ref[row_ref[i * picks + k]].astype(jnp.float32)
        pr = panel[:, :half]
        pi = panel[:, half:]
        prod_re = (pr * ur + pi * ui).astype(jnp.bfloat16).astype(jnp.float32)
        prod_im = (pr * ui - pi * ur).astype(jnp.bfloat16).astype(jnp.float32)
        even = []
        odd = []
        for t in range(mirror):
            even.append(jnp.sum(prod_re * cos_ref[t], axis=0, keepdims=True))
            odd.append(jnp.sum(prod_im * sin_ref[t], axis=0, keepdims=True))
        rows.extend(even[t] + odd[t] for t in range(mirror))
        rows.extend(even[shifts - 1 - t] - odd[shifts - 1 - t] for t in range(mirror, shifts))
    scores = jnp.sum(jnp.concatenate(rows, axis=0), axis=1, keepdims=True) / half
    squared = scores * scores
    mean = jnp.sum(squared, axis=0, keepdims=True) / squared.shape[0]
    weights = squared / (mean + 1e-05)
    w_ref[0] = weights
    wround = weights.astype(jnp.bfloat16).astype(jnp.float32)
    for k in range(picks):
        er = jnp.zeros_like(ur)
        ei = jnp.zeros_like(ur)
        for t in range(mirror):
            wt = wround[k * shifts + t : k * shifts + t + 1, :]
            wm = wround[k * shifts + shifts - 1 - t : k * shifts + shifts - t, :]
            er = er + (wt + wm) * cos_ref[t]
            ei = ei - (wt - wm) * sin_ref[t]
        slice_re = (ur * er - ui * ei).astype(jnp.bfloat16).astype(jnp.float32)
        slice_im = (ur * ei + ui * er).astype(jnp.bfloat16).astype(jnp.float32)
        j = row_ref[i * picks + k]
        acc_ref[j, :, :half] += slice_re
        acc_ref[j, :, half:] += slice_im

    @pl.when(i == pl.num_programs(0) - 1)
    def _():
        out_ref[...] = acc_ref[...].astype(out_ref.dtype)


def correlate_all(panels, images, orient, rows, defocus):
    count, fourier, width = images.shape
    picks = orient.shape[1]
    orient_count = panels.shape[0]
    ctf = contrast(defocus, fourier, BOX)
    freq = (jnp.arange(fourier, dtype=jnp.int32) - fourier // 2).astype(jnp.float32)
    shift_steps = jnp.arange(NS // 2, dtype=jnp.int32)
    shift_x = (2 * (shift_steps // grid_side) - (grid_side - 1)).astype(jnp.float32)
    shift_y = (2 * (shift_steps % grid_side) - (grid_side - 1)).astype(jnp.float32)
    angle = 2.0 * math.pi / BOX * (
        freq[None, :, None] * shift_x[:, None, None] + freq[None, None, :] * shift_y[:, None, None]
    )
    cos_t = jnp.cos(angle).astype(jnp.bfloat16).astype(jnp.float32)
    sin_t = jnp.sin(angle).astype(jnp.bfloat16).astype(jnp.float32)
    grid_spec = pltpu.PrefetchScalarGridSpec(
        num_scalar_prefetch=2,
        grid=(count,),
        in_specs=[
            pl.BlockSpec((orient_count, fourier, width), lambda i, o, w: (0, 0, 0)),
            pl.BlockSpec((1, fourier, width), lambda i, o, w: (i, 0, 0)),
            pl.BlockSpec((1, fourier, fourier), lambda i, o, w: (i, 0, 0)),
            pl.BlockSpec((NS // 2, fourier, fourier), lambda i, o, w: (0, 0, 0)),
            pl.BlockSpec((NS // 2, fourier, fourier), lambda i, o, w: (0, 0, 0)),
        ],
        out_specs=[
            pl.BlockSpec((1, picks * NS, 1), lambda i, o, w: (i, 0, 0)),
            pl.BlockSpec((orient_count, fourier, width), lambda i, o, w: (0, 0, 0)),
        ],
        scratch_shapes=[pltpu.VMEM((orient_count, fourier, width), jnp.float32)],
    )
    weights, contrib = pl.pallas_call(
        _correlate_kernel,
        grid_spec=grid_spec,
        out_shape=[
            jax.ShapeDtypeStruct((count, picks * NS, 1), jnp.float32),
            jax.ShapeDtypeStruct((orient_count, fourier, width), jnp.bfloat16),
        ],
        compiler_params=pltpu.CompilerParams(
            dimension_semantics=("arbitrary",), vmem_limit_bytes=56 * 1024 * 1024
        ),
    )(orient.reshape(-1), rows.reshape(-1), panels, images, ctf, cos_t, sin_t)
    return weights.reshape(count, picks * NS), contrib


def _pair_sum_kernel(x_ref, o_ref, own, recv, send_sem, recv_sem, local_sem):
    half = own.shape[0]
    me = lax.axis_index(SLAB[2])
    mate = 1 - me
    where = (lax.axis_index(SLAB[0]), lax.axis_index(SLAB[1]), mate, lax.axis_index("img"))
    mesh_ids = pl.DeviceIdType.MESH
    barrier = pltpu.get_barrier_semaphore()
    pl.semaphore_signal(barrier, inc=1, device_id=where, device_id_type=mesh_ids)
    pl.semaphore_wait(barrier, 1)
    local = pltpu.make_async_copy(x_ref.at[pl.ds(me * half, half)], own, local_sem)
    local.start()
    copy = pltpu.make_async_remote_copy(
        src_ref=x_ref.at[pl.ds(mate * half, half)], dst_ref=recv, send_sem=send_sem,
        recv_sem=recv_sem, device_id=where, device_id_type=mesh_ids,
    )
    copy.start()
    local.wait()
    copy.wait()

    def add(b, carry):
        o_ref[b] = (own[b].astype(jnp.float32) + recv[b].astype(jnp.float32)).astype(o_ref.dtype)
        return carry

    lax.fori_loop(0, half, add, 0)


def pair_sum(x, cid):
    half = x.shape[0] // 2
    return pl.pallas_call(
        _pair_sum_kernel,
        out_shape=jax.ShapeDtypeStruct((half,) + x.shape[1:], x.dtype),
        in_specs=[pl.BlockSpec(memory_space=pl.ANY)],
        out_specs=pl.BlockSpec(memory_space=pltpu.VMEM),
        scratch_shapes=[
            pltpu.VMEM((half,) + x.shape[1:], x.dtype),
            pltpu.VMEM((half,) + x.shape[1:], x.dtype),
            pltpu.SemaphoreType.DMA,
            pltpu.SemaphoreType.DMA,
            pltpu.SemaphoreType.DMA,
        ],
        compiler_params=pltpu.CompilerParams(
            collective_id=cid, has_side_effects=True, vmem_limit_bytes=48 * 1024 * 1024
        ),
    )(x)


def _axis_sum_kernel(axis, x_ref, o_ref, got, send_sems, recv_sems, local_sem):
    count, chunk = got.shape[0], got.shape[1]
    me = lax.axis_index(axis)
    names = SLAB + ("img",)
    coords = [lax.axis_index(a) for a in names]
    at = names.index(axis)
    mesh_ids = pl.DeviceIdType.MESH
    peers = [lax.rem(me + 1 + i, count) for i in range(count - 1)]

    def where(peer):
        return tuple(coords[:at]) + (peer,) + tuple(coords[at + 1:])

    barrier = pltpu.get_barrier_semaphore()
    for peer in peers:
        pl.semaphore_signal(barrier, inc=1, device_id=where(peer), device_id_type=mesh_ids)
    pl.semaphore_wait(barrier, count - 1)

    def part(p):
        return x_ref.at[pl.ds(p * chunk, chunk)]

    local = pltpu.make_async_copy(part(me), got.at[me], local_sem)
    local.start()
    sends = []
    for i, peer in enumerate(peers):
        copy = pltpu.make_async_remote_copy(
            src_ref=part(peer), dst_ref=got.at[me], send_sem=send_sems.at[i], recv_sem=recv_sems.at[me],
            device_id=where(peer), device_id_type=mesh_ids,
        )
        copy.start()
        sends.append(copy)
    for i, peer in enumerate(peers):
        sends[i].wait_send()
        pltpu.make_async_remote_copy(
            src_ref=part(peer), dst_ref=got.at[peer], send_sem=send_sems.at[i], recv_sem=recv_sems.at[peer],
            device_id=where(peer), device_id_type=mesh_ids,
        ).wait_recv()
    local.wait()

    def add(b, carry):
        total = got[0, b].astype(jnp.float32)
        for p in range(1, count):
            total = total + got[p, b].astype(jnp.float32)
        o_ref[b] = total.astype(o_ref.dtype)
        return carry

    lax.fori_loop(0, chunk, add, 0)


def axis_sum(x, axis, cid):
    count = lax.axis_size(axis)
    chunk = x.shape[0] // count
    return pl.pallas_call(
        functools.partial(_axis_sum_kernel, axis),
        out_shape=jax.ShapeDtypeStruct((chunk,) + x.shape[1:], x.dtype),
        in_specs=[pl.BlockSpec(memory_space=pl.ANY)],
        out_specs=pl.BlockSpec(memory_space=pltpu.VMEM),
        scratch_shapes=[
            pltpu.VMEM((count, chunk) + x.shape[1:], x.dtype),
            pltpu.SemaphoreType.DMA((count,)),
            pltpu.SemaphoreType.DMA((count,)),
            pltpu.SemaphoreType.DMA,
        ],
        compiler_params=pltpu.CompilerParams(
            collective_id=cid, has_side_effects=True, vmem_limit_bytes=48 * 1024 * 1024
        ),
    )(x)


def _axis_gather_kernel(axis, x_ref, o_ref, send_sems, recv_sems, local_sem):
    count = o_ref.shape[0]
    me = lax.axis_index(axis)
    names = SLAB + ("img",)
    coords = [lax.axis_index(a) for a in names]
    at = names.index(axis)
    mesh_ids = pl.DeviceIdType.MESH
    peers = [lax.rem(me + 1 + i, count) for i in range(count - 1)]

    def where(peer):
        return tuple(coords[:at]) + (peer,) + tuple(coords[at + 1:])

    barrier = pltpu.get_barrier_semaphore()
    for peer in peers:
        pl.semaphore_signal(barrier, inc=1, device_id=where(peer), device_id_type=mesh_ids)
    pl.semaphore_wait(barrier, count - 1)
    local = pltpu.make_async_copy(x_ref, o_ref.at[me], local_sem)
    local.start()
    sends = []
    for i, peer in enumerate(peers):
        copy = pltpu.make_async_remote_copy(
            src_ref=x_ref, dst_ref=o_ref.at[me], send_sem=send_sems.at[i], recv_sem=recv_sems.at[me],
            device_id=where(peer), device_id_type=mesh_ids,
        )
        copy.start()
        sends.append(copy)
    for i, peer in enumerate(peers):
        sends[i].wait_send()
        pltpu.make_async_remote_copy(
            src_ref=x_ref, dst_ref=o_ref.at[peer], send_sem=send_sems.at[i], recv_sem=recv_sems.at[peer],
            device_id=where(peer), device_id_type=mesh_ids,
        ).wait_recv()
    local.wait()


def axis_gather(x, axis, cid):
    count = lax.axis_size(axis)
    out = pl.pallas_call(
        functools.partial(_axis_gather_kernel, axis),
        out_shape=jax.ShapeDtypeStruct((count,) + x.shape, x.dtype),
        in_specs=[pl.BlockSpec(memory_space=pl.ANY)],
        out_specs=pl.BlockSpec(memory_space=pl.ANY),
        scratch_shapes=[
            pltpu.SemaphoreType.DMA((count,)),
            pltpu.SemaphoreType.DMA((count,)),
            pltpu.SemaphoreType.DMA,
        ],
        compiler_params=pltpu.CompilerParams(collective_id=cid, has_side_effects=True),
    )(x)
    return out.reshape((-1,) + x.shape[1:])


def _img_sum_kernel(x_ref, o_ref, gat, qbuf, s1, r1, s2, r2, l1, l2):
    count, rows = gat.shape[0], gat.shape[1]
    me = lax.axis_index("img")
    here = tuple(lax.axis_index(a) for a in SLAB)
    mesh_ids = pl.DeviceIdType.MESH
    barrier = pltpu.get_barrier_semaphore()
    peers = [lax.rem(me + 1 + i, count) for i in range(count - 1)]
    for peer in peers:
        pl.semaphore_signal(barrier, inc=1, device_id=here + (peer,), device_id_type=mesh_ids)
    pl.semaphore_wait(barrier, count - 1)

    def part(p):
        return x_ref.at[pl.ds(pl.multiple_of(p * rows, rows), rows)]

    local = pltpu.make_async_copy(part(me), gat.at[me], l1)
    local.start()
    sends = []
    for i, peer in enumerate(peers):
        copy = pltpu.make_async_remote_copy(
            src_ref=part(peer), dst_ref=gat.at[me], send_sem=s1.at[i], recv_sem=r1.at[me],
            device_id=here + (peer,), device_id_type=mesh_ids,
        )
        copy.start()
        sends.append(copy)
    for i, peer in enumerate(peers):
        sends[i].wait_send()
        pltpu.make_async_remote_copy(
            src_ref=part(peer), dst_ref=gat.at[peer], send_sem=s1.at[i], recv_sem=r1.at[peer],
            device_id=here + (peer,), device_id_type=mesh_ids,
        ).wait_recv()
    local.wait()
    qbuf[...] = jnp.sum(gat[...], axis=0)
    local = pltpu.make_async_copy(qbuf, o_ref.at[me], l2)
    local.start()
    sends = []
    for i, peer in enumerate(peers):
        copy = pltpu.make_async_remote_copy(
            src_ref=qbuf, dst_ref=o_ref.at[me], send_sem=s2.at[i], recv_sem=r2.at[me],
            device_id=here + (peer,), device_id_type=mesh_ids,
        )
        copy.start()
        sends.append(copy)
    for i, peer in enumerate(peers):
        sends[i].wait_send()
        pltpu.make_async_remote_copy(
            src_ref=qbuf, dst_ref=o_ref.at[peer], send_sem=s2.at[i], recv_sem=r2.at[peer],
            device_id=here + (peer,), device_id_type=mesh_ids,
        ).wait_recv()
    local.wait()


def img_sum(x, count, cid):
    rows = x.shape[0] // count
    out = pl.pallas_call(
        _img_sum_kernel,
        out_shape=jax.ShapeDtypeStruct((count, rows) + x.shape[1:], x.dtype),
        in_specs=[pl.BlockSpec(memory_space=pltpu.VMEM)],
        out_specs=pl.BlockSpec(memory_space=pl.ANY),
        scratch_shapes=[
            pltpu.VMEM((count, rows) + x.shape[1:], x.dtype),
            pltpu.VMEM((rows,) + x.shape[1:], x.dtype),
            pltpu.SemaphoreType.DMA((count,)),
            pltpu.SemaphoreType.DMA((count,)),
            pltpu.SemaphoreType.DMA((count,)),
            pltpu.SemaphoreType.DMA((count,)),
            pltpu.SemaphoreType.DMA,
            pltpu.SemaphoreType.DMA,
        ],
        compiler_params=pltpu.CompilerParams(collective_id=cid, has_side_effects=True),
    )(x)
    return out.reshape(x.shape)


def _a2a_kernel(x_ref, o_ref, send_sems, recv_sems, local_sem):
    count = x_ref.shape[0]
    sizes = tuple(lax.axis_size(a) for a in SLAB)
    me = lax.axis_index(SLAB)
    grp = lax.axis_index("img")
    mesh_ids = pl.DeviceIdType.MESH
    barrier = pltpu.get_barrier_semaphore()

    def where(peer):
        return (peer // (sizes[1] * sizes[2]), (peer // sizes[2]) % sizes[1], peer % sizes[2], grp)

    def greet(i, carry):
        pl.semaphore_signal(
            barrier, inc=1, device_id=where(lax.rem(me + 1 + i, count)), device_id_type=mesh_ids
        )
        return carry

    lax.fori_loop(0, count - 1, greet, 0)
    pl.semaphore_wait(barrier, count - 1)
    local = pltpu.make_async_copy(x_ref.at[me], o_ref.at[me], local_sem)
    local.start()

    def outgoing(peer):
        return pltpu.make_async_remote_copy(
            src_ref=x_ref.at[peer],
            dst_ref=o_ref.at[me],
            send_sem=send_sems.at[peer],
            recv_sem=recv_sems.at[me],
            device_id=where(peer),
            device_id_type=mesh_ids,
        )

    def incoming(src):
        return pltpu.make_async_remote_copy(
            src_ref=x_ref.at[src],
            dst_ref=o_ref.at[src],
            send_sem=send_sems.at[src],
            recv_sem=recv_sems.at[src],
            device_id=where(src),
            device_id_type=mesh_ids,
        )

    def send(i, carry):
        outgoing(lax.rem(me + 1 + i, count)).start()
        return carry

    lax.fori_loop(0, count - 1, send, 0)

    def finish(i, carry):
        outgoing(lax.rem(me + 1 + i, count)).wait_send()
        incoming(lax.rem(me + count - 1 - i, count)).wait_recv()
        return carry

    lax.fori_loop(0, count - 1, finish, 0)
    local.wait()


def slab_all_to_all(x, cid):
    count = x.shape[0]
    return pl.pallas_call(
        _a2a_kernel,
        out_shape=jax.ShapeDtypeStruct(x.shape, x.dtype),
        in_specs=[pl.BlockSpec(memory_space=pl.ANY)],
        out_specs=pl.BlockSpec(memory_space=pl.ANY),
        scratch_shapes=[
            pltpu.SemaphoreType.DMA((count,)),
            pltpu.SemaphoreType.DMA((count,)),
            pltpu.SemaphoreType.DMA,
        ],
        compiler_params=pltpu.CompilerParams(collective_id=cid, has_side_effects=True),
    )(x)


def on_device(volume, interp, block_index, images, defocus, orient):
    slab_count = lax.axis_size(SLAB)
    slab_index = lax.axis_index(SLAB)
    orient_count = interp.shape[1]
    ori_dev = orient_count // slab_count
    block_rows = interp.shape[2]
    fourier = images.shape[2]
    block_count = fourier // block_rows
    img_dev = images.shape[1]
    picks = orient.shape[2]
    levels = jnp.arange(block_count, dtype=jnp.int32)
    partial_value = jnp.einsum("jpr,rx->jpx", interp[0], volume, preferred_element_type=jnp.float32)
    owned_idx = lax.dynamic_slice_in_dim(block_index[0], slab_index * ori_dev, ori_dev, 0)
    received = slab_all_to_all(
        partial_value.reshape(slab_count, ori_dev * block_rows, 2 * fourier), 1
    ).reshape(slab_count, ori_dev, block_rows, 2 * fourier)
    place = (owned_idx[:, :, None] == levels).astype(jnp.float32)
    summed = jnp.einsum(
        "osb,sopx->obpx", place, received, precision=lax.Precision.HIGHEST,
        preferred_element_type=jnp.float32,
    ).reshape(ori_dev, fourier, 2 * fourier)
    panels = summed.astype(jnp.bfloat16)
    for cid, axis in ((5, SLAB[1]), (6, SLAB[0]), (7, SLAB[2])):
        panels = axis_gather(panels, axis, cid)
    sizes = tuple(lax.axis_size(a) for a in SLAB)
    inv_perm = jnp.arange(orient_count, dtype=jnp.int32).reshape(
        (sizes[2], sizes[0], sizes[1], ori_dev)
    ).transpose(1, 2, 0, 3).reshape(-1)
    weights, contrib = correlate_all(panels, images[0], orient[0], inv_perm[orient[0]], defocus[0])
    contrib = pair_sum(contrib, 2)
    contrib = axis_sum(contrib, SLAB[0], 3)
    back_own = axis_sum(contrib, SLAB[1], 4)
    back_own = back_own.reshape(ori_dev, block_count, block_rows, 2 * fourier)
    chosen_back = (owned_idx[:, :, None] == levels).astype(jnp.bfloat16)
    outgoing = jnp.einsum(
        "osb,obpx->sopx", chosen_back, back_own, preferred_element_type=jnp.float32
    )
    outgoing = outgoing.astype(jnp.bfloat16).reshape(slab_count * ori_dev, block_rows, 2 * fourier)
    incoming = lax.all_to_all(outgoing, SLAB, split_axis=0, concat_axis=0, tiled=True)
    column = jnp.einsum("jpr,jpx->rx", interp[0], incoming, preferred_element_type=jnp.float32)
    summed_cols = img_sum(column, lax.axis_size("img"), 0)
    update = summed_cols / math.sqrt(img_dev * slab_count)
    return (update, weights[None])


def solution(mesh):
    devices = mesh.devices
    cores = 2
    xs = len({d.coords[0] for d in devices.reshape(-1)}) if hasattr(devices.reshape(-1)[0], "coords") else 4
    split = devices.reshape((xs, devices.shape[0] // (xs * cores), cores) + devices.shape[1:])
    fine = jax.sharding.Mesh(split, SLAB + ("img",))
    return jax.shard_map(
        on_device,
        mesh=fine,
        in_specs=(
            P(SLAB, None),
            P("img", None, None, SLAB),
            P("img", None, None),
            P("img", SLAB, None, None),
            P("img", SLAB),
            P("img", SLAB, None),
        ),
        out_specs=(P(SLAB, None), P("img", SLAB, None)),
        check_vma=False,
    )
```

```python
import functools
import math

import jax
import jax.numpy as jnp
from jax import lax
from jax.experimental import pallas as pl
from jax.experimental.pallas import tpu as pltpu
from jax.sharding import PartitionSpec as P

BOX = 256
NS = 16
SLAB = ("sx", "sz", "sc")


wave_length = 0.0197
aberration = 27000000.0
amplitude = 0.1
grid_side = 4


def phase_tables(fourier, shifts, box):
    freq = (jnp.arange(fourier, dtype=jnp.int32) - fourier // 2).astype(jnp.float32)
    shift_steps = jnp.arange(shifts, dtype=jnp.int32)
    shift_x = (2 * (shift_steps // grid_side) - (grid_side - 1)).astype(jnp.float32)
    shift_y = (2 * (shift_steps % grid_side) - (grid_side - 1)).astype(jnp.float32)
    angle = 2.0 * math.pi / box * (freq[:, None, None] * shift_x + freq[None, :, None] * shift_y)
    forward = jnp.stack([jnp.cos(angle), jnp.sin(angle)], axis=1).reshape(
        2 * fourier * fourier, shifts
    )
    backward = jnp.stack([jnp.cos(angle), -jnp.sin(angle)], axis=1).reshape(
        2 * fourier * fourier, shifts
    )
    return (forward.astype(jnp.bfloat16), backward.T.astype(jnp.bfloat16))


def contrast(defocus_blk, fourier, box):
    freq = (jnp.arange(fourier, dtype=jnp.int32) - fourier // 2).astype(jnp.float32)
    wave_sq = (freq[:, None] * freq[:, None] + freq[None, :] * freq[None, :]) / (box * box)
    phase = math.pi * wave_length * defocus_blk[:, None, None] * wave_sq
    phase = phase - 0.5 * math.pi * aberration * wave_length**3 * wave_sq * wave_sq
    return -(math.sqrt(1.0 - amplitude * amplitude) * jnp.sin(phase) + amplitude * jnp.cos(phase))


def correlate(panels, image_blk, list_blk, defocus_blk, phase_fwd, phase_back, box):
    count = image_blk.shape[0]
    fourier = image_blk.shape[1]
    picks = list_blk.shape[1]
    shifts = phase_fwd.shape[1]
    ctf = contrast(defocus_blk, fourier, box)
    weighted = ctf[:, :, None, :] * image_blk.astype(jnp.float32).reshape(
        count, fourier, 2, fourier
    )
    real_u = weighted[:, None, :, 0]
    imag_u = weighted[:, None, :, 1]
    chosen = panels[list_blk].astype(jnp.float32).reshape(count, picks, fourier, 2, fourier)
    real_p = chosen[:, :, :, 0]
    imag_p = chosen[:, :, :, 1]
    product = jnp.stack(
        [real_p * real_u + imag_p * imag_u, real_p * imag_u - imag_p * real_u], axis=3
    )
    product = product.astype(jnp.bfloat16).reshape(count * picks, 2 * fourier * fourier)
    scores = jnp.dot(product, phase_fwd, preferred_element_type=jnp.float32) / fourier
    scores = scores.reshape(count, picks * shifts)
    squared = scores * scores
    weights = squared / (jnp.mean(squared, axis=1, keepdims=True) + 1e-05)
    rounded = weights.astype(jnp.bfloat16).reshape(count * picks, shifts)
    spread = jnp.dot(rounded, phase_back, preferred_element_type=jnp.float32)
    spread = spread.reshape(count, picks, fourier, 2, fourier)
    real_e = spread[:, :, :, 0]
    imag_e = spread[:, :, :, 1]
    backed = jnp.stack(
        [real_u * real_e - imag_u * imag_e, real_u * imag_e + imag_u * real_e], axis=3
    )
    backed = backed.astype(jnp.bfloat16).reshape(count * picks, 2 * fourier * fourier)
    return (weights, backed)


def _correlate_kernel(orient_ref, row_ref, panels_ref, image_ref, ctf_ref, cos_ref, sin_ref, w_ref, out_ref, acc_ref):
    i = pl.program_id(0)
    mirror = cos_ref.shape[0]
    shifts = 2 * mirror
    picks = w_ref.shape[1] // shifts
    half = ctf_ref.shape[2]

    @pl.when(i == 0)
    def _():
        acc_ref[...] = jnp.zeros_like(acc_ref)

    ctf = ctf_ref[0]
    image = image_ref[0].astype(jnp.float32)
    ur = ctf * image[:, :half]
    ui = ctf * image[:, half:]
    rows = []
    for k in range(picks):
        panel = panels_ref[row_ref[i * picks + k]].astype(jnp.float32)
        pr = panel[:, :half]
        pi = panel[:, half:]
        prod_re = (pr * ur + pi * ui).astype(jnp.bfloat16).astype(jnp.float32)
        prod_im = (pr * ui - pi * ur).astype(jnp.bfloat16).astype(jnp.float32)
        even = []
        odd = []
        for t in range(mirror):
            even.append(jnp.sum(prod_re * cos_ref[t], axis=0, keepdims=True))
            odd.append(jnp.sum(prod_im * sin_ref[t], axis=0, keepdims=True))
        rows.extend(even[t] + odd[t] for t in range(mirror))
        rows.extend(even[shifts - 1 - t] - odd[shifts - 1 - t] for t in range(mirror, shifts))
    scores = jnp.sum(jnp.concatenate(rows, axis=0), axis=1, keepdims=True) / half
    squared = scores * scores
    mean = jnp.sum(squared, axis=0, keepdims=True) / squared.shape[0]
    weights = squared / (mean + 1e-05)
    w_ref[0] = weights
    wround = weights.astype(jnp.bfloat16).astype(jnp.float32)
    for k in range(picks):
        er = jnp.zeros_like(ur)
        ei = jnp.zeros_like(ur)
        for t in range(mirror):
            wt = wround[k * shifts + t : k * shifts + t + 1, :]
            wm = wround[k * shifts + shifts - 1 - t : k * shifts + shifts - t, :]
            er = er + (wt + wm) * cos_ref[t]
            ei = ei - (wt - wm) * sin_ref[t]
        slice_re = (ur * er - ui * ei).astype(jnp.bfloat16).astype(jnp.float32)
        slice_im = (ur * ei + ui * er).astype(jnp.bfloat16).astype(jnp.float32)
        j = row_ref[i * picks + k]
        acc_ref[j, :, :half] += slice_re
        acc_ref[j, :, half:] += slice_im

    @pl.when(i == pl.num_programs(0) - 1)
    def _():
        out_ref[...] = acc_ref[...].astype(out_ref.dtype)


def correlate_all(panels, images, orient, rows, defocus):
    count, fourier, width = images.shape
    picks = orient.shape[1]
    orient_count = panels.shape[0]
    ctf = contrast(defocus, fourier, BOX)
    freq = (jnp.arange(fourier, dtype=jnp.int32) - fourier // 2).astype(jnp.float32)
    shift_steps = jnp.arange(NS // 2, dtype=jnp.int32)
    shift_x = (2 * (shift_steps // grid_side) - (grid_side - 1)).astype(jnp.float32)
    shift_y = (2 * (shift_steps % grid_side) - (grid_side - 1)).astype(jnp.float32)
    angle = 2.0 * math.pi / BOX * (
        freq[None, :, None] * shift_x[:, None, None] + freq[None, None, :] * shift_y[:, None, None]
    )
    cos_t = jnp.cos(angle).astype(jnp.bfloat16).astype(jnp.float32)
    sin_t = jnp.sin(angle).astype(jnp.bfloat16).astype(jnp.float32)
    grid_spec = pltpu.PrefetchScalarGridSpec(
        num_scalar_prefetch=2,
        grid=(count,),
        in_specs=[
            pl.BlockSpec((orient_count, fourier, width), lambda i, o, w: (0, 0, 0)),
            pl.BlockSpec((1, fourier, width), lambda i, o, w: (i, 0, 0)),
            pl.BlockSpec((1, fourier, fourier), lambda i, o, w: (i, 0, 0)),
            pl.BlockSpec((NS // 2, fourier, fourier), lambda i, o, w: (0, 0, 0)),
            pl.BlockSpec((NS // 2, fourier, fourier), lambda i, o, w: (0, 0, 0)),
        ],
        out_specs=[
            pl.BlockSpec((1, picks * NS, 1), lambda i, o, w: (i, 0, 0)),
            pl.BlockSpec((orient_count, fourier, width), lambda i, o, w: (0, 0, 0)),
        ],
        scratch_shapes=[pltpu.VMEM((orient_count, fourier, width), jnp.float32)],
    )
    weights, contrib = pl.pallas_call(
        _correlate_kernel,
        grid_spec=grid_spec,
        out_shape=[
            jax.ShapeDtypeStruct((count, picks * NS, 1), jnp.float32),
            jax.ShapeDtypeStruct((orient_count, fourier, width), jnp.bfloat16),
        ],
        compiler_params=pltpu.CompilerParams(
            dimension_semantics=("arbitrary",), vmem_limit_bytes=56 * 1024 * 1024
        ),
    )(orient.reshape(-1), rows.reshape(-1), panels, images, ctf, cos_t, sin_t)
    return weights.reshape(count, picks * NS), contrib


def _pair_sum_kernel(x_ref, o_ref, own, recv, send_sem, recv_sem, local_sem):
    half = own.shape[0]
    me = lax.axis_index(SLAB[2])
    mate = 1 - me
    where = (lax.axis_index(SLAB[0]), lax.axis_index(SLAB[1]), mate, lax.axis_index("img"))
    mesh_ids = pl.DeviceIdType.MESH
    barrier = pltpu.get_barrier_semaphore()
    pl.semaphore_signal(barrier, inc=1, device_id=where, device_id_type=mesh_ids)
    pl.semaphore_wait(barrier, 1)
    local = pltpu.make_async_copy(x_ref.at[pl.ds(me * half, half)], own, local_sem)
    local.start()
    copy = pltpu.make_async_remote_copy(
        src_ref=x_ref.at[pl.ds(mate * half, half)], dst_ref=recv, send_sem=send_sem,
        recv_sem=recv_sem, device_id=where, device_id_type=mesh_ids,
    )
    copy.start()
    local.wait()
    copy.wait()

    def add(b, carry):
        o_ref[b] = (own[b].astype(jnp.float32) + recv[b].astype(jnp.float32)).astype(o_ref.dtype)
        return carry

    lax.fori_loop(0, half, add, 0)


def pair_sum(x, cid):
    half = x.shape[0] // 2
    return pl.pallas_call(
        _pair_sum_kernel,
        out_shape=jax.ShapeDtypeStruct((half,) + x.shape[1:], x.dtype),
        in_specs=[pl.BlockSpec(memory_space=pl.ANY)],
        out_specs=pl.BlockSpec(memory_space=pltpu.VMEM),
        scratch_shapes=[
            pltpu.VMEM((half,) + x.shape[1:], x.dtype),
            pltpu.VMEM((half,) + x.shape[1:], x.dtype),
            pltpu.SemaphoreType.DMA,
            pltpu.SemaphoreType.DMA,
            pltpu.SemaphoreType.DMA,
        ],
        compiler_params=pltpu.CompilerParams(
            collective_id=cid, has_side_effects=True, vmem_limit_bytes=48 * 1024 * 1024
        ),
    )(x)


def _axis_sum_kernel(axis, x_ref, o_ref, got, send_sems, recv_sems, local_sem):
    count, chunk = got.shape[0], got.shape[1]
    me = lax.axis_index(axis)
    names = SLAB + ("img",)
    coords = [lax.axis_index(a) for a in names]
    at = names.index(axis)
    mesh_ids = pl.DeviceIdType.MESH
    peers = [lax.rem(me + 1 + i, count) for i in range(count - 1)]

    def where(peer):
        return tuple(coords[:at]) + (peer,) + tuple(coords[at + 1:])

    barrier = pltpu.get_barrier_semaphore()
    for peer in peers:
        pl.semaphore_signal(barrier, inc=1, device_id=where(peer), device_id_type=mesh_ids)
    pl.semaphore_wait(barrier, count - 1)

    def part(p):
        return x_ref.at[pl.ds(p * chunk, chunk)]

    local = pltpu.make_async_copy(part(me), got.at[me], local_sem)
    local.start()
    sends = []
    for i, peer in enumerate(peers):
        copy = pltpu.make_async_remote_copy(
            src_ref=part(peer), dst_ref=got.at[me], send_sem=send_sems.at[i], recv_sem=recv_sems.at[me],
            device_id=where(peer), device_id_type=mesh_ids,
        )
        copy.start()
        sends.append(copy)
    for i, peer in enumerate(peers):
        sends[i].wait_send()
        pltpu.make_async_remote_copy(
            src_ref=part(peer), dst_ref=got.at[peer], send_sem=send_sems.at[i], recv_sem=recv_sems.at[peer],
            device_id=where(peer), device_id_type=mesh_ids,
        ).wait_recv()
    local.wait()

    def add(b, carry):
        total = got[0, b].astype(jnp.float32)
        for p in range(1, count):
            total = total + got[p, b].astype(jnp.float32)
        o_ref[b] = total.astype(o_ref.dtype)
        return carry

    lax.fori_loop(0, chunk, add, 0)


def axis_sum(x, axis, cid):
    count = lax.axis_size(axis)
    chunk = x.shape[0] // count
    return pl.pallas_call(
        functools.partial(_axis_sum_kernel, axis),
        out_shape=jax.ShapeDtypeStruct((chunk,) + x.shape[1:], x.dtype),
        in_specs=[pl.BlockSpec(memory_space=pl.ANY)],
        out_specs=pl.BlockSpec(memory_space=pltpu.VMEM),
        scratch_shapes=[
            pltpu.VMEM((count, chunk) + x.shape[1:], x.dtype),
            pltpu.SemaphoreType.DMA((count,)),
            pltpu.SemaphoreType.DMA((count,)),
            pltpu.SemaphoreType.DMA,
        ],
        compiler_params=pltpu.CompilerParams(
            collective_id=cid, has_side_effects=True, vmem_limit_bytes=48 * 1024 * 1024
        ),
    )(x)


def _axis_gather_kernel(axis, x_ref, o_ref, send_sems, recv_sems, local_sem):
    count = o_ref.shape[0]
    me = lax.axis_index(axis)
    names = SLAB + ("img",)
    coords = [lax.axis_index(a) for a in names]
    at = names.index(axis)
    mesh_ids = pl.DeviceIdType.MESH
    peers = [lax.rem(me + 1 + i, count) for i in range(count - 1)]

    def where(peer):
        return tuple(coords[:at]) + (peer,) + tuple(coords[at + 1:])

    barrier = pltpu.get_barrier_semaphore()
    for peer in peers:
        pl.semaphore_signal(barrier, inc=1, device_id=where(peer), device_id_type=mesh_ids)
    pl.semaphore_wait(barrier, count - 1)
    local = pltpu.make_async_copy(x_ref, o_ref.at[me], local_sem)
    local.start()
    sends = []
    for i, peer in enumerate(peers):
        copy = pltpu.make_async_remote_copy(
            src_ref=x_ref, dst_ref=o_ref.at[me], send_sem=send_sems.at[i], recv_sem=recv_sems.at[me],
            device_id=where(peer), device_id_type=mesh_ids,
        )
        copy.start()
        sends.append(copy)
    for i, peer in enumerate(peers):
        sends[i].wait_send()
        pltpu.make_async_remote_copy(
            src_ref=x_ref, dst_ref=o_ref.at[peer], send_sem=send_sems.at[i], recv_sem=recv_sems.at[peer],
            device_id=where(peer), device_id_type=mesh_ids,
        ).wait_recv()
    local.wait()


def axis_gather(x, axis, cid):
    count = lax.axis_size(axis)
    out = pl.pallas_call(
        functools.partial(_axis_gather_kernel, axis),
        out_shape=jax.ShapeDtypeStruct((count,) + x.shape, x.dtype),
        in_specs=[pl.BlockSpec(memory_space=pl.ANY)],
        out_specs=pl.BlockSpec(memory_space=pl.ANY),
        scratch_shapes=[
            pltpu.SemaphoreType.DMA((count,)),
            pltpu.SemaphoreType.DMA((count,)),
            pltpu.SemaphoreType.DMA,
        ],
        compiler_params=pltpu.CompilerParams(collective_id=cid, has_side_effects=True),
    )(x)
    return out.reshape((-1,) + x.shape[1:])


def _img_sum_kernel(x_ref, o_ref, gat, qbuf, s1, r1, s2, r2, l1, l2):
    count, rows = gat.shape[0], gat.shape[1]
    me = lax.axis_index("img")
    here = tuple(lax.axis_index(a) for a in SLAB)
    mesh_ids = pl.DeviceIdType.MESH
    barrier = pltpu.get_barrier_semaphore()
    peers = [lax.rem(me + 1 + i, count) for i in range(count - 1)]
    for peer in peers:
        pl.semaphore_signal(barrier, inc=1, device_id=here + (peer,), device_id_type=mesh_ids)
    pl.semaphore_wait(barrier, count - 1)

    def part(p):
        return x_ref.at[pl.ds(pl.multiple_of(p * rows, rows), rows)]

    local = pltpu.make_async_copy(part(me), gat.at[me], l1)
    local.start()
    sends = []
    for i, peer in enumerate(peers):
        copy = pltpu.make_async_remote_copy(
            src_ref=part(peer), dst_ref=gat.at[me], send_sem=s1.at[i], recv_sem=r1.at[me],
            device_id=here + (peer,), device_id_type=mesh_ids,
        )
        copy.start()
        sends.append(copy)
    for i, peer in enumerate(peers):
        sends[i].wait_send()
        pltpu.make_async_remote_copy(
            src_ref=part(peer), dst_ref=gat.at[peer], send_sem=s1.at[i], recv_sem=r1.at[peer],
            device_id=here + (peer,), device_id_type=mesh_ids,
        ).wait_recv()
    local.wait()
    qbuf[...] = jnp.sum(gat[...], axis=0)
    local = pltpu.make_async_copy(qbuf, o_ref.at[me], l2)
    local.start()
    sends = []
    for i, peer in enumerate(peers):
        copy = pltpu.make_async_remote_copy(
            src_ref=qbuf, dst_ref=o_ref.at[me], send_sem=s2.at[i], recv_sem=r2.at[me],
            device_id=here + (peer,), device_id_type=mesh_ids,
        )
        copy.start()
        sends.append(copy)
    for i, peer in enumerate(peers):
        sends[i].wait_send()
        pltpu.make_async_remote_copy(
            src_ref=qbuf, dst_ref=o_ref.at[peer], send_sem=s2.at[i], recv_sem=r2.at[peer],
            device_id=here + (peer,), device_id_type=mesh_ids,
        ).wait_recv()
    local.wait()


def img_sum(x, count, cid):
    rows = x.shape[0] // count
    out = pl.pallas_call(
        _img_sum_kernel,
        out_shape=jax.ShapeDtypeStruct((count, rows) + x.shape[1:], x.dtype),
        in_specs=[pl.BlockSpec(memory_space=pltpu.VMEM)],
        out_specs=pl.BlockSpec(memory_space=pl.ANY),
        scratch_shapes=[
            pltpu.VMEM((count, rows) + x.shape[1:], x.dtype),
            pltpu.VMEM((rows,) + x.shape[1:], x.dtype),
            pltpu.SemaphoreType.DMA((count,)),
            pltpu.SemaphoreType.DMA((count,)),
            pltpu.SemaphoreType.DMA((count,)),
            pltpu.SemaphoreType.DMA((count,)),
            pltpu.SemaphoreType.DMA,
            pltpu.SemaphoreType.DMA,
        ],
        compiler_params=pltpu.CompilerParams(collective_id=cid, has_side_effects=True),
    )(x)
    return out.reshape(x.shape)


def _a2a_kernel(x_ref, o_ref, send_sems, recv_sems, local_sem):
    count = x_ref.shape[0]
    sizes = tuple(lax.axis_size(a) for a in SLAB)
    me = lax.axis_index(SLAB)
    grp = lax.axis_index("img")
    mesh_ids = pl.DeviceIdType.MESH
    barrier = pltpu.get_barrier_semaphore()

    def where(peer):
        return (peer // (sizes[1] * sizes[2]), (peer // sizes[2]) % sizes[1], peer % sizes[2], grp)

    def greet(i, carry):
        pl.semaphore_signal(
            barrier, inc=1, device_id=where(lax.rem(me + 1 + i, count)), device_id_type=mesh_ids
        )
        return carry

    lax.fori_loop(0, count - 1, greet, 0)
    pl.semaphore_wait(barrier, count - 1)
    local = pltpu.make_async_copy(x_ref.at[me], o_ref.at[me], local_sem)
    local.start()

    def outgoing(peer):
        return pltpu.make_async_remote_copy(
            src_ref=x_ref.at[peer],
            dst_ref=o_ref.at[me],
            send_sem=send_sems.at[peer],
            recv_sem=recv_sems.at[me],
            device_id=where(peer),
            device_id_type=mesh_ids,
        )

    def incoming(src):
        return pltpu.make_async_remote_copy(
            src_ref=x_ref.at[src],
            dst_ref=o_ref.at[src],
            send_sem=send_sems.at[src],
            recv_sem=recv_sems.at[src],
            device_id=where(src),
            device_id_type=mesh_ids,
        )

    def send(i, carry):
        outgoing(lax.rem(me + 1 + i, count)).start()
        return carry

    lax.fori_loop(0, count - 1, send, 0)

    def finish(i, carry):
        outgoing(lax.rem(me + 1 + i, count)).wait_send()
        incoming(lax.rem(me + count - 1 - i, count)).wait_recv()
        return carry

    lax.fori_loop(0, count - 1, finish, 0)
    local.wait()


def slab_all_to_all(x, cid):
    count = x.shape[0]
    return pl.pallas_call(
        _a2a_kernel,
        out_shape=jax.ShapeDtypeStruct(x.shape, x.dtype),
        in_specs=[pl.BlockSpec(memory_space=pl.ANY)],
        out_specs=pl.BlockSpec(memory_space=pl.ANY),
        scratch_shapes=[
            pltpu.SemaphoreType.DMA((count,)),
            pltpu.SemaphoreType.DMA((count,)),
            pltpu.SemaphoreType.DMA,
        ],
        compiler_params=pltpu.CompilerParams(collective_id=cid, has_side_effects=True),
    )(x)


def on_device(volume, interp, block_index, images, defocus, orient):
    slab_count = lax.axis_size(SLAB)
    slab_index = lax.axis_index(SLAB)
    orient_count = interp.shape[1]
    ori_dev = orient_count // slab_count
    block_rows = interp.shape[2]
    fourier = images.shape[2]
    block_count = fourier // block_rows
    img_dev = images.shape[1]
    picks = orient.shape[2]
    levels = jnp.arange(block_count, dtype=jnp.int32)
    partial_value = jnp.einsum("jpr,rx->jpx", interp[0], volume, preferred_element_type=jnp.float32)
    owned_idx = lax.dynamic_slice_in_dim(block_index[0], slab_index * ori_dev, ori_dev, 0)
    received = slab_all_to_all(
        partial_value.reshape(slab_count, ori_dev * block_rows, 2 * fourier), 1
    ).reshape(slab_count, ori_dev, block_rows, 2 * fourier)
    place = (owned_idx[:, :, None] == levels).astype(jnp.float32)
    summed = jnp.einsum(
        "osb,sopx->obpx", place, received, precision=lax.Precision.HIGHEST,
        preferred_element_type=jnp.float32,
    ).reshape(ori_dev, fourier, 2 * fourier)
    panels = summed.astype(jnp.bfloat16)
    panels = axis_gather(panels, SLAB[1], 5)
    for axis in (SLAB[0], SLAB[2]):
        parts = lax.axis_size(axis)
        panels = lax.all_to_all(
            jnp.broadcast_to(panels[None], (parts,) + panels.shape),
            axis, split_axis=0, concat_axis=0, tiled=True,
        ).reshape((-1,) + panels.shape[1:])
    sizes = tuple(lax.axis_size(a) for a in SLAB)
    inv_perm = jnp.arange(orient_count, dtype=jnp.int32).reshape(
        (sizes[2], sizes[0], sizes[1], ori_dev)
    ).transpose(1, 2, 0, 3).reshape(-1)
    weights, contrib = correlate_all(panels, images[0], orient[0], inv_perm[orient[0]], defocus[0])
    contrib = pair_sum(contrib, 2)
    contrib = axis_sum(contrib, SLAB[0], 3)
    back_own = axis_sum(contrib, SLAB[1], 4)
    back_own = back_own.reshape(ori_dev, block_count, block_rows, 2 * fourier)
    chosen_back = (owned_idx[:, :, None] == levels).astype(jnp.bfloat16)
    outgoing = jnp.einsum(
        "osb,obpx->sopx", chosen_back, back_own, preferred_element_type=jnp.float32
    )
    outgoing = outgoing.astype(jnp.bfloat16).reshape(slab_count * ori_dev, block_rows, 2 * fourier)
    incoming = lax.all_to_all(outgoing, SLAB, split_axis=0, concat_axis=0, tiled=True)
    column = jnp.einsum("jpr,jpx->rx", interp[0], incoming, preferred_element_type=jnp.float32)
    summed_cols = img_sum(column, lax.axis_size("img"), 0)
    update = summed_cols / math.sqrt(img_dev * slab_count)
    return (update, weights[None])


def solution(mesh):
    devices = mesh.devices
    cores = 2
    xs = len({d.coords[0] for d in devices.reshape(-1)}) if hasattr(devices.reshape(-1)[0], "coords") else 4
    split = devices.reshape((xs, devices.shape[0] // (xs * cores), cores) + devices.shape[1:])
    fine = jax.sharding.Mesh(split, SLAB + ("img",))
    return jax.shard_map(
        on_device,
        mesh=fine,
        in_specs=(
            P(SLAB, None),
            P("img", None, None, SLAB),
            P("img", None, None),
            P("img", SLAB, None, None),
            P("img", SLAB),
            P("img", SLAB, None),
        ),
        out_specs=(P(SLAB, None), P("img", SLAB, None)),
        check_vma=False,
    )
```

```python
import functools
import math

import jax
import jax.numpy as jnp
from jax import lax
from jax.experimental import pallas as pl
from jax.experimental.pallas import tpu as pltpu
from jax.sharding import PartitionSpec as P

BOX = 256
NS = 16
SLAB = ("sx", "sz", "sc")


wave_length = 0.0197
aberration = 27000000.0
amplitude = 0.1
grid_side = 4


def phase_tables(fourier, shifts, box):
    freq = (jnp.arange(fourier, dtype=jnp.int32) - fourier // 2).astype(jnp.float32)
    shift_steps = jnp.arange(shifts, dtype=jnp.int32)
    shift_x = (2 * (shift_steps // grid_side) - (grid_side - 1)).astype(jnp.float32)
    shift_y = (2 * (shift_steps % grid_side) - (grid_side - 1)).astype(jnp.float32)
    angle = 2.0 * math.pi / box * (freq[:, None, None] * shift_x + freq[None, :, None] * shift_y)
    forward = jnp.stack([jnp.cos(angle), jnp.sin(angle)], axis=1).reshape(
        2 * fourier * fourier, shifts
    )
    backward = jnp.stack([jnp.cos(angle), -jnp.sin(angle)], axis=1).reshape(
        2 * fourier * fourier, shifts
    )
    return (forward.astype(jnp.bfloat16), backward.T.astype(jnp.bfloat16))


def contrast(defocus_blk, fourier, box):
    freq = (jnp.arange(fourier, dtype=jnp.int32) - fourier // 2).astype(jnp.float32)
    wave_sq = (freq[:, None] * freq[:, None] + freq[None, :] * freq[None, :]) / (box * box)
    phase = math.pi * wave_length * defocus_blk[:, None, None] * wave_sq
    phase = phase - 0.5 * math.pi * aberration * wave_length**3 * wave_sq * wave_sq
    return -(math.sqrt(1.0 - amplitude * amplitude) * jnp.sin(phase) + amplitude * jnp.cos(phase))


def correlate(panels, image_blk, list_blk, defocus_blk, phase_fwd, phase_back, box):
    count = image_blk.shape[0]
    fourier = image_blk.shape[1]
    picks = list_blk.shape[1]
    shifts = phase_fwd.shape[1]
    ctf = contrast(defocus_blk, fourier, box)
    weighted = ctf[:, :, None, :] * image_blk.astype(jnp.float32).reshape(
        count, fourier, 2, fourier
    )
    real_u = weighted[:, None, :, 0]
    imag_u = weighted[:, None, :, 1]
    chosen = panels[list_blk].astype(jnp.float32).reshape(count, picks, fourier, 2, fourier)
    real_p = chosen[:, :, :, 0]
    imag_p = chosen[:, :, :, 1]
    product = jnp.stack(
        [real_p * real_u + imag_p * imag_u, real_p * imag_u - imag_p * real_u], axis=3
    )
    product = product.astype(jnp.bfloat16).reshape(count * picks, 2 * fourier * fourier)
    scores = jnp.dot(product, phase_fwd, preferred_element_type=jnp.float32) / fourier
    scores = scores.reshape(count, picks * shifts)
    squared = scores * scores
    weights = squared / (jnp.mean(squared, axis=1, keepdims=True) + 1e-05)
    rounded = weights.astype(jnp.bfloat16).reshape(count * picks, shifts)
    spread = jnp.dot(rounded, phase_back, preferred_element_type=jnp.float32)
    spread = spread.reshape(count, picks, fourier, 2, fourier)
    real_e = spread[:, :, :, 0]
    imag_e = spread[:, :, :, 1]
    backed = jnp.stack(
        [real_u * real_e - imag_u * imag_e, real_u * imag_e + imag_u * real_e], axis=3
    )
    backed = backed.astype(jnp.bfloat16).reshape(count * picks, 2 * fourier * fourier)
    return (weights, backed)


def _correlate_kernel(orient_ref, row_ref, panels_ref, image_ref, ctf_ref, cos_ref, sin_ref, w_ref, out_ref, acc_ref):
    i = pl.program_id(0)
    mirror = cos_ref.shape[0]
    shifts = 2 * mirror
    picks = w_ref.shape[1] // shifts
    half = ctf_ref.shape[2]

    @pl.when(i == 0)
    def _():
        acc_ref[...] = jnp.zeros_like(acc_ref)

    ctf = ctf_ref[0]
    image = image_ref[0].astype(jnp.float32)
    ur = ctf * image[:, :half]
    ui = ctf * image[:, half:]
    rows = []
    for k in range(picks):
        panel = panels_ref[row_ref[i * picks + k]].astype(jnp.float32)
        pr = panel[:, :half]
        pi = panel[:, half:]
        prod_re = (pr * ur + pi * ui).astype(jnp.bfloat16).astype(jnp.float32)
        prod_im = (pr * ui - pi * ur).astype(jnp.bfloat16).astype(jnp.float32)
        even = []
        odd = []
        for t in range(mirror):
            even.append(jnp.sum(prod_re * cos_ref[t], axis=0, keepdims=True))
            odd.append(jnp.sum(prod_im * sin_ref[t], axis=0, keepdims=True))
        rows.extend(even[t] + odd[t] for t in range(mirror))
        rows.extend(even[shifts - 1 - t] - odd[shifts - 1 - t] for t in range(mirror, shifts))
    scores = jnp.sum(jnp.concatenate(rows, axis=0), axis=1, keepdims=True) / half
    squared = scores * scores
    mean = jnp.sum(squared, axis=0, keepdims=True) / squared.shape[0]
    weights = squared / (mean + 1e-05)
    w_ref[0] = weights
    wround = weights.astype(jnp.bfloat16).astype(jnp.float32)
    for k in range(picks):
        er = jnp.zeros_like(ur)
        ei = jnp.zeros_like(ur)
        for t in range(mirror):
            wt = wround[k * shifts + t : k * shifts + t + 1, :]
            wm = wround[k * shifts + shifts - 1 - t : k * shifts + shifts - t, :]
            er = er + (wt + wm) * cos_ref[t]
            ei = ei - (wt - wm) * sin_ref[t]
        slice_re = (ur * er - ui * ei).astype(jnp.bfloat16).astype(jnp.float32)
        slice_im = (ur * ei + ui * er).astype(jnp.bfloat16).astype(jnp.float32)
        j = row_ref[i * picks + k]
        acc_ref[j, :, :half] += slice_re
        acc_ref[j, :, half:] += slice_im

    @pl.when(i == pl.num_programs(0) - 1)
    def _():
        out_ref[...] = acc_ref[...].astype(out_ref.dtype)


def correlate_all(panels, images, orient, rows, defocus):
    count, fourier, width = images.shape
    picks = orient.shape[1]
    orient_count = panels.shape[0]
    ctf = contrast(defocus, fourier, BOX)
    freq = (jnp.arange(fourier, dtype=jnp.int32) - fourier // 2).astype(jnp.float32)
    shift_steps = jnp.arange(NS // 2, dtype=jnp.int32)
    shift_x = (2 * (shift_steps // grid_side) - (grid_side - 1)).astype(jnp.float32)
    shift_y = (2 * (shift_steps % grid_side) - (grid_side - 1)).astype(jnp.float32)
    angle = 2.0 * math.pi / BOX * (
        freq[None, :, None] * shift_x[:, None, None] + freq[None, None, :] * shift_y[:, None, None]
    )
    cos_t = jnp.cos(angle).astype(jnp.bfloat16).astype(jnp.float32)
    sin_t = jnp.sin(angle).astype(jnp.bfloat16).astype(jnp.float32)
    grid_spec = pltpu.PrefetchScalarGridSpec(
        num_scalar_prefetch=2,
        grid=(count,),
        in_specs=[
            pl.BlockSpec((orient_count, fourier, width), lambda i, o, w: (0, 0, 0)),
            pl.BlockSpec((1, fourier, width), lambda i, o, w: (i, 0, 0)),
            pl.BlockSpec((1, fourier, fourier), lambda i, o, w: (i, 0, 0)),
            pl.BlockSpec((NS // 2, fourier, fourier), lambda i, o, w: (0, 0, 0)),
            pl.BlockSpec((NS // 2, fourier, fourier), lambda i, o, w: (0, 0, 0)),
        ],
        out_specs=[
            pl.BlockSpec((1, picks * NS, 1), lambda i, o, w: (i, 0, 0)),
            pl.BlockSpec((orient_count, fourier, width), lambda i, o, w: (0, 0, 0)),
        ],
        scratch_shapes=[pltpu.VMEM((orient_count, fourier, width), jnp.float32)],
    )
    weights, contrib = pl.pallas_call(
        _correlate_kernel,
        grid_spec=grid_spec,
        out_shape=[
            jax.ShapeDtypeStruct((count, picks * NS, 1), jnp.float32),
            jax.ShapeDtypeStruct((orient_count, fourier, width), jnp.bfloat16),
        ],
        compiler_params=pltpu.CompilerParams(
            dimension_semantics=("arbitrary",), vmem_limit_bytes=56 * 1024 * 1024
        ),
    )(orient.reshape(-1), rows.reshape(-1), panels, images, ctf, cos_t, sin_t)
    return weights.reshape(count, picks * NS), contrib


def _pair_sum_kernel(x_ref, o_ref, own, recv, send_sem, recv_sem, local_sem):
    half = own.shape[0]
    me = lax.axis_index(SLAB[2])
    mate = 1 - me
    where = (lax.axis_index(SLAB[0]), lax.axis_index(SLAB[1]), mate, lax.axis_index("img"))
    mesh_ids = pl.DeviceIdType.MESH
    barrier = pltpu.get_barrier_semaphore()
    pl.semaphore_signal(barrier, inc=1, device_id=where, device_id_type=mesh_ids)
    pl.semaphore_wait(barrier, 1)
    local = pltpu.make_async_copy(x_ref.at[pl.ds(me * half, half)], own, local_sem)
    local.start()
    copy = pltpu.make_async_remote_copy(
        src_ref=x_ref.at[pl.ds(mate * half, half)], dst_ref=recv, send_sem=send_sem,
        recv_sem=recv_sem, device_id=where, device_id_type=mesh_ids,
    )
    copy.start()
    local.wait()
    copy.wait()

    def add(b, carry):
        o_ref[b] = (own[b].astype(jnp.float32) + recv[b].astype(jnp.float32)).astype(o_ref.dtype)
        return carry

    lax.fori_loop(0, half, add, 0)


def pair_sum(x, cid):
    half = x.shape[0] // 2
    return pl.pallas_call(
        _pair_sum_kernel,
        out_shape=jax.ShapeDtypeStruct((half,) + x.shape[1:], x.dtype),
        in_specs=[pl.BlockSpec(memory_space=pl.ANY)],
        out_specs=pl.BlockSpec(memory_space=pltpu.VMEM),
        scratch_shapes=[
            pltpu.VMEM((half,) + x.shape[1:], x.dtype),
            pltpu.VMEM((half,) + x.shape[1:], x.dtype),
            pltpu.SemaphoreType.DMA,
            pltpu.SemaphoreType.DMA,
            pltpu.SemaphoreType.DMA,
        ],
        compiler_params=pltpu.CompilerParams(
            collective_id=cid, has_side_effects=True, vmem_limit_bytes=48 * 1024 * 1024
        ),
    )(x)


def _axis_sum_kernel(axis, x_ref, o_ref, got, send_sems, recv_sems, local_sem):
    count, chunk = got.shape[0], got.shape[1]
    me = lax.axis_index(axis)
    names = SLAB + ("img",)
    coords = [lax.axis_index(a) for a in names]
    at = names.index(axis)
    mesh_ids = pl.DeviceIdType.MESH
    peers = [lax.rem(me + 1 + i, count) for i in range(count - 1)]

    def where(peer):
        return tuple(coords[:at]) + (peer,) + tuple(coords[at + 1:])

    barrier = pltpu.get_barrier_semaphore()
    for peer in peers:
        pl.semaphore_signal(barrier, inc=1, device_id=where(peer), device_id_type=mesh_ids)
    pl.semaphore_wait(barrier, count - 1)

    def part(p):
        return x_ref.at[pl.ds(p * chunk, chunk)]

    local = pltpu.make_async_copy(part(me), got.at[me], local_sem)
    local.start()
    sends = []
    for i, peer in enumerate(peers):
        copy = pltpu.make_async_remote_copy(
            src_ref=part(peer), dst_ref=got.at[me], send_sem=send_sems.at[i], recv_sem=recv_sems.at[me],
            device_id=where(peer), device_id_type=mesh_ids,
        )
        copy.start()
        sends.append(copy)
    for i, peer in enumerate(peers):
        sends[i].wait_send()
        pltpu.make_async_remote_copy(
            src_ref=part(peer), dst_ref=got.at[peer], send_sem=send_sems.at[i], recv_sem=recv_sems.at[peer],
            device_id=where(peer), device_id_type=mesh_ids,
        ).wait_recv()
    local.wait()

    def add(b, carry):
        total = got[0, b].astype(jnp.float32)
        for p in range(1, count):
            total = total + got[p, b].astype(jnp.float32)
        o_ref[b] = total.astype(o_ref.dtype)
        return carry

    lax.fori_loop(0, chunk, add, 0)


def axis_sum(x, axis, cid):
    count = lax.axis_size(axis)
    chunk = x.shape[0] // count
    return pl.pallas_call(
        functools.partial(_axis_sum_kernel, axis),
        out_shape=jax.ShapeDtypeStruct((chunk,) + x.shape[1:], x.dtype),
        in_specs=[pl.BlockSpec(memory_space=pl.ANY)],
        out_specs=pl.BlockSpec(memory_space=pltpu.VMEM),
        scratch_shapes=[
            pltpu.VMEM((count, chunk) + x.shape[1:], x.dtype),
            pltpu.SemaphoreType.DMA((count,)),
            pltpu.SemaphoreType.DMA((count,)),
            pltpu.SemaphoreType.DMA,
        ],
        compiler_params=pltpu.CompilerParams(
            collective_id=cid, has_side_effects=True, vmem_limit_bytes=48 * 1024 * 1024
        ),
    )(x)


def _axis_gather_kernel(axis, x_ref, o_ref, send_sems, recv_sems, local_sem):
    count = o_ref.shape[0]
    me = lax.axis_index(axis)
    names = SLAB + ("img",)
    coords = [lax.axis_index(a) for a in names]
    at = names.index(axis)
    mesh_ids = pl.DeviceIdType.MESH
    peers = [lax.rem(me + 1 + i, count) for i in range(count - 1)]

    def where(peer):
        return tuple(coords[:at]) + (peer,) + tuple(coords[at + 1:])

    barrier = pltpu.get_barrier_semaphore()
    for peer in peers:
        pl.semaphore_signal(barrier, inc=1, device_id=where(peer), device_id_type=mesh_ids)
    pl.semaphore_wait(barrier, count - 1)
    local = pltpu.make_async_copy(x_ref, o_ref.at[me], local_sem)
    local.start()
    sends = []
    for i, peer in enumerate(peers):
        copy = pltpu.make_async_remote_copy(
            src_ref=x_ref, dst_ref=o_ref.at[me], send_sem=send_sems.at[i], recv_sem=recv_sems.at[me],
            device_id=where(peer), device_id_type=mesh_ids,
        )
        copy.start()
        sends.append(copy)
    for i, peer in enumerate(peers):
        sends[i].wait_send()
        pltpu.make_async_remote_copy(
            src_ref=x_ref, dst_ref=o_ref.at[peer], send_sem=send_sems.at[i], recv_sem=recv_sems.at[peer],
            device_id=where(peer), device_id_type=mesh_ids,
        ).wait_recv()
    local.wait()


def axis_gather(x, axis, cid):
    count = lax.axis_size(axis)
    out = pl.pallas_call(
        functools.partial(_axis_gather_kernel, axis),
        out_shape=jax.ShapeDtypeStruct((count,) + x.shape, x.dtype),
        in_specs=[pl.BlockSpec(memory_space=pl.ANY)],
        out_specs=pl.BlockSpec(memory_space=pl.ANY),
        scratch_shapes=[
            pltpu.SemaphoreType.DMA((count,)),
            pltpu.SemaphoreType.DMA((count,)),
            pltpu.SemaphoreType.DMA,
        ],
        compiler_params=pltpu.CompilerParams(collective_id=cid, has_side_effects=True),
    )(x)
    return out.reshape((-1,) + x.shape[1:])


def _img_sum_kernel(x_ref, o_ref, gat, qbuf, s1, r1, s2, r2, l1, l2):
    count, rows = gat.shape[0], gat.shape[1]
    me = lax.axis_index("img")
    here = tuple(lax.axis_index(a) for a in SLAB)
    mesh_ids = pl.DeviceIdType.MESH
    barrier = pltpu.get_barrier_semaphore()
    peers = [lax.rem(me + 1 + i, count) for i in range(count - 1)]
    for peer in peers:
        pl.semaphore_signal(barrier, inc=1, device_id=here + (peer,), device_id_type=mesh_ids)
    pl.semaphore_wait(barrier, count - 1)

    def part(p):
        return x_ref.at[pl.ds(pl.multiple_of(p * rows, rows), rows)]

    local = pltpu.make_async_copy(part(me), gat.at[me], l1)
    local.start()
    sends = []
    for i, peer in enumerate(peers):
        copy = pltpu.make_async_remote_copy(
            src_ref=part(peer), dst_ref=gat.at[me], send_sem=s1.at[i], recv_sem=r1.at[me],
            device_id=here + (peer,), device_id_type=mesh_ids,
        )
        copy.start()
        sends.append(copy)
    for i, peer in enumerate(peers):
        sends[i].wait_send()
        pltpu.make_async_remote_copy(
            src_ref=part(peer), dst_ref=gat.at[peer], send_sem=s1.at[i], recv_sem=r1.at[peer],
            device_id=here + (peer,), device_id_type=mesh_ids,
        ).wait_recv()
    local.wait()
    qbuf[...] = jnp.sum(gat[...], axis=0)
    local = pltpu.make_async_copy(qbuf, o_ref.at[me], l2)
    local.start()
    sends = []
    for i, peer in enumerate(peers):
        copy = pltpu.make_async_remote_copy(
            src_ref=qbuf, dst_ref=o_ref.at[me], send_sem=s2.at[i], recv_sem=r2.at[me],
            device_id=here + (peer,), device_id_type=mesh_ids,
        )
        copy.start()
        sends.append(copy)
    for i, peer in enumerate(peers):
        sends[i].wait_send()
        pltpu.make_async_remote_copy(
            src_ref=qbuf, dst_ref=o_ref.at[peer], send_sem=s2.at[i], recv_sem=r2.at[peer],
            device_id=here + (peer,), device_id_type=mesh_ids,
        ).wait_recv()
    local.wait()


def img_sum(x, count, cid):
    rows = x.shape[0] // count
    out = pl.pallas_call(
        _img_sum_kernel,
        out_shape=jax.ShapeDtypeStruct((count, rows) + x.shape[1:], x.dtype),
        in_specs=[pl.BlockSpec(memory_space=pltpu.VMEM)],
        out_specs=pl.BlockSpec(memory_space=pl.ANY),
        scratch_shapes=[
            pltpu.VMEM((count, rows) + x.shape[1:], x.dtype),
            pltpu.VMEM((rows,) + x.shape[1:], x.dtype),
            pltpu.SemaphoreType.DMA((count,)),
            pltpu.SemaphoreType.DMA((count,)),
            pltpu.SemaphoreType.DMA((count,)),
            pltpu.SemaphoreType.DMA((count,)),
            pltpu.SemaphoreType.DMA,
            pltpu.SemaphoreType.DMA,
        ],
        compiler_params=pltpu.CompilerParams(collective_id=cid, has_side_effects=True),
    )(x)
    return out.reshape(x.shape)


def _a2a_kernel(x_ref, o_ref, send_sems, recv_sems, local_sem):
    count = x_ref.shape[0]
    sizes = tuple(lax.axis_size(a) for a in SLAB)
    me = lax.axis_index(SLAB)
    grp = lax.axis_index("img")
    mesh_ids = pl.DeviceIdType.MESH
    barrier = pltpu.get_barrier_semaphore()

    def where(peer):
        return (peer // (sizes[1] * sizes[2]), (peer // sizes[2]) % sizes[1], peer % sizes[2], grp)

    def greet(i, carry):
        pl.semaphore_signal(
            barrier, inc=1, device_id=where(lax.rem(me + 1 + i, count)), device_id_type=mesh_ids
        )
        return carry

    lax.fori_loop(0, count - 1, greet, 0)
    pl.semaphore_wait(barrier, count - 1)
    local = pltpu.make_async_copy(x_ref.at[me], o_ref.at[me], local_sem)
    local.start()

    def outgoing(peer):
        return pltpu.make_async_remote_copy(
            src_ref=x_ref.at[peer],
            dst_ref=o_ref.at[me],
            send_sem=send_sems.at[peer],
            recv_sem=recv_sems.at[me],
            device_id=where(peer),
            device_id_type=mesh_ids,
        )

    def incoming(src):
        return pltpu.make_async_remote_copy(
            src_ref=x_ref.at[src],
            dst_ref=o_ref.at[src],
            send_sem=send_sems.at[src],
            recv_sem=recv_sems.at[src],
            device_id=where(src),
            device_id_type=mesh_ids,
        )

    def send(i, carry):
        outgoing(lax.rem(me + 1 + i, count)).start()
        return carry

    lax.fori_loop(0, count - 1, send, 0)

    def finish(i, carry):
        outgoing(lax.rem(me + 1 + i, count)).wait_send()
        incoming(lax.rem(me + count - 1 - i, count)).wait_recv()
        return carry

    lax.fori_loop(0, count - 1, finish, 0)
    local.wait()


def slab_all_to_all(x, cid):
    count = x.shape[0]
    return pl.pallas_call(
        _a2a_kernel,
        out_shape=jax.ShapeDtypeStruct(x.shape, x.dtype),
        in_specs=[pl.BlockSpec(memory_space=pl.ANY)],
        out_specs=pl.BlockSpec(memory_space=pl.ANY),
        scratch_shapes=[
            pltpu.SemaphoreType.DMA((count,)),
            pltpu.SemaphoreType.DMA((count,)),
            pltpu.SemaphoreType.DMA,
        ],
        compiler_params=pltpu.CompilerParams(collective_id=cid, has_side_effects=True),
    )(x)


def on_device(volume, interp, block_index, images, defocus, orient):
    slab_count = lax.axis_size(SLAB)
    slab_index = lax.axis_index(SLAB)
    orient_count = interp.shape[1]
    ori_dev = orient_count // slab_count
    block_rows = interp.shape[2]
    fourier = images.shape[2]
    block_count = fourier // block_rows
    img_dev = images.shape[1]
    picks = orient.shape[2]
    levels = jnp.arange(block_count, dtype=jnp.int32)
    partial_value = jnp.einsum("jpr,rx->jpx", interp[0], volume, preferred_element_type=jnp.float32)
    owned_idx = lax.dynamic_slice_in_dim(block_index[0], slab_index * ori_dev, ori_dev, 0)
    received = slab_all_to_all(
        partial_value.reshape(slab_count, ori_dev * block_rows, 2 * fourier), 1
    ).reshape(slab_count, ori_dev, block_rows, 2 * fourier)
    place = (owned_idx[:, :, None] == levels).astype(jnp.float32)
    summed = jnp.einsum(
        "osb,sopx->obpx", place, received, precision=lax.Precision.HIGHEST,
        preferred_element_type=jnp.float32,
    ).reshape(ori_dev, fourier, 2 * fourier)
    panels = summed.astype(jnp.bfloat16)
    panels = axis_gather(panels, SLAB[1], 5)
    for axis in (SLAB[0], SLAB[2]):
        parts = lax.axis_size(axis)
        panels = lax.all_to_all(
            jnp.broadcast_to(panels[None], (parts,) + panels.shape),
            axis, split_axis=0, concat_axis=0, tiled=True,
        ).reshape((-1,) + panels.shape[1:])
    sizes = tuple(lax.axis_size(a) for a in SLAB)
    inv_perm = jnp.arange(orient_count, dtype=jnp.int32).reshape(
        (sizes[2], sizes[0], sizes[1], ori_dev)
    ).transpose(1, 2, 0, 3).reshape(-1)
    weights, contrib = correlate_all(panels, images[0], orient[0], inv_perm[orient[0]], defocus[0])
    contrib = pair_sum(contrib, 2)
    contrib = axis_sum(contrib, SLAB[0], 3)
    back_own = axis_sum(contrib, SLAB[1], 4)
    back_own = back_own.reshape(ori_dev, block_count, block_rows, 2 * fourier)
    chosen_back = (owned_idx[:, :, None] == levels).astype(jnp.bfloat16)
    outgoing = jnp.einsum(
        "osb,obpx->sopx", chosen_back, back_own, preferred_element_type=jnp.float32
    )
    outgoing = outgoing.astype(jnp.bfloat16).reshape(slab_count * ori_dev, block_rows, 2 * fourier)
    incoming = slab_all_to_all(outgoing, 8)
    column = jnp.einsum("jpr,jpx->rx", interp[0], incoming, preferred_element_type=jnp.float32)
    summed_cols = img_sum(column, lax.axis_size("img"), 0)
    update = summed_cols / math.sqrt(img_dev * slab_count)
    return (update, weights[None])


def solution(mesh):
    devices = mesh.devices
    cores = 2
    xs = len({d.coords[0] for d in devices.reshape(-1)}) if hasattr(devices.reshape(-1)[0], "coords") else 4
    split = devices.reshape((xs, devices.shape[0] // (xs * cores), cores) + devices.shape[1:])
    fine = jax.sharding.Mesh(split, SLAB + ("img",))
    return jax.shard_map(
        on_device,
        mesh=fine,
        in_specs=(
            P(SLAB, None),
            P("img", None, None, SLAB),
            P("img", None, None),
            P("img", SLAB, None, None),
            P("img", SLAB),
            P("img", SLAB, None),
        ),
        out_specs=(P(SLAB, None), P("img", SLAB, None)),
        check_vma=False,
    )
```

```python
import functools
import math

import jax
import jax.numpy as jnp
from jax import lax
from jax.experimental import pallas as pl
from jax.experimental.pallas import tpu as pltpu
from jax.sharding import PartitionSpec as P

BOX = 256
NS = 16
SLAB = ("sx", "sz", "sc")


wave_length = 0.0197
aberration = 27000000.0
amplitude = 0.1
grid_side = 4


def phase_tables(fourier, shifts, box):
    freq = (jnp.arange(fourier, dtype=jnp.int32) - fourier // 2).astype(jnp.float32)
    shift_steps = jnp.arange(shifts, dtype=jnp.int32)
    shift_x = (2 * (shift_steps // grid_side) - (grid_side - 1)).astype(jnp.float32)
    shift_y = (2 * (shift_steps % grid_side) - (grid_side - 1)).astype(jnp.float32)
    angle = 2.0 * math.pi / box * (freq[:, None, None] * shift_x + freq[None, :, None] * shift_y)
    forward = jnp.stack([jnp.cos(angle), jnp.sin(angle)], axis=1).reshape(
        2 * fourier * fourier, shifts
    )
    backward = jnp.stack([jnp.cos(angle), -jnp.sin(angle)], axis=1).reshape(
        2 * fourier * fourier, shifts
    )
    return (forward.astype(jnp.bfloat16), backward.T.astype(jnp.bfloat16))


def contrast(defocus_blk, fourier, box):
    freq = (jnp.arange(fourier, dtype=jnp.int32) - fourier // 2).astype(jnp.float32)
    wave_sq = (freq[:, None] * freq[:, None] + freq[None, :] * freq[None, :]) / (box * box)
    phase = math.pi * wave_length * defocus_blk[:, None, None] * wave_sq
    phase = phase - 0.5 * math.pi * aberration * wave_length**3 * wave_sq * wave_sq
    return -(math.sqrt(1.0 - amplitude * amplitude) * jnp.sin(phase) + amplitude * jnp.cos(phase))


def correlate(panels, image_blk, list_blk, defocus_blk, phase_fwd, phase_back, box):
    count = image_blk.shape[0]
    fourier = image_blk.shape[1]
    picks = list_blk.shape[1]
    shifts = phase_fwd.shape[1]
    ctf = contrast(defocus_blk, fourier, box)
    weighted = ctf[:, :, None, :] * image_blk.astype(jnp.float32).reshape(
        count, fourier, 2, fourier
    )
    real_u = weighted[:, None, :, 0]
    imag_u = weighted[:, None, :, 1]
    chosen = panels[list_blk].astype(jnp.float32).reshape(count, picks, fourier, 2, fourier)
    real_p = chosen[:, :, :, 0]
    imag_p = chosen[:, :, :, 1]
    product = jnp.stack(
        [real_p * real_u + imag_p * imag_u, real_p * imag_u - imag_p * real_u], axis=3
    )
    product = product.astype(jnp.bfloat16).reshape(count * picks, 2 * fourier * fourier)
    scores = jnp.dot(product, phase_fwd, preferred_element_type=jnp.float32) / fourier
    scores = scores.reshape(count, picks * shifts)
    squared = scores * scores
    weights = squared / (jnp.mean(squared, axis=1, keepdims=True) + 1e-05)
    rounded = weights.astype(jnp.bfloat16).reshape(count * picks, shifts)
    spread = jnp.dot(rounded, phase_back, preferred_element_type=jnp.float32)
    spread = spread.reshape(count, picks, fourier, 2, fourier)
    real_e = spread[:, :, :, 0]
    imag_e = spread[:, :, :, 1]
    backed = jnp.stack(
        [real_u * real_e - imag_u * imag_e, real_u * imag_e + imag_u * real_e], axis=3
    )
    backed = backed.astype(jnp.bfloat16).reshape(count * picks, 2 * fourier * fourier)
    return (weights, backed)


def _correlate_kernel(orient_ref, row_ref, panels_ref, image_ref, ctf_ref, cos_ref, sin_ref, w_ref, out_ref, acc_ref):
    i = pl.program_id(0)
    mirror = cos_ref.shape[0]
    shifts = 2 * mirror
    picks = w_ref.shape[1] // shifts
    half = ctf_ref.shape[2]

    @pl.when(i == 0)
    def _():
        acc_ref[...] = jnp.zeros_like(acc_ref)

    ctf = ctf_ref[0]
    image = image_ref[0].astype(jnp.float32)
    ur = ctf * image[:, :half]
    ui = ctf * image[:, half:]
    rows = []
    for k in range(picks):
        panel = panels_ref[row_ref[i * picks + k]].astype(jnp.float32)
        pr = panel[:, :half]
        pi = panel[:, half:]
        prod_re = (pr * ur + pi * ui).astype(jnp.bfloat16).astype(jnp.float32)
        prod_im = (pr * ui - pi * ur).astype(jnp.bfloat16).astype(jnp.float32)
        even = []
        odd = []
        for t in range(mirror):
            even.append(jnp.sum(prod_re * cos_ref[t], axis=0, keepdims=True))
            odd.append(jnp.sum(prod_im * sin_ref[t], axis=0, keepdims=True))
        rows.extend(even[t] + odd[t] for t in range(mirror))
        rows.extend(even[shifts - 1 - t] - odd[shifts - 1 - t] for t in range(mirror, shifts))
    scores = jnp.sum(jnp.concatenate(rows, axis=0), axis=1, keepdims=True) / half
    squared = scores * scores
    mean = jnp.sum(squared, axis=0, keepdims=True) / squared.shape[0]
    weights = squared / (mean + 1e-05)
    w_ref[0] = weights
    wround = weights.astype(jnp.bfloat16).astype(jnp.float32)
    for k in range(picks):
        er = jnp.zeros_like(ur)
        ei = jnp.zeros_like(ur)
        for t in range(mirror):
            wt = wround[k * shifts + t : k * shifts + t + 1, :]
            wm = wround[k * shifts + shifts - 1 - t : k * shifts + shifts - t, :]
            er = er + (wt + wm) * cos_ref[t]
            ei = ei - (wt - wm) * sin_ref[t]
        slice_re = (ur * er - ui * ei).astype(jnp.bfloat16).astype(jnp.float32)
        slice_im = (ur * ei + ui * er).astype(jnp.bfloat16).astype(jnp.float32)
        j = row_ref[i * picks + k]
        acc_ref[j, :, :half] += slice_re
        acc_ref[j, :, half:] += slice_im

    @pl.when(i == pl.num_programs(0) - 1)
    def _():
        out_ref[...] = acc_ref[...].astype(out_ref.dtype)


def correlate_all(panels, images, orient, rows, defocus):
    count, fourier, width = images.shape
    picks = orient.shape[1]
    orient_count = panels.shape[0]
    ctf = contrast(defocus, fourier, BOX)
    freq = (jnp.arange(fourier, dtype=jnp.int32) - fourier // 2).astype(jnp.float32)
    shift_steps = jnp.arange(NS // 2, dtype=jnp.int32)
    shift_x = (2 * (shift_steps // grid_side) - (grid_side - 1)).astype(jnp.float32)
    shift_y = (2 * (shift_steps % grid_side) - (grid_side - 1)).astype(jnp.float32)
    angle = 2.0 * math.pi / BOX * (
        freq[None, :, None] * shift_x[:, None, None] + freq[None, None, :] * shift_y[:, None, None]
    )
    cos_t = jnp.cos(angle).astype(jnp.bfloat16).astype(jnp.float32)
    sin_t = jnp.sin(angle).astype(jnp.bfloat16).astype(jnp.float32)
    grid_spec = pltpu.PrefetchScalarGridSpec(
        num_scalar_prefetch=2,
        grid=(count,),
        in_specs=[
            pl.BlockSpec((orient_count, fourier, width), lambda i, o, w: (0, 0, 0)),
            pl.BlockSpec((1, fourier, width), lambda i, o, w: (i, 0, 0)),
            pl.BlockSpec((1, fourier, fourier), lambda i, o, w: (i, 0, 0)),
            pl.BlockSpec((NS // 2, fourier, fourier), lambda i, o, w: (0, 0, 0)),
            pl.BlockSpec((NS // 2, fourier, fourier), lambda i, o, w: (0, 0, 0)),
        ],
        out_specs=[
            pl.BlockSpec((1, picks * NS, 1), lambda i, o, w: (i, 0, 0)),
            pl.BlockSpec((orient_count, fourier, width), lambda i, o, w: (0, 0, 0)),
        ],
        scratch_shapes=[pltpu.VMEM((orient_count, fourier, width), jnp.float32)],
    )
    weights, contrib = pl.pallas_call(
        _correlate_kernel,
        grid_spec=grid_spec,
        out_shape=[
            jax.ShapeDtypeStruct((count, picks * NS, 1), jnp.float32),
            jax.ShapeDtypeStruct((orient_count, fourier, width), jnp.bfloat16),
        ],
        compiler_params=pltpu.CompilerParams(
            dimension_semantics=("arbitrary",), vmem_limit_bytes=56 * 1024 * 1024
        ),
    )(orient.reshape(-1), rows.reshape(-1), panels, images, ctf, cos_t, sin_t)
    return weights.reshape(count, picks * NS), contrib


def _pair_sum_kernel(x_ref, o_ref, own, recv, send_sem, recv_sem, local_sem):
    half = own.shape[0]
    me = lax.axis_index(SLAB[2])
    mate = 1 - me
    where = (lax.axis_index(SLAB[0]), lax.axis_index(SLAB[1]), mate, lax.axis_index("img"))
    mesh_ids = pl.DeviceIdType.MESH
    barrier = pltpu.get_barrier_semaphore()
    pl.semaphore_signal(barrier, inc=1, device_id=where, device_id_type=mesh_ids)
    pl.semaphore_wait(barrier, 1)
    local = pltpu.make_async_copy(x_ref.at[pl.ds(me * half, half)], own, local_sem)
    local.start()
    copy = pltpu.make_async_remote_copy(
        src_ref=x_ref.at[pl.ds(mate * half, half)], dst_ref=recv, send_sem=send_sem,
        recv_sem=recv_sem, device_id=where, device_id_type=mesh_ids,
    )
    copy.start()
    local.wait()
    copy.wait()

    def add(b, carry):
        o_ref[b] = (own[b].astype(jnp.float32) + recv[b].astype(jnp.float32)).astype(o_ref.dtype)
        return carry

    lax.fori_loop(0, half, add, 0)


def pair_sum(x, cid):
    half = x.shape[0] // 2
    return pl.pallas_call(
        _pair_sum_kernel,
        out_shape=jax.ShapeDtypeStruct((half,) + x.shape[1:], x.dtype),
        in_specs=[pl.BlockSpec(memory_space=pl.ANY)],
        out_specs=pl.BlockSpec(memory_space=pltpu.VMEM),
        scratch_shapes=[
            pltpu.VMEM((half,) + x.shape[1:], x.dtype),
            pltpu.VMEM((half,) + x.shape[1:], x.dtype),
            pltpu.SemaphoreType.DMA,
            pltpu.SemaphoreType.DMA,
            pltpu.SemaphoreType.DMA,
        ],
        compiler_params=pltpu.CompilerParams(
            collective_id=cid, has_side_effects=True, vmem_limit_bytes=48 * 1024 * 1024
        ),
    )(x)


def _axis_sum_kernel(axis, x_ref, o_ref, got, send_sems, recv_sems, local_sem):
    count, chunk = got.shape[0], got.shape[1]
    me = lax.axis_index(axis)
    names = SLAB + ("img",)
    coords = [lax.axis_index(a) for a in names]
    at = names.index(axis)
    mesh_ids = pl.DeviceIdType.MESH
    peers = [lax.rem(me + 1 + i, count) for i in range(count - 1)]

    def where(peer):
        return tuple(coords[:at]) + (peer,) + tuple(coords[at + 1:])

    barrier = pltpu.get_barrier_semaphore()
    for peer in peers:
        pl.semaphore_signal(barrier, inc=1, device_id=where(peer), device_id_type=mesh_ids)
    pl.semaphore_wait(barrier, count - 1)

    def part(p):
        return x_ref.at[pl.ds(p * chunk, chunk)]

    local = pltpu.make_async_copy(part(me), got.at[me], local_sem)
    local.start()
    sends = []
    for i, peer in enumerate(peers):
        copy = pltpu.make_async_remote_copy(
            src_ref=part(peer), dst_ref=got.at[me], send_sem=send_sems.at[i], recv_sem=recv_sems.at[me],
            device_id=where(peer), device_id_type=mesh_ids,
        )
        copy.start()
        sends.append(copy)
    for i, peer in enumerate(peers):
        sends[i].wait_send()
        pltpu.make_async_remote_copy(
            src_ref=part(peer), dst_ref=got.at[peer], send_sem=send_sems.at[i], recv_sem=recv_sems.at[peer],
            device_id=where(peer), device_id_type=mesh_ids,
        ).wait_recv()
    local.wait()

    def add(b, carry):
        total = got[0, b].astype(jnp.float32)
        for p in range(1, count):
            total = total + got[p, b].astype(jnp.float32)
        o_ref[b] = total.astype(o_ref.dtype)
        return carry

    lax.fori_loop(0, chunk, add, 0)


def axis_sum(x, axis, cid):
    count = lax.axis_size(axis)
    chunk = x.shape[0] // count
    return pl.pallas_call(
        functools.partial(_axis_sum_kernel, axis),
        out_shape=jax.ShapeDtypeStruct((chunk,) + x.shape[1:], x.dtype),
        in_specs=[pl.BlockSpec(memory_space=pl.ANY)],
        out_specs=pl.BlockSpec(memory_space=pltpu.VMEM),
        scratch_shapes=[
            pltpu.VMEM((count, chunk) + x.shape[1:], x.dtype),
            pltpu.SemaphoreType.DMA((count,)),
            pltpu.SemaphoreType.DMA((count,)),
            pltpu.SemaphoreType.DMA,
        ],
        compiler_params=pltpu.CompilerParams(
            collective_id=cid, has_side_effects=True, vmem_limit_bytes=48 * 1024 * 1024
        ),
    )(x)


def _axis_gather_kernel(axis, x_ref, o_ref, send_sems, recv_sems, local_sem):
    count = o_ref.shape[0]
    me = lax.axis_index(axis)
    names = SLAB + ("img",)
    coords = [lax.axis_index(a) for a in names]
    at = names.index(axis)
    mesh_ids = pl.DeviceIdType.MESH
    peers = [lax.rem(me + 1 + i, count) for i in range(count - 1)]

    def where(peer):
        return tuple(coords[:at]) + (peer,) + tuple(coords[at + 1:])

    barrier = pltpu.get_barrier_semaphore()
    for peer in peers:
        pl.semaphore_signal(barrier, inc=1, device_id=where(peer), device_id_type=mesh_ids)
    pl.semaphore_wait(barrier, count - 1)
    local = pltpu.make_async_copy(x_ref, o_ref.at[me], local_sem)
    local.start()
    sends = []
    for i, peer in enumerate(peers):
        copy = pltpu.make_async_remote_copy(
            src_ref=x_ref, dst_ref=o_ref.at[me], send_sem=send_sems.at[i], recv_sem=recv_sems.at[me],
            device_id=where(peer), device_id_type=mesh_ids,
        )
        copy.start()
        sends.append(copy)
    for i, peer in enumerate(peers):
        sends[i].wait_send()
        pltpu.make_async_remote_copy(
            src_ref=x_ref, dst_ref=o_ref.at[peer], send_sem=send_sems.at[i], recv_sem=recv_sems.at[peer],
            device_id=where(peer), device_id_type=mesh_ids,
        ).wait_recv()
    local.wait()


def axis_gather(x, axis, cid):
    count = lax.axis_size(axis)
    out = pl.pallas_call(
        functools.partial(_axis_gather_kernel, axis),
        out_shape=jax.ShapeDtypeStruct((count,) + x.shape, x.dtype),
        in_specs=[pl.BlockSpec(memory_space=pl.ANY)],
        out_specs=pl.BlockSpec(memory_space=pl.ANY),
        scratch_shapes=[
            pltpu.SemaphoreType.DMA((count,)),
            pltpu.SemaphoreType.DMA((count,)),
            pltpu.SemaphoreType.DMA,
        ],
        compiler_params=pltpu.CompilerParams(collective_id=cid, has_side_effects=True),
    )(x)
    return out.reshape((-1,) + x.shape[1:])


def _pair_gather_kernel(x_ref, o_ref, recv, send_sem, recv_sem, local_sem, move_sem):
    me = lax.axis_index(SLAB[2])
    mate = 1 - me
    where = (lax.axis_index(SLAB[0]), lax.axis_index(SLAB[1]), mate, lax.axis_index("img"))
    mesh_ids = pl.DeviceIdType.MESH
    barrier = pltpu.get_barrier_semaphore()
    pl.semaphore_signal(barrier, inc=1, device_id=where, device_id_type=mesh_ids)
    pl.semaphore_wait(barrier, 1)
    local = pltpu.make_async_copy(x_ref, o_ref.at[me], local_sem)
    local.start()
    copy = pltpu.make_async_remote_copy(
        src_ref=x_ref, dst_ref=recv, send_sem=send_sem,
        recv_sem=recv_sem, device_id=where, device_id_type=mesh_ids,
    )
    copy.start()
    copy.wait()
    move = pltpu.make_async_copy(recv, o_ref.at[mate], move_sem)
    move.start()
    local.wait()
    move.wait()


def pair_gather(x, cid):
    out = pl.pallas_call(
        _pair_gather_kernel,
        out_shape=jax.ShapeDtypeStruct((2,) + x.shape, x.dtype),
        in_specs=[pl.BlockSpec(memory_space=pl.ANY)],
        out_specs=pl.BlockSpec(memory_space=pltpu.VMEM),
        scratch_shapes=[
            pltpu.VMEM(x.shape, x.dtype),
            pltpu.SemaphoreType.DMA,
            pltpu.SemaphoreType.DMA,
            pltpu.SemaphoreType.DMA,
            pltpu.SemaphoreType.DMA,
        ],
        compiler_params=pltpu.CompilerParams(
            collective_id=cid, has_side_effects=True, vmem_limit_bytes=48 * 1024 * 1024
        ),
    )(x)
    return out.reshape((-1,) + x.shape[1:])


def _img_sum_kernel(x_ref, o_ref, gat, qbuf, s1, r1, s2, r2, l1, l2):
    count, rows = gat.shape[0], gat.shape[1]
    me = lax.axis_index("img")
    here = tuple(lax.axis_index(a) for a in SLAB)
    mesh_ids = pl.DeviceIdType.MESH
    barrier = pltpu.get_barrier_semaphore()
    peers = [lax.rem(me + 1 + i, count) for i in range(count - 1)]
    for peer in peers:
        pl.semaphore_signal(barrier, inc=1, device_id=here + (peer,), device_id_type=mesh_ids)
    pl.semaphore_wait(barrier, count - 1)

    def part(p):
        return x_ref.at[pl.ds(pl.multiple_of(p * rows, rows), rows)]

    local = pltpu.make_async_copy(part(me), gat.at[me], l1)
    local.start()
    sends = []
    for i, peer in enumerate(peers):
        copy = pltpu.make_async_remote_copy(
            src_ref=part(peer), dst_ref=gat.at[me], send_sem=s1.at[i], recv_sem=r1.at[me],
            device_id=here + (peer,), device_id_type=mesh_ids,
        )
        copy.start()
        sends.append(copy)
    for i, peer in enumerate(peers):
        sends[i].wait_send()
        pltpu.make_async_remote_copy(
            src_ref=part(peer), dst_ref=gat.at[peer], send_sem=s1.at[i], recv_sem=r1.at[peer],
            device_id=here + (peer,), device_id_type=mesh_ids,
        ).wait_recv()
    local.wait()
    qbuf[...] = jnp.sum(gat[...], axis=0)
    local = pltpu.make_async_copy(qbuf, o_ref.at[me], l2)
    local.start()
    sends = []
    for i, peer in enumerate(peers):
        copy = pltpu.make_async_remote_copy(
            src_ref=qbuf, dst_ref=o_ref.at[me], send_sem=s2.at[i], recv_sem=r2.at[me],
            device_id=here + (peer,), device_id_type=mesh_ids,
        )
        copy.start()
        sends.append(copy)
    for i, peer in enumerate(peers):
        sends[i].wait_send()
        pltpu.make_async_remote_copy(
            src_ref=qbuf, dst_ref=o_ref.at[peer], send_sem=s2.at[i], recv_sem=r2.at[peer],
            device_id=here + (peer,), device_id_type=mesh_ids,
        ).wait_recv()
    local.wait()


def img_sum(x, count, cid):
    rows = x.shape[0] // count
    out = pl.pallas_call(
        _img_sum_kernel,
        out_shape=jax.ShapeDtypeStruct((count, rows) + x.shape[1:], x.dtype),
        in_specs=[pl.BlockSpec(memory_space=pltpu.VMEM)],
        out_specs=pl.BlockSpec(memory_space=pl.ANY),
        scratch_shapes=[
            pltpu.VMEM((count, rows) + x.shape[1:], x.dtype),
            pltpu.VMEM((rows,) + x.shape[1:], x.dtype),
            pltpu.SemaphoreType.DMA((count,)),
            pltpu.SemaphoreType.DMA((count,)),
            pltpu.SemaphoreType.DMA((count,)),
            pltpu.SemaphoreType.DMA((count,)),
            pltpu.SemaphoreType.DMA,
            pltpu.SemaphoreType.DMA,
        ],
        compiler_params=pltpu.CompilerParams(collective_id=cid, has_side_effects=True),
    )(x)
    return out.reshape(x.shape)


def _a2a_kernel(x_ref, o_ref, send_sems, recv_sems, local_sem):
    count = x_ref.shape[0]
    sizes = tuple(lax.axis_size(a) for a in SLAB)
    me = lax.axis_index(SLAB)
    grp = lax.axis_index("img")
    mesh_ids = pl.DeviceIdType.MESH
    barrier = pltpu.get_barrier_semaphore()

    def where(peer):
        return (peer // (sizes[1] * sizes[2]), (peer // sizes[2]) % sizes[1], peer % sizes[2], grp)

    def greet(i, carry):
        pl.semaphore_signal(
            barrier, inc=1, device_id=where(lax.rem(me + 1 + i, count)), device_id_type=mesh_ids
        )
        return carry

    lax.fori_loop(0, count - 1, greet, 0)
    pl.semaphore_wait(barrier, count - 1)
    local = pltpu.make_async_copy(x_ref.at[me], o_ref.at[me], local_sem)
    local.start()

    def outgoing(peer):
        return pltpu.make_async_remote_copy(
            src_ref=x_ref.at[peer],
            dst_ref=o_ref.at[me],
            send_sem=send_sems.at[peer],
            recv_sem=recv_sems.at[me],
            device_id=where(peer),
            device_id_type=mesh_ids,
        )

    def incoming(src):
        return pltpu.make_async_remote_copy(
            src_ref=x_ref.at[src],
            dst_ref=o_ref.at[src],
            send_sem=send_sems.at[src],
            recv_sem=recv_sems.at[src],
            device_id=where(src),
            device_id_type=mesh_ids,
        )

    def send(i, carry):
        outgoing(lax.rem(me + 1 + i, count)).start()
        return carry

    lax.fori_loop(0, count - 1, send, 0)

    def finish(i, carry):
        outgoing(lax.rem(me + 1 + i, count)).wait_send()
        incoming(lax.rem(me + count - 1 - i, count)).wait_recv()
        return carry

    lax.fori_loop(0, count - 1, finish, 0)
    local.wait()


def slab_all_to_all(x, cid):
    count = x.shape[0]
    return pl.pallas_call(
        _a2a_kernel,
        out_shape=jax.ShapeDtypeStruct(x.shape, x.dtype),
        in_specs=[pl.BlockSpec(memory_space=pl.ANY)],
        out_specs=pl.BlockSpec(memory_space=pl.ANY),
        scratch_shapes=[
            pltpu.SemaphoreType.DMA((count,)),
            pltpu.SemaphoreType.DMA((count,)),
            pltpu.SemaphoreType.DMA,
        ],
        compiler_params=pltpu.CompilerParams(collective_id=cid, has_side_effects=True),
    )(x)


def on_device(volume, interp, block_index, images, defocus, orient):
    slab_count = lax.axis_size(SLAB)
    slab_index = lax.axis_index(SLAB)
    orient_count = interp.shape[1]
    ori_dev = orient_count // slab_count
    block_rows = interp.shape[2]
    fourier = images.shape[2]
    block_count = fourier // block_rows
    img_dev = images.shape[1]
    picks = orient.shape[2]
    levels = jnp.arange(block_count, dtype=jnp.int32)
    partial_value = jnp.einsum("jpr,rx->jpx", interp[0], volume, preferred_element_type=jnp.float32)
    owned_idx = lax.dynamic_slice_in_dim(block_index[0], slab_index * ori_dev, ori_dev, 0)
    received = slab_all_to_all(
        partial_value.reshape(slab_count, ori_dev * block_rows, 2 * fourier), 1
    ).reshape(slab_count, ori_dev, block_rows, 2 * fourier)
    place = (owned_idx[:, :, None] == levels).astype(jnp.float32)
    summed = jnp.einsum(
        "osb,sopx->obpx", place, received, precision=lax.Precision.HIGHEST,
        preferred_element_type=jnp.float32,
    ).reshape(ori_dev, fourier, 2 * fourier)
    panels = summed.astype(jnp.bfloat16)
    panels = axis_gather(panels, SLAB[1], 5)
    parts = lax.axis_size(SLAB[0])
    panels = lax.all_to_all(
        jnp.broadcast_to(panels[None], (parts,) + panels.shape),
        SLAB[0], split_axis=0, concat_axis=0, tiled=True,
    ).reshape((-1,) + panels.shape[1:])
    panels = pair_gather(panels, 9)
    sizes = tuple(lax.axis_size(a) for a in SLAB)
    inv_perm = jnp.arange(orient_count, dtype=jnp.int32).reshape(
        (sizes[2], sizes[0], sizes[1], ori_dev)
    ).transpose(1, 2, 0, 3).reshape(-1)
    weights, contrib = correlate_all(panels, images[0], orient[0], inv_perm[orient[0]], defocus[0])
    contrib = pair_sum(contrib, 2)
    contrib = axis_sum(contrib, SLAB[0], 3)
    back_own = axis_sum(contrib, SLAB[1], 4)
    back_own = back_own.reshape(ori_dev, block_count, block_rows, 2 * fourier)
    chosen_back = (owned_idx[:, :, None] == levels).astype(jnp.bfloat16)
    outgoing = jnp.einsum(
        "osb,obpx->sopx", chosen_back, back_own, preferred_element_type=jnp.float32
    )
    outgoing = outgoing.astype(jnp.bfloat16).reshape(slab_count * ori_dev, block_rows, 2 * fourier)
    incoming = slab_all_to_all(outgoing, 8)
    column = jnp.einsum("jpr,jpx->rx", interp[0], incoming, preferred_element_type=jnp.float32)
    summed_cols = img_sum(column, lax.axis_size("img"), 0)
    update = summed_cols / math.sqrt(img_dev * slab_count)
    return (update, weights[None])


def solution(mesh):
    devices = mesh.devices
    cores = 2
    xs = len({d.coords[0] for d in devices.reshape(-1)}) if hasattr(devices.reshape(-1)[0], "coords") else 4
    split = devices.reshape((xs, devices.shape[0] // (xs * cores), cores) + devices.shape[1:])
    fine = jax.sharding.Mesh(split, SLAB + ("img",))
    return jax.shard_map(
        on_device,
        mesh=fine,
        in_specs=(
            P(SLAB, None),
            P("img", None, None, SLAB),
            P("img", None, None),
            P("img", SLAB, None, None),
            P("img", SLAB),
            P("img", SLAB, None),
        ),
        out_specs=(P(SLAB, None), P("img", SLAB, None)),
        check_vma=False,
    )
```

```python
import functools
import math

import jax
import jax.numpy as jnp
from jax import lax
from jax.experimental import pallas as pl
from jax.experimental.pallas import tpu as pltpu
from jax.sharding import PartitionSpec as P

BOX = 256
NS = 16
SLAB = ("sx", "sz", "sc")


wave_length = 0.0197
aberration = 27000000.0
amplitude = 0.1
grid_side = 4


def phase_tables(fourier, shifts, box):
    freq = (jnp.arange(fourier, dtype=jnp.int32) - fourier // 2).astype(jnp.float32)
    shift_steps = jnp.arange(shifts, dtype=jnp.int32)
    shift_x = (2 * (shift_steps // grid_side) - (grid_side - 1)).astype(jnp.float32)
    shift_y = (2 * (shift_steps % grid_side) - (grid_side - 1)).astype(jnp.float32)
    angle = 2.0 * math.pi / box * (freq[:, None, None] * shift_x + freq[None, :, None] * shift_y)
    forward = jnp.stack([jnp.cos(angle), jnp.sin(angle)], axis=1).reshape(
        2 * fourier * fourier, shifts
    )
    backward = jnp.stack([jnp.cos(angle), -jnp.sin(angle)], axis=1).reshape(
        2 * fourier * fourier, shifts
    )
    return (forward.astype(jnp.bfloat16), backward.T.astype(jnp.bfloat16))


def contrast(defocus_blk, fourier, box):
    freq = (jnp.arange(fourier, dtype=jnp.int32) - fourier // 2).astype(jnp.float32)
    wave_sq = (freq[:, None] * freq[:, None] + freq[None, :] * freq[None, :]) / (box * box)
    phase = math.pi * wave_length * defocus_blk[:, None, None] * wave_sq
    phase = phase - 0.5 * math.pi * aberration * wave_length**3 * wave_sq * wave_sq
    return -(math.sqrt(1.0 - amplitude * amplitude) * jnp.sin(phase) + amplitude * jnp.cos(phase))


def correlate(panels, image_blk, list_blk, defocus_blk, phase_fwd, phase_back, box):
    count = image_blk.shape[0]
    fourier = image_blk.shape[1]
    picks = list_blk.shape[1]
    shifts = phase_fwd.shape[1]
    ctf = contrast(defocus_blk, fourier, box)
    weighted = ctf[:, :, None, :] * image_blk.astype(jnp.float32).reshape(
        count, fourier, 2, fourier
    )
    real_u = weighted[:, None, :, 0]
    imag_u = weighted[:, None, :, 1]
    chosen = panels[list_blk].astype(jnp.float32).reshape(count, picks, fourier, 2, fourier)
    real_p = chosen[:, :, :, 0]
    imag_p = chosen[:, :, :, 1]
    product = jnp.stack(
        [real_p * real_u + imag_p * imag_u, real_p * imag_u - imag_p * real_u], axis=3
    )
    product = product.astype(jnp.bfloat16).reshape(count * picks, 2 * fourier * fourier)
    scores = jnp.dot(product, phase_fwd, preferred_element_type=jnp.float32) / fourier
    scores = scores.reshape(count, picks * shifts)
    squared = scores * scores
    weights = squared / (jnp.mean(squared, axis=1, keepdims=True) + 1e-05)
    rounded = weights.astype(jnp.bfloat16).reshape(count * picks, shifts)
    spread = jnp.dot(rounded, phase_back, preferred_element_type=jnp.float32)
    spread = spread.reshape(count, picks, fourier, 2, fourier)
    real_e = spread[:, :, :, 0]
    imag_e = spread[:, :, :, 1]
    backed = jnp.stack(
        [real_u * real_e - imag_u * imag_e, real_u * imag_e + imag_u * real_e], axis=3
    )
    backed = backed.astype(jnp.bfloat16).reshape(count * picks, 2 * fourier * fourier)
    return (weights, backed)


def _correlate_kernel(orient_ref, row_ref, panels_ref, image_ref, ctf_ref, cos_ref, sin_ref, w_ref, out_ref, acc_ref):
    i = pl.program_id(0)
    mirror = cos_ref.shape[0]
    shifts = 2 * mirror
    picks = w_ref.shape[1] // shifts
    half = ctf_ref.shape[2]

    @pl.when(i == 0)
    def _():
        acc_ref[...] = jnp.zeros_like(acc_ref)

    ctf = ctf_ref[0]
    image = image_ref[0].astype(jnp.float32)
    ur = ctf * image[:, :half]
    ui = ctf * image[:, half:]
    rows = []
    for k in range(picks):
        panel = panels_ref[row_ref[i * picks + k]].astype(jnp.float32)
        pr = panel[:, :half]
        pi = panel[:, half:]
        prod_re = (pr * ur + pi * ui).astype(jnp.bfloat16).astype(jnp.float32)
        prod_im = (pr * ui - pi * ur).astype(jnp.bfloat16).astype(jnp.float32)
        even = []
        odd = []
        for t in range(mirror):
            even.append(jnp.sum(prod_re * cos_ref[t], axis=0, keepdims=True))
            odd.append(jnp.sum(prod_im * sin_ref[t], axis=0, keepdims=True))
        rows.extend(even[t] + odd[t] for t in range(mirror))
        rows.extend(even[shifts - 1 - t] - odd[shifts - 1 - t] for t in range(mirror, shifts))
    scores = jnp.sum(jnp.concatenate(rows, axis=0), axis=1, keepdims=True) / half
    squared = scores * scores
    mean = jnp.sum(squared, axis=0, keepdims=True) / squared.shape[0]
    weights = squared / (mean + 1e-05)
    w_ref[0] = weights
    wround = weights.astype(jnp.bfloat16).astype(jnp.float32)
    for k in range(picks):
        er = jnp.zeros_like(ur)
        ei = jnp.zeros_like(ur)
        for t in range(mirror):
            wt = wround[k * shifts + t : k * shifts + t + 1, :]
            wm = wround[k * shifts + shifts - 1 - t : k * shifts + shifts - t, :]
            er = er + (wt + wm) * cos_ref[t]
            ei = ei - (wt - wm) * sin_ref[t]
        slice_re = (ur * er - ui * ei).astype(jnp.bfloat16).astype(jnp.float32)
        slice_im = (ur * ei + ui * er).astype(jnp.bfloat16).astype(jnp.float32)
        j = row_ref[i * picks + k]
        acc_ref[j, :, :half] += slice_re
        acc_ref[j, :, half:] += slice_im

    @pl.when(i == pl.num_programs(0) - 1)
    def _():
        out_ref[...] = acc_ref[...].astype(out_ref.dtype)


def correlate_all(panels, images, orient, rows, defocus):
    count, fourier, width = images.shape
    picks = orient.shape[1]
    orient_count = panels.shape[0]
    ctf = contrast(defocus, fourier, BOX)
    freq = (jnp.arange(fourier, dtype=jnp.int32) - fourier // 2).astype(jnp.float32)
    shift_steps = jnp.arange(NS // 2, dtype=jnp.int32)
    shift_x = (2 * (shift_steps // grid_side) - (grid_side - 1)).astype(jnp.float32)
    shift_y = (2 * (shift_steps % grid_side) - (grid_side - 1)).astype(jnp.float32)
    angle = 2.0 * math.pi / BOX * (
        freq[None, :, None] * shift_x[:, None, None] + freq[None, None, :] * shift_y[:, None, None]
    )
    cos_t = jnp.cos(angle).astype(jnp.bfloat16).astype(jnp.float32)
    sin_t = jnp.sin(angle).astype(jnp.bfloat16).astype(jnp.float32)
    grid_spec = pltpu.PrefetchScalarGridSpec(
        num_scalar_prefetch=2,
        grid=(count,),
        in_specs=[
            pl.BlockSpec((orient_count, fourier, width), lambda i, o, w: (0, 0, 0)),
            pl.BlockSpec((1, fourier, width), lambda i, o, w: (i, 0, 0)),
            pl.BlockSpec((1, fourier, fourier), lambda i, o, w: (i, 0, 0)),
            pl.BlockSpec((NS // 2, fourier, fourier), lambda i, o, w: (0, 0, 0)),
            pl.BlockSpec((NS // 2, fourier, fourier), lambda i, o, w: (0, 0, 0)),
        ],
        out_specs=[
            pl.BlockSpec((1, picks * NS, 1), lambda i, o, w: (i, 0, 0)),
            pl.BlockSpec((orient_count, fourier, width), lambda i, o, w: (0, 0, 0)),
        ],
        scratch_shapes=[pltpu.VMEM((orient_count, fourier, width), jnp.float32)],
    )
    weights, contrib = pl.pallas_call(
        _correlate_kernel,
        grid_spec=grid_spec,
        out_shape=[
            jax.ShapeDtypeStruct((count, picks * NS, 1), jnp.float32),
            jax.ShapeDtypeStruct((orient_count, fourier, width), jnp.bfloat16),
        ],
        compiler_params=pltpu.CompilerParams(
            dimension_semantics=("arbitrary",), vmem_limit_bytes=56 * 1024 * 1024
        ),
    )(orient.reshape(-1), rows.reshape(-1), panels, images, ctf, cos_t, sin_t)
    return weights.reshape(count, picks * NS), contrib


def _pair_sum_kernel(x_ref, o_ref, own, recv, send_sem, recv_sem, local_sem):
    half = own.shape[0]
    me = lax.axis_index(SLAB[2])
    mate = 1 - me
    where = (lax.axis_index(SLAB[0]), lax.axis_index(SLAB[1]), mate, lax.axis_index("img"))
    mesh_ids = pl.DeviceIdType.MESH
    barrier = pltpu.get_barrier_semaphore()
    pl.semaphore_signal(barrier, inc=1, device_id=where, device_id_type=mesh_ids)
    pl.semaphore_wait(barrier, 1)
    local = pltpu.make_async_copy(x_ref.at[pl.ds(me * half, half)], own, local_sem)
    local.start()
    copy = pltpu.make_async_remote_copy(
        src_ref=x_ref.at[pl.ds(mate * half, half)], dst_ref=recv, send_sem=send_sem,
        recv_sem=recv_sem, device_id=where, device_id_type=mesh_ids,
    )
    copy.start()
    local.wait()
    copy.wait()

    def add(b, carry):
        o_ref[b] = (own[b].astype(jnp.float32) + recv[b].astype(jnp.float32)).astype(o_ref.dtype)
        return carry

    lax.fori_loop(0, half, add, 0)


def pair_sum(x, cid):
    half = x.shape[0] // 2
    return pl.pallas_call(
        _pair_sum_kernel,
        out_shape=jax.ShapeDtypeStruct((half,) + x.shape[1:], x.dtype),
        in_specs=[pl.BlockSpec(memory_space=pl.ANY)],
        out_specs=pl.BlockSpec(memory_space=pltpu.VMEM),
        scratch_shapes=[
            pltpu.VMEM((half,) + x.shape[1:], x.dtype),
            pltpu.VMEM((half,) + x.shape[1:], x.dtype),
            pltpu.SemaphoreType.DMA,
            pltpu.SemaphoreType.DMA,
            pltpu.SemaphoreType.DMA,
        ],
        compiler_params=pltpu.CompilerParams(
            collective_id=cid, has_side_effects=True, vmem_limit_bytes=48 * 1024 * 1024
        ),
    )(x)


def _axis_sum_kernel(axis, x_ref, o_ref, got, send_sems, recv_sems, local_sem):
    count, chunk = got.shape[0], got.shape[1]
    me = lax.axis_index(axis)
    names = SLAB + ("img",)
    coords = [lax.axis_index(a) for a in names]
    at = names.index(axis)
    mesh_ids = pl.DeviceIdType.MESH
    peers = [lax.rem(me + 1 + i, count) for i in range(count - 1)]

    def where(peer):
        return tuple(coords[:at]) + (peer,) + tuple(coords[at + 1:])

    barrier = pltpu.get_barrier_semaphore()
    for peer in peers:
        pl.semaphore_signal(barrier, inc=1, device_id=where(peer), device_id_type=mesh_ids)
    pl.semaphore_wait(barrier, count - 1)

    def part(p):
        return x_ref.at[pl.ds(p * chunk, chunk)]

    local = pltpu.make_async_copy(part(me), got.at[me], local_sem)
    local.start()
    sends = []
    for i, peer in enumerate(peers):
        copy = pltpu.make_async_remote_copy(
            src_ref=part(peer), dst_ref=got.at[me], send_sem=send_sems.at[i], recv_sem=recv_sems.at[me],
            device_id=where(peer), device_id_type=mesh_ids,
        )
        copy.start()
        sends.append(copy)
    for i, peer in enumerate(peers):
        sends[i].wait_send()
        pltpu.make_async_remote_copy(
            src_ref=part(peer), dst_ref=got.at[peer], send_sem=send_sems.at[i], recv_sem=recv_sems.at[peer],
            device_id=where(peer), device_id_type=mesh_ids,
        ).wait_recv()
    local.wait()

    def add(b, carry):
        total = got[0, b].astype(jnp.float32)
        for p in range(1, count):
            total = total + got[p, b].astype(jnp.float32)
        o_ref[b] = total.astype(o_ref.dtype)
        return carry

    lax.fori_loop(0, chunk, add, 0)


def axis_sum(x, axis, cid):
    count = lax.axis_size(axis)
    chunk = x.shape[0] // count
    return pl.pallas_call(
        functools.partial(_axis_sum_kernel, axis),
        out_shape=jax.ShapeDtypeStruct((chunk,) + x.shape[1:], x.dtype),
        in_specs=[pl.BlockSpec(memory_space=pl.ANY)],
        out_specs=pl.BlockSpec(memory_space=pltpu.VMEM),
        scratch_shapes=[
            pltpu.VMEM((count, chunk) + x.shape[1:], x.dtype),
            pltpu.SemaphoreType.DMA((count,)),
            pltpu.SemaphoreType.DMA((count,)),
            pltpu.SemaphoreType.DMA,
        ],
        compiler_params=pltpu.CompilerParams(
            collective_id=cid, has_side_effects=True, vmem_limit_bytes=48 * 1024 * 1024
        ),
    )(x)


def _axis_gather_kernel(axis, x_ref, o_ref, send_sems, recv_sems, local_sem):
    count = o_ref.shape[0]
    me = lax.axis_index(axis)
    names = SLAB + ("img",)
    coords = [lax.axis_index(a) for a in names]
    at = names.index(axis)
    mesh_ids = pl.DeviceIdType.MESH
    peers = [lax.rem(me + 1 + i, count) for i in range(count - 1)]

    def where(peer):
        return tuple(coords[:at]) + (peer,) + tuple(coords[at + 1:])

    barrier = pltpu.get_barrier_semaphore()
    for peer in peers:
        pl.semaphore_signal(barrier, inc=1, device_id=where(peer), device_id_type=mesh_ids)
    pl.semaphore_wait(barrier, count - 1)
    local = pltpu.make_async_copy(x_ref, o_ref.at[me], local_sem)
    local.start()
    sends = []
    for i, peer in enumerate(peers):
        copy = pltpu.make_async_remote_copy(
            src_ref=x_ref, dst_ref=o_ref.at[me], send_sem=send_sems.at[i], recv_sem=recv_sems.at[me],
            device_id=where(peer), device_id_type=mesh_ids,
        )
        copy.start()
        sends.append(copy)
    for i, peer in enumerate(peers):
        sends[i].wait_send()
        pltpu.make_async_remote_copy(
            src_ref=x_ref, dst_ref=o_ref.at[peer], send_sem=send_sems.at[i], recv_sem=recv_sems.at[peer],
            device_id=where(peer), device_id_type=mesh_ids,
        ).wait_recv()
    local.wait()


def axis_gather(x, axis, cid):
    count = lax.axis_size(axis)
    out = pl.pallas_call(
        functools.partial(_axis_gather_kernel, axis),
        out_shape=jax.ShapeDtypeStruct((count,) + x.shape, x.dtype),
        in_specs=[pl.BlockSpec(memory_space=pl.ANY)],
        out_specs=pl.BlockSpec(memory_space=pl.ANY),
        scratch_shapes=[
            pltpu.SemaphoreType.DMA((count,)),
            pltpu.SemaphoreType.DMA((count,)),
            pltpu.SemaphoreType.DMA,
        ],
        compiler_params=pltpu.CompilerParams(collective_id=cid, has_side_effects=True),
    )(x)
    return out.reshape((-1,) + x.shape[1:])


def _pair_gather_kernel(x_ref, o_ref, recv, send_sem, recv_sem, local_sem, move_sem):
    me = lax.axis_index(SLAB[2])
    mate = 1 - me
    where = (lax.axis_index(SLAB[0]), lax.axis_index(SLAB[1]), mate, lax.axis_index("img"))
    mesh_ids = pl.DeviceIdType.MESH
    barrier = pltpu.get_barrier_semaphore()
    pl.semaphore_signal(barrier, inc=1, device_id=where, device_id_type=mesh_ids)
    pl.semaphore_wait(barrier, 1)
    local = pltpu.make_async_copy(x_ref, o_ref.at[me], local_sem)
    local.start()
    copy = pltpu.make_async_remote_copy(
        src_ref=x_ref, dst_ref=recv, send_sem=send_sem,
        recv_sem=recv_sem, device_id=where, device_id_type=mesh_ids,
    )
    copy.start()
    copy.wait()
    move = pltpu.make_async_copy(recv, o_ref.at[mate], move_sem)
    move.start()
    local.wait()
    move.wait()


def pair_gather(x, cid):
    out = pl.pallas_call(
        _pair_gather_kernel,
        out_shape=jax.ShapeDtypeStruct((2,) + x.shape, x.dtype),
        in_specs=[pl.BlockSpec(memory_space=pl.ANY)],
        out_specs=pl.BlockSpec(memory_space=pltpu.VMEM),
        scratch_shapes=[
            pltpu.VMEM(x.shape, x.dtype),
            pltpu.SemaphoreType.DMA,
            pltpu.SemaphoreType.DMA,
            pltpu.SemaphoreType.DMA,
            pltpu.SemaphoreType.DMA,
        ],
        compiler_params=pltpu.CompilerParams(
            collective_id=cid, has_side_effects=True, vmem_limit_bytes=48 * 1024 * 1024
        ),
    )(x)
    return out.reshape((-1,) + x.shape[1:])


def _img_sum_kernel(x_ref, o_ref, gat, qbuf, s1, r1, s2, r2, l1, l2):
    count, rows = gat.shape[0], gat.shape[1]
    me = lax.axis_index("img")
    here = tuple(lax.axis_index(a) for a in SLAB)
    mesh_ids = pl.DeviceIdType.MESH
    barrier = pltpu.get_barrier_semaphore()
    peers = [lax.rem(me + 1 + i, count) for i in range(count - 1)]
    for peer in peers:
        pl.semaphore_signal(barrier, inc=1, device_id=here + (peer,), device_id_type=mesh_ids)
    pl.semaphore_wait(barrier, count - 1)

    def part(p):
        return x_ref.at[pl.ds(pl.multiple_of(p * rows, rows), rows)]

    local = pltpu.make_async_copy(part(me), gat.at[me], l1)
    local.start()
    sends = []
    for i, peer in enumerate(peers):
        copy = pltpu.make_async_remote_copy(
            src_ref=part(peer), dst_ref=gat.at[me], send_sem=s1.at[i], recv_sem=r1.at[me],
            device_id=here + (peer,), device_id_type=mesh_ids,
        )
        copy.start()
        sends.append(copy)
    for i, peer in enumerate(peers):
        sends[i].wait_send()
        pltpu.make_async_remote_copy(
            src_ref=part(peer), dst_ref=gat.at[peer], send_sem=s1.at[i], recv_sem=r1.at[peer],
            device_id=here + (peer,), device_id_type=mesh_ids,
        ).wait_recv()
    local.wait()
    qbuf[...] = jnp.sum(gat[...], axis=0)
    local = pltpu.make_async_copy(qbuf, o_ref.at[me], l2)
    local.start()
    sends = []
    for i, peer in enumerate(peers):
        copy = pltpu.make_async_remote_copy(
            src_ref=qbuf, dst_ref=o_ref.at[me], send_sem=s2.at[i], recv_sem=r2.at[me],
            device_id=here + (peer,), device_id_type=mesh_ids,
        )
        copy.start()
        sends.append(copy)
    for i, peer in enumerate(peers):
        sends[i].wait_send()
        pltpu.make_async_remote_copy(
            src_ref=qbuf, dst_ref=o_ref.at[peer], send_sem=s2.at[i], recv_sem=r2.at[peer],
            device_id=here + (peer,), device_id_type=mesh_ids,
        ).wait_recv()
    local.wait()


def img_sum(x, count, cid):
    rows = x.shape[0] // count
    out = pl.pallas_call(
        _img_sum_kernel,
        out_shape=jax.ShapeDtypeStruct((count, rows) + x.shape[1:], x.dtype),
        in_specs=[pl.BlockSpec(memory_space=pltpu.VMEM)],
        out_specs=pl.BlockSpec(memory_space=pl.ANY),
        scratch_shapes=[
            pltpu.VMEM((count, rows) + x.shape[1:], x.dtype),
            pltpu.VMEM((rows,) + x.shape[1:], x.dtype),
            pltpu.SemaphoreType.DMA((count,)),
            pltpu.SemaphoreType.DMA((count,)),
            pltpu.SemaphoreType.DMA((count,)),
            pltpu.SemaphoreType.DMA((count,)),
            pltpu.SemaphoreType.DMA,
            pltpu.SemaphoreType.DMA,
        ],
        compiler_params=pltpu.CompilerParams(collective_id=cid, has_side_effects=True),
    )(x)
    return out.reshape(x.shape)


def _a2a_kernel(x_ref, o_ref, send_sems, recv_sems, local_sem):
    count = x_ref.shape[0]
    sizes = tuple(lax.axis_size(a) for a in SLAB)
    me = lax.axis_index(SLAB)
    grp = lax.axis_index("img")
    mesh_ids = pl.DeviceIdType.MESH
    barrier = pltpu.get_barrier_semaphore()

    def where(peer):
        return (peer // (sizes[1] * sizes[2]), (peer // sizes[2]) % sizes[1], peer % sizes[2], grp)

    def greet(i, carry):
        pl.semaphore_signal(
            barrier, inc=1, device_id=where(lax.rem(me + 1 + i, count)), device_id_type=mesh_ids
        )
        return carry

    lax.fori_loop(0, count - 1, greet, 0)
    pl.semaphore_wait(barrier, count - 1)
    local = pltpu.make_async_copy(x_ref.at[me], o_ref.at[me], local_sem)
    local.start()

    def outgoing(peer):
        return pltpu.make_async_remote_copy(
            src_ref=x_ref.at[peer],
            dst_ref=o_ref.at[me],
            send_sem=send_sems.at[peer],
            recv_sem=recv_sems.at[me],
            device_id=where(peer),
            device_id_type=mesh_ids,
        )

    def incoming(src):
        return pltpu.make_async_remote_copy(
            src_ref=x_ref.at[src],
            dst_ref=o_ref.at[src],
            send_sem=send_sems.at[src],
            recv_sem=recv_sems.at[src],
            device_id=where(src),
            device_id_type=mesh_ids,
        )

    def send(i, carry):
        outgoing(lax.rem(me + 1 + i, count)).start()
        return carry

    lax.fori_loop(0, count - 1, send, 0)

    def finish(i, carry):
        outgoing(lax.rem(me + 1 + i, count)).wait_send()
        incoming(lax.rem(me + count - 1 - i, count)).wait_recv()
        return carry

    lax.fori_loop(0, count - 1, finish, 0)
    local.wait()


def slab_all_to_all(x, cid):
    count = x.shape[0]
    return pl.pallas_call(
        _a2a_kernel,
        out_shape=jax.ShapeDtypeStruct(x.shape, x.dtype),
        in_specs=[pl.BlockSpec(memory_space=pltpu.VMEM)],
        out_specs=pl.BlockSpec(memory_space=pl.ANY),
        scratch_shapes=[
            pltpu.SemaphoreType.DMA((count,)),
            pltpu.SemaphoreType.DMA((count,)),
            pltpu.SemaphoreType.DMA,
        ],
        compiler_params=pltpu.CompilerParams(collective_id=cid, has_side_effects=True),
    )(x)


def on_device(volume, interp, block_index, images, defocus, orient):
    slab_count = lax.axis_size(SLAB)
    slab_index = lax.axis_index(SLAB)
    orient_count = interp.shape[1]
    ori_dev = orient_count // slab_count
    block_rows = interp.shape[2]
    fourier = images.shape[2]
    block_count = fourier // block_rows
    img_dev = images.shape[1]
    picks = orient.shape[2]
    levels = jnp.arange(block_count, dtype=jnp.int32)
    partial_value = jnp.einsum("jpr,rx->jpx", interp[0], volume, preferred_element_type=jnp.float32)
    owned_idx = lax.dynamic_slice_in_dim(block_index[0], slab_index * ori_dev, ori_dev, 0)
    received = slab_all_to_all(
        partial_value.reshape(slab_count, ori_dev * block_rows, 2 * fourier), 1
    ).reshape(slab_count, ori_dev, block_rows, 2 * fourier)
    place = (owned_idx[:, :, None] == levels).astype(jnp.float32)
    summed = jnp.einsum(
        "osb,sopx->obpx", place, received, precision=lax.Precision.HIGHEST,
        preferred_element_type=jnp.float32,
    ).reshape(ori_dev, fourier, 2 * fourier)
    panels = summed.astype(jnp.bfloat16)
    panels = axis_gather(panels, SLAB[1], 5)
    parts = lax.axis_size(SLAB[0])
    panels = lax.all_to_all(
        jnp.broadcast_to(panels[None], (parts,) + panels.shape),
        SLAB[0], split_axis=0, concat_axis=0, tiled=True,
    ).reshape((-1,) + panels.shape[1:])
    panels = pair_gather(panels, 9)
    sizes = tuple(lax.axis_size(a) for a in SLAB)
    inv_perm = jnp.arange(orient_count, dtype=jnp.int32).reshape(
        (sizes[2], sizes[0], sizes[1], ori_dev)
    ).transpose(1, 2, 0, 3).reshape(-1)
    weights, contrib = correlate_all(panels, images[0], orient[0], inv_perm[orient[0]], defocus[0])
    contrib = pair_sum(contrib, 2)
    contrib = axis_sum(contrib, SLAB[0], 3)
    back_own = axis_sum(contrib, SLAB[1], 4)
    back_own = back_own.reshape(ori_dev, block_count, block_rows, 2 * fourier)
    chosen_back = (owned_idx[:, :, None] == levels).astype(jnp.bfloat16)
    outgoing = jnp.einsum(
        "osb,obpx->sopx", chosen_back, back_own, preferred_element_type=jnp.float32
    )
    outgoing = outgoing.astype(jnp.bfloat16).reshape(slab_count * ori_dev, block_rows, 2 * fourier)
    incoming = slab_all_to_all(outgoing, 8)
    column = jnp.einsum("jpr,jpx->rx", interp[0], incoming, preferred_element_type=jnp.float32)
    summed_cols = img_sum(column, lax.axis_size("img"), 0)
    update = summed_cols / math.sqrt(img_dev * slab_count)
    return (update, weights[None])


def solution(mesh):
    devices = mesh.devices
    cores = 2
    xs = len({d.coords[0] for d in devices.reshape(-1)}) if hasattr(devices.reshape(-1)[0], "coords") else 4
    split = devices.reshape((xs, devices.shape[0] // (xs * cores), cores) + devices.shape[1:])
    fine = jax.sharding.Mesh(split, SLAB + ("img",))
    return jax.shard_map(
        on_device,
        mesh=fine,
        in_specs=(
            P(SLAB, None),
            P("img", None, None, SLAB),
            P("img", None, None),
            P("img", SLAB, None, None),
            P("img", SLAB),
            P("img", SLAB, None),
        ),
        out_specs=(P(SLAB, None), P("img", SLAB, None)),
        check_vma=False,
    )
```

```python
import functools
import math

import jax
import jax.numpy as jnp
from jax import lax
from jax.experimental import pallas as pl
from jax.experimental.pallas import tpu as pltpu
from jax.sharding import PartitionSpec as P

BOX = 256
NS = 16
SLAB = ("sx", "sz", "sc")
STEP = 2


wave_length = 0.0197
aberration = 27000000.0
amplitude = 0.1
grid_side = 4


def phase_tables(fourier, shifts, box):
    freq = (jnp.arange(fourier, dtype=jnp.int32) - fourier // 2).astype(jnp.float32)
    shift_steps = jnp.arange(shifts, dtype=jnp.int32)
    shift_x = (2 * (shift_steps // grid_side) - (grid_side - 1)).astype(jnp.float32)
    shift_y = (2 * (shift_steps % grid_side) - (grid_side - 1)).astype(jnp.float32)
    angle = 2.0 * math.pi / box * (freq[:, None, None] * shift_x + freq[None, :, None] * shift_y)
    forward = jnp.stack([jnp.cos(angle), jnp.sin(angle)], axis=1).reshape(
        2 * fourier * fourier, shifts
    )
    backward = jnp.stack([jnp.cos(angle), -jnp.sin(angle)], axis=1).reshape(
        2 * fourier * fourier, shifts
    )
    return (forward.astype(jnp.bfloat16), backward.T.astype(jnp.bfloat16))


def contrast(defocus_blk, fourier, box):
    freq = (jnp.arange(fourier, dtype=jnp.int32) - fourier // 2).astype(jnp.float32)
    wave_sq = (freq[:, None] * freq[:, None] + freq[None, :] * freq[None, :]) / (box * box)
    phase = math.pi * wave_length * defocus_blk[:, None, None] * wave_sq
    phase = phase - 0.5 * math.pi * aberration * wave_length**3 * wave_sq * wave_sq
    return -(math.sqrt(1.0 - amplitude * amplitude) * jnp.sin(phase) + amplitude * jnp.cos(phase))


def correlate(panels, image_blk, list_blk, defocus_blk, phase_fwd, phase_back, box):
    count = image_blk.shape[0]
    fourier = image_blk.shape[1]
    picks = list_blk.shape[1]
    shifts = phase_fwd.shape[1]
    ctf = contrast(defocus_blk, fourier, box)
    weighted = ctf[:, :, None, :] * image_blk.astype(jnp.float32).reshape(
        count, fourier, 2, fourier
    )
    real_u = weighted[:, None, :, 0]
    imag_u = weighted[:, None, :, 1]
    chosen = panels[list_blk].astype(jnp.float32).reshape(count, picks, fourier, 2, fourier)
    real_p = chosen[:, :, :, 0]
    imag_p = chosen[:, :, :, 1]
    product = jnp.stack(
        [real_p * real_u + imag_p * imag_u, real_p * imag_u - imag_p * real_u], axis=3
    )
    product = product.astype(jnp.bfloat16).reshape(count * picks, 2 * fourier * fourier)
    scores = jnp.dot(product, phase_fwd, preferred_element_type=jnp.float32) / fourier
    scores = scores.reshape(count, picks * shifts)
    squared = scores * scores
    weights = squared / (jnp.mean(squared, axis=1, keepdims=True) + 1e-05)
    rounded = weights.astype(jnp.bfloat16).reshape(count * picks, shifts)
    spread = jnp.dot(rounded, phase_back, preferred_element_type=jnp.float32)
    spread = spread.reshape(count, picks, fourier, 2, fourier)
    real_e = spread[:, :, :, 0]
    imag_e = spread[:, :, :, 1]
    backed = jnp.stack(
        [real_u * real_e - imag_u * imag_e, real_u * imag_e + imag_u * real_e], axis=3
    )
    backed = backed.astype(jnp.bfloat16).reshape(count * picks, 2 * fourier * fourier)
    return (weights, backed)


def _correlate_kernel(orient_ref, row_ref, panels_ref, image_ref, ctf_ref, cos_ref, sin_ref, w_ref, out_ref, acc_ref):
    i = pl.program_id(0)
    mirror = cos_ref.shape[0]
    shifts = 2 * mirror
    picks = w_ref.shape[1] // shifts
    half = ctf_ref.shape[2]

    @pl.when(i == 0)
    def _():
        acc_ref[...] = jnp.zeros_like(acc_ref)

    for m in range(image_ref.shape[0]):
        n = i * image_ref.shape[0] + m
        ctf = ctf_ref[m]
        image = image_ref[m].astype(jnp.float32)
        ur = ctf * image[:, :half]
        ui = ctf * image[:, half:]
        rows = []
        for k in range(picks):
            panel = panels_ref[row_ref[n * picks + k]].astype(jnp.float32)
            pr = panel[:, :half]
            pi = panel[:, half:]
            prod_re = (pr * ur + pi * ui).astype(jnp.bfloat16).astype(jnp.float32)
            prod_im = (pr * ui - pi * ur).astype(jnp.bfloat16).astype(jnp.float32)
            even = []
            odd = []
            for t in range(mirror):
                even.append(jnp.sum(prod_re * cos_ref[t], axis=0, keepdims=True))
                odd.append(jnp.sum(prod_im * sin_ref[t], axis=0, keepdims=True))
            rows.extend(even[t] + odd[t] for t in range(mirror))
            rows.extend(even[shifts - 1 - t] - odd[shifts - 1 - t] for t in range(mirror, shifts))
        scores = jnp.sum(jnp.concatenate(rows, axis=0), axis=1, keepdims=True) / half
        squared = scores * scores
        mean = jnp.sum(squared, axis=0, keepdims=True) / squared.shape[0]
        weights = squared / (mean + 1e-05)
        w_ref[m] = weights
        wround = weights.astype(jnp.bfloat16).astype(jnp.float32)
        for k in range(picks):
            er = jnp.zeros_like(ur)
            ei = jnp.zeros_like(ur)
            for t in range(mirror):
                wt = wround[k * shifts + t : k * shifts + t + 1, :]
                wm = wround[k * shifts + shifts - 1 - t : k * shifts + shifts - t, :]
                er = er + (wt + wm) * cos_ref[t]
                ei = ei - (wt - wm) * sin_ref[t]
            slice_re = (ur * er - ui * ei).astype(jnp.bfloat16).astype(jnp.float32)
            slice_im = (ur * ei + ui * er).astype(jnp.bfloat16).astype(jnp.float32)
            j = row_ref[n * picks + k]
            acc_ref[j, :, :half] += slice_re
            acc_ref[j, :, half:] += slice_im

    @pl.when(i == pl.num_programs(0) - 1)
    def _():
        out_ref[...] = acc_ref[...].astype(out_ref.dtype)


def correlate_all(panels, images, orient, rows, defocus):
    count, fourier, width = images.shape
    picks = orient.shape[1]
    orient_count = panels.shape[0]
    ctf = contrast(defocus, fourier, BOX)
    freq = (jnp.arange(fourier, dtype=jnp.int32) - fourier // 2).astype(jnp.float32)
    shift_steps = jnp.arange(NS // 2, dtype=jnp.int32)
    shift_x = (2 * (shift_steps // grid_side) - (grid_side - 1)).astype(jnp.float32)
    shift_y = (2 * (shift_steps % grid_side) - (grid_side - 1)).astype(jnp.float32)
    angle = 2.0 * math.pi / BOX * (
        freq[None, :, None] * shift_x[:, None, None] + freq[None, None, :] * shift_y[:, None, None]
    )
    cos_t = jnp.cos(angle).astype(jnp.bfloat16).astype(jnp.float32)
    sin_t = jnp.sin(angle).astype(jnp.bfloat16).astype(jnp.float32)
    grid_spec = pltpu.PrefetchScalarGridSpec(
        num_scalar_prefetch=2,
        grid=(count // STEP,),
        in_specs=[
            pl.BlockSpec((orient_count, fourier, width), lambda i, o, w: (0, 0, 0)),
            pl.BlockSpec((STEP, fourier, width), lambda i, o, w: (i, 0, 0)),
            pl.BlockSpec((STEP, fourier, fourier), lambda i, o, w: (i, 0, 0)),
            pl.BlockSpec((NS // 2, fourier, fourier), lambda i, o, w: (0, 0, 0)),
            pl.BlockSpec((NS // 2, fourier, fourier), lambda i, o, w: (0, 0, 0)),
        ],
        out_specs=[
            pl.BlockSpec((STEP, picks * NS, 1), lambda i, o, w: (i, 0, 0)),
            pl.BlockSpec((orient_count, fourier, width), lambda i, o, w: (0, 0, 0)),
        ],
        scratch_shapes=[pltpu.VMEM((orient_count, fourier, width), jnp.float32)],
    )
    weights, contrib = pl.pallas_call(
        _correlate_kernel,
        grid_spec=grid_spec,
        out_shape=[
            jax.ShapeDtypeStruct((count, picks * NS, 1), jnp.float32),
            jax.ShapeDtypeStruct((orient_count, fourier, width), jnp.bfloat16),
        ],
        compiler_params=pltpu.CompilerParams(
            dimension_semantics=("arbitrary",), vmem_limit_bytes=56 * 1024 * 1024
        ),
    )(orient.reshape(-1), rows.reshape(-1), panels, images, ctf, cos_t, sin_t)
    return weights.reshape(count, picks * NS), contrib


def _pair_sum_kernel(x_ref, o_ref, own, recv, send_sem, recv_sem, local_sem):
    half = own.shape[0]
    me = lax.axis_index(SLAB[2])
    mate = 1 - me
    where = (lax.axis_index(SLAB[0]), lax.axis_index(SLAB[1]), mate, lax.axis_index("img"))
    mesh_ids = pl.DeviceIdType.MESH
    barrier = pltpu.get_barrier_semaphore()
    pl.semaphore_signal(barrier, inc=1, device_id=where, device_id_type=mesh_ids)
    pl.semaphore_wait(barrier, 1)
    local = pltpu.make_async_copy(x_ref.at[pl.ds(me * half, half)], own, local_sem)
    local.start()
    copy = pltpu.make_async_remote_copy(
        src_ref=x_ref.at[pl.ds(mate * half, half)], dst_ref=recv, send_sem=send_sem,
        recv_sem=recv_sem, device_id=where, device_id_type=mesh_ids,
    )
    copy.start()
    local.wait()
    copy.wait()

    def add(b, carry):
        o_ref[b] = (own[b].astype(jnp.float32) + recv[b].astype(jnp.float32)).astype(o_ref.dtype)
        return carry

    lax.fori_loop(0, half, add, 0)


def pair_sum(x, cid):
    half = x.shape[0] // 2
    return pl.pallas_call(
        _pair_sum_kernel,
        out_shape=jax.ShapeDtypeStruct((half,) + x.shape[1:], x.dtype),
        in_specs=[pl.BlockSpec(memory_space=pl.ANY)],
        out_specs=pl.BlockSpec(memory_space=pltpu.VMEM),
        scratch_shapes=[
            pltpu.VMEM((half,) + x.shape[1:], x.dtype),
            pltpu.VMEM((half,) + x.shape[1:], x.dtype),
            pltpu.SemaphoreType.DMA,
            pltpu.SemaphoreType.DMA,
            pltpu.SemaphoreType.DMA,
        ],
        compiler_params=pltpu.CompilerParams(
            collective_id=cid, has_side_effects=True, vmem_limit_bytes=48 * 1024 * 1024
        ),
    )(x)


def _axis_sum_kernel(axis, x_ref, o_ref, got, send_sems, recv_sems, local_sem):
    count, chunk = got.shape[0], got.shape[1]
    me = lax.axis_index(axis)
    names = SLAB + ("img",)
    coords = [lax.axis_index(a) for a in names]
    at = names.index(axis)
    mesh_ids = pl.DeviceIdType.MESH
    peers = [lax.rem(me + 1 + i, count) for i in range(count - 1)]

    def where(peer):
        return tuple(coords[:at]) + (peer,) + tuple(coords[at + 1:])

    barrier = pltpu.get_barrier_semaphore()
    for peer in peers:
        pl.semaphore_signal(barrier, inc=1, device_id=where(peer), device_id_type=mesh_ids)
    pl.semaphore_wait(barrier, count - 1)

    def part(p):
        return x_ref.at[pl.ds(p * chunk, chunk)]

    local = pltpu.make_async_copy(part(me), got.at[me], local_sem)
    local.start()
    sends = []
    for i, peer in enumerate(peers):
        copy = pltpu.make_async_remote_copy(
            src_ref=part(peer), dst_ref=got.at[me], send_sem=send_sems.at[i], recv_sem=recv_sems.at[me],
            device_id=where(peer), device_id_type=mesh_ids,
        )
        copy.start()
        sends.append(copy)
    for i, peer in enumerate(peers):
        sends[i].wait_send()
        pltpu.make_async_remote_copy(
            src_ref=part(peer), dst_ref=got.at[peer], send_sem=send_sems.at[i], recv_sem=recv_sems.at[peer],
            device_id=where(peer), device_id_type=mesh_ids,
        ).wait_recv()
    local.wait()

    def add(b, carry):
        total = got[0, b].astype(jnp.float32)
        for p in range(1, count):
            total = total + got[p, b].astype(jnp.float32)
        o_ref[b] = total.astype(o_ref.dtype)
        return carry

    lax.fori_loop(0, chunk, add, 0)


def axis_sum(x, axis, cid):
    count = lax.axis_size(axis)
    chunk = x.shape[0] // count
    return pl.pallas_call(
        functools.partial(_axis_sum_kernel, axis),
        out_shape=jax.ShapeDtypeStruct((chunk,) + x.shape[1:], x.dtype),
        in_specs=[pl.BlockSpec(memory_space=pl.ANY)],
        out_specs=pl.BlockSpec(memory_space=pltpu.VMEM),
        scratch_shapes=[
            pltpu.VMEM((count, chunk) + x.shape[1:], x.dtype),
            pltpu.SemaphoreType.DMA((count,)),
            pltpu.SemaphoreType.DMA((count,)),
            pltpu.SemaphoreType.DMA,
        ],
        compiler_params=pltpu.CompilerParams(
            collective_id=cid, has_side_effects=True, vmem_limit_bytes=48 * 1024 * 1024
        ),
    )(x)


def _axis_gather_kernel(axis, x_ref, o_ref, send_sems, recv_sems, local_sem):
    count = o_ref.shape[0]
    me = lax.axis_index(axis)
    names = SLAB + ("img",)
    coords = [lax.axis_index(a) for a in names]
    at = names.index(axis)
    mesh_ids = pl.DeviceIdType.MESH
    peers = [lax.rem(me + 1 + i, count) for i in range(count - 1)]

    def where(peer):
        return tuple(coords[:at]) + (peer,) + tuple(coords[at + 1:])

    barrier = pltpu.get_barrier_semaphore()
    for peer in peers:
        pl.semaphore_signal(barrier, inc=1, device_id=where(peer), device_id_type=mesh_ids)
    pl.semaphore_wait(barrier, count - 1)
    local = pltpu.make_async_copy(x_ref, o_ref.at[me], local_sem)
    local.start()
    sends = []
    for i, peer in enumerate(peers):
        copy = pltpu.make_async_remote_copy(
            src_ref=x_ref, dst_ref=o_ref.at[me], send_sem=send_sems.at[i], recv_sem=recv_sems.at[me],
            device_id=where(peer), device_id_type=mesh_ids,
        )
        copy.start()
        sends.append(copy)
    for i, peer in enumerate(peers):
        sends[i].wait_send()
        pltpu.make_async_remote_copy(
            src_ref=x_ref, dst_ref=o_ref.at[peer], send_sem=send_sems.at[i], recv_sem=recv_sems.at[peer],
            device_id=where(peer), device_id_type=mesh_ids,
        ).wait_recv()
    local.wait()


def axis_gather(x, axis, cid):
    count = lax.axis_size(axis)
    out = pl.pallas_call(
        functools.partial(_axis_gather_kernel, axis),
        out_shape=jax.ShapeDtypeStruct((count,) + x.shape, x.dtype),
        in_specs=[pl.BlockSpec(memory_space=pl.ANY)],
        out_specs=pl.BlockSpec(memory_space=pl.ANY),
        scratch_shapes=[
            pltpu.SemaphoreType.DMA((count,)),
            pltpu.SemaphoreType.DMA((count,)),
            pltpu.SemaphoreType.DMA,
        ],
        compiler_params=pltpu.CompilerParams(collective_id=cid, has_side_effects=True),
    )(x)
    return out.reshape((-1,) + x.shape[1:])


def _pair_gather_kernel(x_ref, o_ref, recv, send_sem, recv_sem, local_sem, move_sem):
    me = lax.axis_index(SLAB[2])
    mate = 1 - me
    where = (lax.axis_index(SLAB[0]), lax.axis_index(SLAB[1]), mate, lax.axis_index("img"))
    mesh_ids = pl.DeviceIdType.MESH
    barrier = pltpu.get_barrier_semaphore()
    pl.semaphore_signal(barrier, inc=1, device_id=where, device_id_type=mesh_ids)
    pl.semaphore_wait(barrier, 1)
    local = pltpu.make_async_copy(x_ref, o_ref.at[me], local_sem)
    local.start()
    copy = pltpu.make_async_remote_copy(
        src_ref=x_ref, dst_ref=recv, send_sem=send_sem,
        recv_sem=recv_sem, device_id=where, device_id_type=mesh_ids,
    )
    copy.start()
    copy.wait()
    move = pltpu.make_async_copy(recv, o_ref.at[mate], move_sem)
    move.start()
    local.wait()
    move.wait()


def pair_gather(x, cid):
    out = pl.pallas_call(
        _pair_gather_kernel,
        out_shape=jax.ShapeDtypeStruct((2,) + x.shape, x.dtype),
        in_specs=[pl.BlockSpec(memory_space=pl.ANY)],
        out_specs=pl.BlockSpec(memory_space=pltpu.VMEM),
        scratch_shapes=[
            pltpu.VMEM(x.shape, x.dtype),
            pltpu.SemaphoreType.DMA,
            pltpu.SemaphoreType.DMA,
            pltpu.SemaphoreType.DMA,
            pltpu.SemaphoreType.DMA,
        ],
        compiler_params=pltpu.CompilerParams(
            collective_id=cid, has_side_effects=True, vmem_limit_bytes=48 * 1024 * 1024
        ),
    )(x)
    return out.reshape((-1,) + x.shape[1:])


def _img_sum_kernel(x_ref, o_ref, gat, qbuf, s1, r1, s2, r2, l1, l2):
    count, rows = gat.shape[0], gat.shape[1]
    me = lax.axis_index("img")
    here = tuple(lax.axis_index(a) for a in SLAB)
    mesh_ids = pl.DeviceIdType.MESH
    barrier = pltpu.get_barrier_semaphore()
    peers = [lax.rem(me + 1 + i, count) for i in range(count - 1)]
    for peer in peers:
        pl.semaphore_signal(barrier, inc=1, device_id=here + (peer,), device_id_type=mesh_ids)
    pl.semaphore_wait(barrier, count - 1)

    def part(p):
        return x_ref.at[pl.ds(pl.multiple_of(p * rows, rows), rows)]

    local = pltpu.make_async_copy(part(me), gat.at[me], l1)
    local.start()
    sends = []
    for i, peer in enumerate(peers):
        copy = pltpu.make_async_remote_copy(
            src_ref=part(peer), dst_ref=gat.at[me], send_sem=s1.at[i], recv_sem=r1.at[me],
            device_id=here + (peer,), device_id_type=mesh_ids,
        )
        copy.start()
        sends.append(copy)
    for i, peer in enumerate(peers):
        sends[i].wait_send()
        pltpu.make_async_remote_copy(
            src_ref=part(peer), dst_ref=gat.at[peer], send_sem=s1.at[i], recv_sem=r1.at[peer],
            device_id=here + (peer,), device_id_type=mesh_ids,
        ).wait_recv()
    local.wait()
    qbuf[...] = jnp.sum(gat[...], axis=0)
    local = pltpu.make_async_copy(qbuf, o_ref.at[me], l2)
    local.start()
    sends = []
    for i, peer in enumerate(peers):
        copy = pltpu.make_async_remote_copy(
            src_ref=qbuf, dst_ref=o_ref.at[me], send_sem=s2.at[i], recv_sem=r2.at[me],
            device_id=here + (peer,), device_id_type=mesh_ids,
        )
        copy.start()
        sends.append(copy)
    for i, peer in enumerate(peers):
        sends[i].wait_send()
        pltpu.make_async_remote_copy(
            src_ref=qbuf, dst_ref=o_ref.at[peer], send_sem=s2.at[i], recv_sem=r2.at[peer],
            device_id=here + (peer,), device_id_type=mesh_ids,
        ).wait_recv()
    local.wait()


def img_sum(x, count, cid):
    rows = x.shape[0] // count
    out = pl.pallas_call(
        _img_sum_kernel,
        out_shape=jax.ShapeDtypeStruct((count, rows) + x.shape[1:], x.dtype),
        in_specs=[pl.BlockSpec(memory_space=pltpu.VMEM)],
        out_specs=pl.BlockSpec(memory_space=pl.ANY),
        scratch_shapes=[
            pltpu.VMEM((count, rows) + x.shape[1:], x.dtype),
            pltpu.VMEM((rows,) + x.shape[1:], x.dtype),
            pltpu.SemaphoreType.DMA((count,)),
            pltpu.SemaphoreType.DMA((count,)),
            pltpu.SemaphoreType.DMA((count,)),
            pltpu.SemaphoreType.DMA((count,)),
            pltpu.SemaphoreType.DMA,
            pltpu.SemaphoreType.DMA,
        ],
        compiler_params=pltpu.CompilerParams(collective_id=cid, has_side_effects=True),
    )(x)
    return out.reshape(x.shape)


def _a2a_kernel(x_ref, o_ref, send_sems, recv_sems, local_sem):
    count = x_ref.shape[0]
    sizes = tuple(lax.axis_size(a) for a in SLAB)
    me = lax.axis_index(SLAB)
    grp = lax.axis_index("img")
    mesh_ids = pl.DeviceIdType.MESH
    barrier = pltpu.get_barrier_semaphore()

    def where(peer):
        return (peer // (sizes[1] * sizes[2]), (peer // sizes[2]) % sizes[1], peer % sizes[2], grp)

    def greet(i, carry):
        pl.semaphore_signal(
            barrier, inc=1, device_id=where(lax.rem(me + 1 + i, count)), device_id_type=mesh_ids
        )
        return carry

    lax.fori_loop(0, count - 1, greet, 0)
    pl.semaphore_wait(barrier, count - 1)
    local = pltpu.make_async_copy(x_ref.at[me], o_ref.at[me], local_sem)
    local.start()

    def outgoing(peer):
        return pltpu.make_async_remote_copy(
            src_ref=x_ref.at[peer],
            dst_ref=o_ref.at[me],
            send_sem=send_sems.at[peer],
            recv_sem=recv_sems.at[me],
            device_id=where(peer),
            device_id_type=mesh_ids,
        )

    def incoming(src):
        return pltpu.make_async_remote_copy(
            src_ref=x_ref.at[src],
            dst_ref=o_ref.at[src],
            send_sem=send_sems.at[src],
            recv_sem=recv_sems.at[src],
            device_id=where(src),
            device_id_type=mesh_ids,
        )

    def send(i, carry):
        outgoing(lax.rem(me + 1 + i, count)).start()
        return carry

    lax.fori_loop(0, count - 1, send, 0)

    def finish(i, carry):
        outgoing(lax.rem(me + 1 + i, count)).wait_send()
        incoming(lax.rem(me + count - 1 - i, count)).wait_recv()
        return carry

    lax.fori_loop(0, count - 1, finish, 0)
    local.wait()


def slab_all_to_all(x, cid):
    count = x.shape[0]
    return pl.pallas_call(
        _a2a_kernel,
        out_shape=jax.ShapeDtypeStruct(x.shape, x.dtype),
        in_specs=[pl.BlockSpec(memory_space=pl.ANY)],
        out_specs=pl.BlockSpec(memory_space=pl.ANY),
        scratch_shapes=[
            pltpu.SemaphoreType.DMA((count,)),
            pltpu.SemaphoreType.DMA((count,)),
            pltpu.SemaphoreType.DMA,
        ],
        compiler_params=pltpu.CompilerParams(collective_id=cid, has_side_effects=True),
    )(x)


def on_device(volume, interp, block_index, images, defocus, orient):
    slab_count = lax.axis_size(SLAB)
    slab_index = lax.axis_index(SLAB)
    orient_count = interp.shape[1]
    ori_dev = orient_count // slab_count
    block_rows = interp.shape[2]
    fourier = images.shape[2]
    block_count = fourier // block_rows
    img_dev = images.shape[1]
    picks = orient.shape[2]
    levels = jnp.arange(block_count, dtype=jnp.int32)
    partial_value = jnp.einsum("jpr,rx->jpx", interp[0], volume, preferred_element_type=jnp.float32)
    owned_idx = lax.dynamic_slice_in_dim(block_index[0], slab_index * ori_dev, ori_dev, 0)
    received = slab_all_to_all(
        partial_value.reshape(slab_count, ori_dev * block_rows, 2 * fourier), 1
    ).reshape(slab_count, ori_dev, block_rows, 2 * fourier)
    place = (owned_idx[:, :, None] == levels).astype(jnp.float32)
    summed = jnp.einsum(
        "osb,sopx->obpx", place, received, precision=lax.Precision.HIGHEST,
        preferred_element_type=jnp.float32,
    ).reshape(ori_dev, fourier, 2 * fourier)
    panels = summed.astype(jnp.bfloat16)
    panels = axis_gather(panels, SLAB[1], 5)
    parts = lax.axis_size(SLAB[0])
    panels = lax.all_to_all(
        jnp.broadcast_to(panels[None], (parts,) + panels.shape),
        SLAB[0], split_axis=0, concat_axis=0, tiled=True,
    ).reshape((-1,) + panels.shape[1:])
    panels = pair_gather(panels, 9)
    sizes = tuple(lax.axis_size(a) for a in SLAB)
    inv_perm = jnp.arange(orient_count, dtype=jnp.int32).reshape(
        (sizes[2], sizes[0], sizes[1], ori_dev)
    ).transpose(1, 2, 0, 3).reshape(-1)
    weights, contrib = correlate_all(panels, images[0], orient[0], inv_perm[orient[0]], defocus[0])
    contrib = pair_sum(contrib, 2)
    contrib = axis_sum(contrib, SLAB[0], 3)
    back_own = axis_sum(contrib, SLAB[1], 4)
    back_own = back_own.reshape(ori_dev, block_count, block_rows, 2 * fourier)
    chosen_back = (owned_idx[:, :, None] == levels).astype(jnp.bfloat16)
    outgoing = jnp.einsum(
        "osb,obpx->sopx", chosen_back, back_own, preferred_element_type=jnp.float32
    )
    outgoing = outgoing.astype(jnp.bfloat16).reshape(slab_count * ori_dev, block_rows, 2 * fourier)
    incoming = slab_all_to_all(outgoing, 8)
    column = jnp.einsum("jpr,jpx->rx", interp[0], incoming, preferred_element_type=jnp.float32)
    summed_cols = img_sum(column, lax.axis_size("img"), 0)
    update = summed_cols / math.sqrt(img_dev * slab_count)
    return (update, weights[None])


def solution(mesh):
    devices = mesh.devices
    cores = 2
    xs = len({d.coords[0] for d in devices.reshape(-1)}) if hasattr(devices.reshape(-1)[0], "coords") else 4
    split = devices.reshape((xs, devices.shape[0] // (xs * cores), cores) + devices.shape[1:])
    fine = jax.sharding.Mesh(split, SLAB + ("img",))
    return jax.shard_map(
        on_device,
        mesh=fine,
        in_specs=(
            P(SLAB, None),
            P("img", None, None, SLAB),
            P("img", None, None),
            P("img", SLAB, None, None),
            P("img", SLAB),
            P("img", SLAB, None),
        ),
        out_specs=(P(SLAB, None), P("img", SLAB, None)),
        check_vma=False,
    )
```

```python
import functools
import math

import jax
import jax.numpy as jnp
from jax import lax
from jax.experimental import pallas as pl
from jax.experimental.pallas import tpu as pltpu
from jax.sharding import PartitionSpec as P

BOX = 256
NS = 16
SLAB = ("sx", "sz", "sc")
STEP = 4


wave_length = 0.0197
aberration = 27000000.0
amplitude = 0.1
grid_side = 4


def phase_tables(fourier, shifts, box):
    freq = (jnp.arange(fourier, dtype=jnp.int32) - fourier // 2).astype(jnp.float32)
    shift_steps = jnp.arange(shifts, dtype=jnp.int32)
    shift_x = (2 * (shift_steps // grid_side) - (grid_side - 1)).astype(jnp.float32)
    shift_y = (2 * (shift_steps % grid_side) - (grid_side - 1)).astype(jnp.float32)
    angle = 2.0 * math.pi / box * (freq[:, None, None] * shift_x + freq[None, :, None] * shift_y)
    forward = jnp.stack([jnp.cos(angle), jnp.sin(angle)], axis=1).reshape(
        2 * fourier * fourier, shifts
    )
    backward = jnp.stack([jnp.cos(angle), -jnp.sin(angle)], axis=1).reshape(
        2 * fourier * fourier, shifts
    )
    return (forward.astype(jnp.bfloat16), backward.T.astype(jnp.bfloat16))


def contrast(defocus_blk, fourier, box):
    freq = (jnp.arange(fourier, dtype=jnp.int32) - fourier // 2).astype(jnp.float32)
    wave_sq = (freq[:, None] * freq[:, None] + freq[None, :] * freq[None, :]) / (box * box)
    phase = math.pi * wave_length * defocus_blk[:, None, None] * wave_sq
    phase = phase - 0.5 * math.pi * aberration * wave_length**3 * wave_sq * wave_sq
    return -(math.sqrt(1.0 - amplitude * amplitude) * jnp.sin(phase) + amplitude * jnp.cos(phase))


def correlate(panels, image_blk, list_blk, defocus_blk, phase_fwd, phase_back, box):
    count = image_blk.shape[0]
    fourier = image_blk.shape[1]
    picks = list_blk.shape[1]
    shifts = phase_fwd.shape[1]
    ctf = contrast(defocus_blk, fourier, box)
    weighted = ctf[:, :, None, :] * image_blk.astype(jnp.float32).reshape(
        count, fourier, 2, fourier
    )
    real_u = weighted[:, None, :, 0]
    imag_u = weighted[:, None, :, 1]
    chosen = panels[list_blk].astype(jnp.float32).reshape(count, picks, fourier, 2, fourier)
    real_p = chosen[:, :, :, 0]
    imag_p = chosen[:, :, :, 1]
    product = jnp.stack(
        [real_p * real_u + imag_p * imag_u, real_p * imag_u - imag_p * real_u], axis=3
    )
    product = product.astype(jnp.bfloat16).reshape(count * picks, 2 * fourier * fourier)
    scores = jnp.dot(product, phase_fwd, preferred_element_type=jnp.float32) / fourier
    scores = scores.reshape(count, picks * shifts)
    squared = scores * scores
    weights = squared / (jnp.mean(squared, axis=1, keepdims=True) + 1e-05)
    rounded = weights.astype(jnp.bfloat16).reshape(count * picks, shifts)
    spread = jnp.dot(rounded, phase_back, preferred_element_type=jnp.float32)
    spread = spread.reshape(count, picks, fourier, 2, fourier)
    real_e = spread[:, :, :, 0]
    imag_e = spread[:, :, :, 1]
    backed = jnp.stack(
        [real_u * real_e - imag_u * imag_e, real_u * imag_e + imag_u * real_e], axis=3
    )
    backed = backed.astype(jnp.bfloat16).reshape(count * picks, 2 * fourier * fourier)
    return (weights, backed)


def _correlate_kernel(orient_ref, row_ref, panels_ref, image_ref, ctf_ref, cos_ref, sin_ref, w_ref, out_ref, acc_ref):
    i = pl.program_id(0)
    mirror = cos_ref.shape[0]
    shifts = 2 * mirror
    picks = w_ref.shape[1] // shifts
    half = ctf_ref.shape[2]

    @pl.when(i == 0)
    def _():
        acc_ref[...] = jnp.zeros_like(acc_ref)

    for m in range(image_ref.shape[0]):
        n = i * image_ref.shape[0] + m
        ctf = ctf_ref[m]
        image = image_ref[m].astype(jnp.float32)
        ur = ctf * image[:, :half]
        ui = ctf * image[:, half:]
        rows = []
        for k in range(picks):
            panel = panels_ref[row_ref[n * picks + k]].astype(jnp.float32)
            pr = panel[:, :half]
            pi = panel[:, half:]
            prod_re = (pr * ur + pi * ui).astype(jnp.bfloat16).astype(jnp.float32)
            prod_im = (pr * ui - pi * ur).astype(jnp.bfloat16).astype(jnp.float32)
            even = []
            odd = []
            for t in range(mirror):
                even.append(jnp.sum(prod_re * cos_ref[t], axis=0, keepdims=True))
                odd.append(jnp.sum(prod_im * sin_ref[t], axis=0, keepdims=True))
            rows.extend(even[t] + odd[t] for t in range(mirror))
            rows.extend(even[shifts - 1 - t] - odd[shifts - 1 - t] for t in range(mirror, shifts))
        scores = jnp.sum(jnp.concatenate(rows, axis=0), axis=1, keepdims=True) / half
        squared = scores * scores
        mean = jnp.sum(squared, axis=0, keepdims=True) / squared.shape[0]
        weights = squared / (mean + 1e-05)
        w_ref[m] = weights
        wround = weights.astype(jnp.bfloat16).astype(jnp.float32)
        for k in range(picks):
            er = jnp.zeros_like(ur)
            ei = jnp.zeros_like(ur)
            for t in range(mirror):
                wt = wround[k * shifts + t : k * shifts + t + 1, :]
                wm = wround[k * shifts + shifts - 1 - t : k * shifts + shifts - t, :]
                er = er + (wt + wm) * cos_ref[t]
                ei = ei - (wt - wm) * sin_ref[t]
            slice_re = (ur * er - ui * ei).astype(jnp.bfloat16).astype(jnp.float32)
            slice_im = (ur * ei + ui * er).astype(jnp.bfloat16).astype(jnp.float32)
            j = row_ref[n * picks + k]
            acc_ref[j, :, :half] += slice_re
            acc_ref[j, :, half:] += slice_im

    @pl.when(i == pl.num_programs(0) - 1)
    def _():
        out_ref[...] = acc_ref[...].astype(out_ref.dtype)


def correlate_all(panels, images, orient, rows, defocus):
    count, fourier, width = images.shape
    picks = orient.shape[1]
    orient_count = panels.shape[0]
    ctf = contrast(defocus, fourier, BOX)
    freq = (jnp.arange(fourier, dtype=jnp.int32) - fourier // 2).astype(jnp.float32)
    shift_steps = jnp.arange(NS // 2, dtype=jnp.int32)
    shift_x = (2 * (shift_steps // grid_side) - (grid_side - 1)).astype(jnp.float32)
    shift_y = (2 * (shift_steps % grid_side) - (grid_side - 1)).astype(jnp.float32)
    angle = 2.0 * math.pi / BOX * (
        freq[None, :, None] * shift_x[:, None, None] + freq[None, None, :] * shift_y[:, None, None]
    )
    cos_t = jnp.cos(angle).astype(jnp.bfloat16).astype(jnp.float32)
    sin_t = jnp.sin(angle).astype(jnp.bfloat16).astype(jnp.float32)
    grid_spec = pltpu.PrefetchScalarGridSpec(
        num_scalar_prefetch=2,
        grid=(count // STEP,),
        in_specs=[
            pl.BlockSpec((orient_count, fourier, width), lambda i, o, w: (0, 0, 0)),
            pl.BlockSpec((STEP, fourier, width), lambda i, o, w: (i, 0, 0)),
            pl.BlockSpec((STEP, fourier, fourier), lambda i, o, w: (i, 0, 0)),
            pl.BlockSpec((NS // 2, fourier, fourier), lambda i, o, w: (0, 0, 0)),
            pl.BlockSpec((NS // 2, fourier, fourier), lambda i, o, w: (0, 0, 0)),
        ],
        out_specs=[
            pl.BlockSpec((STEP, picks * NS, 1), lambda i, o, w: (i, 0, 0)),
            pl.BlockSpec((orient_count, fourier, width), lambda i, o, w: (0, 0, 0)),
        ],
        scratch_shapes=[pltpu.VMEM((orient_count, fourier, width), jnp.float32)],
    )
    weights, contrib = pl.pallas_call(
        _correlate_kernel,
        grid_spec=grid_spec,
        out_shape=[
            jax.ShapeDtypeStruct((count, picks * NS, 1), jnp.float32),
            jax.ShapeDtypeStruct((orient_count, fourier, width), jnp.bfloat16),
        ],
        compiler_params=pltpu.CompilerParams(
            dimension_semantics=("arbitrary",), vmem_limit_bytes=56 * 1024 * 1024
        ),
    )(orient.reshape(-1), rows.reshape(-1), panels, images, ctf, cos_t, sin_t)
    return weights.reshape(count, picks * NS), contrib


def _pair_sum_kernel(x_ref, o_ref, own, recv, send_sem, recv_sem, local_sem):
    half = own.shape[0]
    me = lax.axis_index(SLAB[2])
    mate = 1 - me
    where = (lax.axis_index(SLAB[0]), lax.axis_index(SLAB[1]), mate, lax.axis_index("img"))
    mesh_ids = pl.DeviceIdType.MESH
    barrier = pltpu.get_barrier_semaphore()
    pl.semaphore_signal(barrier, inc=1, device_id=where, device_id_type=mesh_ids)
    pl.semaphore_wait(barrier, 1)
    local = pltpu.make_async_copy(x_ref.at[pl.ds(me * half, half)], own, local_sem)
    local.start()
    copy = pltpu.make_async_remote_copy(
        src_ref=x_ref.at[pl.ds(mate * half, half)], dst_ref=recv, send_sem=send_sem,
        recv_sem=recv_sem, device_id=where, device_id_type=mesh_ids,
    )
    copy.start()
    local.wait()
    copy.wait()

    def add(b, carry):
        o_ref[b] = (own[b].astype(jnp.float32) + recv[b].astype(jnp.float32)).astype(o_ref.dtype)
        return carry

    lax.fori_loop(0, half, add, 0)


def pair_sum(x, cid):
    half = x.shape[0] // 2
    return pl.pallas_call(
        _pair_sum_kernel,
        out_shape=jax.ShapeDtypeStruct((half,) + x.shape[1:], x.dtype),
        in_specs=[pl.BlockSpec(memory_space=pl.ANY)],
        out_specs=pl.BlockSpec(memory_space=pltpu.VMEM),
        scratch_shapes=[
            pltpu.VMEM((half,) + x.shape[1:], x.dtype),
            pltpu.VMEM((half,) + x.shape[1:], x.dtype),
            pltpu.SemaphoreType.DMA,
            pltpu.SemaphoreType.DMA,
            pltpu.SemaphoreType.DMA,
        ],
        compiler_params=pltpu.CompilerParams(
            collective_id=cid, has_side_effects=True, vmem_limit_bytes=48 * 1024 * 1024
        ),
    )(x)


def _axis_sum_kernel(axis, x_ref, o_ref, got, send_sems, recv_sems, local_sem):
    count, chunk = got.shape[0], got.shape[1]
    me = lax.axis_index(axis)
    names = SLAB + ("img",)
    coords = [lax.axis_index(a) for a in names]
    at = names.index(axis)
    mesh_ids = pl.DeviceIdType.MESH
    peers = [lax.rem(me + 1 + i, count) for i in range(count - 1)]

    def where(peer):
        return tuple(coords[:at]) + (peer,) + tuple(coords[at + 1:])

    barrier = pltpu.get_barrier_semaphore()
    for peer in peers:
        pl.semaphore_signal(barrier, inc=1, device_id=where(peer), device_id_type=mesh_ids)
    pl.semaphore_wait(barrier, count - 1)

    def part(p):
        return x_ref.at[pl.ds(p * chunk, chunk)]

    local = pltpu.make_async_copy(part(me), got.at[me], local_sem)
    local.start()
    sends = []
    for i, peer in enumerate(peers):
        copy = pltpu.make_async_remote_copy(
            src_ref=part(peer), dst_ref=got.at[me], send_sem=send_sems.at[i], recv_sem=recv_sems.at[me],
            device_id=where(peer), device_id_type=mesh_ids,
        )
        copy.start()
        sends.append(copy)
    for i, peer in enumerate(peers):
        sends[i].wait_send()
        pltpu.make_async_remote_copy(
            src_ref=part(peer), dst_ref=got.at[peer], send_sem=send_sems.at[i], recv_sem=recv_sems.at[peer],
            device_id=where(peer), device_id_type=mesh_ids,
        ).wait_recv()
    local.wait()

    def add(b, carry):
        total = got[0, b].astype(jnp.float32)
        for p in range(1, count):
            total = total + got[p, b].astype(jnp.float32)
        o_ref[b] = total.astype(o_ref.dtype)
        return carry

    lax.fori_loop(0, chunk, add, 0)


def axis_sum(x, axis, cid):
    count = lax.axis_size(axis)
    chunk = x.shape[0] // count
    return pl.pallas_call(
        functools.partial(_axis_sum_kernel, axis),
        out_shape=jax.ShapeDtypeStruct((chunk,) + x.shape[1:], x.dtype),
        in_specs=[pl.BlockSpec(memory_space=pl.ANY)],
        out_specs=pl.BlockSpec(memory_space=pltpu.VMEM),
        scratch_shapes=[
            pltpu.VMEM((count, chunk) + x.shape[1:], x.dtype),
            pltpu.SemaphoreType.DMA((count,)),
            pltpu.SemaphoreType.DMA((count,)),
            pltpu.SemaphoreType.DMA,
        ],
        compiler_params=pltpu.CompilerParams(
            collective_id=cid, has_side_effects=True, vmem_limit_bytes=48 * 1024 * 1024
        ),
    )(x)


def _axis_gather_kernel(axis, x_ref, o_ref, send_sems, recv_sems, local_sem):
    count = o_ref.shape[0]
    me = lax.axis_index(axis)
    names = SLAB + ("img",)
    coords = [lax.axis_index(a) for a in names]
    at = names.index(axis)
    mesh_ids = pl.DeviceIdType.MESH
    peers = [lax.rem(me + 1 + i, count) for i in range(count - 1)]

    def where(peer):
        return tuple(coords[:at]) + (peer,) + tuple(coords[at + 1:])

    barrier = pltpu.get_barrier_semaphore()
    for peer in peers:
        pl.semaphore_signal(barrier, inc=1, device_id=where(peer), device_id_type=mesh_ids)
    pl.semaphore_wait(barrier, count - 1)
    local = pltpu.make_async_copy(x_ref, o_ref.at[me], local_sem)
    local.start()
    sends = []
    for i, peer in enumerate(peers):
        copy = pltpu.make_async_remote_copy(
            src_ref=x_ref, dst_ref=o_ref.at[me], send_sem=send_sems.at[i], recv_sem=recv_sems.at[me],
            device_id=where(peer), device_id_type=mesh_ids,
        )
        copy.start()
        sends.append(copy)
    for i, peer in enumerate(peers):
        sends[i].wait_send()
        pltpu.make_async_remote_copy(
            src_ref=x_ref, dst_ref=o_ref.at[peer], send_sem=send_sems.at[i], recv_sem=recv_sems.at[peer],
            device_id=where(peer), device_id_type=mesh_ids,
        ).wait_recv()
    local.wait()


def axis_gather(x, axis, cid):
    count = lax.axis_size(axis)
    out = pl.pallas_call(
        functools.partial(_axis_gather_kernel, axis),
        out_shape=jax.ShapeDtypeStruct((count,) + x.shape, x.dtype),
        in_specs=[pl.BlockSpec(memory_space=pl.ANY)],
        out_specs=pl.BlockSpec(memory_space=pl.ANY),
        scratch_shapes=[
            pltpu.SemaphoreType.DMA((count,)),
            pltpu.SemaphoreType.DMA((count,)),
            pltpu.SemaphoreType.DMA,
        ],
        compiler_params=pltpu.CompilerParams(collective_id=cid, has_side_effects=True),
    )(x)
    return out.reshape((-1,) + x.shape[1:])


def _pair_gather_kernel(x_ref, o_ref, recv, send_sem, recv_sem, local_sem, move_sem):
    me = lax.axis_index(SLAB[2])
    mate = 1 - me
    where = (lax.axis_index(SLAB[0]), lax.axis_index(SLAB[1]), mate, lax.axis_index("img"))
    mesh_ids = pl.DeviceIdType.MESH
    barrier = pltpu.get_barrier_semaphore()
    pl.semaphore_signal(barrier, inc=1, device_id=where, device_id_type=mesh_ids)
    pl.semaphore_wait(barrier, 1)
    local = pltpu.make_async_copy(x_ref, o_ref.at[me], local_sem)
    local.start()
    copy = pltpu.make_async_remote_copy(
        src_ref=x_ref, dst_ref=recv, send_sem=send_sem,
        recv_sem=recv_sem, device_id=where, device_id_type=mesh_ids,
    )
    copy.start()
    copy.wait()
    move = pltpu.make_async_copy(recv, o_ref.at[mate], move_sem)
    move.start()
    local.wait()
    move.wait()


def pair_gather(x, cid):
    out = pl.pallas_call(
        _pair_gather_kernel,
        out_shape=jax.ShapeDtypeStruct((2,) + x.shape, x.dtype),
        in_specs=[pl.BlockSpec(memory_space=pl.ANY)],
        out_specs=pl.BlockSpec(memory_space=pltpu.VMEM),
        scratch_shapes=[
            pltpu.VMEM(x.shape, x.dtype),
            pltpu.SemaphoreType.DMA,
            pltpu.SemaphoreType.DMA,
            pltpu.SemaphoreType.DMA,
            pltpu.SemaphoreType.DMA,
        ],
        compiler_params=pltpu.CompilerParams(
            collective_id=cid, has_side_effects=True, vmem_limit_bytes=48 * 1024 * 1024
        ),
    )(x)
    return out.reshape((-1,) + x.shape[1:])


def _img_sum_kernel(x_ref, o_ref, gat, qbuf, s1, r1, s2, r2, l1, l2):
    count, rows = gat.shape[0], gat.shape[1]
    me = lax.axis_index("img")
    here = tuple(lax.axis_index(a) for a in SLAB)
    mesh_ids = pl.DeviceIdType.MESH
    barrier = pltpu.get_barrier_semaphore()
    peers = [lax.rem(me + 1 + i, count) for i in range(count - 1)]
    for peer in peers:
        pl.semaphore_signal(barrier, inc=1, device_id=here + (peer,), device_id_type=mesh_ids)
    pl.semaphore_wait(barrier, count - 1)

    def part(p):
        return x_ref.at[pl.ds(pl.multiple_of(p * rows, rows), rows)]

    local = pltpu.make_async_copy(part(me), gat.at[me], l1)
    local.start()
    sends = []
    for i, peer in enumerate(peers):
        copy = pltpu.make_async_remote_copy(
            src_ref=part(peer), dst_ref=gat.at[me], send_sem=s1.at[i], recv_sem=r1.at[me],
            device_id=here + (peer,), device_id_type=mesh_ids,
        )
        copy.start()
        sends.append(copy)
    for i, peer in enumerate(peers):
        sends[i].wait_send()
        pltpu.make_async_remote_copy(
            src_ref=part(peer), dst_ref=gat.at[peer], send_sem=s1.at[i], recv_sem=r1.at[peer],
            device_id=here + (peer,), device_id_type=mesh_ids,
        ).wait_recv()
    local.wait()
    qbuf[...] = jnp.sum(gat[...], axis=0)
    local = pltpu.make_async_copy(qbuf, o_ref.at[me], l2)
    local.start()
    sends = []
    for i, peer in enumerate(peers):
        copy = pltpu.make_async_remote_copy(
            src_ref=qbuf, dst_ref=o_ref.at[me], send_sem=s2.at[i], recv_sem=r2.at[me],
            device_id=here + (peer,), device_id_type=mesh_ids,
        )
        copy.start()
        sends.append(copy)
    for i, peer in enumerate(peers):
        sends[i].wait_send()
        pltpu.make_async_remote_copy(
            src_ref=qbuf, dst_ref=o_ref.at[peer], send_sem=s2.at[i], recv_sem=r2.at[peer],
            device_id=here + (peer,), device_id_type=mesh_ids,
        ).wait_recv()
    local.wait()


def img_sum(x, count, cid):
    rows = x.shape[0] // count
    out = pl.pallas_call(
        _img_sum_kernel,
        out_shape=jax.ShapeDtypeStruct((count, rows) + x.shape[1:], x.dtype),
        in_specs=[pl.BlockSpec(memory_space=pltpu.VMEM)],
        out_specs=pl.BlockSpec(memory_space=pl.ANY),
        scratch_shapes=[
            pltpu.VMEM((count, rows) + x.shape[1:], x.dtype),
            pltpu.VMEM((rows,) + x.shape[1:], x.dtype),
            pltpu.SemaphoreType.DMA((count,)),
            pltpu.SemaphoreType.DMA((count,)),
            pltpu.SemaphoreType.DMA((count,)),
            pltpu.SemaphoreType.DMA((count,)),
            pltpu.SemaphoreType.DMA,
            pltpu.SemaphoreType.DMA,
        ],
        compiler_params=pltpu.CompilerParams(collective_id=cid, has_side_effects=True),
    )(x)
    return out.reshape(x.shape)


def _a2a_kernel(x_ref, o_ref, send_sems, recv_sems, local_sem):
    count = x_ref.shape[0]
    sizes = tuple(lax.axis_size(a) for a in SLAB)
    me = lax.axis_index(SLAB)
    grp = lax.axis_index("img")
    mesh_ids = pl.DeviceIdType.MESH
    barrier = pltpu.get_barrier_semaphore()

    def where(peer):
        return (peer // (sizes[1] * sizes[2]), (peer // sizes[2]) % sizes[1], peer % sizes[2], grp)

    def greet(i, carry):
        pl.semaphore_signal(
            barrier, inc=1, device_id=where(lax.rem(me + 1 + i, count)), device_id_type=mesh_ids
        )
        return carry

    lax.fori_loop(0, count - 1, greet, 0)
    pl.semaphore_wait(barrier, count - 1)
    local = pltpu.make_async_copy(x_ref.at[me], o_ref.at[me], local_sem)
    local.start()

    def outgoing(peer):
        return pltpu.make_async_remote_copy(
            src_ref=x_ref.at[peer],
            dst_ref=o_ref.at[me],
            send_sem=send_sems.at[peer],
            recv_sem=recv_sems.at[me],
            device_id=where(peer),
            device_id_type=mesh_ids,
        )

    def incoming(src):
        return pltpu.make_async_remote_copy(
            src_ref=x_ref.at[src],
            dst_ref=o_ref.at[src],
            send_sem=send_sems.at[src],
            recv_sem=recv_sems.at[src],
            device_id=where(src),
            device_id_type=mesh_ids,
        )

    def send(i, carry):
        outgoing(lax.rem(me + 1 + i, count)).start()
        return carry

    lax.fori_loop(0, count - 1, send, 0)

    def finish(i, carry):
        outgoing(lax.rem(me + 1 + i, count)).wait_send()
        incoming(lax.rem(me + count - 1 - i, count)).wait_recv()
        return carry

    lax.fori_loop(0, count - 1, finish, 0)
    local.wait()


def slab_all_to_all(x, cid):
    count = x.shape[0]
    return pl.pallas_call(
        _a2a_kernel,
        out_shape=jax.ShapeDtypeStruct(x.shape, x.dtype),
        in_specs=[pl.BlockSpec(memory_space=pl.ANY)],
        out_specs=pl.BlockSpec(memory_space=pl.ANY),
        scratch_shapes=[
            pltpu.SemaphoreType.DMA((count,)),
            pltpu.SemaphoreType.DMA((count,)),
            pltpu.SemaphoreType.DMA,
        ],
        compiler_params=pltpu.CompilerParams(collective_id=cid, has_side_effects=True),
    )(x)


def on_device(volume, interp, block_index, images, defocus, orient):
    slab_count = lax.axis_size(SLAB)
    slab_index = lax.axis_index(SLAB)
    orient_count = interp.shape[1]
    ori_dev = orient_count // slab_count
    block_rows = interp.shape[2]
    fourier = images.shape[2]
    block_count = fourier // block_rows
    img_dev = images.shape[1]
    picks = orient.shape[2]
    levels = jnp.arange(block_count, dtype=jnp.int32)
    partial_value = jnp.einsum("jpr,rx->jpx", interp[0], volume, preferred_element_type=jnp.float32)
    owned_idx = lax.dynamic_slice_in_dim(block_index[0], slab_index * ori_dev, ori_dev, 0)
    received = slab_all_to_all(
        partial_value.reshape(slab_count, ori_dev * block_rows, 2 * fourier), 1
    ).reshape(slab_count, ori_dev, block_rows, 2 * fourier)
    place = (owned_idx[:, :, None] == levels).astype(jnp.float32)
    summed = jnp.einsum(
        "osb,sopx->obpx", place, received, precision=lax.Precision.HIGHEST,
        preferred_element_type=jnp.float32,
    ).reshape(ori_dev, fourier, 2 * fourier)
    panels = summed.astype(jnp.bfloat16)
    panels = axis_gather(panels, SLAB[1], 5)
    parts = lax.axis_size(SLAB[0])
    panels = lax.all_to_all(
        jnp.broadcast_to(panels[None], (parts,) + panels.shape),
        SLAB[0], split_axis=0, concat_axis=0, tiled=True,
    ).reshape((-1,) + panels.shape[1:])
    panels = pair_gather(panels, 9)
    sizes = tuple(lax.axis_size(a) for a in SLAB)
    inv_perm = jnp.arange(orient_count, dtype=jnp.int32).reshape(
        (sizes[2], sizes[0], sizes[1], ori_dev)
    ).transpose(1, 2, 0, 3).reshape(-1)
    weights, contrib = correlate_all(panels, images[0], orient[0], inv_perm[orient[0]], defocus[0])
    contrib = pair_sum(contrib, 2)
    contrib = axis_sum(contrib, SLAB[0], 3)
    back_own = axis_sum(contrib, SLAB[1], 4)
    back_own = back_own.reshape(ori_dev, block_count, block_rows, 2 * fourier)
    chosen_back = (owned_idx[:, :, None] == levels).astype(jnp.bfloat16)
    outgoing = jnp.einsum(
        "osb,obpx->sopx", chosen_back, back_own, preferred_element_type=jnp.float32
    )
    outgoing = outgoing.astype(jnp.bfloat16).reshape(slab_count * ori_dev, block_rows, 2 * fourier)
    incoming = slab_all_to_all(outgoing, 8)
    column = jnp.einsum("jpr,jpx->rx", interp[0], incoming, preferred_element_type=jnp.float32)
    summed_cols = img_sum(column, lax.axis_size("img"), 0)
    update = summed_cols / math.sqrt(img_dev * slab_count)
    return (update, weights[None])


def solution(mesh):
    devices = mesh.devices
    cores = 2
    xs = len({d.coords[0] for d in devices.reshape(-1)}) if hasattr(devices.reshape(-1)[0], "coords") else 4
    split = devices.reshape((xs, devices.shape[0] // (xs * cores), cores) + devices.shape[1:])
    fine = jax.sharding.Mesh(split, SLAB + ("img",))
    return jax.shard_map(
        on_device,
        mesh=fine,
        in_specs=(
            P(SLAB, None),
            P("img", None, None, SLAB),
            P("img", None, None),
            P("img", SLAB, None, None),
            P("img", SLAB),
            P("img", SLAB, None),
        ),
        out_specs=(P(SLAB, None), P("img", SLAB, None)),
        check_vma=False,
    )
```

```python
import functools
import math

import jax
import jax.numpy as jnp
from jax import lax
from jax.experimental import pallas as pl
from jax.experimental.pallas import tpu as pltpu
from jax.sharding import PartitionSpec as P

BOX = 256
NS = 16
SLAB = ("sx", "sz", "sc")
STEP = 8


wave_length = 0.0197
aberration = 27000000.0
amplitude = 0.1
grid_side = 4


def phase_tables(fourier, shifts, box):
    freq = (jnp.arange(fourier, dtype=jnp.int32) - fourier // 2).astype(jnp.float32)
    shift_steps = jnp.arange(shifts, dtype=jnp.int32)
    shift_x = (2 * (shift_steps // grid_side) - (grid_side - 1)).astype(jnp.float32)
    shift_y = (2 * (shift_steps % grid_side) - (grid_side - 1)).astype(jnp.float32)
    angle = 2.0 * math.pi / box * (freq[:, None, None] * shift_x + freq[None, :, None] * shift_y)
    forward = jnp.stack([jnp.cos(angle), jnp.sin(angle)], axis=1).reshape(
        2 * fourier * fourier, shifts
    )
    backward = jnp.stack([jnp.cos(angle), -jnp.sin(angle)], axis=1).reshape(
        2 * fourier * fourier, shifts
    )
    return (forward.astype(jnp.bfloat16), backward.T.astype(jnp.bfloat16))


def contrast(defocus_blk, fourier, box):
    freq = (jnp.arange(fourier, dtype=jnp.int32) - fourier // 2).astype(jnp.float32)
    wave_sq = (freq[:, None] * freq[:, None] + freq[None, :] * freq[None, :]) / (box * box)
    phase = math.pi * wave_length * defocus_blk[:, None, None] * wave_sq
    phase = phase - 0.5 * math.pi * aberration * wave_length**3 * wave_sq * wave_sq
    return -(math.sqrt(1.0 - amplitude * amplitude) * jnp.sin(phase) + amplitude * jnp.cos(phase))


def correlate(panels, image_blk, list_blk, defocus_blk, phase_fwd, phase_back, box):
    count = image_blk.shape[0]
    fourier = image_blk.shape[1]
    picks = list_blk.shape[1]
    shifts = phase_fwd.shape[1]
    ctf = contrast(defocus_blk, fourier, box)
    weighted = ctf[:, :, None, :] * image_blk.astype(jnp.float32).reshape(
        count, fourier, 2, fourier
    )
    real_u = weighted[:, None, :, 0]
    imag_u = weighted[:, None, :, 1]
    chosen = panels[list_blk].astype(jnp.float32).reshape(count, picks, fourier, 2, fourier)
    real_p = chosen[:, :, :, 0]
    imag_p = chosen[:, :, :, 1]
    product = jnp.stack(
        [real_p * real_u + imag_p * imag_u, real_p * imag_u - imag_p * real_u], axis=3
    )
    product = product.astype(jnp.bfloat16).reshape(count * picks, 2 * fourier * fourier)
    scores = jnp.dot(product, phase_fwd, preferred_element_type=jnp.float32) / fourier
    scores = scores.reshape(count, picks * shifts)
    squared = scores * scores
    weights = squared / (jnp.mean(squared, axis=1, keepdims=True) + 1e-05)
    rounded = weights.astype(jnp.bfloat16).reshape(count * picks, shifts)
    spread = jnp.dot(rounded, phase_back, preferred_element_type=jnp.float32)
    spread = spread.reshape(count, picks, fourier, 2, fourier)
    real_e = spread[:, :, :, 0]
    imag_e = spread[:, :, :, 1]
    backed = jnp.stack(
        [real_u * real_e - imag_u * imag_e, real_u * imag_e + imag_u * real_e], axis=3
    )
    backed = backed.astype(jnp.bfloat16).reshape(count * picks, 2 * fourier * fourier)
    return (weights, backed)


def _correlate_kernel(orient_ref, row_ref, panels_ref, image_ref, ctf_ref, cos_ref, sin_ref, w_ref, out_ref, acc_ref):
    i = pl.program_id(0)
    mirror = cos_ref.shape[0]
    shifts = 2 * mirror
    picks = w_ref.shape[1] // shifts
    half = ctf_ref.shape[2]

    @pl.when(i == 0)
    def _():
        acc_ref[...] = jnp.zeros_like(acc_ref)

    for m in range(image_ref.shape[0]):
        n = i * image_ref.shape[0] + m
        ctf = ctf_ref[m]
        image = image_ref[m].astype(jnp.float32)
        ur = ctf * image[:, :half]
        ui = ctf * image[:, half:]
        rows = []
        for k in range(picks):
            panel = panels_ref[row_ref[n * picks + k]].astype(jnp.float32)
            pr = panel[:, :half]
            pi = panel[:, half:]
            prod_re = (pr * ur + pi * ui).astype(jnp.bfloat16).astype(jnp.float32)
            prod_im = (pr * ui - pi * ur).astype(jnp.bfloat16).astype(jnp.float32)
            even = []
            odd = []
            for t in range(mirror):
                even.append(jnp.sum(prod_re * cos_ref[t], axis=0, keepdims=True))
                odd.append(jnp.sum(prod_im * sin_ref[t], axis=0, keepdims=True))
            rows.extend(even[t] + odd[t] for t in range(mirror))
            rows.extend(even[shifts - 1 - t] - odd[shifts - 1 - t] for t in range(mirror, shifts))
        scores = jnp.sum(jnp.concatenate(rows, axis=0), axis=1, keepdims=True) / half
        squared = scores * scores
        mean = jnp.sum(squared, axis=0, keepdims=True) / squared.shape[0]
        weights = squared / (mean + 1e-05)
        w_ref[m] = weights
        wround = weights.astype(jnp.bfloat16).astype(jnp.float32)
        for k in range(picks):
            er = jnp.zeros_like(ur)
            ei = jnp.zeros_like(ur)
            for t in range(mirror):
                wt = wround[k * shifts + t : k * shifts + t + 1, :]
                wm = wround[k * shifts + shifts - 1 - t : k * shifts + shifts - t, :]
                er = er + (wt + wm) * cos_ref[t]
                ei = ei - (wt - wm) * sin_ref[t]
            slice_re = (ur * er - ui * ei).astype(jnp.bfloat16).astype(jnp.float32)
            slice_im = (ur * ei + ui * er).astype(jnp.bfloat16).astype(jnp.float32)
            j = row_ref[n * picks + k]
            acc_ref[j, :, :half] += slice_re
            acc_ref[j, :, half:] += slice_im

    @pl.when(i == pl.num_programs(0) - 1)
    def _():
        out_ref[...] = acc_ref[...].astype(out_ref.dtype)


def correlate_all(panels, images, orient, rows, defocus):
    count, fourier, width = images.shape
    picks = orient.shape[1]
    orient_count = panels.shape[0]
    ctf = contrast(defocus, fourier, BOX)
    freq = (jnp.arange(fourier, dtype=jnp.int32) - fourier // 2).astype(jnp.float32)
    shift_steps = jnp.arange(NS // 2, dtype=jnp.int32)
    shift_x = (2 * (shift_steps // grid_side) - (grid_side - 1)).astype(jnp.float32)
    shift_y = (2 * (shift_steps % grid_side) - (grid_side - 1)).astype(jnp.float32)
    angle = 2.0 * math.pi / BOX * (
        freq[None, :, None] * shift_x[:, None, None] + freq[None, None, :] * shift_y[:, None, None]
    )
    cos_t = jnp.cos(angle).astype(jnp.bfloat16).astype(jnp.float32)
    sin_t = jnp.sin(angle).astype(jnp.bfloat16).astype(jnp.float32)
    grid_spec = pltpu.PrefetchScalarGridSpec(
        num_scalar_prefetch=2,
        grid=(count // STEP,),
        in_specs=[
            pl.BlockSpec((orient_count, fourier, width), lambda i, o, w: (0, 0, 0)),
            pl.BlockSpec((STEP, fourier, width), lambda i, o, w: (i, 0, 0)),
            pl.BlockSpec((STEP, fourier, fourier), lambda i, o, w: (i, 0, 0)),
            pl.BlockSpec((NS // 2, fourier, fourier), lambda i, o, w: (0, 0, 0)),
            pl.BlockSpec((NS // 2, fourier, fourier), lambda i, o, w: (0, 0, 0)),
        ],
        out_specs=[
            pl.BlockSpec((STEP, picks * NS, 1), lambda i, o, w: (i, 0, 0)),
            pl.BlockSpec((orient_count, fourier, width), lambda i, o, w: (0, 0, 0)),
        ],
        scratch_shapes=[pltpu.VMEM((orient_count, fourier, width), jnp.float32)],
    )
    weights, contrib = pl.pallas_call(
        _correlate_kernel,
        grid_spec=grid_spec,
        out_shape=[
            jax.ShapeDtypeStruct((count, picks * NS, 1), jnp.float32),
            jax.ShapeDtypeStruct((orient_count, fourier, width), jnp.bfloat16),
        ],
        compiler_params=pltpu.CompilerParams(
            dimension_semantics=("arbitrary",), vmem_limit_bytes=56 * 1024 * 1024
        ),
    )(orient.reshape(-1), rows.reshape(-1), panels, images, ctf, cos_t, sin_t)
    return weights.reshape(count, picks * NS), contrib


def _pair_sum_kernel(x_ref, o_ref, own, recv, send_sem, recv_sem, local_sem):
    half = own.shape[0]
    me = lax.axis_index(SLAB[2])
    mate = 1 - me
    where = (lax.axis_index(SLAB[0]), lax.axis_index(SLAB[1]), mate, lax.axis_index("img"))
    mesh_ids = pl.DeviceIdType.MESH
    barrier = pltpu.get_barrier_semaphore()
    pl.semaphore_signal(barrier, inc=1, device_id=where, device_id_type=mesh_ids)
    pl.semaphore_wait(barrier, 1)
    local = pltpu.make_async_copy(x_ref.at[pl.ds(me * half, half)], own, local_sem)
    local.start()
    copy = pltpu.make_async_remote_copy(
        src_ref=x_ref.at[pl.ds(mate * half, half)], dst_ref=recv, send_sem=send_sem,
        recv_sem=recv_sem, device_id=where, device_id_type=mesh_ids,
    )
    copy.start()
    local.wait()
    copy.wait()

    def add(b, carry):
        o_ref[b] = (own[b].astype(jnp.float32) + recv[b].astype(jnp.float32)).astype(o_ref.dtype)
        return carry

    lax.fori_loop(0, half, add, 0)


def pair_sum(x, cid):
    half = x.shape[0] // 2
    return pl.pallas_call(
        _pair_sum_kernel,
        out_shape=jax.ShapeDtypeStruct((half,) + x.shape[1:], x.dtype),
        in_specs=[pl.BlockSpec(memory_space=pl.ANY)],
        out_specs=pl.BlockSpec(memory_space=pltpu.VMEM),
        scratch_shapes=[
            pltpu.VMEM((half,) + x.shape[1:], x.dtype),
            pltpu.VMEM((half,) + x.shape[1:], x.dtype),
            pltpu.SemaphoreType.DMA,
            pltpu.SemaphoreType.DMA,
            pltpu.SemaphoreType.DMA,
        ],
        compiler_params=pltpu.CompilerParams(
            collective_id=cid, has_side_effects=True, vmem_limit_bytes=48 * 1024 * 1024
        ),
    )(x)


def _axis_sum_kernel(axis, x_ref, o_ref, got, send_sems, recv_sems, local_sem):
    count, chunk = got.shape[0], got.shape[1]
    me = lax.axis_index(axis)
    names = SLAB + ("img",)
    coords = [lax.axis_index(a) for a in names]
    at = names.index(axis)
    mesh_ids = pl.DeviceIdType.MESH
    peers = [lax.rem(me + 1 + i, count) for i in range(count - 1)]

    def where(peer):
        return tuple(coords[:at]) + (peer,) + tuple(coords[at + 1:])

    barrier = pltpu.get_barrier_semaphore()
    for peer in peers:
        pl.semaphore_signal(barrier, inc=1, device_id=where(peer), device_id_type=mesh_ids)
    pl.semaphore_wait(barrier, count - 1)

    def part(p):
        return x_ref.at[pl.ds(p * chunk, chunk)]

    local = pltpu.make_async_copy(part(me), got.at[me], local_sem)
    local.start()
    sends = []
    for i, peer in enumerate(peers):
        copy = pltpu.make_async_remote_copy(
            src_ref=part(peer), dst_ref=got.at[me], send_sem=send_sems.at[i], recv_sem=recv_sems.at[me],
            device_id=where(peer), device_id_type=mesh_ids,
        )
        copy.start()
        sends.append(copy)
    for i, peer in enumerate(peers):
        sends[i].wait_send()
        pltpu.make_async_remote_copy(
            src_ref=part(peer), dst_ref=got.at[peer], send_sem=send_sems.at[i], recv_sem=recv_sems.at[peer],
            device_id=where(peer), device_id_type=mesh_ids,
        ).wait_recv()
    local.wait()

    def add(b, carry):
        total = got[0, b].astype(jnp.float32)
        for p in range(1, count):
            total = total + got[p, b].astype(jnp.float32)
        o_ref[b] = total.astype(o_ref.dtype)
        return carry

    lax.fori_loop(0, chunk, add, 0)


def axis_sum(x, axis, cid):
    count = lax.axis_size(axis)
    chunk = x.shape[0] // count
    return pl.pallas_call(
        functools.partial(_axis_sum_kernel, axis),
        out_shape=jax.ShapeDtypeStruct((chunk,) + x.shape[1:], x.dtype),
        in_specs=[pl.BlockSpec(memory_space=pl.ANY)],
        out_specs=pl.BlockSpec(memory_space=pltpu.VMEM),
        scratch_shapes=[
            pltpu.VMEM((count, chunk) + x.shape[1:], x.dtype),
            pltpu.SemaphoreType.DMA((count,)),
            pltpu.SemaphoreType.DMA((count,)),
            pltpu.SemaphoreType.DMA,
        ],
        compiler_params=pltpu.CompilerParams(
            collective_id=cid, has_side_effects=True, vmem_limit_bytes=48 * 1024 * 1024
        ),
    )(x)


def _axis_gather_kernel(axis, x_ref, o_ref, send_sems, recv_sems, local_sem):
    count = o_ref.shape[0]
    me = lax.axis_index(axis)
    names = SLAB + ("img",)
    coords = [lax.axis_index(a) for a in names]
    at = names.index(axis)
    mesh_ids = pl.DeviceIdType.MESH
    peers = [lax.rem(me + 1 + i, count) for i in range(count - 1)]

    def where(peer):
        return tuple(coords[:at]) + (peer,) + tuple(coords[at + 1:])

    barrier = pltpu.get_barrier_semaphore()
    for peer in peers:
        pl.semaphore_signal(barrier, inc=1, device_id=where(peer), device_id_type=mesh_ids)
    pl.semaphore_wait(barrier, count - 1)
    local = pltpu.make_async_copy(x_ref, o_ref.at[me], local_sem)
    local.start()
    sends = []
    for i, peer in enumerate(peers):
        copy = pltpu.make_async_remote_copy(
            src_ref=x_ref, dst_ref=o_ref.at[me], send_sem=send_sems.at[i], recv_sem=recv_sems.at[me],
            device_id=where(peer), device_id_type=mesh_ids,
        )
        copy.start()
        sends.append(copy)
    for i, peer in enumerate(peers):
        sends[i].wait_send()
        pltpu.make_async_remote_copy(
            src_ref=x_ref, dst_ref=o_ref.at[peer], send_sem=send_sems.at[i], recv_sem=recv_sems.at[peer],
            device_id=where(peer), device_id_type=mesh_ids,
        ).wait_recv()
    local.wait()


def axis_gather(x, axis, cid):
    count = lax.axis_size(axis)
    out = pl.pallas_call(
        functools.partial(_axis_gather_kernel, axis),
        out_shape=jax.ShapeDtypeStruct((count,) + x.shape, x.dtype),
        in_specs=[pl.BlockSpec(memory_space=pl.ANY)],
        out_specs=pl.BlockSpec(memory_space=pl.ANY),
        scratch_shapes=[
            pltpu.SemaphoreType.DMA((count,)),
            pltpu.SemaphoreType.DMA((count,)),
            pltpu.SemaphoreType.DMA,
        ],
        compiler_params=pltpu.CompilerParams(collective_id=cid, has_side_effects=True),
    )(x)
    return out.reshape((-1,) + x.shape[1:])


def _pair_gather_kernel(x_ref, o_ref, recv, send_sem, recv_sem, local_sem, move_sem):
    me = lax.axis_index(SLAB[2])
    mate = 1 - me
    where = (lax.axis_index(SLAB[0]), lax.axis_index(SLAB[1]), mate, lax.axis_index("img"))
    mesh_ids = pl.DeviceIdType.MESH
    barrier = pltpu.get_barrier_semaphore()
    pl.semaphore_signal(barrier, inc=1, device_id=where, device_id_type=mesh_ids)
    pl.semaphore_wait(barrier, 1)
    local = pltpu.make_async_copy(x_ref, o_ref.at[me], local_sem)
    local.start()
    copy = pltpu.make_async_remote_copy(
        src_ref=x_ref, dst_ref=recv, send_sem=send_sem,
        recv_sem=recv_sem, device_id=where, device_id_type=mesh_ids,
    )
    copy.start()
    copy.wait()
    move = pltpu.make_async_copy(recv, o_ref.at[mate], move_sem)
    move.start()
    local.wait()
    move.wait()


def pair_gather(x, cid):
    out = pl.pallas_call(
        _pair_gather_kernel,
        out_shape=jax.ShapeDtypeStruct((2,) + x.shape, x.dtype),
        in_specs=[pl.BlockSpec(memory_space=pl.ANY)],
        out_specs=pl.BlockSpec(memory_space=pltpu.VMEM),
        scratch_shapes=[
            pltpu.VMEM(x.shape, x.dtype),
            pltpu.SemaphoreType.DMA,
            pltpu.SemaphoreType.DMA,
            pltpu.SemaphoreType.DMA,
            pltpu.SemaphoreType.DMA,
        ],
        compiler_params=pltpu.CompilerParams(
            collective_id=cid, has_side_effects=True, vmem_limit_bytes=48 * 1024 * 1024
        ),
    )(x)
    return out.reshape((-1,) + x.shape[1:])


def _img_sum_kernel(x_ref, o_ref, gat, qbuf, s1, r1, s2, r2, l1, l2):
    count, rows = gat.shape[0], gat.shape[1]
    me = lax.axis_index("img")
    here = tuple(lax.axis_index(a) for a in SLAB)
    mesh_ids = pl.DeviceIdType.MESH
    barrier = pltpu.get_barrier_semaphore()
    peers = [lax.rem(me + 1 + i, count) for i in range(count - 1)]
    for peer in peers:
        pl.semaphore_signal(barrier, inc=1, device_id=here + (peer,), device_id_type=mesh_ids)
    pl.semaphore_wait(barrier, count - 1)

    def part(p):
        return x_ref.at[pl.ds(pl.multiple_of(p * rows, rows), rows)]

    local = pltpu.make_async_copy(part(me), gat.at[me], l1)
    local.start()
    sends = []
    for i, peer in enumerate(peers):
        copy = pltpu.make_async_remote_copy(
            src_ref=part(peer), dst_ref=gat.at[me], send_sem=s1.at[i], recv_sem=r1.at[me],
            device_id=here + (peer,), device_id_type=mesh_ids,
        )
        copy.start()
        sends.append(copy)
    for i, peer in enumerate(peers):
        sends[i].wait_send()
        pltpu.make_async_remote_copy(
            src_ref=part(peer), dst_ref=gat.at[peer], send_sem=s1.at[i], recv_sem=r1.at[peer],
            device_id=here + (peer,), device_id_type=mesh_ids,
        ).wait_recv()
    local.wait()
    qbuf[...] = jnp.sum(gat[...], axis=0)
    local = pltpu.make_async_copy(qbuf, o_ref.at[me], l2)
    local.start()
    sends = []
    for i, peer in enumerate(peers):
        copy = pltpu.make_async_remote_copy(
            src_ref=qbuf, dst_ref=o_ref.at[me], send_sem=s2.at[i], recv_sem=r2.at[me],
            device_id=here + (peer,), device_id_type=mesh_ids,
        )
        copy.start()
        sends.append(copy)
    for i, peer in enumerate(peers):
        sends[i].wait_send()
        pltpu.make_async_remote_copy(
            src_ref=qbuf, dst_ref=o_ref.at[peer], send_sem=s2.at[i], recv_sem=r2.at[peer],
            device_id=here + (peer,), device_id_type=mesh_ids,
        ).wait_recv()
    local.wait()


def img_sum(x, count, cid):
    rows = x.shape[0] // count
    out = pl.pallas_call(
        _img_sum_kernel,
        out_shape=jax.ShapeDtypeStruct((count, rows) + x.shape[1:], x.dtype),
        in_specs=[pl.BlockSpec(memory_space=pltpu.VMEM)],
        out_specs=pl.BlockSpec(memory_space=pl.ANY),
        scratch_shapes=[
            pltpu.VMEM((count, rows) + x.shape[1:], x.dtype),
            pltpu.VMEM((rows,) + x.shape[1:], x.dtype),
            pltpu.SemaphoreType.DMA((count,)),
            pltpu.SemaphoreType.DMA((count,)),
            pltpu.SemaphoreType.DMA((count,)),
            pltpu.SemaphoreType.DMA((count,)),
            pltpu.SemaphoreType.DMA,
            pltpu.SemaphoreType.DMA,
        ],
        compiler_params=pltpu.CompilerParams(collective_id=cid, has_side_effects=True),
    )(x)
    return out.reshape(x.shape)


def _a2a_kernel(x_ref, o_ref, send_sems, recv_sems, local_sem):
    count = x_ref.shape[0]
    sizes = tuple(lax.axis_size(a) for a in SLAB)
    me = lax.axis_index(SLAB)
    grp = lax.axis_index("img")
    mesh_ids = pl.DeviceIdType.MESH
    barrier = pltpu.get_barrier_semaphore()

    def where(peer):
        return (peer // (sizes[1] * sizes[2]), (peer // sizes[2]) % sizes[1], peer % sizes[2], grp)

    def greet(i, carry):
        pl.semaphore_signal(
            barrier, inc=1, device_id=where(lax.rem(me + 1 + i, count)), device_id_type=mesh_ids
        )
        return carry

    lax.fori_loop(0, count - 1, greet, 0)
    pl.semaphore_wait(barrier, count - 1)
    local = pltpu.make_async_copy(x_ref.at[me], o_ref.at[me], local_sem)
    local.start()

    def outgoing(peer):
        return pltpu.make_async_remote_copy(
            src_ref=x_ref.at[peer],
            dst_ref=o_ref.at[me],
            send_sem=send_sems.at[peer],
            recv_sem=recv_sems.at[me],
            device_id=where(peer),
            device_id_type=mesh_ids,
        )

    def incoming(src):
        return pltpu.make_async_remote_copy(
            src_ref=x_ref.at[src],
            dst_ref=o_ref.at[src],
            send_sem=send_sems.at[src],
            recv_sem=recv_sems.at[src],
            device_id=where(src),
            device_id_type=mesh_ids,
        )

    def send(i, carry):
        outgoing(lax.rem(me + 1 + i, count)).start()
        return carry

    lax.fori_loop(0, count - 1, send, 0)

    def finish(i, carry):
        outgoing(lax.rem(me + 1 + i, count)).wait_send()
        incoming(lax.rem(me + count - 1 - i, count)).wait_recv()
        return carry

    lax.fori_loop(0, count - 1, finish, 0)
    local.wait()


def slab_all_to_all(x, cid):
    count = x.shape[0]
    return pl.pallas_call(
        _a2a_kernel,
        out_shape=jax.ShapeDtypeStruct(x.shape, x.dtype),
        in_specs=[pl.BlockSpec(memory_space=pl.ANY)],
        out_specs=pl.BlockSpec(memory_space=pl.ANY),
        scratch_shapes=[
            pltpu.SemaphoreType.DMA((count,)),
            pltpu.SemaphoreType.DMA((count,)),
            pltpu.SemaphoreType.DMA,
        ],
        compiler_params=pltpu.CompilerParams(collective_id=cid, has_side_effects=True),
    )(x)


def on_device(volume, interp, block_index, images, defocus, orient):
    slab_count = lax.axis_size(SLAB)
    slab_index = lax.axis_index(SLAB)
    orient_count = interp.shape[1]
    ori_dev = orient_count // slab_count
    block_rows = interp.shape[2]
    fourier = images.shape[2]
    block_count = fourier // block_rows
    img_dev = images.shape[1]
    picks = orient.shape[2]
    levels = jnp.arange(block_count, dtype=jnp.int32)
    partial_value = jnp.einsum("jpr,rx->jpx", interp[0], volume, preferred_element_type=jnp.float32)
    owned_idx = lax.dynamic_slice_in_dim(block_index[0], slab_index * ori_dev, ori_dev, 0)
    received = slab_all_to_all(
        partial_value.reshape(slab_count, ori_dev * block_rows, 2 * fourier), 1
    ).reshape(slab_count, ori_dev, block_rows, 2 * fourier)
    place = (owned_idx[:, :, None] == levels).astype(jnp.float32)
    summed = jnp.einsum(
        "osb,sopx->obpx", place, received, precision=lax.Precision.HIGHEST,
        preferred_element_type=jnp.float32,
    ).reshape(ori_dev, fourier, 2 * fourier)
    panels = summed.astype(jnp.bfloat16)
    panels = axis_gather(panels, SLAB[1], 5)
    parts = lax.axis_size(SLAB[0])
    panels = lax.all_to_all(
        jnp.broadcast_to(panels[None], (parts,) + panels.shape),
        SLAB[0], split_axis=0, concat_axis=0, tiled=True,
    ).reshape((-1,) + panels.shape[1:])
    panels = pair_gather(panels, 9)
    sizes = tuple(lax.axis_size(a) for a in SLAB)
    inv_perm = jnp.arange(orient_count, dtype=jnp.int32).reshape(
        (sizes[2], sizes[0], sizes[1], ori_dev)
    ).transpose(1, 2, 0, 3).reshape(-1)
    weights, contrib = correlate_all(panels, images[0], orient[0], inv_perm[orient[0]], defocus[0])
    contrib = pair_sum(contrib, 2)
    contrib = axis_sum(contrib, SLAB[0], 3)
    back_own = axis_sum(contrib, SLAB[1], 4)
    back_own = back_own.reshape(ori_dev, block_count, block_rows, 2 * fourier)
    chosen_back = (owned_idx[:, :, None] == levels).astype(jnp.bfloat16)
    outgoing = jnp.einsum(
        "osb,obpx->sopx", chosen_back, back_own, preferred_element_type=jnp.float32
    )
    outgoing = outgoing.astype(jnp.bfloat16).reshape(slab_count * ori_dev, block_rows, 2 * fourier)
    incoming = slab_all_to_all(outgoing, 8)
    column = jnp.einsum("jpr,jpx->rx", interp[0], incoming, preferred_element_type=jnp.float32)
    summed_cols = img_sum(column, lax.axis_size("img"), 0)
    update = summed_cols / math.sqrt(img_dev * slab_count)
    return (update, weights[None])


def solution(mesh):
    devices = mesh.devices
    cores = 2
    xs = len({d.coords[0] for d in devices.reshape(-1)}) if hasattr(devices.reshape(-1)[0], "coords") else 4
    split = devices.reshape((xs, devices.shape[0] // (xs * cores), cores) + devices.shape[1:])
    fine = jax.sharding.Mesh(split, SLAB + ("img",))
    return jax.shard_map(
        on_device,
        mesh=fine,
        in_specs=(
            P(SLAB, None),
            P("img", None, None, SLAB),
            P("img", None, None),
            P("img", SLAB, None, None),
            P("img", SLAB),
            P("img", SLAB, None),
        ),
        out_specs=(P(SLAB, None), P("img", SLAB, None)),
        check_vma=False,
    )
```
